32 devices in a mesh: dp: 4 (over y, x), expert: 4 (over z), context: 2 (over core).
Axes of the slice: x: 2, y: 2, z: 4, core: 2. Of those that a mesh axis runs over, the one named last changes fastest.
Arguments:
- inputs: bfloat16 [48, 592, 512], P(('dp', 'expert'), 'context'), may hold values from -6 to 6
- key_mask: int32 [48, 592], P(('dp', 'expert')), may hold values from 0 to 1, as said below
- routes: int32 [16, 2, 888, 2], P(('dp', 'expert'), 'context'), may hold values from 0 to 7, all different within a row; in each aligned block of 888 rows (0 to 887, 888 to 1775, ..., all dimensions but the last counted through in order) at most 666 rows name the same one
- priority: int32 [16, 2, 888], P(('dp', 'expert'), 'context'), may hold values from 0 to 65535
- vectors: float32 [7, 512], P(None, 'dp'), may hold values from -1 to 2.1, as said below
- w_qkv: float32 [512, 1536], P('dp'), may hold values from -0.25 to 0.25
- w_out: float32 [512, 512], P('dp'), may hold values from -1.5 to 1.5
- w_router: float32 [512, 8], P('dp'), may hold values from -0.1875 to 0.1875
- w_in: float32 [8, 512, 2048], P('expert', 'dp'), may hold values from -0.25 to 0.25
- b_in: float32 [8, 2048], P('expert', 'dp'), may hold values from -3 to 3
- w_back: float32 [8, 2048, 512], P('expert', 'dp'), may hold values from -2 to 2
- b_back: float32 [8, 512], P('expert', 'dp'), may hold values from -6 to 6
- cotangent: bfloat16 [48, 592, 512], P(('dp', 'expert'), 'context'), may hold values from -6 to 6
Outputs:
- output: bfloat16 [48, 592, 512], P(('dp', 'expert'), 'context')
- grad_inputs: bfloat16 [48, 592, 512], P(('dp', 'expert'), 'context')
- grad_vectors: float32 [7, 512], P(None, 'dp')
- grad_w_qkv: float32 [512, 1536], P('dp')
- grad_w_out: float32 [512, 512], P('dp')
- grad_w_router: float32 [512, 8], P('dp')
- grad_w_in: float32 [8, 512, 2048], P('expert', 'dp')
- grad_b_in: float32 [8, 2048], P('expert', 'dp')
- grad_w_back: float32 [8, 2048, 512], P('expert', 'dp')
- grad_b_back: float32 [8, 512], P('expert', 'dp')
The draws below stay inside these ranges and needn't reach their ends.
Inputs may be any that keep to these rules, and one draw needn't show every extreme that they name: `key_mask`: each image's row is 1 on its first L positions and 0 after, with L from three quarters of 577, rounded down, to 577; some image has L = 577. `routes`: each row names two different experts and every expert is named; among the rows of one device no expert is named by more than 666 rows, a bound that some block reaches. `vectors`: rows 0 and 5 are positive.
All inputs are finite; a program needn't handle non-finite values.
Results may differ from the reference program's by a relative error of at most 0.02.
Values may be sent and summed in bfloat16 or wider, within the bound.
A program may use at most 256 MiB of HBM per device.

```python
import math
from functools import partial
import jax
import jax.numpy as jnp
import numpy as np
from jax import lax

D = 512
HEADS = 8
HEAD_DIM = 64
FF = 2048
SEQ = 592
VALID = 577
IMG = 3
EXPERTS = 8
GROUPS = 16
BATCH = 48
HALF = 296
TOK_DEV = 888
CAP = 333
MOST = 666
N_CONTEXT = 2


def draw_vectors(key, part):
    gain_key, bias_key = jax.random.split(key)
    biases = jnp.clip(jax.random.normal(bias_key, (7, D), jnp.float32) * 0.2, -1.0, 1.0)
    gains = jax.random.uniform(gain_key, (7, D), jnp.float32, 0.5, 1.5)
    rows_iota = jnp.arange(7)[:, None]
    return jnp.where((rows_iota == 0) | (rows_iota == 5), gains, biases)


def draw_key_mask(key, part):
    lengths = jax.random.randint(key, (BATCH,), 3 * VALID // 4, VALID + 1)
    lengths = lengths.at[0].set(VALID)
    return (jnp.arange(SEQ)[None, :] < lengths[:, None]).astype(jnp.int32)


def touch_ends(values, stream_key, smallest, high):
    shape = values.shape
    place = [jax.random.randint(jax.random.fold_in(stream_key, axis), (), 0, shape[axis]) for axis in range(len(shape))]
    values = values.at[tuple(place)].set(smallest)
    longest = shape.index(max(shape))
    place[longest] = (place[longest] + 1) % shape[longest]
    return values.at[tuple(place)].set(high)


def steps_of(rng, extent, cuts, smallest, high):
    factor_of, own = 1.0, jax.random.fold_in(rng, 6)
    for axis_at, shards_of in cuts:
        steps = jnp.exp(jax.random.uniform(jax.random.fold_in(own, axis_at), (shards_of,), jnp.float32, smallest / len(cuts), high / len(cuts)))
        factor_of = factor_of * jnp.repeat(steps, extent[axis_at] // shards_of).reshape([-1 if axis == axis_at else 1 for axis in range(len(extent))])
    return factor_of


def deal_out(rng, own, number, rows, number_of, top, most, skew):
    sequence = jax.random.permutation(rng, number_of)
    heavy_load, usual = portions_of(number_of, rows * top, most, skew, True), portions_of(number_of, rows * top, most, skew, False)
    places = jnp.arange(number_of)

    def named(sizes, turn):
        used = int((sizes > 0).sum())
        fixed = max(1, used // 4)
        moved = fixed + (places - fixed + turn * (used - fixed)) % max(1, number_of - fixed)
        return jnp.zeros((number_of,), jnp.int32).at[sequence[jnp.where(places < fixed, places, moved)]].set(jnp.asarray(sizes, jnp.int32))

    sizes = jnp.where(number % 4 == 0, named(heavy_load, number // 4), named(usual, number - number // 4 - 1))
    mixed = jax.random.permutation(jax.random.fold_in(own, 3), number_of)
    source_of, sink = mixed[0:number_of // 2 * 2:2], mixed[1:number_of // 2 * 2:2]
    room = jnp.minimum(sizes[source_of] - 1, most - sizes[sink]) // 2
    room = jnp.where((source_of == sequence[0]) | (sink == sequence[0]) | (sizes[sink] == 0), 0, jnp.maximum(room, 0))
    moved = jax.random.randint(jax.random.fold_in(own, 4), (number_of // 2,), 0, 1 << 20) % (room + 1)
    sizes = sizes.at[source_of].add(-moved).at[sink].add(moved)
    members = jnp.searchsorted(jnp.cumsum(sizes), jnp.arange(rows * top), side="right").astype(jnp.int32)
    grid = members.reshape(top, rows).T
    grid = grid[jax.random.permutation(jax.random.fold_in(own, 1), rows)]
    turn = jax.random.randint(jax.random.fold_in(own, 2), (rows, 1), 0, top)
    return jnp.take_along_axis(grid, (jnp.arange(top)[None, :] + turn) % top, axis=1)


def portions_of(amount, total, reach, lean, full):
    portions = [(1 << 20) // math.isqrt(standing ** lean) + 1 for standing in range(1, amount + 1)]
    largest = reach if full else min(reach, max(-(-total // amount), total * portions[0] // sum(portions)))
    least = 1 if total - largest >= amount - 1 else 0
    counts, spare = [largest] + [least] * (amount - 1), total - largest - least * (amount - 1)
    while spare > 0:
        movable = [i for i in range(1, amount) if counts[i] < largest] or [i for i in range(1, amount) if counts[i] < reach]
        pool, left = sum([portions[i] for i in movable]), spare
        for i in movable:
            extra = min(reach - counts[i], max(1, left * portions[i] // pool), spare)
            counts[i] = counts[i] + extra
            spare = spare - extra
    return np.array(counts)


def gaussian(rng, dims, spread, reach, pieces=(), kind=jnp.bfloat16):
    entries = jax.random.normal(rng, dims, jnp.float32) * spread
    if len(pieces) > 0:
        entries = steps_of(rng, dims, pieces, -0.22, 0.18) * entries
    return jnp.clip(entries, min=-reach, max=reach).astype(kind)


def setup_inputs(seed: int = 0) -> dict:
    key_of = jax.random.split(jax.random.key(seed), 14)
    inputs = gaussian(key_of[0], (BATCH, SEQ, D), 1.0, 6.0, ((0, 16), (1, 2)))
    key_mask = draw_key_mask(jax.random.fold_in(key_of[13], 71), 0)
    routes_keys = jax.random.split(jax.random.fold_in(key_of[2], 1), GROUPS * N_CONTEXT * TOK_DEV // TOK_DEV)
    routes_turns = jax.random.permutation(jax.random.fold_in(key_of[2], 3), GROUPS * N_CONTEXT * TOK_DEV // TOK_DEV)
    routes = jax.vmap(lambda own, number: deal_out(jax.random.fold_in(key_of[2], 2), own, number, TOK_DEV, EXPERTS, 2, MOST, 1))(routes_keys, routes_turns).reshape((GROUPS, N_CONTEXT, TOK_DEV, 2))
    priority = touch_ends(jax.random.randint(key_of[3], (GROUPS, N_CONTEXT, TOK_DEV), 0, 65536), jax.random.fold_in(key_of[3], 1), 0, 65535).astype(jnp.int32)
    vectors = draw_vectors(jax.random.fold_in(key_of[13], 71), 0)
    w_qkv = gaussian(key_of[5], (D, 3 * D), D ** -0.5, 0.25, ((0, 4),), jnp.float32)
    w_out = gaussian(key_of[6], (D, D), (max(1, D // 32)) ** -0.5, 1.5, ((0, 4),), jnp.float32)
    w_router = gaussian(key_of[7], (D, EXPERTS), (2 * D) ** -0.5, 0.1875, ((0, 4),), jnp.float32)
    w_in = gaussian(key_of[8], (EXPERTS, D, FF), D ** -0.5, 0.25, ((0, 4), (1, 4)), jnp.float32)
    b_in = gaussian(key_of[9], (EXPERTS, FF), 0.3, 3.0, ((0, 4), (1, 4)), jnp.float32)
    w_back = gaussian(key_of[10], (EXPERTS, FF, D), (max(1, FF // 256)) ** -0.5, 2.0, ((0, 4), (1, 4)), jnp.float32)
    b_back = gaussian(key_of[11], (EXPERTS, D), 1.0, 6.0, ((0, 4), (1, 4)), jnp.float32)
    cotangent = gaussian(key_of[12], (BATCH, SEQ, D), 1.0, 6.0, ((0, 16), (1, 2)))
    return {"inputs": inputs, "key_mask": key_mask, "routes": routes, "priority": priority, "vectors": vectors, "w_qkv": w_qkv, "w_out": w_out, "w_router": w_router, "w_in": w_in, "b_in": b_in, "w_back": w_back, "b_back": b_back, "cotangent": cotangent}


@jax.custom_vjp
def low(v):
    return lax.optimization_barrier(v.astype(jnp.bfloat16)).astype(jnp.float32)

@jax.custom_vjp
def low_back(v):
    return v

def low_keep(v):
    return (low(v), None)

def low_pass(kept, grad):
    return (grad,)

def back_keep(v):
    return (v, None)

def back_low(kept, grad):
    return (low(grad),)
low.defvjp(low_keep, low_pass)
low_back.defvjp(back_keep, back_low)
EPSILON = 1e-06
HIGHEST = lax.Precision.HIGHEST

def high_dot(left, right):
    return jnp.dot(left, right, precision=HIGHEST, preferred_element_type=jnp.float32)

def layer_norm(values, gain_row, offset_row):
    average = lax.optimization_barrier(jnp.mean(values, axis=-1, keepdims=True))
    centred = values - average
    variance = lax.optimization_barrier(jnp.mean(centred * centred, axis=-1, keepdims=True))
    return centred * lax.rsqrt(variance + EPSILON) * gain_row + offset_row

def attend(block):
    queries, keys_all, values_all, mask_rows = block
    raw_scores = jnp.einsum('iqhd,ikhd->ihqk', queries, keys_all, precision=HIGHEST) * HEAD_DIM ** (-0.5)
    raw_scores = jnp.where(mask_rows[:, None, None, :] > 0, raw_scores, -1e+30)
    attn_probs = jax.nn.softmax(low_back(raw_scores), axis=-1)
    return jnp.einsum('ihqk,ikhd->iqhd', low(attn_probs), values_all, precision=HIGHEST)

def assign(route_rows, prio_rows, expert_count, capacity):
    row_count = route_rows.shape[0]
    order_key = prio_rows * row_count + jnp.arange(row_count, dtype=jnp.int32)
    order = jnp.argsort(order_key)
    inverse = jnp.argsort(order)
    ranked = route_rows[order]
    expert_iota = jnp.arange(expert_count, dtype=jnp.int32)
    first_hot = (ranked[:, 0:1] == expert_iota[None, :]).astype(jnp.int32)
    second_hot = (ranked[:, 1:2] == expert_iota[None, :]).astype(jnp.int32)
    first_rank = lax.optimization_barrier(jnp.sum((jnp.cumsum(first_hot, axis=0) - first_hot) * first_hot, axis=1))
    second_base = jnp.cumsum(second_hot, axis=0) - second_hot + lax.optimization_barrier(jnp.sum(first_hot, axis=0))[None, :]
    second_rank = lax.optimization_barrier(jnp.sum(second_base * second_hot, axis=1))
    ranks = jnp.stack([first_rank, second_rank], axis=1)[inverse].astype(jnp.int32)
    flat_slot = route_rows * capacity + ranks
    return jnp.where(ranks < capacity, flat_slot, expert_count * capacity).astype(jnp.int32)

def dispatch(rows_in, slot_table, expert_count, capacity):
    buffer = jnp.zeros((expert_count * capacity + 1, rows_in.shape[1]), rows_in.dtype)
    buffer = buffer.at[slot_table[:, 0]].set(rows_in).at[slot_table[:, 1]].set(rows_in)
    return buffer[:-1]

def pick_rows(table, slot_table):
    return table[slot_table]

def expert_block(block):
    rows_in, weight_in, bias_in, weight_back, bias_back = block
    pre_act = low_back(high_dot(rows_in, weight_in)) + bias_in
    hidden = low(jax.nn.gelu(pre_act, approximate=False))
    return low(low_back(high_dot(hidden, weight_back) + bias_back))

def to_local(values):
    return values.reshape(GROUPS, IMG, N_CONTEXT, HALF, D).transpose(0, 2, 1, 3, 4).reshape(GROUPS, N_CONTEXT, TOK_DEV, D)

def from_local(values):
    return values.reshape(GROUPS, N_CONTEXT, IMG, HALF, D).transpose(0, 2, 1, 3, 4).reshape(BATCH, SEQ, D)

def forward(params, key_mask, routes, priority):
    inputs, vectors, w_qkv, w_out, w_router, w_in, b_in, w_back, b_back = params
    vec_low = low(vectors)
    qkv_low = low(w_qkv)
    out_low = low(w_out)
    router_low = low(w_router)
    in_low = low(w_in)
    in_bias = low(b_in)
    back_weight = low(w_back)
    back_bias = low(b_back)
    normed = layer_norm(inputs, vec_low[0], vec_low[1])
    acts_one = low(normed).reshape(BATCH * SEQ, D)
    projected = high_dot(acts_one, qkv_low)
    queries = low(low_back(projected[:, :D] + vec_low[2]))
    keys_all = low(low_back(projected[:, D:2 * D]))
    values_all = low(low_back(projected[:, 2 * D:] + vec_low[3]))
    head_shape = (GROUPS, IMG, SEQ, HEADS, HEAD_DIM)
    mixed = lax.map(jax.checkpoint(attend), (queries.reshape(head_shape), keys_all.reshape(head_shape), values_all.reshape(head_shape), key_mask.reshape(GROUPS, IMG, SEQ)))
    mixed = low(low_back(mixed.reshape(BATCH * SEQ, D)))
    branch = low_back(high_dot(mixed, out_low)) + vec_low[4]
    after_attn = inputs + branch.reshape(BATCH, SEQ, D)
    local_rows = to_local(after_attn)
    acts_two = low(layer_norm(local_rows, vec_low[5], vec_low[6]))
    logits = low_back(high_dot(acts_two.reshape(-1, D), router_low)).reshape(GROUPS, N_CONTEXT, TOK_DEV, EXPERTS)
    router_probs = jax.nn.softmax(logits, axis=-1)
    slot_table = jax.vmap(jax.vmap(partial(assign, expert_count=EXPERTS, capacity=CAP)))(routes, priority)
    buffers = low_back(jax.vmap(jax.vmap(partial(dispatch, expert_count=EXPERTS, capacity=CAP)))(acts_two, slot_table))
    device_count = GROUPS * N_CONTEXT
    by_expert = buffers.reshape(device_count, EXPERTS, CAP, D).transpose(1, 0, 2, 3).reshape(EXPERTS, device_count * CAP, D)
    expert_out = lax.map(jax.checkpoint(expert_block), (by_expert, in_low, in_bias, back_weight, back_bias))
    expert_out = expert_out.reshape(EXPERTS, device_count, CAP, D).transpose(1, 0, 2, 3).reshape(GROUPS, N_CONTEXT, EXPERTS * CAP, D)
    padded = jnp.concatenate([expert_out, jnp.zeros((GROUPS, N_CONTEXT, 1, D), jnp.float32)], axis=2)
    picked = jax.vmap(jax.vmap(pick_rows))(padded, slot_table)
    gate_values = jnp.take_along_axis(router_probs, routes, axis=-1)
    mixture = lax.optimization_barrier(jnp.sum(gate_values[..., None] * picked, axis=-2))
    return from_local(local_rows + mixture)

def reference(inputs, key_mask, routes, priority, vectors, w_qkv, w_out, w_router, w_in, b_in, w_back, b_back, cotangent):
    params = (inputs.astype(jnp.float32), vectors, w_qkv, w_out, w_router, w_in, b_in, w_back, b_back)
    result, pullback = jax.vjp(partial(forward, key_mask=key_mask, routes=routes, priority=priority), params)
    grads = pullback(cotangent.astype(jnp.float32))[0]
    return (result.astype(jnp.bfloat16), grads[0].astype(jnp.bfloat16), grads[1], grads[2], grads[3], grads[4], grads[5], grads[6], grads[7], grads[8])
```

```python
from functools import partial

import jax
import jax.numpy as jnp
from jax import lax
from jax.experimental import pallas as pl
from jax.experimental.pallas import tpu as pltpu
from jax.sharding import PartitionSpec as P

HEADS = 8
EPSILON = 1e-06
LANES = 128
BF = jnp.bfloat16
F32 = jnp.float32
I32 = jnp.int32
MIB = 1 << 20


def up(size, unit):
    return -(-size // unit) * unit


def nn(a, b):
    return jnp.dot(a, b, preferred_element_type=F32)


def nt(a, b):
    return lax.dot_general(a, b, (((1,), (1,)), ((), ())), preferred_element_type=F32)


def tn(a, b):
    return lax.dot_general(a, b, (((0,), (0,)), ((), ())), preferred_element_type=F32)


def iota(shape, dim):
    return lax.broadcasted_iota(I32, shape, dim)


def call(body, name, grid, ins, outs, scratch=(), flops=0, moved=0, vmem=56, aliases=None):
    in_specs = [pl.BlockSpec(*spec) if spec else pl.BlockSpec(memory_space=pltpu.VMEM) for spec in ins]
    out_specs = [pl.BlockSpec(*spec) if spec else pl.BlockSpec(memory_space=pltpu.VMEM) for spec, _ in outs]
    return pl.pallas_call(
        body,
        name=name,
        grid=grid,
        in_specs=in_specs,
        out_specs=out_specs,
        out_shape=[jax.ShapeDtypeStruct(*shape) for _, shape in outs],
        scratch_shapes=list(scratch),
        input_output_aliases=aliases or {},
        cost_estimate=pl.CostEstimate(flops=int(flops), bytes_accessed=int(moved), transcendentals=0),
        compiler_params=pltpu.CompilerParams(vmem_limit_bytes=vmem * MIB),
    )


def normed(values):
    average = jnp.mean(values, axis=-1, keepdims=True)
    centred = values - average
    inv_scale = lax.rsqrt(jnp.mean(centred * centred, axis=-1, keepdims=True) + EPSILON)
    return centred * inv_scale, inv_scale


def norm_backward(grad, unit, inv_scale, gain):
    scaled = grad * gain
    centre = jnp.mean(scaled, axis=-1, keepdims=True)
    along = jnp.mean(scaled * unit, axis=-1, keepdims=True)
    return inv_scale * (scaled - centre - unit * along)


def split3(value):
    high = value.astype(BF).astype(F32)
    rest = value - high
    mid = rest.astype(BF).astype(F32)
    return high, mid, rest - mid


def pick(slots, first, rows):
    own = iota((rows, slots.shape[1]), 0) + first
    hit = (own == slots[0:1, :]) | (own == slots[1:2, :])
    return jnp.where(hit, 1.0, 0.0).astype(BF)


def plan_kernel(experts, cap, cap_pad, routes, key_col, key_row, grad, slots, send):
    expert = pl.program_id(0)

    @pl.when(expert == 0)
    def _():
        ids = iota((experts, routes.shape[1]), 0)
        before = jnp.where(key_col[...] < key_row[...], 1.0, 0.0).astype(BF)
        first = jnp.where(routes[0:1, :] == ids, 1.0, 0.0)
        second = jnp.where(routes[1:2, :] == ids, 1.0, 0.0)
        count = jnp.sum(first, axis=1, keepdims=True)
        rank_first = jnp.sum(nn(first.astype(BF), before) * first, axis=0, keepdims=True)
        rank_second = jnp.sum((nn(second.astype(BF), before) + count) * second, axis=0, keepdims=True)
        ranks = jnp.concatenate([rank_first, rank_second], axis=0).astype(I32)
        owned = jnp.where(ranks < cap, routes[...] * cap_pad + ranks, -1)
        slots[...] = jnp.concatenate([owned, jnp.full((6, owned.shape[1]), -1, I32)], axis=0)

    one_hot = pick(slots[...], expert * cap_pad, cap_pad)
    send[0] = nn(one_hot, grad[...]).astype(BF)


def dispatch_kernel(experts, cap, cap_pad, acts, router, routes, slots, send, gates):
    expert = pl.program_id(0)
    tokens, width = acts.shape
    lanes = up(cap_pad, LANES)

    @pl.when(expert == 0)
    def _():
        logits = nt(router[...], acts[...])
        logits = jnp.exp(logits - jnp.max(logits, axis=0, keepdims=True))
        probs = logits / jnp.sum(logits, axis=0, keepdims=True)
        ids = iota((experts, tokens), 0)
        for choice in range(2):
            gate = jnp.sum(jnp.where(routes[choice : choice + 1, :] == ids, probs, 0.0), axis=0, keepdims=True)
            high, mid, low = split3(gate)
            gates[choice] = jnp.concatenate([high, mid, low, jnp.zeros((5, tokens), F32)], axis=0)

    own = iota((lanes, tokens), 0) + expert * cap_pad
    hit_first = own == slots[0:1, :]
    hit_second = own == slots[1:2, :]
    one_first = jnp.where(hit_first, 1.0, 0.0).astype(BF)
    one_second = jnp.where(hit_second, 1.0, 0.0).astype(BF)
    rows = nn((one_first + one_second)[:cap_pad], acts[...])
    gate = nt(gates[0].astype(BF), one_first) + nt(gates[1].astype(BF), one_second)
    gate = jnp.concatenate([gate, jnp.zeros((8, width - lanes), F32)], axis=1)
    at = iota((cap_pad, 1), 0) - cap
    for part in range(3):
        rows = jnp.where(at == part, gate[part : part + 1, :], rows)
    send[0] = rows.astype(BF)


def gelu_parts(z):
    share = 0.5 * (1.0 + lax.erf(z * 0.7071067811865476))
    slope = share + z * (0.3989422804014327 * jnp.exp(-0.5 * z * z))
    return z * share, slope


def expert_kernel(
    cap, chunk, got, got_grad, w_in, b_in, w_back, b_back,
    out_rows, out_back, grad_in, grad_b_in, grad_back, grad_b_back,
    acts, hidden, slope, delta, grad_pre,
):
    groups, cap_pad, width = got.shape
    ff = w_in.shape[1]
    lanes = up(cap_pad, LANES)
    at = iota((cap_pad, 1), 0)
    same = at == iota((1, lanes), 1)
    for src in range(groups):
        rows = pl.ds(src * cap_pad, cap_pad)
        block = got[src]
        acts[rows, :] = jnp.where(at < cap, block.astype(F32), 0.0).astype(BF)
        wide = block.astype(F32)
        gate = wide[cap : cap + 1, :lanes] + wide[cap + 1 : cap + 2, :lanes] + wide[cap + 2 : cap + 3, :lanes]
        gate = jnp.sum(jnp.where(same, gate, 0.0), axis=1, keepdims=True)
        delta[rows, :] = (gate * got_grad[src].astype(F32)).astype(BF)
        for lo in range(0, ff, chunk):
            cols = pl.ds(lo, chunk)
            z = nn(acts[rows, :], w_in[:, cols]) + b_in[:, cols]
            value, rise = gelu_parts(z)
            hidden[rows, cols] = value.astype(BF)
            slope[rows, cols] = rise.astype(BF)
        made = (nn(hidden[rows, :], w_back[...]) + b_back[...]).astype(BF).astype(F32)
        out_rows[src] = (gate * made).astype(BF)
        dot = jnp.sum(made * got_grad[src].astype(F32), axis=1, keepdims=True)
        dot = jnp.sum(jnp.where(same, dot, 0.0), axis=0, keepdims=True)
        parts = split3(jnp.concatenate([dot, jnp.zeros((1, width - lanes), F32)], axis=1))
        for lo in range(0, ff, chunk):
            cols = pl.ds(lo, chunk)
            dz = nt(delta[rows, :], w_back[cols, :]) * slope[rows, cols].astype(F32)
            total = jnp.sum(dz, axis=0, keepdims=True)
            grad_b_in[:, cols] = total if src == 0 else grad_b_in[:, cols] + total
            grad_pre[rows, cols] = dz.astype(BF)
        back = nt(grad_pre[rows, :], w_in[...])
        for part in range(3):
            back = jnp.where(at == cap + part, parts[part], back)
        out_back[src] = back.astype(BF)
    grad_b_back[...] = jnp.sum(delta[...].astype(F32), axis=0, keepdims=True)
    for lo in range(0, ff, chunk):
        cols = pl.ds(lo, chunk)
        grad_back[cols, :] = tn(hidden[:, cols], delta[...]).astype(BF)
        grad_in[:, cols] = tn(acts[...], grad_pre[:, cols]).astype(BF)


def forward_kernel(half, x_own, x_other, bias, vec, w_qkv, w_out, q_ref, k_ref, v_ref, p_ref, o_ref, h_ref, a_ref):
    width = x_own.shape[1]
    half_pad = up(half, 16)
    head_dim = width // HEADS
    scale = head_dim ** (-0.5)
    gain, offset, bias_q, bias_v = (vec[row : row + 1, :] for row in range(4))
    own = x_own[...].astype(F32)
    unit, _ = normed(own)
    acts = (unit * gain + offset).astype(BF)
    unit, _ = normed(x_other[...].astype(F32))
    other = (unit * gain + offset).astype(BF)
    q_ref[...] = ((nn(acts, w_qkv[:, :width]) + bias_q).astype(BF).astype(F32) * scale).astype(BF)
    pad = jnp.zeros((half_pad - half, width), BF)
    for part, rows in enumerate((acts, other)):
        start = part * half_pad
        k_ref[0, pl.ds(start, half), :] = nn(rows, w_qkv[:, width : 2 * width]).astype(BF)
        v_ref[0, pl.ds(start, half), :] = (nn(rows, w_qkv[:, 2 * width :]) + bias_v).astype(BF)
        if half_pad > half:
            k_ref[0, pl.ds(start + half, half_pad - half), :] = pad
            v_ref[0, pl.ds(start + half, half_pad - half), :] = pad
    low = iota((1, LANES), 1) < head_dim
    zero = jnp.zeros((), BF)
    for pair in range(width // LANES):
        cols = pl.ds(pair * LANES, LANES)
        q_pair, k_pair, v_pair = q_ref[:, cols], k_ref[0, :, cols], v_ref[0, :, cols]
        mixed = []
        for sub in range(2):
            mask = low if sub == 0 else jnp.logical_not(low)
            scores = nt(jnp.where(mask, q_pair, zero), k_pair) + bias[0]
            raised = jnp.exp(scores - jnp.max(scores, axis=1, keepdims=True))
            probs = (raised * (1.0 / jnp.sum(raised, axis=1, keepdims=True))).astype(BF)
            p_ref[0, 2 * pair + sub] = probs
            mixed.append(nn(probs, v_pair))
        o_ref[:, cols] = jnp.where(low, mixed[0], mixed[1]).astype(BF)
    after = own + nn(o_ref[...], w_out[...]) + vec[4:5, :]
    h_ref[...] = after
    unit, _ = normed(after)
    a_ref[...] = (unit * vec[5:6, :] + vec[6:7, :]).astype(BF)


def backward_kernel(
    experts, cap, cap_pad, grad, table, slots, h_ref, o_ref, a_ref, router, vec, w_out, q_ref, k_ref, v_ref, p_ref,
    dh_ref, dq_ref, dk_ref, dv_ref, g_out, g_router, g_vec, hits,
):
    image = pl.program_id(0)
    half, width = grad.shape
    head_dim = width // HEADS
    half_pad = up(half, 16)
    lanes = up(cap_pad, LANES)
    lane = iota((1, LANES), 1)
    acts = a_ref[...]
    logits = jnp.where(lane < experts, nn(acts, router[...]), -1e30)
    logits = jnp.exp(logits - jnp.max(logits, axis=1, keepdims=True))
    probs = logits / jnp.sum(logits, axis=1, keepdims=True)
    grad_probs = jnp.zeros((half, LANES), F32)
    first, second = slots[:, 0:1], slots[:, 1:2]
    back = jnp.zeros((half, width), F32)
    for expert in range(experts):
        own = iota((half, lanes), 1)
        own = jnp.where(own < cap_pad, own + expert * cap_pad, -2)
        hit = (own == first) | (own == second)
        one_hot = jnp.where(hit, 1.0, 0.0)
        start = expert * cap_pad
        tail = table[pl.ds(start + cap_pad - 16, 16), :].astype(F32)
        at = cap - (cap_pad - 16)
        dots = tail[at : at + 1, :lanes] + tail[at + 1 : at + 2, :lanes] + tail[at + 2 : at + 3, :lanes]
        dots = jnp.sum(jnp.where(hit, dots, 0.0), axis=1, keepdims=True)
        grad_probs = jnp.where(lane == expert, dots, grad_probs)
        back = back + nn(one_hot[:, :cap_pad].astype(BF), table[pl.ds(start, cap_pad), :])
    inner = jnp.sum(probs * grad_probs, axis=1, keepdims=True)
    grad_logits = (probs * (grad_probs - inner)).astype(BF)
    part_router = tn(acts, grad_logits)
    back = back + nt(grad_logits, router[...])
    unit, inv_scale = normed(h_ref[...])
    out_grad = grad[...].astype(F32)
    dh = out_grad + norm_backward(back, unit, inv_scale, vec[5:6, :])
    dh_ref[...] = dh
    dh_low = dh.astype(BF)
    part_out = tn(o_ref[...], dh_low)
    rows = [
        jnp.sum(dh, axis=0, keepdims=True),
        jnp.sum(back * unit, axis=0, keepdims=True),
        jnp.sum(back, axis=0, keepdims=True),
    ]
    part_vec = jnp.concatenate(rows + [jnp.zeros((5, width), F32)], axis=0)

    @pl.when(image == 0)
    def _():
        g_out[...] = part_out
        g_router[...] = part_router
        g_vec[...] = part_vec

    @pl.when(image > 0)
    def _():
        g_out[...] += part_out
        g_router[...] += part_router
        g_vec[...] += part_vec

    do = nt(dh_low, w_out[...]).astype(BF)
    low = lane < head_dim
    zero = jnp.zeros((), BF)
    scale = head_dim ** (-0.5)
    for pair in range(width // LANES):
        cols = slice(pair * LANES, (pair + 1) * LANES)
        do_pair = do[:, cols]
        q_pair, k_pair, v_pair = q_ref[:, cols], k_ref[0, :, cols], v_ref[0, :, cols]
        dq, dk, dv = [], [], []
        for sub in range(2):
            mask = low if sub == 0 else jnp.logical_not(low)
            p_low = p_ref[0, 2 * pair + sub]
            p = p_low.astype(F32)
            dp = nt(jnp.where(mask, do_pair, zero), v_pair)
            inner = jnp.sum(p * dp, axis=1, keepdims=True)
            ds = (p * (dp - inner)).astype(BF)
            dv.append(tn(p_low, do_pair))
            dk.append(tn(ds, q_pair))
            dq.append(nn(ds, k_pair))
        dq_ref[:, cols] = (jnp.where(low, dq[0], dq[1]) * scale).astype(BF)
        dk_pair = jnp.where(low, dk[0], dk[1]).astype(BF)
        dv_pair = jnp.where(low, dv[0], dv[1]).astype(BF)
        for part in range(2):
            dk_ref[part, :, cols] = dk_pair[part * half_pad : part * half_pad + half]
            dv_ref[part, :, cols] = dv_pair[part * half_pad : part * half_pad + half]


def input_kernel(x_ref, dh_ref, dq_ref, dk_own, dk_got, dv_own, dv_got, vec, w_qkv, dx_ref, g_qkv, g_vec):
    image = pl.program_id(0)
    width = x_ref.shape[1]
    unit, inv_scale = normed(x_ref[...].astype(F32))
    acts = (unit * vec[0:1, :] + vec[1:2, :]).astype(BF)
    dq = dq_ref[...]
    dk = (dk_own[0].astype(F32) + dk_got[...].astype(F32)).astype(BF)
    dv = (dv_own[0].astype(F32) + dv_got[...].astype(F32)).astype(BF)
    da = jnp.zeros(unit.shape, F32)
    parts = []
    for at, piece in enumerate((dq, dk, dv)):
        parts.append(tn(acts, piece))
        da = da + nt(piece, w_qkv[:, at * width : (at + 1) * width])
    dx_ref[...] = (dh_ref[...] + norm_backward(da, unit, inv_scale, vec[0:1, :])).astype(BF)
    rows = [
        jnp.sum(da * unit, axis=0, keepdims=True),
        jnp.sum(da, axis=0, keepdims=True),
        jnp.sum(dq.astype(F32), axis=0, keepdims=True),
        jnp.sum(dv.astype(F32), axis=0, keepdims=True),
    ]
    part_vec = jnp.concatenate(rows + [jnp.zeros((4, width), F32)], axis=0)

    @pl.when(image == 0)
    def _():
        g_vec[...] = part_vec
        for at in range(3):
            g_qkv[:, at * width : (at + 1) * width] = parts[at]

    @pl.when(image > 0)
    def _():
        g_vec[...] += part_vec
        for at in range(3):
            g_qkv[:, at * width : (at + 1) * width] += parts[at]


def combine_kernel(slots, table, h_ref, out_ref):
    half = slots.shape[0]
    total = table.shape[0]
    own = iota((half, total), 1)
    hit = (own == slots[:, 0:1]) | (own == slots[:, 1:2])
    out_ref[...] = (h_ref[...] + nn(jnp.where(hit, 1.0, 0.0).astype(BF), table[...])).astype(BF)


def shards(
    inputs, key_mask, routes, priority, vectors, w_qkv, w_out, w_router, w_in, b_in, w_back, b_back, cotangent
):
    images, half, width = inputs.shape
    tokens = images * half
    groups = lax.axis_size("expert")
    dps = lax.axis_size("dp")
    per_device = w_in.shape[0]
    experts = groups * per_device
    ff = w_in.shape[2]
    cap = max(2, 3 * tokens // experts)
    cap_pad = up(cap + 3, 16)
    half_pad = up(half, 16)
    total = experts * cap_pad
    context = lax.axis_index("context")
    swap = [(0, 1), (1, 0)]

    x = inputs.reshape(tokens, width)
    grad = cotangent.reshape(tokens, width)
    x_other = lax.ppermute(x, "context", swap)

    dense = jnp.concatenate([w_qkv, w_out, w_router, vectors.T], axis=1).astype(BF)
    dense = lax.all_gather(dense, "dp", axis=0, tiled=True)
    qkv_all, out_all = dense[:, : 3 * width], dense[:, 3 * width : 4 * width]
    router_all = dense[:, 4 * width : 4 * width + experts]
    vec = dense[:, 4 * width + experts :].astype(F32).T
    vec = jnp.concatenate([vec, jnp.zeros((1, width), F32)], axis=0)
    router_pad = jnp.concatenate([router_all, jnp.zeros((width, LANES - experts), BF)], axis=1)

    in_w = lax.all_gather(w_in.astype(BF), "dp", axis=1, tiled=True)
    back_w = lax.all_gather(w_back.astype(BF), "dp", axis=1, tiled=True)
    in_b = lax.all_gather(b_in.astype(BF), "dp", axis=1, tiled=True).astype(F32)
    back_b = lax.all_gather(b_back.astype(BF), "dp", axis=1, tiled=True).astype(F32)

    route_rows = routes.reshape(tokens, 2).T
    keys = priority.reshape(tokens) * tokens + jnp.arange(tokens, dtype=I32)
    block = ((1, cap_pad, width), lambda e: (e, 0, 0))
    slots, send_grad = call(
        partial(plan_kernel, experts, cap, cap_pad),
        "plan",
        (experts,),
        [None] * 4,
        [(((8, tokens), lambda e: (0, 0)), ((8, tokens), I32)), (block, ((experts, cap_pad, width), BF))],
        flops=2 * total * tokens * width,
        moved=4 * total * width,
    )(route_rows, keys[:, None], keys[None, :], grad)
    slot_cols = slots.T

    def exchange(rows):
        return lax.all_to_all(rows, "expert", split_axis=0, concat_axis=0, tiled=True)

    def by_expert(rows, which):
        return rows.reshape(groups, per_device, cap_pad, width)[:, which]

    got_grad = [exchange(by_expert(send_grad, which)) for which in range(per_device)]

    mask = jnp.where(key_mask > 0, 0.0, -1e30).astype(F32)
    first, second = mask[:, :half], mask[:, half:]
    own = jnp.where(context == 0, first, second)
    other = jnp.where(context == 0, second, first)
    off = jnp.full((images, half_pad - half), -1e30, F32)
    bias = jnp.concatenate([own, off, other, off], axis=1)[:, None, :]
    keys_pad = 2 * half_pad
    row = ((half, width), lambda i: (i, 0))
    cube = ((1, keys_pad, width), lambda i: (i, 0, 0))
    prob = ((1, HEADS, half, keys_pad), lambda i: (i, 0, 0, 0))
    q, k, v, p, o, after, acts = call(
        partial(forward_kernel, half),
        "forward",
        (images,),
        [row, row, ((1, 1, keys_pad), lambda i: (i, 0, 0)), None, None, None],
        [
            (row, ((tokens, width), BF)),
            (cube, ((images, keys_pad, width), BF)),
            (cube, ((images, keys_pad, width), BF)),
            (prob, ((images, HEADS, half, keys_pad), BF)),
            (row, ((tokens, width), BF)),
            (row, ((tokens, width), F32)),
            (row, ((tokens, width), BF)),
        ],
        flops=2 * tokens * width * (6 * width + 4 * keys_pad),
        moved=20 * tokens * width,
    )(x, x_other, bias, vec, qkv_all, out_all)

    (send_rows,) = call(
        partial(dispatch_kernel, experts, cap, cap_pad),
        "dispatch",
        (experts,),
        [None] * 4,
        [(block, ((experts, cap_pad, width), BF))],
        scratch=[pltpu.VMEM((2, 8, tokens), F32)],
        flops=2 * total * tokens * width,
        moved=4 * total * width,
    )(acts, router_all.T, route_rows, slots)
    got = [exchange(by_expert(send_rows, which)) for which in range(per_device)]

    out_rows, back_rows, g_in, g_b_in, g_back, g_b_back = [], [], [], [], [], []
    slab = (groups, cap_pad, width)
    rows_all = groups * cap_pad
    for which in range(per_device):
        made = call(
            partial(expert_kernel, cap, 512),
            "expert",
            (),
            [None] * 6,
            [
                (None, (slab, BF)),
                (None, (slab, BF)),
                (None, ((width, ff), BF)),
                (None, ((1, ff), F32)),
                (None, ((ff, width), BF)),
                (None, ((1, width), F32)),
            ],
            scratch=[
                pltpu.VMEM((rows_all, width), BF),
                pltpu.VMEM((rows_all, ff), BF),
                pltpu.VMEM((rows_all, ff), BF),
                pltpu.VMEM((rows_all, width), BF),
                pltpu.VMEM((rows_all, ff), BF),
            ],
            flops=12 * rows_all * width * ff,
            moved=8 * rows_all * width + 8 * width * ff,
        )(
            got[which], got_grad[which], in_w[which], in_b[which][None], back_w[which], back_b[which][None]
        )
        for kept, piece in zip((out_rows, back_rows, g_in, g_b_in, g_back, g_b_back), made):
            kept.append(piece)

    def returned(parts):
        moved = [exchange(part) for part in parts]
        return jnp.stack(moved, axis=1).reshape(total, width)

    back_table = returned(back_rows)
    out_table = returned(out_rows)

    def expert_sum(parts):
        share = lax.psum_scatter(jnp.stack(parts), ("dp", "context"), scatter_dimension=1, tiled=True)
        return lax.all_gather(share, "context", axis=1, tiled=True).astype(F32)

    grad_w_in = expert_sum(g_in)
    grad_w_back = expert_sum(g_back)

    halves = ((2, half, width), lambda i: (0, i, 0))
    fixed = lambda i: (0, 0)
    dh, dq, dk, dv, g_out, g_router, g_vec_two = call(
        partial(backward_kernel, experts, cap, cap_pad),
        "backward",
        (images,),
        [row, None, ((half, 8), lambda i: (i, 0)), row, row, row, None, None, None, row, cube, cube, prob],
        [
            (row, ((tokens, width), F32)),
            (row, ((tokens, width), BF)),
            (halves, ((2, tokens, width), BF)),
            (halves, ((2, tokens, width), BF)),
            (((width, width), fixed), ((width, width), F32)),
            (((width, LANES), fixed), ((width, LANES), F32)),
            (((8, width), fixed), ((8, width), F32)),
        ],
        scratch=[pltpu.VMEM((8, LANES), F32)],
        flops=2 * tokens * width * (total + 2 * width + 8 * keys_pad),
        moved=30 * tokens * width,
    )(grad, back_table, slot_cols, after, o, acts, router_pad, vec, out_all, q, k, v, p)

    dk_got = lax.ppermute(dk[1], "context", swap)
    dv_got = lax.ppermute(dv[1], "context", swap)
    own_half = ((1, half, width), lambda i: (0, i, 0))
    dx, g_qkv, g_vec_one = call(
        input_kernel,
        "input",
        (images,),
        [row, row, row, own_half, row, own_half, row, None, None],
        [
            (row, ((tokens, width), BF)),
            (((width, 3 * width), fixed), ((width, 3 * width), F32)),
            (((8, width), fixed), ((8, width), F32)),
        ],
        flops=12 * tokens * width * width,
        moved=20 * tokens * width,
    )(x, dh, dq, dk, dk_got, dv, dv_got, vec, qkv_all)

    (output,) = call(
        combine_kernel,
        "combine",
        (images,),
        [((half, 8), lambda i: (i, 0)), None, row],
        [(row, ((tokens, width), BF))],
        flops=2 * tokens * width * total,
        moved=10 * tokens * width,
    )(slot_cols, out_table, after)

    mine = (jnp.arange(groups) == lax.axis_index("expert")).astype(F32)
    wide_b = jnp.concatenate(g_b_in, axis=0).reshape(per_device, dps, ff // dps)
    wide_b = wide_b.transpose(1, 0, 2).reshape(width, -1)
    b_cols = wide_b.shape[1]
    wide_b = (mine[None, :, None] * wide_b[:, None, :]).reshape(width, groups * b_cols)
    slim_b = jnp.concatenate(g_b_back, axis=0).T
    slim_b = (mine[None, :, None] * slim_b[:, None, :]).reshape(width, experts)
    vec_cols = jnp.concatenate([g_vec_one[:4], g_vec_two[:3]], axis=0).T
    pack = jnp.concatenate([g_qkv, g_out, g_router[:, :experts], vec_cols, wide_b, slim_b], axis=1).astype(BF)
    pack = lax.psum_scatter(pack, "dp", scatter_dimension=0, tiled=True)
    pack = lax.psum(pack, ("expert", "context")).astype(F32)
    cuts = [3 * width, width, experts, 7, groups * b_cols, experts]
    pieces, at = [], 0
    for size in cuts:
        pieces.append(pack[:, at : at + size])
        at += size
    grad_qkv, grad_out, grad_router, grad_vec, wide_b, slim_b = pieces
    group = lax.axis_index("expert")
    wide_b = lax.dynamic_slice_in_dim(wide_b, group * b_cols, b_cols, axis=1)
    grad_b_in = wide_b.reshape(per_device, ff // dps)
    slim_b = lax.dynamic_slice_in_dim(slim_b, group * per_device, per_device, axis=1)
    return (
        output.reshape(images, half, width),
        dx.reshape(images, half, width),
        grad_vec.T,
        grad_qkv,
        grad_out,
        grad_router,
        grad_w_in,
        grad_b_in,
        grad_w_back,
        slim_b.T,
    )


def solution(mesh):
    tokens = P(("dp", "expert"), "context", None)
    by_rows = P("dp", None)
    experts = P("expert", "dp", None)
    expert_bias = P("expert", "dp")
    return jax.shard_map(
        shards,
        mesh=mesh,
        in_specs=(
            tokens,
            P(("dp", "expert"), None),
            P(("dp", "expert"), "context", None, None),
            tokens,
            P(None, "dp"),
            by_rows,
            by_rows,
            by_rows,
            experts,
            expert_bias,
            experts,
            expert_bias,
            tokens,
        ),
        out_specs=(
            tokens,
            tokens,
            P(None, "dp"),
            by_rows,
            by_rows,
            by_rows,
            experts,
            expert_bias,
            experts,
            expert_bias,
        ),
        check_vma=False,
    )
```

```python
from functools import partial

import jax
import jax.numpy as jnp
from jax import lax
from jax.experimental import pallas as pl
from jax.experimental.pallas import tpu as pltpu
from jax.sharding import PartitionSpec as P

HEADS = 8
EPSILON = 1e-06
LANES = 128
BF = jnp.bfloat16
F32 = jnp.float32
I32 = jnp.int32
MIB = 1 << 20


def up(size, unit):
    return -(-size // unit) * unit


def nn(a, b):
    return jnp.dot(a, b, preferred_element_type=F32)


def nt(a, b):
    return lax.dot_general(a, b, (((1,), (1,)), ((), ())), preferred_element_type=F32)


def tn(a, b):
    return lax.dot_general(a, b, (((0,), (0,)), ((), ())), preferred_element_type=F32)


def iota(shape, dim):
    return lax.broadcasted_iota(I32, shape, dim)


def call(body, name, grid, ins, outs, scratch=(), flops=0, moved=0, vmem=56, aliases=None):
    in_specs = [pl.BlockSpec(*spec) if spec else pl.BlockSpec(memory_space=pltpu.VMEM) for spec in ins]
    out_specs = [pl.BlockSpec(*spec) if spec else pl.BlockSpec(memory_space=pltpu.VMEM) for spec, _ in outs]
    return pl.pallas_call(
        body,
        name=name,
        grid=grid,
        in_specs=in_specs,
        out_specs=out_specs,
        out_shape=[jax.ShapeDtypeStruct(*shape) for _, shape in outs],
        scratch_shapes=list(scratch),
        input_output_aliases=aliases or {},
        cost_estimate=pl.CostEstimate(flops=int(flops), bytes_accessed=int(moved), transcendentals=0),
        compiler_params=pltpu.CompilerParams(vmem_limit_bytes=vmem * MIB),
    )


def normed(values):
    average = jnp.mean(values, axis=-1, keepdims=True)
    centred = values - average
    inv_scale = lax.rsqrt(jnp.mean(centred * centred, axis=-1, keepdims=True) + EPSILON)
    return centred * inv_scale, inv_scale


def norm_backward(grad, unit, inv_scale, gain):
    scaled = grad * gain
    centre = jnp.mean(scaled, axis=-1, keepdims=True)
    along = jnp.mean(scaled * unit, axis=-1, keepdims=True)
    return inv_scale * (scaled - centre - unit * along)


def split3(value):
    high = value.astype(BF).astype(F32)
    rest = value - high
    mid = rest.astype(BF).astype(F32)
    return high, mid, rest - mid


def pick(slots, first, rows):
    own = iota((rows, slots.shape[1]), 0) + first
    hit = (own == slots[0:1, :]) | (own == slots[1:2, :])
    return jnp.where(hit, 1.0, 0.0).astype(BF)


def plan_kernel(experts, cap, cap_pad, routes, key_col, key_row, grad, slots, send):
    expert = pl.program_id(0)

    @pl.when(expert == 0)
    def _():
        ids = iota((experts, routes.shape[1]), 0)
        before = jnp.where(key_col[...] < key_row[...], 1.0, 0.0).astype(BF)
        first = jnp.where(routes[0:1, :] == ids, 1.0, 0.0)
        second = jnp.where(routes[1:2, :] == ids, 1.0, 0.0)
        count = jnp.sum(first, axis=1, keepdims=True)
        rank_first = jnp.sum(nn(first.astype(BF), before) * first, axis=0, keepdims=True)
        rank_second = jnp.sum((nn(second.astype(BF), before) + count) * second, axis=0, keepdims=True)
        ranks = jnp.concatenate([rank_first, rank_second], axis=0).astype(I32)
        owned = jnp.where(ranks < cap, routes[...] * cap_pad + ranks, -1)
        slots[...] = jnp.concatenate([owned, jnp.full((6, owned.shape[1]), -1, I32)], axis=0)

    one_hot = pick(slots[...], expert * cap_pad, cap_pad)
    send[0] = nn(one_hot, grad[...]).astype(BF)


def dispatch_kernel(experts, cap, cap_pad, acts, router, routes, slots, send, gates):
    expert = pl.program_id(0)
    tokens, width = acts.shape
    lanes = up(cap_pad, LANES)

    @pl.when(expert == 0)
    def _():
        logits = nt(router[...], acts[...])
        logits = jnp.exp(logits - jnp.max(logits, axis=0, keepdims=True))
        probs = logits / jnp.sum(logits, axis=0, keepdims=True)
        ids = iota((experts, tokens), 0)
        for choice in range(2):
            gate = jnp.sum(jnp.where(routes[choice : choice + 1, :] == ids, probs, 0.0), axis=0, keepdims=True)
            high, mid, low = split3(gate)
            gates[choice] = jnp.concatenate([high, mid, low, jnp.zeros((5, tokens), F32)], axis=0)

    own = iota((lanes, tokens), 0) + expert * cap_pad
    hit_first = own == slots[0:1, :]
    hit_second = own == slots[1:2, :]
    one_first = jnp.where(hit_first, 1.0, 0.0).astype(BF)
    one_second = jnp.where(hit_second, 1.0, 0.0).astype(BF)
    rows = nn((one_first + one_second)[:cap_pad], acts[...])
    gate = nt(gates[0].astype(BF), one_first) + nt(gates[1].astype(BF), one_second)
    gate = jnp.concatenate([gate, jnp.zeros((8, width - lanes), F32)], axis=1)
    at = iota((cap_pad, 1), 0) - cap
    for part in range(3):
        rows = jnp.where(at == part, gate[part : part + 1, :], rows)
    send[0] = rows.astype(BF)


def gelu_parts(z):
    share = 0.5 * (1.0 + lax.erf(z * 0.7071067811865476))
    slope = share + z * (0.3989422804014327 * jnp.exp(-0.5 * z * z))
    return z * share, slope


def expert_kernel(
    cap, chunk, got, got_grad, w_in, b_in, w_back, b_back,
    out_rows, out_back, grad_in, grad_b_in, grad_back, grad_b_back,
    acts, hidden, slope, delta, grad_pre,
):
    groups, cap_pad, width = got.shape
    ff = w_in.shape[1]
    lanes = up(cap_pad, LANES)
    at = iota((cap_pad, 1), 0)
    same = at == iota((1, lanes), 1)
    for src in range(groups):
        rows = pl.ds(src * cap_pad, cap_pad)
        block = got[src]
        acts[rows, :] = jnp.where(at < cap, block.astype(F32), 0.0).astype(BF)
        wide = block.astype(F32)
        gate = wide[cap : cap + 1, :lanes] + wide[cap + 1 : cap + 2, :lanes] + wide[cap + 2 : cap + 3, :lanes]
        gate = jnp.sum(jnp.where(same, gate, 0.0), axis=1, keepdims=True)
        delta[rows, :] = (gate * got_grad[src].astype(F32)).astype(BF)
        for lo in range(0, ff, chunk):
            cols = pl.ds(lo, chunk)
            z = nn(acts[rows, :], w_in[:, cols]) + b_in[lo // chunk].astype(F32)
            value, rise = gelu_parts(z)
            hidden[rows, cols] = value.astype(BF)
            slope[rows, cols] = rise.astype(BF)
        made = (nn(hidden[rows, :], w_back[...]) + b_back[...]).astype(BF).astype(F32)
        out_rows[src] = (gate * made).astype(BF)
        dot = jnp.sum(made * got_grad[src].astype(F32), axis=1, keepdims=True)
        dot = jnp.sum(jnp.where(same, dot, 0.0), axis=0, keepdims=True)
        parts = split3(jnp.concatenate([dot, jnp.zeros((1, width - lanes), F32)], axis=1))
        for lo in range(0, ff, chunk):
            cols = pl.ds(lo, chunk)
            dz = nt(delta[rows, :], w_back[cols, :]) * slope[rows, cols].astype(F32)
            total = jnp.sum(dz, axis=0, keepdims=True)
            grad_b_in[:, cols] = total if src == 0 else grad_b_in[:, cols] + total
            grad_pre[rows, cols] = dz.astype(BF)
        back = nt(grad_pre[rows, :], w_in[...])
        for part in range(3):
            back = jnp.where(at == cap + part, parts[part], back)
        out_back[src] = back.astype(BF)
    grad_b_back[...] = jnp.sum(delta[...].astype(F32), axis=0, keepdims=True)
    for lo in range(0, ff, chunk):
        cols = pl.ds(lo, chunk)
        grad_back[cols, :] = tn(hidden[:, cols], delta[...]).astype(BF)
        grad_in[:, cols] = tn(acts[...], grad_pre[:, cols]).astype(BF)


def forward_kernel(half, x_own, x_other, bias, vec, w_qkv, w_out, q_ref, k_ref, v_ref, p_ref, o_ref, h_ref, a_ref):
    width = x_own.shape[1]
    half_pad = up(half, 16)
    head_dim = width // HEADS
    scale = head_dim ** (-0.5)
    gain, offset, bias_q, bias_v = (vec[row : row + 1, :] for row in range(4))
    own = x_own[...].astype(F32)
    unit, _ = normed(own)
    acts = (unit * gain + offset).astype(BF)
    unit, _ = normed(x_other[...].astype(F32))
    other = (unit * gain + offset).astype(BF)
    q_ref[...] = ((nn(acts, w_qkv[:, :width]) + bias_q).astype(BF).astype(F32) * scale).astype(BF)
    pad = jnp.zeros((half_pad - half, width), BF)
    for part, rows in enumerate((acts, other)):
        start = part * half_pad
        k_ref[0, pl.ds(start, half), :] = nn(rows, w_qkv[:, width : 2 * width]).astype(BF)
        v_ref[0, pl.ds(start, half), :] = (nn(rows, w_qkv[:, 2 * width :]) + bias_v).astype(BF)
        if half_pad > half:
            k_ref[0, pl.ds(start + half, half_pad - half), :] = pad
            v_ref[0, pl.ds(start + half, half_pad - half), :] = pad
    low = iota((1, LANES), 1) < head_dim
    zero = jnp.zeros((), BF)
    for pair in range(width // LANES):
        cols = pl.ds(pair * LANES, LANES)
        q_pair, k_pair, v_pair = q_ref[:, cols], k_ref[0, :, cols], v_ref[0, :, cols]
        mixed = []
        for sub in range(2):
            mask = low if sub == 0 else jnp.logical_not(low)
            scores = nt(jnp.where(mask, q_pair, zero), k_pair) + bias[0]
            raised = jnp.exp(scores - jnp.max(scores, axis=1, keepdims=True))
            probs = (raised * (1.0 / jnp.sum(raised, axis=1, keepdims=True))).astype(BF)
            p_ref[0, 2 * pair + sub] = probs
            mixed.append(nn(probs, v_pair))
        o_ref[:, cols] = jnp.where(low, mixed[0], mixed[1]).astype(BF)
    after = own + nn(o_ref[...], w_out[...]) + vec[4:5, :]
    h_ref[...] = after
    unit, _ = normed(after)
    a_ref[...] = (unit * vec[5:6, :] + vec[6:7, :]).astype(BF)


def backward_kernel(
    experts, cap, cap_pad, grad, table, slots, h_ref, o_ref, a_ref, router, vec, w_out, q_ref, k_ref, v_ref, p_ref,
    dh_ref, dq_ref, dk_ref, dv_ref, g_out, g_router, g_vec, hits,
):
    image = pl.program_id(0)
    half, width = grad.shape
    head_dim = width // HEADS
    half_pad = up(half, 16)
    lanes = up(cap_pad, LANES)
    lane = iota((1, LANES), 1)
    acts = a_ref[...]
    logits = jnp.where(lane < experts, nn(acts, router[...]), -1e30)
    logits = jnp.exp(logits - jnp.max(logits, axis=1, keepdims=True))
    probs = logits / jnp.sum(logits, axis=1, keepdims=True)
    grad_probs = jnp.zeros((half, LANES), F32)
    first, second = slots[:, 0:1], slots[:, 1:2]
    back = jnp.zeros((half, width), F32)
    for expert in range(experts):
        own = iota((half, lanes), 1)
        own = jnp.where(own < cap_pad, own + expert * cap_pad, -2)
        hit = (own == first) | (own == second)
        one_hot = jnp.where(hit, 1.0, 0.0)
        start = expert * cap_pad
        tail = table[pl.ds(start + cap_pad - 16, 16), :].astype(F32)
        at = cap - (cap_pad - 16)
        dots = tail[at : at + 1, :lanes] + tail[at + 1 : at + 2, :lanes] + tail[at + 2 : at + 3, :lanes]
        dots = jnp.sum(jnp.where(hit, dots, 0.0), axis=1, keepdims=True)
        grad_probs = jnp.where(lane == expert, dots, grad_probs)
        back = back + nn(one_hot[:, :cap_pad].astype(BF), table[pl.ds(start, cap_pad), :])
    inner = jnp.sum(probs * grad_probs, axis=1, keepdims=True)
    grad_logits = (probs * (grad_probs - inner)).astype(BF)
    part_router = tn(acts, grad_logits)
    back = back + nt(grad_logits, router[...])
    unit, inv_scale = normed(h_ref[...])
    out_grad = grad[...].astype(F32)
    dh = out_grad + norm_backward(back, unit, inv_scale, vec[5:6, :])
    dh_ref[...] = dh
    dh_low = dh.astype(BF)
    part_out = tn(o_ref[...], dh_low)
    rows = [
        jnp.sum(dh, axis=0, keepdims=True),
        jnp.sum(back * unit, axis=0, keepdims=True),
        jnp.sum(back, axis=0, keepdims=True),
    ]
    part_vec = jnp.concatenate(rows + [jnp.zeros((5, width), F32)], axis=0)

    @pl.when(image == 0)
    def _():
        g_out[...] = part_out
        g_router[...] = part_router
        g_vec[...] = part_vec

    @pl.when(image > 0)
    def _():
        g_out[...] += part_out
        g_router[...] += part_router
        g_vec[...] += part_vec

    do = nt(dh_low, w_out[...]).astype(BF)
    low = lane < head_dim
    zero = jnp.zeros((), BF)
    scale = head_dim ** (-0.5)
    for pair in range(width // LANES):
        cols = slice(pair * LANES, (pair + 1) * LANES)
        do_pair = do[:, cols]
        q_pair, k_pair, v_pair = q_ref[:, cols], k_ref[0, :, cols], v_ref[0, :, cols]
        dq, dk, dv = [], [], []
        for sub in range(2):
            mask = low if sub == 0 else jnp.logical_not(low)
            p_low = p_ref[0, 2 * pair + sub]
            p = p_low.astype(F32)
            dp = nt(jnp.where(mask, do_pair, zero), v_pair)
            inner = jnp.sum(p * dp, axis=1, keepdims=True)
            ds = (p * (dp - inner)).astype(BF)
            dv.append(tn(p_low, do_pair))
            dk.append(tn(ds, q_pair))
            dq.append(nn(ds, k_pair))
        dq_ref[:, cols] = (jnp.where(low, dq[0], dq[1]) * scale).astype(BF)
        dk_pair = jnp.where(low, dk[0], dk[1]).astype(BF)
        dv_pair = jnp.where(low, dv[0], dv[1]).astype(BF)
        for part in range(2):
            dk_ref[part, :, cols] = dk_pair[part * half_pad : part * half_pad + half]
            dv_ref[part, :, cols] = dv_pair[part * half_pad : part * half_pad + half]


def input_kernel(x_ref, dh_ref, dq_ref, dk_own, dk_got, dv_own, dv_got, vec, w_qkv, dx_ref, g_qkv, g_vec):
    image = pl.program_id(0)
    width = x_ref.shape[1]
    unit, inv_scale = normed(x_ref[...].astype(F32))
    acts = (unit * vec[0:1, :] + vec[1:2, :]).astype(BF)
    dq = dq_ref[...]
    dk = (dk_own[0].astype(F32) + dk_got[...].astype(F32)).astype(BF)
    dv = (dv_own[0].astype(F32) + dv_got[...].astype(F32)).astype(BF)
    da = jnp.zeros(unit.shape, F32)
    parts = []
    for at, piece in enumerate((dq, dk, dv)):
        parts.append(tn(acts, piece))
        da = da + nt(piece, w_qkv[:, at * width : (at + 1) * width])
    dx_ref[...] = (dh_ref[...] + norm_backward(da, unit, inv_scale, vec[0:1, :])).astype(BF)
    rows = [
        jnp.sum(da * unit, axis=0, keepdims=True),
        jnp.sum(da, axis=0, keepdims=True),
        jnp.sum(dq.astype(F32), axis=0, keepdims=True),
        jnp.sum(dv.astype(F32), axis=0, keepdims=True),
    ]
    part_vec = jnp.concatenate(rows + [jnp.zeros((4, width), F32)], axis=0)

    @pl.when(image == 0)
    def _():
        g_vec[...] = part_vec
        for at in range(3):
            g_qkv[:, at * width : (at + 1) * width] = parts[at]

    @pl.when(image > 0)
    def _():
        g_vec[...] += part_vec
        for at in range(3):
            g_qkv[:, at * width : (at + 1) * width] += parts[at]


def combine_kernel(slots, table, h_ref, out_ref):
    half = slots.shape[0]
    total = table.shape[0]
    own = iota((half, total), 1)
    hit = (own == slots[:, 0:1]) | (own == slots[:, 1:2])
    out_ref[...] = (h_ref[...] + nn(jnp.where(hit, 1.0, 0.0).astype(BF), table[...])).astype(BF)


MESH = pl.DeviceIdType.MESH


def send(src, dst, sems, slot, device):
    copy = pltpu.make_async_remote_copy(
        src_ref=src, dst_ref=dst, send_sem=sems[0].at[slot], recv_sem=sems[1].at[slot],
        device_id=device, device_id_type=MESH,
    )
    copy.start()
    return copy


def greet(devices):
    barrier = pltpu.get_barrier_semaphore()
    for device in devices:
        pl.semaphore_signal(barrier, inc=1, device_id=device, device_id_type=MESH)
    pl.semaphore_wait(barrier, len(devices))


def comm_call(body, name, number, ins, outs, scratch, flops=0, moved=0, vmem=56):
    return pl.pallas_call(
        body,
        name=name,
        in_specs=[pl.BlockSpec(memory_space=space) for space in ins],
        out_specs=[pl.BlockSpec(memory_space=space) for _, _, space in outs],
        out_shape=[jax.ShapeDtypeStruct(shape, dtype) for shape, dtype, _ in outs],
        scratch_shapes=list(scratch),
        cost_estimate=pl.CostEstimate(flops=int(flops), bytes_accessed=int(moved), transcendentals=0),
        compiler_params=pltpu.CompilerParams(
            vmem_limit_bytes=vmem * MIB, collective_id=number, has_side_effects=True
        ),
    )


def start_kernel(
    dps, x, w_qkv, w_out, w_router, vectors, b_in, b_back,
    qkv_all, out_all, router_all, b_in_all, vec, bias_back, x_other,
    vec_all, back_all, far_send, far_recv, near_send, near_recv,
):
    dp, group, core = lax.axis_index("dp"), lax.axis_index("expert"), lax.axis_index("context")
    rows = w_qkv.shape[0]
    half = rows // 2
    near = (dp, group, 1 - core)
    peers = [(lax.rem(dp + step, dps), group, core) for step in range(1, dps)]
    greet(peers + [near])
    far, close = (far_send, far_recv), (near_send, near_recv)
    waits = [send(x, x_other, close, 0, near)]
    qkv_all[dp] = w_qkv[...].astype(BF)
    own = pl.ds(pl.multiple_of(core * half, half), half)
    copies = []
    for step, peer in enumerate(peers):
        copies.append(send(qkv_all.at[dp, own], qkv_all.at[dp, own], far, step * 6, peer))
    out_all[dp] = w_out[...].astype(BF)
    spare = router_all.shape[2] - w_router.shape[1]
    router_all[dp] = jnp.concatenate([w_router[...], jnp.zeros((rows, spare), F32)], axis=1).astype(BF)
    vec_all[dp] = jnp.concatenate([vectors[...], jnp.zeros((1, rows), F32)], axis=0).astype(BF)
    b_in_all[dp] = b_in[...].astype(BF)
    back_all[dp] = b_back[...].astype(BF)
    for step, peer in enumerate(peers):
        copies.append(send(out_all.at[dp, own], out_all.at[dp, own], far, step * 6 + 1, peer))
    for step, peer in enumerate(peers):
        for at, ref in enumerate((router_all, vec_all, b_in_all, back_all)):
            waits.append(send(ref.at[dp], ref.at[dp], far, step * 6 + 2 + at, peer))
    for at, copy in enumerate(copies):
        step, ref = at % len(peers), (qkv_all, out_all)[at // len(peers)]
        copy.wait()
        source = lax.rem(dp - step - 1 + dps, dps)
        waits.append(send(ref.at[source, own], ref.at[source, own], close, 1 + at, near))
    for copy in waits:
        copy.wait()
    vec[...] = jnp.concatenate([vec_all[at].astype(F32) for at in range(dps)], axis=1)
    bias_back[...] = jnp.concatenate([back_all[at].astype(F32) for at in range(dps)], axis=1)


def reduce_kernel(
    dps, groups, g_qkv, g_out, g_router, g_one, g_two, b_in, b_back,
    o_qkv, o_out, o_router, o_vec, o_in, o_back,
    near_out, near_in, far_out, far_in, deep_out, deep_in, total,
    small_near, small_far, small_got, small_deep, bin_near, bin_far, bin_got,
    near_s, near_r, far_s, far_r, deep_s, deep_r, last_s, last_r,
):
    dp, group, core = lax.axis_index("dp"), lax.axis_index("expert"), lax.axis_index("context")
    width = g_out.shape[0]
    rows = width // dps
    half = rows // 2
    near = (dp, group, 1 - core)
    peers = [(lax.rem(dp + step, dps), group, core) for step in range(1, dps)]
    others = [(dp, lax.rem(group + step, groups), core) for step in range(1, groups)]
    greet(peers + others + [near])
    near_sems, far_sems, deep_sems, last_sems = (near_s, near_r), (far_s, far_r), (deep_s, deep_r), (last_s, last_r)
    chunk = g_router.shape[1]
    sources = [(g_qkv, at) for at in range(0, g_qkv.shape[1], width)] + [(g_out, 0), (g_router, 0)]
    sizes = [width] * (len(sources) - 1) + [chunk]
    starts = [width * at for at in range(len(sources))]

    small = jnp.concatenate([g_one[0:4], g_two[0:3], jnp.zeros((1, width), F32), b_back[...]], axis=0)
    small = jnp.concatenate([small, jnp.zeros((16 - small.shape[0], width), F32)], axis=0)
    for at in range(dps):
        small_near[0, at] = small[:, at * rows : (at + 1) * rows]
        bin_near[0, at] = b_in[:, at * bin_near.shape[3] : (at + 1) * bin_near.shape[3]]
    first = [
        send(small_near.at[0], small_near.at[1], near_sems, 0, near),
        send(bin_near.at[0], bin_near.at[1], near_sems, 1, near),
    ]
    theirs = pl.multiple_of((1 - core) * half, half)
    ours = pl.multiple_of(core * half, half)
    for at, (ref, lane) in enumerate(sources):
        cols = pl.ds(starts[at], sizes[at])
        for block in range(dps):
            near_out[block, :, cols] = ref[pl.ds(block * rows + theirs, half), lane : lane + sizes[at]].astype(BF)
        first.append(send(near_out.at[:, :, cols], near_in.at[:, :, cols], near_sems, 2 + at, near))
    second = []
    for copy in first[:2]:
        copy.wait()
    small_far[...] = small_near[0] + small_near[1]
    bin_far[...] = bin_near[0] + bin_near[1]
    smalls = []
    for step, peer in enumerate(peers):
        target = lax.rem(dp + step + 1, dps)
        smalls.append(send(small_far.at[target], small_got.at[step], far_sems, step, peer))
        smalls.append(send(bin_far.at[target], bin_got.at[step], far_sems, dps + step, peer))
    for at, (ref, lane) in enumerate(sources):
        cols = pl.ds(starts[at], sizes[at])
        first[2 + at].wait()
        for step, peer in enumerate(peers):
            target = lax.rem(dp + step + 1, dps)
            block = ref[pl.ds(pl.multiple_of(target * rows, rows) + ours, half), lane : lane + sizes[at]]
            far_out[step, :, cols] = (block + near_in[target, :, cols].astype(F32)).astype(BF)
            second.append(
                send(far_out.at[step, :, cols], far_in.at[step, :, cols], far_sems, (2 + at) * dps + step, peer)
            )
    for copy in smalls:
        copy.wait()
    lone = small_far[dp]
    lone_in = bin_far[dp]
    for step in range(dps - 1):
        lone = lone + small_got[step]
        lone_in = lone_in + bin_got[step]
    o_in[...] = lone_in
    o_back[...] = lone[8 : 8 + o_back.shape[0]]
    small_deep[group] = lone
    third = []
    for step, peer in enumerate(others):
        third.append(send(small_deep.at[group], small_deep.at[group], deep_sems, step, peer))
    for at, (ref, lane) in enumerate(sources):
        cols = pl.ds(starts[at], sizes[at])
        mine = ref[pl.ds(pl.multiple_of(dp * rows, rows) + ours, half), lane : lane + sizes[at]]
        mine = mine + near_in[dp, :, cols].astype(F32)
        for step in range(dps - 1):
            second[at * (dps - 1) + step].wait()
            mine = mine + far_in[step, :, cols].astype(F32)
        deep_in[group, :, cols] = mine.astype(BF)
        for step, peer in enumerate(others):
            third.append(
                send(deep_in.at[group, :, cols], deep_in.at[group, :, cols], deep_sems, (1 + at) * groups + step, peer)
            )
    for copy in third[: groups - 1]:
        copy.wait()
    lone = small_deep[0]
    for at in range(1, groups):
        lone = lone + small_deep[at]
    o_vec[...] = lone[0:7]
    last = []
    here = pl.ds(ours, half)
    for at in range(len(sources)):
        cols = pl.ds(starts[at], sizes[at])
        for step in range(groups - 1):
            third[(1 + at) * (groups - 1) + step].wait()
        done = deep_in[0, :, cols].astype(F32)
        for source in range(1, groups):
            done = done + deep_in[source, :, cols].astype(F32)
        total[here, cols] = done
        last.append(send(total.at[here, cols], total.at[here, cols], last_sems, at, near))
    for at in range(len(sources)):
        last[at].wait()
    o_qkv[...] = total[:, : 3 * width]
    o_out[...] = total[:, 3 * width : 4 * width]
    o_router[...] = total[:, 4 * width : 4 * width + o_router.shape[1]]


def shards(
    inputs, key_mask, routes, priority, vectors, w_qkv, w_out, w_router, w_in, b_in, w_back, b_back, cotangent
):
    images, half, width = inputs.shape
    tokens = images * half
    groups = lax.axis_size("expert")
    dps = lax.axis_size("dp")
    per_device = w_in.shape[0]
    experts = groups * per_device
    ff = w_in.shape[2]
    cap = max(2, 3 * tokens // experts)
    cap_pad = up(cap + 3, 16)
    half_pad = up(half, 16)
    total = experts * cap_pad
    context = lax.axis_index("context")
    swap = [(0, 1), (1, 0)]

    x = inputs.reshape(tokens, width)
    grad = cotangent.reshape(tokens, width)
    V, A = pltpu.VMEM, pl.ANY
    rows = w_qkv.shape[0]
    qkv_all, out_all, router_all, in_b, vec, back_b, x_other = comm_call(
        partial(start_kernel, dps),
        "start",
        0,
        [V] * 7,
        [
            ((dps, rows, 3 * width), BF, V),
            ((dps, rows, width), BF, V),
            ((dps, rows, LANES), BF, V),
            ((dps, per_device, ff // dps), BF, V),
            ((8, width), F32, V),
            ((per_device, width), F32, V),
            ((tokens, width), BF, V),
        ],
        [
            pltpu.VMEM((dps, 8, rows), BF),
            pltpu.VMEM((dps, per_device, width // dps), BF),
            pltpu.SemaphoreType.DMA((6 * (dps - 1),)),
            pltpu.SemaphoreType.DMA((6 * (dps - 1),)),
            pltpu.SemaphoreType.DMA((1 + 2 * (dps - 1),)),
            pltpu.SemaphoreType.DMA((1 + 2 * (dps - 1),)),
        ],
        moved=8 * width * width * 4,
    )(x, w_qkv, w_out, w_router, vectors, b_in, b_back)
    qkv_all = qkv_all.reshape(width, 3 * width)
    out_all = out_all.reshape(width, width)
    router_pad = router_all.reshape(width, LANES)
    router_rows = router_pad[:, :experts].T

    in_w, back_w, x_other = lax.optimization_barrier((w_in.astype(BF), w_back.astype(BF), x_other))
    in_w = lax.all_gather(in_w, "dp", axis=1, tiled=True)
    back_w = lax.all_gather(back_w, "dp", axis=1, tiled=True)

    route_rows = routes.reshape(tokens, 2).T
    keys = priority.reshape(tokens) * tokens + jnp.arange(tokens, dtype=I32)
    block = ((1, cap_pad, width), lambda e: (e, 0, 0))
    slots, send_grad = call(
        partial(plan_kernel, experts, cap, cap_pad),
        "plan",
        (experts,),
        [None] * 4,
        [(((8, tokens), lambda e: (0, 0)), ((8, tokens), I32)), (block, ((experts, cap_pad, width), BF))],
        flops=2 * total * tokens * width,
        moved=4 * total * width,
    )(route_rows, keys[:, None], keys[None, :], grad)
    slot_cols = slots.T

    def exchange(rows):
        return lax.all_to_all(rows, "expert", split_axis=0, concat_axis=0, tiled=True)

    def by_expert(rows, which):
        return rows.reshape(groups, per_device, cap_pad, width)[:, which]

    got_grad = [exchange(by_expert(send_grad, which)) for which in range(per_device)]

    mask = jnp.where(key_mask > 0, 0.0, -1e30).astype(F32)
    first, second = mask[:, :half], mask[:, half:]
    own = jnp.where(context == 0, first, second)
    other = jnp.where(context == 0, second, first)
    off = jnp.full((images, half_pad - half), -1e30, F32)
    bias = jnp.concatenate([own, off, other, off], axis=1)[:, None, :]
    keys_pad = 2 * half_pad
    row = ((half, width), lambda i: (i, 0))
    cube = ((1, keys_pad, width), lambda i: (i, 0, 0))
    prob = ((1, HEADS, half, keys_pad), lambda i: (i, 0, 0, 0))
    q, k, v, p, o, after, acts = call(
        partial(forward_kernel, half),
        "forward",
        (images,),
        [row, row, ((1, 1, keys_pad), lambda i: (i, 0, 0)), None, None, None],
        [
            (row, ((tokens, width), BF)),
            (cube, ((images, keys_pad, width), BF)),
            (cube, ((images, keys_pad, width), BF)),
            (prob, ((images, HEADS, half, keys_pad), BF)),
            (row, ((tokens, width), BF)),
            (row, ((tokens, width), F32)),
            (row, ((tokens, width), BF)),
        ],
        flops=2 * tokens * width * (6 * width + 4 * keys_pad),
        moved=20 * tokens * width,
    )(x, x_other, bias, vec, qkv_all, out_all)

    (send_rows,) = call(
        partial(dispatch_kernel, experts, cap, cap_pad),
        "dispatch",
        (experts,),
        [None] * 4,
        [(block, ((experts, cap_pad, width), BF))],
        scratch=[pltpu.VMEM((2, 8, tokens), F32)],
        flops=2 * total * tokens * width,
        moved=4 * total * width,
    )(acts, router_rows, route_rows, slots)
    got = [exchange(by_expert(send_rows, which)) for which in range(per_device)]

    out_rows, back_rows, g_in, g_b_in, g_back, g_b_back = [], [], [], [], [], []
    slab = (groups, cap_pad, width)
    rows_all = groups * cap_pad
    for which in range(per_device):
        made = call(
            partial(expert_kernel, cap, ff // dps),
            "expert",
            (),
            [None] * 6,
            [
                (None, (slab, BF)),
                (None, (slab, BF)),
                (None, ((width, ff), BF)),
                (None, ((1, ff), F32)),
                (None, ((ff, width), BF)),
                (None, ((1, width), F32)),
            ],
            scratch=[
                pltpu.VMEM((rows_all, width), BF),
                pltpu.VMEM((rows_all, ff), BF),
                pltpu.VMEM((rows_all, ff), BF),
                pltpu.VMEM((rows_all, width), BF),
                pltpu.VMEM((rows_all, ff), BF),
            ],
            flops=12 * rows_all * width * ff,
            moved=8 * rows_all * width + 8 * width * ff,
        )(
            got[which], got_grad[which], in_w[which], in_b[:, which][:, None], back_w[which], back_b[which][None]
        )
        for kept, piece in zip((out_rows, back_rows, g_in, g_b_in, g_back, g_b_back), made):
            kept.append(piece)

    def returned(parts):
        moved = [exchange(part) for part in parts]
        return jnp.stack(moved, axis=1).reshape(total, width)

    back_table = returned(back_rows)
    out_table = returned(out_rows)

    def expert_sum(parts):
        share = lax.psum_scatter(jnp.stack(parts), ("dp", "context"), scatter_dimension=1, tiled=True)
        return lax.all_gather(share, "context", axis=1, tiled=True).astype(F32)

    grad_w_in = expert_sum(g_in)
    grad_w_back = expert_sum(g_back)

    halves = ((2, half, width), lambda i: (0, i, 0))
    fixed = lambda i: (0, 0)
    dh, dq, dk, dv, g_out, g_router, g_vec_two = call(
        partial(backward_kernel, experts, cap, cap_pad),
        "backward",
        (images,),
        [row, None, ((half, 8), lambda i: (i, 0)), row, row, row, None, None, None, row, cube, cube, prob],
        [
            (row, ((tokens, width), F32)),
            (row, ((tokens, width), BF)),
            (halves, ((2, tokens, width), BF)),
            (halves, ((2, tokens, width), BF)),
            (((width, width), fixed), ((width, width), F32)),
            (((width, LANES), fixed), ((width, LANES), F32)),
            (((8, width), fixed), ((8, width), F32)),
        ],
        scratch=[pltpu.VMEM((8, LANES), F32)],
        flops=2 * tokens * width * (total + 2 * width + 8 * keys_pad),
        moved=30 * tokens * width,
    )(grad, back_table, slot_cols, after, o, acts, router_pad, vec, out_all, q, k, v, p)

    dk_got = lax.ppermute(dk[1], "context", swap)
    dv_got = lax.ppermute(dv[1], "context", swap)
    own_half = ((1, half, width), lambda i: (0, i, 0))
    dx, g_qkv, g_vec_one = call(
        input_kernel,
        "input",
        (images,),
        [row, row, row, own_half, row, own_half, row, None, None],
        [
            (row, ((tokens, width), BF)),
            (((width, 3 * width), fixed), ((width, 3 * width), F32)),
            (((8, width), fixed), ((8, width), F32)),
        ],
        flops=12 * tokens * width * width,
        moved=20 * tokens * width,
    )(x, dh, dq, dk, dk_got, dv, dv_got, vec, qkv_all)

    (output,) = call(
        combine_kernel,
        "combine",
        (images,),
        [((half, 8), lambda i: (i, 0)), None, row],
        [(row, ((tokens, width), BF))],
        flops=2 * tokens * width * total,
        moved=10 * tokens * width,
    )(slot_cols, out_table, after)

    wide = 4 * width + LANES
    dma = pltpu.SemaphoreType.DMA
    halves_of = rows // 2
    grad_qkv, grad_out, grad_router, grad_vec, grad_b_in, grad_b_back = comm_call(
        partial(reduce_kernel, dps, groups),
        "reduce",
        1,
        [V] * 7,
        [
            ((rows, 3 * width), F32, V),
            ((rows, width), F32, V),
            ((rows, experts), F32, V),
            ((7, rows), F32, V),
            ((per_device, ff // dps), F32, V),
            ((per_device, rows), F32, V),
        ],
        [
            pltpu.VMEM((dps, halves_of, wide), BF),
            pltpu.VMEM((dps, halves_of, wide), BF),
            pltpu.VMEM((dps - 1, halves_of, wide), BF),
            pltpu.VMEM((dps - 1, halves_of, wide), BF),
            pltpu.VMEM((8, LANES), BF),
            pltpu.VMEM((groups, halves_of, wide), BF),
            pltpu.VMEM((rows, wide), F32),
            pltpu.VMEM((2, dps, 16, rows), F32),
            pltpu.VMEM((dps, 16, rows), F32),
            pltpu.VMEM((dps - 1, 16, rows), F32),
            pltpu.VMEM((groups, 16, rows), F32),
            pltpu.VMEM((2, dps, per_device, ff // dps), F32),
            pltpu.VMEM((dps, per_device, ff // dps), F32),
            pltpu.VMEM((dps - 1, per_device, ff // dps), F32),
            dma((7,)), dma((7,)), dma((7 * dps,)), dma((7 * dps,)),
            dma((6 * groups,)), dma((6 * groups,)), dma((5,)), dma((5,)),
        ],
        moved=20 * width * wide,
    )(
        g_qkv, g_out, g_router, g_vec_one, g_vec_two,
        jnp.concatenate(g_b_in, axis=0), jnp.concatenate(g_b_back, axis=0),
    )
    return (
        output.reshape(images, half, width),
        dx.reshape(images, half, width),
        grad_vec,
        grad_qkv,
        grad_out,
        grad_router,
        grad_w_in,
        grad_b_in,
        grad_w_back,
        grad_b_back,
    )


def solution(mesh):
    tokens = P(("dp", "expert"), "context", None)
    by_rows = P("dp", None)
    experts = P("expert", "dp", None)
    expert_bias = P("expert", "dp")
    return jax.shard_map(
        shards,
        mesh=mesh,
        in_specs=(
            tokens,
            P(("dp", "expert"), None),
            P(("dp", "expert"), "context", None, None),
            tokens,
            P(None, "dp"),
            by_rows,
            by_rows,
            by_rows,
            experts,
            expert_bias,
            experts,
            expert_bias,
            tokens,
        ),
        out_specs=(
            tokens,
            tokens,
            P(None, "dp"),
            by_rows,
            by_rows,
            by_rows,
            experts,
            expert_bias,
            experts,
            expert_bias,
        ),
        check_vma=False,
    )
```

```python
from functools import partial

import jax
import jax.numpy as jnp
from jax import lax
from jax.experimental import pallas as pl
from jax.experimental.pallas import tpu as pltpu
from jax.sharding import PartitionSpec as P

HEADS = 8
EPSILON = 1e-06
LANES = 128
BF = jnp.bfloat16
F32 = jnp.float32
I32 = jnp.int32
MIB = 1 << 20


def up(size, unit):
    return -(-size // unit) * unit


def nn(a, b):
    return jnp.dot(a, b, preferred_element_type=F32)


def nt(a, b):
    return lax.dot_general(a, b, (((1,), (1,)), ((), ())), preferred_element_type=F32)


def tn(a, b):
    return lax.dot_general(a, b, (((0,), (0,)), ((), ())), preferred_element_type=F32)


def iota(shape, dim):
    return lax.broadcasted_iota(I32, shape, dim)


def call(body, name, grid, ins, outs, scratch=(), flops=0, moved=0, vmem=56, aliases=None):
    in_specs = [pl.BlockSpec(*spec) if spec else pl.BlockSpec(memory_space=pltpu.VMEM) for spec in ins]
    out_specs = [pl.BlockSpec(*spec) if spec else pl.BlockSpec(memory_space=pltpu.VMEM) for spec, _ in outs]
    return pl.pallas_call(
        body,
        name=name,
        grid=grid,
        in_specs=in_specs,
        out_specs=out_specs,
        out_shape=[jax.ShapeDtypeStruct(*shape) for _, shape in outs],
        scratch_shapes=list(scratch),
        input_output_aliases=aliases or {},
        cost_estimate=pl.CostEstimate(flops=int(flops), bytes_accessed=int(moved), transcendentals=0),
        compiler_params=pltpu.CompilerParams(vmem_limit_bytes=vmem * MIB),
    )


def normed(values):
    average = jnp.mean(values, axis=-1, keepdims=True)
    centred = values - average
    inv_scale = lax.rsqrt(jnp.mean(centred * centred, axis=-1, keepdims=True) + EPSILON)
    return centred * inv_scale, inv_scale


def norm_backward(grad, unit, inv_scale, gain):
    scaled = grad * gain
    centre = jnp.mean(scaled, axis=-1, keepdims=True)
    along = jnp.mean(scaled * unit, axis=-1, keepdims=True)
    return inv_scale * (scaled - centre - unit * along)


def split3(value):
    high = value.astype(BF).astype(F32)
    rest = value - high
    mid = rest.astype(BF).astype(F32)
    return high, mid, rest - mid


def pick(slots, first, rows):
    own = iota((rows, slots.shape[1]), 0) + first
    hit = (own == slots[0:1, :]) | (own == slots[1:2, :])
    return jnp.where(hit, 1.0, 0.0).astype(BF)


def plan_kernel(experts, cap, cap_pad, routes, key_col, key_row, grad, slots, send):
    expert = pl.program_id(0)

    @pl.when(expert == 0)
    def _():
        ids = iota((experts, routes.shape[1]), 0)
        before = jnp.where(key_col[...] < key_row[...], 1.0, 0.0).astype(BF)
        first = jnp.where(routes[0:1, :] == ids, 1.0, 0.0)
        second = jnp.where(routes[1:2, :] == ids, 1.0, 0.0)
        count = jnp.sum(first, axis=1, keepdims=True)
        rank_first = jnp.sum(nn(first.astype(BF), before) * first, axis=0, keepdims=True)
        rank_second = jnp.sum((nn(second.astype(BF), before) + count) * second, axis=0, keepdims=True)
        ranks = jnp.concatenate([rank_first, rank_second], axis=0).astype(I32)
        owned = jnp.where(ranks < cap, routes[...] * cap_pad + ranks, -1)
        slots[...] = jnp.concatenate([owned, jnp.full((6, owned.shape[1]), -1, I32)], axis=0)

    one_hot = pick(slots[...], expert * cap_pad, cap_pad)
    send[0] = nn(one_hot, grad[...]).astype(BF)


def gelu_parts(z):
    share = 0.5 * (1.0 + lax.erf(z * 0.7071067811865476))
    slope = share + z * (0.3989422804014327 * jnp.exp(-0.5 * z * z))
    return z * share, slope


def experts_kernel(
    groups, cap, acts, router, routes, slots, send_grad, w_in, b_in, w_back, b_back,
    table, out_rows, g_in, g_b_in, g_back, g_b_back,
    gates, a_send, a_recv, g_recv, d_send, w_in_v, w_back_v, rows_v, hidden, grad_pre, delta, slope, g_in_v, g_back_v,
    a_s, a_r, g_s, g_r, d_s, d_r, w_sem, out_sem,
):
    dp, group, core = lax.axis_index("dp"), lax.axis_index("expert"), lax.axis_index("context")
    own, _, cap_pad, width = a_send.shape
    tokens = acts.shape[0]
    experts = groups * own
    ff = w_in_v.shape[1]
    chunk = b_in.shape[3]
    lanes = up(cap_pad, LANES)
    at = iota((cap_pad, 1), 0)
    same = at == iota((1, lanes), 1)

    def device(step):
        return (dp, lax.rem(group + step, groups), core)

    def remote(src, dst, sems, slot, target):
        return pltpu.make_async_remote_copy(
            src_ref=src, dst_ref=dst, send_sem=sems[0].at[slot], recv_sem=sems[1].at[slot],
            device_id=target, device_id_type=MESH,
        )

    def rows_out(which, step):
        return remote(a_send.at[which, step], a_recv.at[which, step], (a_s, a_r), which * groups + step, device(step))

    def grad_out(which, step):
        expert = lax.rem(group + step, groups) * own + which
        return remote(send_grad.at[expert], g_recv.at[which, step], (g_s, g_r), which * groups + step, device(step))

    def back_out(which, step):
        target = (dp, lax.rem(group - step + groups, groups), core)
        place = table.at[group * own + which]
        return remote(d_send.at[which, step], place, (d_s, d_r), which * groups + step, target)

    def load(which):
        return (
            pltpu.make_async_copy(w_in.at[which], w_in_v, w_sem.at[0]),
            pltpu.make_async_copy(w_back.at[which], w_back_v, w_sem.at[1]),
        )

    def store(which):
        return (
            pltpu.make_async_copy(g_in_v, g_in.at[which], out_sem.at[0]),
            pltpu.make_async_copy(g_back_v, g_back.at[which], out_sem.at[1]),
        )

    greet([device(step) for step in range(1, groups)])
    for copy in load(0):
        copy.start()
    logits = nt(router[...], acts[...])
    logits = jnp.exp(logits - jnp.max(logits, axis=0, keepdims=True))
    probs = logits / jnp.sum(logits, axis=0, keepdims=True)
    ids = iota((experts, tokens), 0)
    for choice in range(2):
        gate = jnp.sum(jnp.where(routes[choice : choice + 1, :] == ids, probs, 0.0), axis=0, keepdims=True)
        gates[choice] = jnp.concatenate(list(split3(gate)) + [jnp.zeros((5, tokens), F32)], axis=0)

    def dispatch(turn, _):
        which = turn // groups
        step = lax.rem(turn + 1, groups)
        expert = lax.rem(group + step, groups) * own + which
        ids = iota((lanes, tokens), 0) + expert * cap_pad
        first = jnp.where(ids == slots[0:1, :], 1.0, 0.0).astype(BF)
        second = jnp.where(ids == slots[1:2, :], 1.0, 0.0).astype(BF)
        rows = nn((first + second)[:cap_pad], acts[...])
        gate = nt(gates[0].astype(BF), first) + nt(gates[1].astype(BF), second)
        gate = jnp.concatenate([gate, jnp.zeros((8, width - lanes), F32)], axis=1)
        for part in range(3):
            rows = jnp.where(at == cap + part, gate[part : part + 1, :], rows)
        rows = rows.astype(BF)

        @pl.when(step > 0)
        def _():
            a_send[which, step] = rows
            rows_out(which, step).start()
            grad_out(which, step).start()

        @pl.when(step == 0)
        def _():
            a_recv[which, 0] = rows
            g_recv[which, 0] = send_grad[expert]

        return 0

    lax.fori_loop(0, own * groups, dispatch, 0)

    def expert(which, _):
        for copy in load(which):
            copy.wait()

        def block(step, _):
            @pl.when(step > 0)
            def _():
                rows_out(which, step).wait_recv()

            src = lax.rem(group - step + groups, groups)
            rows = pl.ds(pl.multiple_of(step * cap_pad, 16), cap_pad)
            got = a_recv[which, step].astype(F32)
            acts_in = jnp.where(at < cap, got, 0.0).astype(BF)
            rows_v[rows, :] = acts_in
            gate = got[cap : cap + 1, :lanes] + got[cap + 1 : cap + 2, :lanes] + got[cap + 2 : cap + 3, :lanes]
            gate = jnp.sum(jnp.where(same, gate, 0.0), axis=1, keepdims=True)
            for part in range(ff // chunk):
                cols = slice(part * chunk, (part + 1) * chunk)
                z = nn(acts_in, w_in_v[:, cols]) + b_in[part, which].astype(F32)
                value, rise = gelu_parts(z)
                hidden[rows, cols] = value.astype(BF)
                slope[:, cols] = rise.astype(BF)
            made = (nn(hidden[rows, :], w_back_v[...]) + b_back[which]).astype(BF).astype(F32)
            out_rows[src, which] = (gate * made).astype(BF)

            @pl.when(step > 0)
            def _():
                grad_out(which, step).wait_recv()

            got_grad = g_recv[which, step].astype(F32)
            low = (gate * got_grad).astype(BF)
            delta[rows, :] = low
            dot = jnp.sum(made * got_grad, axis=1, keepdims=True)
            dot = jnp.sum(jnp.where(same, dot, 0.0), axis=0, keepdims=True)
            parts = split3(jnp.concatenate([dot, jnp.zeros((1, width - lanes), F32)], axis=1))
            for part in range(ff // chunk):
                cols = slice(part * chunk, (part + 1) * chunk)
                dz = nt(low, w_back_v[cols, :]) * slope[:, cols].astype(F32)
                so_far = jnp.where(step > 0, g_b_in[which, :, cols], 0.0)
                g_b_in[which, :, cols] = so_far + jnp.sum(dz, axis=0, keepdims=True)
                grad_pre[rows, cols] = dz.astype(BF)
            back = nt(grad_pre[rows, :], w_in_v[...])
            for part in range(3):
                back = jnp.where(at == cap + part, parts[part], back)
            back = back.astype(BF)

            @pl.when(step > 0)
            def _():
                d_send[which, step] = back
                back_out(which, step).start()

            @pl.when(step == 0)
            def _():
                table[group * own + which] = back

            return 0

        lax.fori_loop(0, groups, block, 0)

        @pl.when(which + 1 < own)
        def _():
            for copy in load(which + 1):
                copy.start()

        @pl.when(which > 0)
        def _():
            for copy in store(which - 1):
                copy.wait()

        g_b_back[which] = jnp.sum(delta[...].astype(F32), axis=0, keepdims=True)

        def weights(part, _):
            cols = pl.ds(pl.multiple_of(part * chunk, LANES), chunk)
            g_back_v[cols, :] = tn(hidden[:, cols], delta[...]).astype(BF)
            g_in_v[:, cols] = tn(rows_v[...], grad_pre[:, cols]).astype(BF)
            return 0

        lax.fori_loop(0, ff // chunk, weights, 0)
        for copy in store(which):
            copy.start()
        return 0

    lax.fori_loop(0, own, expert, 0)
    for copy in store(own - 1):
        copy.wait()

    def finish(turn, _):
        which, step = turn // (groups - 1), 1 + lax.rem(turn, groups - 1)
        rows_out(which, step).wait_send()
        grad_out(which, step).wait_send()
        back_out(which, step).wait()
        return 0

    lax.fori_loop(0, own * (groups - 1), finish, 0)


def forward_kernel(half, x_own, x_other, bias, vec, w_qkv, w_out, q_ref, k_ref, v_ref, p_ref, o_ref, h_ref, a_ref):
    width = x_own.shape[1]
    half_pad = up(half, 16)
    head_dim = width // HEADS
    scale = head_dim ** (-0.5)
    gain, offset, bias_q, bias_v = (vec[row : row + 1, :] for row in range(4))
    own = x_own[...].astype(F32)
    unit, _ = normed(own)
    acts = (unit * gain + offset).astype(BF)
    unit, _ = normed(x_other[...].astype(F32))
    other = (unit * gain + offset).astype(BF)
    q_ref[...] = ((nn(acts, w_qkv[:, :width]) + bias_q).astype(BF).astype(F32) * scale).astype(BF)
    pad = jnp.zeros((half_pad - half, width), BF)
    for part, rows in enumerate((acts, other)):
        start = part * half_pad
        k_ref[0, pl.ds(start, half), :] = nn(rows, w_qkv[:, width : 2 * width]).astype(BF)
        v_ref[0, pl.ds(start, half), :] = (nn(rows, w_qkv[:, 2 * width :]) + bias_v).astype(BF)
        if half_pad > half:
            k_ref[0, pl.ds(start + half, half_pad - half), :] = pad
            v_ref[0, pl.ds(start + half, half_pad - half), :] = pad
    low = iota((1, LANES), 1) < head_dim
    zero = jnp.zeros((), BF)
    for pair in range(width // LANES):
        cols = pl.ds(pair * LANES, LANES)
        q_pair, k_pair, v_pair = q_ref[:, cols], k_ref[0, :, cols], v_ref[0, :, cols]
        mixed = []
        for sub in range(2):
            mask = low if sub == 0 else jnp.logical_not(low)
            scores = nt(jnp.where(mask, q_pair, zero), k_pair) + bias[0]
            raised = jnp.exp(scores - jnp.max(scores, axis=1, keepdims=True))
            probs = (raised * (1.0 / jnp.sum(raised, axis=1, keepdims=True))).astype(BF)
            p_ref[0, 2 * pair + sub] = probs
            mixed.append(nn(probs, v_pair))
        o_ref[:, cols] = jnp.where(low, mixed[0], mixed[1]).astype(BF)
    after = own + nn(o_ref[...], w_out[...]) + vec[4:5, :]
    h_ref[...] = after
    unit, _ = normed(after)
    a_ref[...] = (unit * vec[5:6, :] + vec[6:7, :]).astype(BF)


def backward_kernel(
    experts, cap, cap_pad, grad, table, slots, h_ref, o_ref, a_ref, router, vec, w_out, q_ref, k_ref, v_ref, p_ref,
    dh_ref, dq_ref, dk_ref, dv_ref, g_out, g_router, g_vec, hits,
):
    image = pl.program_id(0)
    half, width = grad.shape
    head_dim = width // HEADS
    half_pad = up(half, 16)
    lanes = up(cap_pad, LANES)
    lane = iota((1, LANES), 1)
    acts = a_ref[...]
    logits = jnp.where(lane < experts, nn(acts, router[...]), -1e30)
    logits = jnp.exp(logits - jnp.max(logits, axis=1, keepdims=True))
    probs = logits / jnp.sum(logits, axis=1, keepdims=True)
    grad_probs = jnp.zeros((half, LANES), F32)
    first, second = slots[:, 0:1], slots[:, 1:2]
    back = jnp.zeros((half, width), F32)
    for expert in range(experts):
        own = iota((half, lanes), 1)
        own = jnp.where(own < cap_pad, own + expert * cap_pad, -2)
        hit = (own == first) | (own == second)
        one_hot = jnp.where(hit, 1.0, 0.0)
        start = expert * cap_pad
        tail = table[pl.ds(start + cap_pad - 16, 16), :].astype(F32)
        at = cap - (cap_pad - 16)
        dots = tail[at : at + 1, :lanes] + tail[at + 1 : at + 2, :lanes] + tail[at + 2 : at + 3, :lanes]
        dots = jnp.sum(jnp.where(hit, dots, 0.0), axis=1, keepdims=True)
        grad_probs = jnp.where(lane == expert, dots, grad_probs)
        back = back + nn(one_hot[:, :cap_pad].astype(BF), table[pl.ds(start, cap_pad), :])
    inner = jnp.sum(probs * grad_probs, axis=1, keepdims=True)
    grad_logits = (probs * (grad_probs - inner)).astype(BF)
    part_router = tn(acts, grad_logits)
    back = back + nt(grad_logits, router[...])
    unit, inv_scale = normed(h_ref[...])
    out_grad = grad[...].astype(F32)
    dh = out_grad + norm_backward(back, unit, inv_scale, vec[5:6, :])
    dh_ref[...] = dh
    dh_low = dh.astype(BF)
    part_out = tn(o_ref[...], dh_low)
    rows = [
        jnp.sum(dh, axis=0, keepdims=True),
        jnp.sum(back * unit, axis=0, keepdims=True),
        jnp.sum(back, axis=0, keepdims=True),
    ]
    part_vec = jnp.concatenate(rows + [jnp.zeros((5, width), F32)], axis=0)

    @pl.when(image == 0)
    def _():
        g_out[...] = part_out
        g_router[...] = part_router
        g_vec[...] = part_vec

    @pl.when(image > 0)
    def _():
        g_out[...] += part_out
        g_router[...] += part_router
        g_vec[...] += part_vec

    do = nt(dh_low, w_out[...]).astype(BF)
    low = lane < head_dim
    zero = jnp.zeros((), BF)
    scale = head_dim ** (-0.5)
    for pair in range(width // LANES):
        cols = slice(pair * LANES, (pair + 1) * LANES)
        do_pair = do[:, cols]
        q_pair, k_pair, v_pair = q_ref[:, cols], k_ref[0, :, cols], v_ref[0, :, cols]
        dq, dk, dv = [], [], []
        for sub in range(2):
            mask = low if sub == 0 else jnp.logical_not(low)
            p_low = p_ref[0, 2 * pair + sub]
            p = p_low.astype(F32)
            dp = nt(jnp.where(mask, do_pair, zero), v_pair)
            inner = jnp.sum(p * dp, axis=1, keepdims=True)
            ds = (p * (dp - inner)).astype(BF)
            dv.append(tn(p_low, do_pair))
            dk.append(tn(ds, q_pair))
            dq.append(nn(ds, k_pair))
        dq_ref[:, cols] = (jnp.where(low, dq[0], dq[1]) * scale).astype(BF)
        dk_pair = jnp.where(low, dk[0], dk[1]).astype(BF)
        dv_pair = jnp.where(low, dv[0], dv[1]).astype(BF)
        for part in range(2):
            dk_ref[part, :, cols] = dk_pair[part * half_pad : part * half_pad + half]
            dv_ref[part, :, cols] = dv_pair[part * half_pad : part * half_pad + half]


def input_kernel(x_ref, dh_ref, dq_ref, dk_own, dk_got, dv_own, dv_got, vec, w_qkv, dx_ref, g_qkv, g_vec):
    image = pl.program_id(0)
    width = x_ref.shape[1]
    unit, inv_scale = normed(x_ref[...].astype(F32))
    acts = (unit * vec[0:1, :] + vec[1:2, :]).astype(BF)
    dq = dq_ref[...]
    dk = (dk_own[0].astype(F32) + dk_got[...].astype(F32)).astype(BF)
    dv = (dv_own[0].astype(F32) + dv_got[...].astype(F32)).astype(BF)
    da = jnp.zeros(unit.shape, F32)
    parts = []
    for at, piece in enumerate((dq, dk, dv)):
        parts.append(tn(acts, piece))
        da = da + nt(piece, w_qkv[:, at * width : (at + 1) * width])
    dx_ref[...] = (dh_ref[...] + norm_backward(da, unit, inv_scale, vec[0:1, :])).astype(BF)
    rows = [
        jnp.sum(da * unit, axis=0, keepdims=True),
        jnp.sum(da, axis=0, keepdims=True),
        jnp.sum(dq.astype(F32), axis=0, keepdims=True),
        jnp.sum(dv.astype(F32), axis=0, keepdims=True),
    ]
    part_vec = jnp.concatenate(rows + [jnp.zeros((4, width), F32)], axis=0)

    @pl.when(image == 0)
    def _():
        g_vec[...] = part_vec
        for at in range(3):
            g_qkv[:, at * width : (at + 1) * width] = parts[at]

    @pl.when(image > 0)
    def _():
        g_vec[...] += part_vec
        for at in range(3):
            g_qkv[:, at * width : (at + 1) * width] += parts[at]


def combine_kernel(slots, table, h_ref, out_ref):
    half = slots.shape[0]
    total = table.shape[0]
    own = iota((half, total), 1)
    hit = (own == slots[:, 0:1]) | (own == slots[:, 1:2])
    out_ref[...] = (h_ref[...] + nn(jnp.where(hit, 1.0, 0.0).astype(BF), table[...])).astype(BF)


MESH = pl.DeviceIdType.MESH


def send(src, dst, sems, slot, device):
    copy = pltpu.make_async_remote_copy(
        src_ref=src, dst_ref=dst, send_sem=sems[0].at[slot], recv_sem=sems[1].at[slot],
        device_id=device, device_id_type=MESH,
    )
    copy.start()
    return copy


def greet(devices):
    barrier = pltpu.get_barrier_semaphore()
    for device in devices:
        pl.semaphore_signal(barrier, inc=1, device_id=device, device_id_type=MESH)
    pl.semaphore_wait(barrier, len(devices))


def comm_call(body, name, number, ins, outs, scratch, flops=0, moved=0, vmem=56):
    return pl.pallas_call(
        body,
        name=name,
        in_specs=[pl.BlockSpec(memory_space=space) for space in ins],
        out_specs=[pl.BlockSpec(memory_space=space) for _, _, space in outs],
        out_shape=[jax.ShapeDtypeStruct(shape, dtype) for shape, dtype, _ in outs],
        scratch_shapes=list(scratch),
        cost_estimate=pl.CostEstimate(flops=int(flops), bytes_accessed=int(moved), transcendentals=0),
        compiler_params=pltpu.CompilerParams(
            vmem_limit_bytes=vmem * MIB, collective_id=number, has_side_effects=True
        ),
    )


def start_kernel(
    dps, x, w_qkv, w_out, w_router, vectors, b_in, b_back,
    qkv_all, out_all, router_all, b_in_all, vec, bias_back, x_other,
    vec_all, back_all, far_send, far_recv, near_send, near_recv,
):
    dp, group, core = lax.axis_index("dp"), lax.axis_index("expert"), lax.axis_index("context")
    rows = w_qkv.shape[0]
    half = rows // 2
    near = (dp, group, 1 - core)
    peers = [(lax.rem(dp + step, dps), group, core) for step in range(1, dps)]
    greet(peers + [near])
    far, close = (far_send, far_recv), (near_send, near_recv)
    waits = [send(x, x_other, close, 0, near)]
    qkv_all[dp] = w_qkv[...].astype(BF)
    own = pl.ds(pl.multiple_of(core * half, half), half)
    copies = []
    for step, peer in enumerate(peers):
        copies.append(send(qkv_all.at[dp, own], qkv_all.at[dp, own], far, step * 6, peer))
    out_all[dp] = w_out[...].astype(BF)
    spare = router_all.shape[2] - w_router.shape[1]
    router_all[dp] = jnp.concatenate([w_router[...], jnp.zeros((rows, spare), F32)], axis=1).astype(BF)
    vec_all[dp] = jnp.concatenate([vectors[...], jnp.zeros((1, rows), F32)], axis=0).astype(BF)
    b_in_all[dp] = b_in[...].astype(BF)
    back_all[dp] = b_back[...].astype(BF)
    for step, peer in enumerate(peers):
        copies.append(send(out_all.at[dp, own], out_all.at[dp, own], far, step * 6 + 1, peer))
    for step, peer in enumerate(peers):
        for at, ref in enumerate((router_all, vec_all, b_in_all, back_all)):
            waits.append(send(ref.at[dp], ref.at[dp], far, step * 6 + 2 + at, peer))
    for at, copy in enumerate(copies):
        step, ref = at % len(peers), (qkv_all, out_all)[at // len(peers)]
        copy.wait()
        source = lax.rem(dp - step - 1 + dps, dps)
        waits.append(send(ref.at[source, own], ref.at[source, own], close, 1 + at, near))
    for copy in waits:
        copy.wait()
    vec[...] = jnp.concatenate([vec_all[at].astype(F32) for at in range(dps)], axis=1)
    bias_back[...] = jnp.concatenate([back_all[at].astype(F32) for at in range(dps)], axis=1)


def reduce_kernel(
    dps, groups, g_qkv, g_out, g_router, g_one, g_two, b_in, b_back,
    o_qkv, o_out, o_router, o_vec, o_in, o_back,
    near_out, near_in, far_out, far_in, deep_out, deep_in, total,
    small_near, small_far, small_got, small_deep, bin_near, bin_far, bin_got,
    near_s, near_r, far_s, far_r, deep_s, deep_r, last_s, last_r,
):
    dp, group, core = lax.axis_index("dp"), lax.axis_index("expert"), lax.axis_index("context")
    width = g_out.shape[0]
    rows = width // dps
    half = rows // 2
    near = (dp, group, 1 - core)
    peers = [(lax.rem(dp + step, dps), group, core) for step in range(1, dps)]
    others = [(dp, lax.rem(group + step, groups), core) for step in range(1, groups)]
    greet(peers + others + [near])
    near_sems, far_sems, deep_sems, last_sems = (near_s, near_r), (far_s, far_r), (deep_s, deep_r), (last_s, last_r)
    chunk = g_router.shape[1]
    sources = [(g_qkv, at) for at in range(0, g_qkv.shape[1], width)] + [(g_out, 0), (g_router, 0)]
    sizes = [width] * (len(sources) - 1) + [chunk]
    starts = [width * at for at in range(len(sources))]

    small = jnp.concatenate([g_one[0:4], g_two[0:3], jnp.zeros((1, width), F32), b_back[...]], axis=0)
    small = jnp.concatenate([small, jnp.zeros((16 - small.shape[0], width), F32)], axis=0)
    for at in range(dps):
        small_near[0, at] = small[:, at * rows : (at + 1) * rows]
        bin_near[0, at] = b_in[:, at * bin_near.shape[3] : (at + 1) * bin_near.shape[3]]
    first = [
        send(small_near.at[0], small_near.at[1], near_sems, 0, near),
        send(bin_near.at[0], bin_near.at[1], near_sems, 1, near),
    ]
    theirs = pl.multiple_of((1 - core) * half, half)
    ours = pl.multiple_of(core * half, half)
    for at, (ref, lane) in enumerate(sources):
        cols = pl.ds(starts[at], sizes[at])
        for block in range(dps):
            near_out[block, :, cols] = ref[pl.ds(block * rows + theirs, half), lane : lane + sizes[at]].astype(BF)
        first.append(send(near_out.at[:, :, cols], near_in.at[:, :, cols], near_sems, 2 + at, near))
    second = []
    for copy in first[:2]:
        copy.wait()
    small_far[...] = small_near[0] + small_near[1]
    bin_far[...] = bin_near[0] + bin_near[1]
    smalls = []
    for step, peer in enumerate(peers):
        target = lax.rem(dp + step + 1, dps)
        smalls.append(send(small_far.at[target], small_got.at[step], far_sems, step, peer))
        smalls.append(send(bin_far.at[target], bin_got.at[step], far_sems, dps + step, peer))
    for at, (ref, lane) in enumerate(sources):
        cols = pl.ds(starts[at], sizes[at])
        first[2 + at].wait()
        for step, peer in enumerate(peers):
            target = lax.rem(dp + step + 1, dps)
            block = ref[pl.ds(pl.multiple_of(target * rows, rows) + ours, half), lane : lane + sizes[at]]
            far_out[step, :, cols] = (block + near_in[target, :, cols].astype(F32)).astype(BF)
            second.append(
                send(far_out.at[step, :, cols], far_in.at[step, :, cols], far_sems, (2 + at) * dps + step, peer)
            )
    for copy in smalls:
        copy.wait()
    lone = small_far[dp]
    lone_in = bin_far[dp]
    for step in range(dps - 1):
        lone = lone + small_got[step]
        lone_in = lone_in + bin_got[step]
    o_in[...] = lone_in
    o_back[...] = lone[8 : 8 + o_back.shape[0]]
    small_deep[group] = lone
    third = []
    for step, peer in enumerate(others):
        third.append(send(small_deep.at[group], small_deep.at[group], deep_sems, step, peer))
    for at, (ref, lane) in enumerate(sources):
        cols = pl.ds(starts[at], sizes[at])
        mine = ref[pl.ds(pl.multiple_of(dp * rows, rows) + ours, half), lane : lane + sizes[at]]
        mine = mine + near_in[dp, :, cols].astype(F32)
        for step in range(dps - 1):
            second[at * (dps - 1) + step].wait()
            mine = mine + far_in[step, :, cols].astype(F32)
        deep_in[group, :, cols] = mine.astype(BF)
        for step, peer in enumerate(others):
            third.append(
                send(deep_in.at[group, :, cols], deep_in.at[group, :, cols], deep_sems, (1 + at) * groups + step, peer)
            )
    for copy in third[: groups - 1]:
        copy.wait()
    lone = small_deep[0]
    for at in range(1, groups):
        lone = lone + small_deep[at]
    o_vec[...] = lone[0:7]
    last = []
    here = pl.ds(ours, half)
    for at in range(len(sources)):
        cols = pl.ds(starts[at], sizes[at])
        for step in range(groups - 1):
            third[(1 + at) * (groups - 1) + step].wait()
        done = deep_in[0, :, cols].astype(F32)
        for source in range(1, groups):
            done = done + deep_in[source, :, cols].astype(F32)
        total[here, cols] = done
        last.append(send(total.at[here, cols], total.at[here, cols], last_sems, at, near))
    for at in range(len(sources)):
        last[at].wait()
    o_qkv[...] = total[:, : 3 * width]
    o_out[...] = total[:, 3 * width : 4 * width]
    o_router[...] = total[:, 4 * width : 4 * width + o_router.shape[1]]


def shards(
    inputs, key_mask, routes, priority, vectors, w_qkv, w_out, w_router, w_in, b_in, w_back, b_back, cotangent
):
    images, half, width = inputs.shape
    tokens = images * half
    groups = lax.axis_size("expert")
    dps = lax.axis_size("dp")
    per_device = w_in.shape[0]
    experts = groups * per_device
    ff = w_in.shape[2]
    cap = max(2, 3 * tokens // experts)
    cap_pad = up(cap + 3, 16)
    half_pad = up(half, 16)
    total = experts * cap_pad
    context = lax.axis_index("context")
    swap = [(0, 1), (1, 0)]

    x = inputs.reshape(tokens, width)
    grad = cotangent.reshape(tokens, width)
    V, A = pltpu.VMEM, pl.ANY
    rows = w_qkv.shape[0]
    qkv_all, out_all, router_all, in_b, vec, back_b, x_other = comm_call(
        partial(start_kernel, dps),
        "start",
        0,
        [V] * 7,
        [
            ((dps, rows, 3 * width), BF, V),
            ((dps, rows, width), BF, V),
            ((dps, rows, LANES), BF, V),
            ((dps, per_device, ff // dps), BF, V),
            ((8, width), F32, V),
            ((per_device, width), F32, V),
            ((tokens, width), BF, V),
        ],
        [
            pltpu.VMEM((dps, 8, rows), BF),
            pltpu.VMEM((dps, per_device, width // dps), BF),
            pltpu.SemaphoreType.DMA((6 * (dps - 1),)),
            pltpu.SemaphoreType.DMA((6 * (dps - 1),)),
            pltpu.SemaphoreType.DMA((1 + 2 * (dps - 1),)),
            pltpu.SemaphoreType.DMA((1 + 2 * (dps - 1),)),
        ],
        moved=8 * width * width * 4,
    )(x, w_qkv, w_out, w_router, vectors, b_in, b_back)
    qkv_all = qkv_all.reshape(width, 3 * width)
    out_all = out_all.reshape(width, width)
    router_pad = router_all.reshape(width, LANES)
    router_rows = router_pad[:, :experts].T

    in_w, back_w, x_other = lax.optimization_barrier((w_in.astype(BF), w_back.astype(BF), x_other))
    in_w = lax.all_gather(in_w, "dp", axis=1, tiled=True)
    back_w = lax.all_gather(back_w, "dp", axis=1, tiled=True)

    route_rows = routes.reshape(tokens, 2).T
    keys = priority.reshape(tokens) * tokens + jnp.arange(tokens, dtype=I32)
    block = ((1, cap_pad, width), lambda e: (e, 0, 0))
    slots, send_grad = call(
        partial(plan_kernel, experts, cap, cap_pad),
        "plan",
        (experts,),
        [None] * 4,
        [(((8, tokens), lambda e: (0, 0)), ((8, tokens), I32)), (block, ((experts, cap_pad, width), BF))],
        flops=2 * total * tokens * width,
        moved=4 * total * width,
    )(route_rows, keys[:, None], keys[None, :], grad)
    slot_cols = slots.T

    mask = jnp.where(key_mask > 0, 0.0, -1e30).astype(F32)
    first, second = mask[:, :half], mask[:, half:]
    own = jnp.where(context == 0, first, second)
    other = jnp.where(context == 0, second, first)
    off = jnp.full((images, half_pad - half), -1e30, F32)
    bias = jnp.concatenate([own, off, other, off], axis=1)[:, None, :]
    keys_pad = 2 * half_pad
    row = ((half, width), lambda i: (i, 0))
    cube = ((1, keys_pad, width), lambda i: (i, 0, 0))
    prob = ((1, HEADS, half, keys_pad), lambda i: (i, 0, 0, 0))
    q, k, v, p, o, after, acts = call(
        partial(forward_kernel, half),
        "forward",
        (images,),
        [row, row, ((1, 1, keys_pad), lambda i: (i, 0, 0)), None, None, None],
        [
            (row, ((tokens, width), BF)),
            (cube, ((images, keys_pad, width), BF)),
            (cube, ((images, keys_pad, width), BF)),
            (prob, ((images, HEADS, half, keys_pad), BF)),
            (row, ((tokens, width), BF)),
            (row, ((tokens, width), F32)),
            (row, ((tokens, width), BF)),
        ],
        flops=2 * tokens * width * (6 * width + 4 * keys_pad),
        moved=20 * tokens * width,
    )(x, x_other, bias, vec, qkv_all, out_all)

    rows_all = groups * cap_pad
    dma = pltpu.SemaphoreType.DMA
    turns = per_device * groups
    back_table, out_rows, g_in, g_b_in, g_back, g_b_back = comm_call(
        partial(experts_kernel, groups, cap),
        "experts",
        2,
        [V, V, V, V, V, A, V, A, V],
        [
            ((experts, cap_pad, width), BF, V),
            ((groups, per_device, cap_pad, width), BF, V),
            ((per_device, width, ff), BF, A),
            ((per_device, 1, ff), F32, V),
            ((per_device, ff, width), BF, A),
            ((per_device, 1, width), F32, V),
        ],
        [
            pltpu.VMEM((2, 8, tokens), F32),
            pltpu.VMEM((per_device, groups, cap_pad, width), BF),
            pltpu.VMEM((per_device, groups, cap_pad, width), BF),
            pltpu.VMEM((per_device, groups, cap_pad, width), BF),
            pltpu.VMEM((per_device, groups, cap_pad, width), BF),
            pltpu.VMEM((width, ff), BF),
            pltpu.VMEM((ff, width), BF),
            pltpu.VMEM((rows_all, width), BF),
            pltpu.VMEM((rows_all, ff), BF),
            pltpu.VMEM((rows_all, ff), BF),
            pltpu.VMEM((rows_all, width), BF),
            pltpu.VMEM((cap_pad, ff), BF),
            pltpu.VMEM((width, ff), BF),
            pltpu.VMEM((ff, width), BF),
        ]
        + [dma((turns,))] * 6
        + [dma((2,))] * 2,
        flops=12 * per_device * rows_all * width * ff,
        moved=8 * per_device * rows_all * width + 8 * per_device * width * ff,
    )(acts, router_rows, route_rows, slots, send_grad, in_w, in_b[:, :, None], back_w, back_b[:, None])
    back_table = back_table.reshape(total, width)
    out_rows = out_rows.reshape(groups, per_device * cap_pad, width)
    out_table = lax.all_to_all(out_rows, "expert", split_axis=0, concat_axis=0, tiled=True).reshape(total, width)

    def expert_sum(parts):
        share = lax.psum_scatter(parts, ("dp", "context"), scatter_dimension=1, tiled=True)
        return lax.all_gather(share, "context", axis=1, tiled=True).astype(F32)

    grad_w_in = expert_sum(g_in)
    grad_w_back = expert_sum(g_back)

    halves = ((2, half, width), lambda i: (0, i, 0))
    fixed = lambda i: (0, 0)
    dh, dq, dk, dv, g_out, g_router, g_vec_two = call(
        partial(backward_kernel, experts, cap, cap_pad),
        "backward",
        (images,),
        [row, None, ((half, 8), lambda i: (i, 0)), row, row, row, None, None, None, row, cube, cube, prob],
        [
            (row, ((tokens, width), F32)),
            (row, ((tokens, width), BF)),
            (halves, ((2, tokens, width), BF)),
            (halves, ((2, tokens, width), BF)),
            (((width, width), fixed), ((width, width), F32)),
            (((width, LANES), fixed), ((width, LANES), F32)),
            (((8, width), fixed), ((8, width), F32)),
        ],
        scratch=[pltpu.VMEM((8, LANES), F32)],
        flops=2 * tokens * width * (total + 2 * width + 8 * keys_pad),
        moved=30 * tokens * width,
    )(grad, back_table, slot_cols, after, o, acts, router_pad, vec, out_all, q, k, v, p)

    dk_got = lax.ppermute(dk[1], "context", swap)
    dv_got = lax.ppermute(dv[1], "context", swap)
    own_half = ((1, half, width), lambda i: (0, i, 0))
    dx, g_qkv, g_vec_one = call(
        input_kernel,
        "input",
        (images,),
        [row, row, row, own_half, row, own_half, row, None, None],
        [
            (row, ((tokens, width), BF)),
            (((width, 3 * width), fixed), ((width, 3 * width), F32)),
            (((8, width), fixed), ((8, width), F32)),
        ],
        flops=12 * tokens * width * width,
        moved=20 * tokens * width,
    )(x, dh, dq, dk, dk_got, dv, dv_got, vec, qkv_all)

    (output,) = call(
        combine_kernel,
        "combine",
        (images,),
        [((half, 8), lambda i: (i, 0)), None, row],
        [(row, ((tokens, width), BF))],
        flops=2 * tokens * width * total,
        moved=10 * tokens * width,
    )(slot_cols, out_table, after)

    wide = 4 * width + LANES
    halves_of = rows // 2
    grad_qkv, grad_out, grad_router, grad_vec, grad_b_in, grad_b_back = comm_call(
        partial(reduce_kernel, dps, groups),
        "reduce",
        1,
        [V] * 7,
        [
            ((rows, 3 * width), F32, V),
            ((rows, width), F32, V),
            ((rows, experts), F32, V),
            ((7, rows), F32, V),
            ((per_device, ff // dps), F32, V),
            ((per_device, rows), F32, V),
        ],
        [
            pltpu.VMEM((dps, halves_of, wide), BF),
            pltpu.VMEM((dps, halves_of, wide), BF),
            pltpu.VMEM((dps - 1, halves_of, wide), BF),
            pltpu.VMEM((dps - 1, halves_of, wide), BF),
            pltpu.VMEM((8, LANES), BF),
            pltpu.VMEM((groups, halves_of, wide), BF),
            pltpu.VMEM((rows, wide), F32),
            pltpu.VMEM((2, dps, 16, rows), F32),
            pltpu.VMEM((dps, 16, rows), F32),
            pltpu.VMEM((dps - 1, 16, rows), F32),
            pltpu.VMEM((groups, 16, rows), F32),
            pltpu.VMEM((2, dps, per_device, ff // dps), F32),
            pltpu.VMEM((dps, per_device, ff // dps), F32),
            pltpu.VMEM((dps - 1, per_device, ff // dps), F32),
            dma((7,)), dma((7,)), dma((7 * dps,)), dma((7 * dps,)),
            dma((6 * groups,)), dma((6 * groups,)), dma((5,)), dma((5,)),
        ],
        moved=20 * width * wide,
    )(
        g_qkv, g_out, g_router, g_vec_one, g_vec_two,
        g_b_in[:, 0], g_b_back[:, 0],
    )
    return (
        output.reshape(images, half, width),
        dx.reshape(images, half, width),
        grad_vec,
        grad_qkv,
        grad_out,
        grad_router,
        grad_w_in,
        grad_b_in,
        grad_w_back,
        grad_b_back,
    )


def solution(mesh):
    tokens = P(("dp", "expert"), "context", None)
    by_rows = P("dp", None)
    experts = P("expert", "dp", None)
    expert_bias = P("expert", "dp")
    return jax.shard_map(
        shards,
        mesh=mesh,
        in_specs=(
            tokens,
            P(("dp", "expert"), None),
            P(("dp", "expert"), "context", None, None),
            tokens,
            P(None, "dp"),
            by_rows,
            by_rows,
            by_rows,
            experts,
            expert_bias,
            experts,
            expert_bias,
            tokens,
        ),
        out_specs=(
            tokens,
            tokens,
            P(None, "dp"),
            by_rows,
            by_rows,
            by_rows,
            experts,
            expert_bias,
            experts,
            expert_bias,
        ),
        check_vma=False,
    )
```

```python
from functools import partial

import jax
import jax.numpy as jnp
from jax import lax
from jax.experimental import pallas as pl
from jax.experimental.pallas import tpu as pltpu
from jax.sharding import PartitionSpec as P

HEADS = 8
EPSILON = 1e-06
LANES = 128
BF = jnp.bfloat16
F32 = jnp.float32
I32 = jnp.int32
MIB = 1 << 20


def up(size, unit):
    return -(-size // unit) * unit


def nn(a, b):
    return jnp.dot(a, b, preferred_element_type=F32)


def nt(a, b):
    return lax.dot_general(a, b, (((1,), (1,)), ((), ())), preferred_element_type=F32)


def tn(a, b):
    return lax.dot_general(a, b, (((0,), (0,)), ((), ())), preferred_element_type=F32)


def iota(shape, dim):
    return lax.broadcasted_iota(I32, shape, dim)


def call(body, name, grid, ins, outs, scratch=(), flops=0, moved=0, vmem=56, aliases=None):
    in_specs = [pl.BlockSpec(*spec) if spec else pl.BlockSpec(memory_space=pltpu.VMEM) for spec in ins]
    out_specs = [pl.BlockSpec(*spec) if spec else pl.BlockSpec(memory_space=pltpu.VMEM) for spec, _ in outs]
    return pl.pallas_call(
        body,
        name=name,
        grid=grid,
        in_specs=in_specs,
        out_specs=out_specs,
        out_shape=[jax.ShapeDtypeStruct(*shape) for _, shape in outs],
        scratch_shapes=list(scratch),
        input_output_aliases=aliases or {},
        cost_estimate=pl.CostEstimate(flops=int(flops), bytes_accessed=int(moved), transcendentals=0),
        compiler_params=pltpu.CompilerParams(vmem_limit_bytes=vmem * MIB),
    )


def normed(values):
    average = jnp.mean(values, axis=-1, keepdims=True)
    centred = values - average
    inv_scale = lax.rsqrt(jnp.mean(centred * centred, axis=-1, keepdims=True) + EPSILON)
    return centred * inv_scale, inv_scale


def norm_backward(grad, unit, inv_scale, gain):
    scaled = grad * gain
    centre = jnp.mean(scaled, axis=-1, keepdims=True)
    along = jnp.mean(scaled * unit, axis=-1, keepdims=True)
    return inv_scale * (scaled - centre - unit * along)


def split3(value):
    high = value.astype(BF).astype(F32)
    rest = value - high
    mid = rest.astype(BF).astype(F32)
    return high, mid, rest - mid


def pick(slots, first, rows):
    own = iota((rows, slots.shape[1]), 0) + first
    hit = (own == slots[0:1, :]) | (own == slots[1:2, :])
    return jnp.where(hit, 1.0, 0.0).astype(BF)


def gelu_parts(z):
    share = 0.5 * (1.0 + lax.erf(z * 0.7071067811865476))
    slope = share + z * (0.3989422804014327 * jnp.exp(-0.5 * z * z))
    return z * share, slope


def experts_kernel(
    groups, dps, images, cap_pad, acts, grad, after, router, routes, slots, b_in, b_back, *rest
):
    hosted = groups // 2
    w_in, kin_in, w_back, kin_back, rest = *rest[:4], rest[4:]
    back_rows, output, g_router, g_in, g_back, g_in_other, g_back_other, g_b_in, g_b_back = rest[:9]
    w_in_far, w_back_far, rest = rest[9], rest[10], rest[11:]
    tok, info, made_rows, w_in_v, w_back_v, rows_v, hidden, grad_pre, delta, slope = rest[:10]
    in_send, in_recv, back_send, back_recv, dots, dots_got, to_near, from_near, to_far, from_far = rest[10:20]
    places, x_s, x_r, w_sem, r_s, r_r, p_s, p_r, store_sem, load_sem, w_s, w_r, w_own = rest[20:]
    dp, group, core = lax.axis_index("dp"), lax.axis_index("expert"), lax.axis_index("context")
    tokens, width = output.shape
    ff = w_in_v.shape[1]
    rows_in, rows_back = width // dps, ff // dps
    mate = group + 1 - 2 * lax.rem(group, 2)
    near, across, diagonal = (dp, group, 1 - core), (dp, mate, core), (dp, mate, 1 - core)

    def remote(src, dst, sems, slot, target):
        return pltpu.make_async_remote_copy(
            src_ref=src, dst_ref=dst, send_sem=sems[0].at[slot], recv_sem=sems[1].at[slot],
            device_id=target, device_id_type=MESH,
        )

    pools = (info, tok.at[0], tok.at[1])
    moves = {}
    for at, pool in enumerate(pools):
        moves[at, 1] = remote(pool.at[0], pool.at[1], (x_s, x_r), 3 * at, near)
        moves[at, 2] = remote(pool.at[0], pool.at[2], (x_s, x_r), 3 * at + 1, across)
        moves[at, 3] = remote(pool.at[2], pool.at[3], (x_s, x_r), 3 * at + 2, near)

    def along(step):
        return (lax.rem(dp + step, dps), group, core)

    def sum_out(which, step):
        src, dst = ((in_send, in_recv), (back_send, back_recv))[which]
        return remote(src.at[step], dst.at[step - 1], (r_s, r_r), which * dps + step, along(step))

    def gather(at, which, step):
        kin, far = ((kin_in, w_in_far), (kin_back, w_back_far))[which]
        size = kin.shape[1]
        part = far.at[at, pl.ds(pl.multiple_of(dp * size, size), size)]
        if step == 0:
            return pltpu.make_async_copy(kin.at[at], part, w_own.at[2 * at + which])
        return remote(kin.at[at], part, (w_s, w_r), (2 * at + which) * dps + step, along(step))

    def load(which, wait):
        for at in range(hosted):
            copies = (
                pltpu.make_async_copy(w_in_far.at[at - 1] if at else w_in, w_in_v, w_sem.at[0]),
                pltpu.make_async_copy(w_back_far.at[at - 1] if at else w_back, w_back_v, w_sem.at[1]),
            )

            @pl.when(which == at)
            def _():
                if at and not wait:
                    for part in range(2):
                        for step in range(dps):
                            gather(at - 1, part, step).wait()
                for copy in copies:
                    copy.wait() if wait else copy.start()

    def store(which, to, step):
        return (
            pltpu.make_async_copy(
                in_send.at[step],
                g_in_other.at[which - 1, pl.ds(pl.multiple_of(to * rows_in, rows_in), rows_in)],
                store_sem.at[step],
            ),
            pltpu.make_async_copy(
                back_send.at[step],
                g_back_other.at[which - 1, pl.ds(pl.multiple_of(to * rows_back, rows_back), rows_back)],
                store_sem.at[dps + step],
            ),
        )

    mine = (
        pltpu.make_async_copy(acts, tok.at[0, 0], load_sem.at[0]),
        pltpu.make_async_copy(grad, tok.at[1, 0], load_sem.at[1]),
    )
    for copy in mine:
        copy.start()
    load(0, False)
    greet([near, across, diagonal] + [along(step) for step in range(1, dps)])
    mine[0].wait()
    for hop in (2, 1):
        moves[1, hop].start()
    for at in range(hosted - 1):
        for part in range(2):
            for step in range(dps):
                gather(at, part, step).start()
    logits = nt(router[...], tok[0, 0])
    logits = jnp.exp(logits - jnp.max(logits, axis=0, keepdims=True))
    probs = logits / jnp.sum(logits, axis=0, keepdims=True)
    ids = iota(probs.shape, 0)
    info[0, 2:4, :] = slots[0:2, :].astype(F32)
    for choice in range(2):
        info[0, choice : choice + 1, :] = jnp.sum(
            jnp.where(routes[choice : choice + 1, :] == ids, probs, 0.0), axis=0, keepdims=True
        )
    info[0, 4:8, :] = jnp.zeros((4, tokens), F32)
    mine[1].wait()
    for hop in (2, 1):
        moves[0, hop].start()
        moves[2, hop].start()
    g_b_in[...] = jnp.zeros_like(g_b_in)
    g_b_back[...] = jnp.zeros_like(g_b_back)

    def near_out(at):
        return remote(to_near.at[at], from_near.at[at], (p_s, p_r), at, near)

    def far_out(at):
        return remote(to_far.at[at], from_far.at[at], (p_s, p_r), 4 + at, across)

    def dots_out(source, target):
        return remote(dots.at[source], dots_got.at[source - 1], (p_s, p_r), 5 + source, target)

    def own_row(pair):
        pair = pair.astype(F32)
        return jnp.where(core == 0, pair[0:1], pair[1:2])

    half = tokens // images
    deep = hosted * cap_pad
    slot_ids = jnp.zeros((1, deep), F32)
    lane = iota((1, deep), 1)
    for which in range(hosted):
        first = (lax.rem(group + 2 * which, groups) * 2 + core - which) * cap_pad
        slot_ids = jnp.where(lane // cap_pad == which, (lane + first).astype(F32), slot_ids)

    def place(source):
        slot = info[source, 2:4, :]
        high = jnp.floor(slot * (1.0 / 64.0))
        parts = jnp.concatenate([high, slot - 64.0 * high, jnp.zeros((4, tokens), F32)], axis=0).astype(BF)
        row, col = iota((8, LANES), 0), iota((8, LANES), 1)
        weight = jnp.where(row == col, 64.0, jnp.where(row == col + 2, 1.0, 0.0))
        weight = jnp.where(col < 2, weight, 0.0).astype(BF)
        places[...] = tn(parts, weight)

    def summed(source, image):
        rows = pl.ds(pl.multiple_of(image * half, 8), half)
        hit = (places[rows, 0:1] == slot_ids) | (places[rows, 1:2] == slot_ids)
        return rows, nn(jnp.where(hit, 1.0, 0.0).astype(BF), made_rows[source])

    def to_core(source, at):
        place(source)

        def chunk(image, _):
            rows, part = summed(source, image)
            to_near[at, rows, :] = part[:, :width].astype(BF)
            to_near[at + 1, rows, :] = part[:, width:].astype(BF)
            return 0

        lax.fori_loop(0, images, chunk, 0)
        near_out(at).start()
        near_out(at + 1).start()

    def to_chip():
        place(2)
        near_out(0).wait_recv()
        near_out(1).wait_recv()

        def chunk(image, _):
            rows, part = summed(2, image)
            to_far[0, rows, :] = (part[:, :width] + from_near[0, rows, :].astype(F32)).astype(BF)
            to_far[1, rows, :] = (part[:, width:] + from_near[1, rows, :].astype(F32)).astype(BF)
            return 0

        lax.fori_loop(0, images, chunk, 0)
        far_out(0).start()
        far_out(1).start()

    def expert(which, _):
        load(which, True)
        own = lax.rem(group + 2 * which, groups) * 2 + core
        last = which // (hosted - 1)

        def block(turn, _):
            source = turn + (3 - 2 * turn) * last

            @pl.when(jnp.logical_and(which == 0, source == 1))
            def _():
                for at in range(3):
                    moves[at, 1].wait_recv()

            @pl.when(jnp.logical_and(which == 0, source == 2))
            def _():
                for at in range(3):
                    moves[at, 2].wait_recv()
                    moves[at, 3].start()

            @pl.when(jnp.logical_and(which == 0, source == 3))
            def _():
                for at in range(3):
                    moves[at, 3].wait_recv()

            rows = pl.ds(pl.multiple_of(source * cap_pad, 16), cap_pad)
            spot = pl.ds(pl.multiple_of(which * cap_pad, 16), cap_pad)
            ids = iota((cap_pad, tokens), 0) + own * cap_pad
            hit_first = ids == info[source, 2:3, :].astype(I32)
            hit_second = ids == info[source, 3:4, :].astype(I32)
            hit = jnp.logical_or(hit_first, hit_second)
            one_hot = jnp.where(hit, 1.0, 0.0).astype(BF)
            gate = jnp.where(hit_first, info[source, 0:1, :], 0.0) + jnp.where(hit_second, info[source, 1:2, :], 0.0)
            gate = jnp.sum(gate, axis=1, keepdims=True)
            acts_in = nn(one_hot, tok[0, source]).astype(BF)
            for part in range(dps):
                rows_v[part, rows, :] = acts_in[:, part * rows_in : (part + 1) * rows_in]
            for part in range(dps):
                cols = slice(part * rows_back, (part + 1) * rows_back)
                z = nn(acts_in, w_in_v[:, cols]) + own_row(b_in[which, part])
                value, rise = gelu_parts(z)
                hidden[rows, cols] = value.astype(BF)
                slope[:, cols] = rise.astype(BF)
            bias = jnp.concatenate([own_row(b_back[which, part]) for part in range(dps)], axis=1)
            made = (nn(hidden[rows, :], w_back_v[...]) + bias).astype(BF).astype(F32)
            made_rows[source, spot, width:] = (gate * made).astype(BF)
            got_grad = nn(one_hot, tok[1, source])
            low = (gate * got_grad).astype(BF)
            delta[rows, :] = low
            g_b_back[which, core] += jnp.sum(low.astype(F32), axis=0, keepdims=True)
            dot = jnp.sum(made * got_grad, axis=1, keepdims=True)
            dots[source, which] = jnp.sum(jnp.where(hit, dot, 0.0), axis=0, keepdims=True)
            for part in range(dps):
                cols = slice(part * rows_back, (part + 1) * rows_back)
                dz = nt(low, w_back_v[cols, :]) * slope[:, cols].astype(F32)
                g_b_in[which, core, :, cols] += jnp.sum(dz, axis=0, keepdims=True)
                grad_pre[rows, cols] = dz.astype(BF)
            made_rows[source, spot, :width] = nt(grad_pre[rows, :], w_in_v[...]).astype(BF)

            @pl.when(jnp.logical_and(last == 1, source == 3))
            def _():
                dots_out(3, diagonal).start()
                to_core(3, 0)

            @pl.when(jnp.logical_and(last == 1, source == 2))
            def _():
                dots_out(2, across).start()
                to_chip()

            @pl.when(jnp.logical_and(last == 1, source == 1))
            def _():
                dots_out(1, near).start()
                to_core(1, 2)

            return 0

        lax.fori_loop(0, 4, block, 0)
        @pl.when(which + 1 < hosted)
        def _():
            load(which + 1, False)

        def weights(step, _):
            step = lax.rem(step + 1, dps)
            to = lax.rem(dp + step, dps)
            part_back = tn(hidden[:, pl.ds(pl.multiple_of(to * rows_back, LANES), rows_back)], delta[...])
            part_in = tn(rows_v[to], grad_pre[...])

            @pl.when(jnp.logical_and(which == 1, step > 0))
            def _():
                sum_out(0, step).wait_send()
                sum_out(1, step).wait_send()

            @pl.when(which > 1)
            def _():
                for copy in store(which - 1, to, step):
                    copy.wait()

            back_send[step] = part_back.astype(BF)
            in_send[step] = part_in.astype(BF)

            @pl.when(jnp.logical_and(which == 0, step > 0))
            def _():
                sum_out(1, step).start()
                sum_out(0, step).start()

            @pl.when(jnp.logical_and(which == 0, step == 0))
            def _():
                g_back[...] = part_back
                g_in[...] = part_in

            @pl.when(which > 0)
            def _():
                for copy in store(which, to, step):
                    copy.start()

            return 0

        lax.fori_loop(0, dps, weights, 0)
        return 0

    lax.fori_loop(0, hosted, expert, 0)
    for source, target in ((1, near), (2, across), (3, diagonal)):
        dots_out(source, target).wait_recv()
    at_near, at_far = 1 - core, core
    whole = jnp.zeros(probs.shape, F32)
    for which in range(hosted):
        here, there = lax.rem(group + 2 * which, groups) * 2, lax.rem(mate + 2 * which, groups) * 2
        whole = jnp.where(ids == here + core, dots[0, which], whole)
        whole = jnp.where(ids == here + at_near, dots_got[0, which], whole)
        whole = jnp.where(ids == there + at_far, dots_got[1, which], whole)
        whole = jnp.where(ids == there + at_near, dots_got[2, which], whole)
    low = (probs * (whole - jnp.sum(probs * whole, axis=0, keepdims=True))).astype(BF)
    g_router[...] = nn(low, tok[0, 0])
    back_rows[...] = tn(low, router[...])
    place(0)
    near_out(2).wait_recv()
    near_out(3).wait_recv()
    far_out(0).wait_recv()
    far_out(1).wait_recv()

    def chunk(image, _):
        rows, part = summed(0, image)
        back_rows[rows, :] += part[:, :width] + from_near[2, rows, :].astype(F32) + from_far[0, rows, :].astype(F32)
        out = part[:, width:] + from_near[3, rows, :].astype(F32) + from_far[1, rows, :].astype(F32)
        output[rows, :] = (after[rows, :] + out).astype(BF)
        return 0

    lax.fori_loop(0, images, chunk, 0)
    for step in range(1, dps):
        for which in range(2):
            sum_out(which, step).wait_recv()
        g_back[...] += back_recv[step - 1].astype(F32)
        g_in[...] += in_recv[step - 1].astype(F32)

    for step in range(dps):
        for copy in store(hosted - 1, lax.rem(dp + step, dps), step):
            copy.wait()
    for copy in moves.values():
        copy.wait_send()
    for at in range(4):
        near_out(at).wait_send()
    for at in range(2):
        far_out(at).wait_send()
    for source, target in ((1, near), (2, across), (3, diagonal)):
        dots_out(source, target).wait_send()


def forward_image(
    half, image, dps, x, x_other, bias, vec, w_qkv, w_out, q_ref, k_ref, v_ref, p_ref, o_ref, h_ref, a_ref
):
    width = x.shape[1]
    rows = pl.ds(pl.multiple_of(image * half, 8), half)
    half_pad = up(half, 16)
    head_dim = width // HEADS
    scale = head_dim ** (-0.5)
    gain, offset, bias_q, bias_v = (vec[row : row + 1, :] for row in range(4))
    own = x[rows, :].astype(F32)
    unit, _ = normed(own)
    acts = (unit * gain + offset).astype(BF)
    unit, _ = normed(x_other[rows, :].astype(F32))
    other = (unit * gain + offset).astype(BF)

    def weight(at):
        return w_qkv[:, :, at * width : (at + 1) * width].reshape(width, width)

    q_ref[rows, :] = ((nn(acts, weight(0)) + bias_q).astype(BF).astype(F32) * scale).astype(BF)
    pad = jnp.zeros((half_pad - half, width), BF)
    for part, piece in enumerate((acts, other)):
        start = part * half_pad
        k_ref[image, pl.ds(start, half), :] = nn(piece, weight(1)).astype(BF)
        v_ref[image, pl.ds(start, half), :] = (nn(piece, weight(2)) + bias_v).astype(BF)
        if half_pad > half:
            k_ref[image, pl.ds(start + half, half_pad - half), :] = pad
            v_ref[image, pl.ds(start + half, half_pad - half), :] = pad
    low = iota((1, LANES), 1) < head_dim
    zero = jnp.zeros((), BF)
    for pair in range(width // LANES):
        cols = pl.ds(pair * LANES, LANES)
        q_pair, k_pair, v_pair = q_ref[rows, cols], k_ref[image, :, cols], v_ref[image, :, cols]
        mixed = []
        for sub in range(2):
            mask = low if sub == 0 else jnp.logical_not(low)
            scores = nt(jnp.where(mask, q_pair, zero), k_pair) + bias[image]
            raised = jnp.exp(scores - jnp.max(scores, axis=1, keepdims=True))
            probs = (raised * (1.0 / jnp.sum(raised, axis=1, keepdims=True))).astype(BF)
            p_ref[image, 2 * pair + sub] = probs
            mixed.append(nn(probs, v_pair))
        o_ref[rows, cols] = jnp.where(low, mixed[0], mixed[1]).astype(BF)
    after = own + nn(o_ref[rows, :], w_out[...].reshape(width, width)) + vec[4:5, :]
    h_ref[rows, :] = after
    unit, _ = normed(after)
    a_ref[rows, :] = (unit * vec[5:6, :] + vec[6:7, :]).astype(BF)


def backward_kernel(
    grad, back_ref, h_ref, o_ref, vec, w_out, q_ref, k_ref, v_ref, p_ref,
    dh_ref, dq_ref, dk_ref, dv_ref, g_out, g_vec,
):
    image = pl.program_id(0)
    half, width = grad.shape
    head_dim = width // HEADS
    half_pad = up(half, 16)
    lane = iota((1, LANES), 1)
    back = back_ref[...]
    unit, inv_scale = normed(h_ref[...])
    out_grad = grad[...].astype(F32)
    dh = out_grad + norm_backward(back, unit, inv_scale, vec[5:6, :])
    dh_ref[...] = dh
    dh_low = dh.astype(BF)
    part_out = tn(o_ref[...], dh_low)
    rows = [
        jnp.sum(dh, axis=0, keepdims=True),
        jnp.sum(back * unit, axis=0, keepdims=True),
        jnp.sum(back, axis=0, keepdims=True),
    ]
    part_vec = jnp.concatenate(rows + [jnp.zeros((5, width), F32)], axis=0)

    @pl.when(image == 0)
    def _():
        g_out[...] = part_out
        g_vec[...] = part_vec

    @pl.when(image > 0)
    def _():
        g_out[...] += part_out
        g_vec[...] += part_vec

    do = nt(dh_low, w_out[...]).astype(BF)
    low = lane < head_dim
    zero = jnp.zeros((), BF)
    scale = head_dim ** (-0.5)
    for pair in range(width // LANES):
        cols = slice(pair * LANES, (pair + 1) * LANES)
        do_pair = do[:, cols]
        q_pair, k_pair, v_pair = q_ref[:, cols], k_ref[0, :, cols], v_ref[0, :, cols]
        dq, dk, dv = [], [], []
        for sub in range(2):
            mask = low if sub == 0 else jnp.logical_not(low)
            p_low = p_ref[0, 2 * pair + sub]
            p = p_low.astype(F32)
            dp = nt(jnp.where(mask, do_pair, zero), v_pair)
            inner = jnp.sum(p * dp, axis=1, keepdims=True)
            ds = (p * (dp - inner)).astype(BF)
            dv.append(tn(p_low, do_pair))
            dk.append(tn(ds, q_pair))
            dq.append(nn(ds, k_pair))
        dq_ref[:, cols] = (jnp.where(low, dq[0], dq[1]) * scale).astype(BF)
        dk_pair = jnp.where(low, dk[0], dk[1]).astype(BF)
        dv_pair = jnp.where(low, dv[0], dv[1]).astype(BF)
        for part in range(2):
            dk_ref[part, :, cols] = dk_pair[part * half_pad : part * half_pad + half]
            dv_ref[part, :, cols] = dv_pair[part * half_pad : part * half_pad + half]


def input_kernel(x_ref, dh_ref, dq_ref, dk_own, dk_got, dv_own, dv_got, vec, w_qkv, dx_ref, g_qkv, g_vec):
    image = pl.program_id(0)
    width = x_ref.shape[1]
    unit, inv_scale = normed(x_ref[...].astype(F32))
    acts = (unit * vec[0:1, :] + vec[1:2, :]).astype(BF)
    dq = dq_ref[...]
    dk = (dk_own[0].astype(F32) + dk_got[...].astype(F32)).astype(BF)
    dv = (dv_own[0].astype(F32) + dv_got[...].astype(F32)).astype(BF)
    da = jnp.zeros(unit.shape, F32)
    parts = []
    for at, piece in enumerate((dq, dk, dv)):
        parts.append(tn(acts, piece))
        da = da + nt(piece, w_qkv[:, at * width : (at + 1) * width])
    dx_ref[...] = (dh_ref[...] + norm_backward(da, unit, inv_scale, vec[0:1, :])).astype(BF)
    rows = [
        jnp.sum(da * unit, axis=0, keepdims=True),
        jnp.sum(da, axis=0, keepdims=True),
        jnp.sum(dq.astype(F32), axis=0, keepdims=True),
        jnp.sum(dv.astype(F32), axis=0, keepdims=True),
    ]
    part_vec = jnp.concatenate(rows + [jnp.zeros((4, width), F32)], axis=0)

    @pl.when(image == 0)
    def _():
        g_vec[...] = part_vec
        for at in range(3):
            g_qkv[:, at * width : (at + 1) * width] = parts[at]

    @pl.when(image > 0)
    def _():
        g_vec[...] += part_vec
        for at in range(3):
            g_qkv[:, at * width : (at + 1) * width] += parts[at]


MESH = pl.DeviceIdType.MESH


def send(src, dst, sems, slot, device):
    copy = pltpu.make_async_remote_copy(
        src_ref=src, dst_ref=dst, send_sem=sems[0].at[slot], recv_sem=sems[1].at[slot],
        device_id=device, device_id_type=MESH,
    )
    copy.start()
    return copy


def greet(devices):
    barrier = pltpu.get_barrier_semaphore()
    for device in devices:
        pl.semaphore_signal(barrier, inc=1, device_id=device, device_id_type=MESH)
    pl.semaphore_wait(barrier, len(devices))


def comm_call(body, name, number, ins, outs, scratch, flops=0, moved=0, vmem=56):
    return pl.pallas_call(
        body,
        name=name,
        in_specs=[pl.BlockSpec(memory_space=space) for space in ins],
        out_specs=[pl.BlockSpec(memory_space=space) for _, _, space in outs],
        out_shape=[jax.ShapeDtypeStruct(shape, dtype) for shape, dtype, _ in outs],
        scratch_shapes=list(scratch),
        cost_estimate=pl.CostEstimate(flops=int(flops), bytes_accessed=int(moved), transcendentals=0),
        compiler_params=pltpu.CompilerParams(
            vmem_limit_bytes=vmem * MIB, collective_id=number, has_side_effects=True
        ),
    )


def start_kernel(
    dps, groups, images, cap, cap_pad, x, w_qkv, w_out, w_router, vectors, b_in, b_back, routes, key_col, key_row, bias,
    w_in, w_back,
    qkv_all, out_all, router_rows, b_in_all, back_all, vec, slots,
    q_ref, k_ref, v_ref, p_ref, o_ref, h_ref, a_ref, in_all, in_kin, back_w_all, back_kin,
    x_other, router_all, vec_all, p_all, w_in_f, w_back_f, w_in_v, w_back_v,
    far_send, far_recv, near_send, near_recv, deep_send, deep_recv, w_s, w_r, local,
):
    dp, group, core = lax.axis_index("dp"), lax.axis_index("expert"), lax.axis_index("context")
    rows = w_qkv.shape[0]
    half = rows // 2
    hosted = groups // 2
    near = (dp, group, 1 - core)
    peers = [(lax.rem(dp + step, dps), group, core) for step in range(1, dps)]
    kin = [(dp, lax.rem(group + 2 * step, groups), core) for step in range(1, hosted)]
    loads = [
        pltpu.make_async_copy(w_in.at[core], w_in_f, local.at[0]),
        pltpu.make_async_copy(w_back.at[core], w_back_f, local.at[1]),
    ]
    for copy in loads:
        copy.start()
    greet(peers + kin + [near])
    far, close, deep = (far_send, far_recv), (near_send, near_recv), (deep_send, deep_recv)
    waits = [send(x, x_other, close, 0, near)]
    qkv_all[dp] = w_qkv[...].astype(BF)
    own = pl.ds(pl.multiple_of(core * half, half), half)
    copies = []
    for step, peer in enumerate(peers):
        copies.append(send(qkv_all.at[dp, own], qkv_all.at[dp, own], far, step * 6, peer))
    out_all[dp] = w_out[...].astype(BF)
    spare = router_all.shape[2] - w_router.shape[1]
    router_all[dp] = jnp.concatenate([w_router[...], jnp.zeros((rows, spare), F32)], axis=1).astype(BF)
    vec_all[dp] = jnp.concatenate([vectors[...], jnp.zeros((1, rows), F32)], axis=0).astype(BF)
    b_in_all[0, dp] = b_in[...].astype(BF)
    back_all[0, dp] = b_back[...].astype(BF)
    for step, peer in enumerate(peers):
        copies.append(send(out_all.at[dp, own], out_all.at[dp, own], far, step * 6 + 1, peer))
    smalls, biases = [], []
    for step, peer in enumerate(peers):
        for at, ref in enumerate((router_all, vec_all)):
            smalls.append(send(ref.at[dp], ref.at[dp], far, step * 6 + 2 + at, peer))
        for at, ref in enumerate((b_in_all, back_all)):
            biases.append(send(ref.at[0, dp], ref.at[0, dp], far, step * 6 + 4 + at, peer))
    own_copies = []
    for at, (wide, low, out, kin_out) in enumerate(
        ((w_in_f, w_in_v, in_all, in_kin), (w_back_f, w_back_v, back_w_all, back_kin))
    ):
        loads[at].wait()
        low[...] = wide[...].astype(BF)
        size = low.shape[0]
        part = pl.ds(pl.multiple_of(dp * size, size), size)
        for step, peer in enumerate(kin):
            own_copies.append(
                send(low, kin_out.at[hosted - 2 - step], (w_s, w_r), at * (dps + hosted) + dps + step, peer)
            )
        for step, peer in enumerate(peers):
            own_copies.append(send(low, out.at[part], (w_s, w_r), at * (dps + hosted) + step, peer))
        here = pltpu.make_async_copy(low, out.at[part], local.at[2 + at])
        here.start()
        own_copies.append(here)

    tokens = routes.shape[1]
    experts = w_router.shape[1]
    ids = iota((experts, tokens), 0)
    before = jnp.where(key_col[...] < key_row[...], 1.0, 0.0).astype(BF)
    first = jnp.where(routes[0:1, :] == ids, 1.0, 0.0)
    second = jnp.where(routes[1:2, :] == ids, 1.0, 0.0)
    count = jnp.sum(first, axis=1, keepdims=True)
    rank_first = jnp.sum(nn(first.astype(BF), before) * first, axis=0, keepdims=True)
    rank_second = jnp.sum((nn(second.astype(BF), before) + count) * second, axis=0, keepdims=True)
    ranks = jnp.concatenate([rank_first, rank_second], axis=0).astype(I32)
    owned = jnp.where(ranks < cap, routes[...] * cap_pad + ranks, -1)
    slots[...] = jnp.concatenate([owned, jnp.full((6, tokens), -1, I32)], axis=0)

    for copy in biases:
        copy.wait()
    for step, peer in enumerate(kin):
        for at, ref in enumerate((b_in_all, back_all)):
            waits.append(send(ref.at[0], ref.at[hosted - 1 - step], deep, 2 * step + at, peer))
    for at, copy in enumerate(copies):
        step, ref = at % len(peers), (qkv_all, out_all)[at // len(peers)]
        copy.wait()
        source = lax.rem(dp - step - 1 + dps, dps)
        waits.append(send(ref.at[source, own], ref.at[source, own], close, 1 + at, near))
    for copy in smalls:
        copy.wait()
    vec[...] = jnp.concatenate([vec_all[at].astype(F32) for at in range(dps)], axis=1)
    turned = [router_all[at].astype(F32).T[: w_router.shape[1]] for at in range(dps)]
    router_rows[...] = jnp.concatenate(turned, axis=1).astype(BF)
    for copy in waits:
        copy.wait()

    half = tokens // images

    def image_step(image, _):
        forward_image(
            half, image, dps, x, x_other, bias, vec, qkv_all, out_all, q_ref, k_ref, v_ref, p_all, o_ref, h_ref, a_ref
        )
        pltpu.make_async_copy(p_all.at[image], p_ref.at[image], local.at[4]).start()
        return 0

    lax.fori_loop(0, images, image_step, 0)
    pltpu.make_async_copy(p_all, p_ref, local.at[4]).wait()
    for copy in own_copies:
        copy.wait()


def reduce_kernel(
    dps, groups, g_qkv, g_out, g_router, g_one, g_two, b_in, b_back,
    o_qkv, o_out, o_router, o_vec, o_in, o_back,
    near_out, near_in, far_out, far_in, deep_out, deep_in, total,
    small_near, small_far, small_got, small_deep, bin_near, bin_far, bin_got, bin_deep,
    near_s, near_r, far_s, far_r, deep_s, deep_r, last_s, last_r,
):
    dp, group, core = lax.axis_index("dp"), lax.axis_index("expert"), lax.axis_index("context")
    width = g_out.shape[0]
    rows = width // dps
    half = rows // 2
    near = (dp, group, 1 - core)
    peers = [(lax.rem(dp + step, dps), group, core) for step in range(1, dps)]
    others = [(dp, lax.rem(group + step, groups), core) for step in range(1, groups)]
    greet(peers + others + [near])
    near_sems, far_sems, deep_sems, last_sems = (near_s, near_r), (far_s, far_r), (deep_s, deep_r), (last_s, last_r)
    sources = [(g_qkv, at) for at in range(0, g_qkv.shape[1], width)] + [(g_out, 0)]
    sizes = [width] * len(sources)
    starts = [width * at for at in range(len(sources))]

    deep = small_near.shape[2]
    hosted = groups // 2
    tall = 2 * hosted
    router = 8 + tall
    bias_rows = [b_back[at // 2, at % 2] for at in range(tall)]
    bias_in = jnp.concatenate([b_in[at // 2, at % 2] for at in range(tall)], axis=0)
    small = [g_one[0:4], g_two[0:3], jnp.zeros((1, width), F32)] + bias_rows + [g_router[...]]
    spare = deep - router - g_router.shape[0]
    small = jnp.concatenate(small + ([jnp.zeros((spare, width), F32)] if spare else []), axis=0)
    for at in range(dps):
        small_near[0, at] = small[:, at * rows : (at + 1) * rows]
        bin_near[0, at] = bias_in[:, at * bin_near.shape[3] : (at + 1) * bin_near.shape[3]]
    first = [
        send(small_near.at[0], small_near.at[1], near_sems, 0, near),
        send(bin_near.at[0], bin_near.at[1], near_sems, 1, near),
    ]
    theirs = pl.multiple_of((1 - core) * half, half)
    ours = pl.multiple_of(core * half, half)
    for at, (ref, lane) in enumerate(sources):
        cols = pl.ds(starts[at], sizes[at])
        for block in range(dps):
            near_out[block, :, cols] = ref[pl.ds(block * rows + theirs, half), lane : lane + sizes[at]].astype(BF)
        first.append(send(near_out.at[:, :, cols], near_in.at[:, :, cols], near_sems, 2 + at, near))
    second = []
    for copy in first[:2]:
        copy.wait()
    small_far[...] = small_near[0] + small_near[1]
    bin_far[...] = bin_near[0] + bin_near[1]
    smalls = []
    for step, peer in enumerate(peers):
        target = lax.rem(dp + step + 1, dps)
        smalls.append(send(small_far.at[target], small_got.at[step], far_sems, step, peer))
        smalls.append(send(bin_far.at[target], bin_got.at[step], far_sems, dps + step, peer))
    for at, (ref, lane) in enumerate(sources):
        cols = pl.ds(starts[at], sizes[at])
        first[2 + at].wait()
        for step, peer in enumerate(peers):
            target = lax.rem(dp + step + 1, dps)
            block = ref[pl.ds(pl.multiple_of(target * rows, rows) + ours, half), lane : lane + sizes[at]]
            far_out[step, :, cols] = (block + near_in[target, :, cols].astype(F32)).astype(BF)
            second.append(
                send(far_out.at[step, :, cols], far_in.at[step, :, cols], far_sems, (2 + at) * dps + step, peer)
            )
    for copy in smalls:
        copy.wait()
    lone = small_far[dp]
    lone_in = bin_far[dp]
    for step in range(dps - 1):
        lone = lone + small_got[step]
        lone_in = lone_in + bin_got[step]
    small_deep[group] = lone
    bin_deep[group] = lone_in
    third, deep_bin = [], []
    for step, peer in enumerate(others):
        third.append(send(small_deep.at[group], small_deep.at[group], deep_sems, step, peer))
        deep_bin.append(
            send(bin_deep.at[group], bin_deep.at[group], deep_sems, (1 + len(sources)) * groups + step, peer)
        )
    for at, (ref, lane) in enumerate(sources):
        cols = pl.ds(starts[at], sizes[at])
        mine = ref[pl.ds(pl.multiple_of(dp * rows, rows) + ours, half), lane : lane + sizes[at]]
        mine = mine + near_in[dp, :, cols].astype(F32)
        for step in range(dps - 1):
            second[at * (dps - 1) + step].wait()
            mine = mine + far_in[step, :, cols].astype(F32)
        deep_in[group, :, cols] = mine.astype(BF)
        for step, peer in enumerate(others):
            third.append(
                send(deep_in.at[group, :, cols], deep_in.at[group, :, cols], deep_sems, (1 + at) * groups + step, peer)
            )
    for copy in third[: groups - 1]:
        copy.wait()
    for copy in deep_bin:
        copy.wait()
    lone = small_deep[0]
    for at in range(1, groups):
        lone = lone + small_deep[at]
    o_vec[...] = lone[0:7]
    o_router[...] = lone[router : router + o_router.shape[0]]
    grad_in, grad_back = jnp.zeros(o_in.shape, F32), jnp.zeros(o_back.shape, F32)
    for at in range(groups):
        away = lax.rem(group - at + groups, groups)
        kin = lax.rem(away, 2) == 0
        pick_in, pick_back = jnp.zeros(o_in.shape, F32), jnp.zeros(o_back.shape, F32)
        for which in range(hosted):
            here = away // 2 == which
            pick_in = jnp.where(here, bin_deep[at, 2 * which : 2 * which + 2], pick_in)
            pick_back = jnp.where(here, small_deep[at, 8 + 2 * which : 10 + 2 * which], pick_back)
        grad_in = grad_in + jnp.where(kin, pick_in, 0.0)
        grad_back = grad_back + jnp.where(kin, pick_back, 0.0)
    o_in[...] = grad_in
    o_back[...] = grad_back
    last = []
    here = pl.ds(ours, half)
    for at in range(len(sources)):
        cols = pl.ds(starts[at], sizes[at])
        for step in range(groups - 1):
            third[(1 + at) * (groups - 1) + step].wait()
        done = deep_in[0, :, cols].astype(F32)
        for source in range(1, groups):
            done = done + deep_in[source, :, cols].astype(F32)
        total[here, cols] = done
        last.append(send(total.at[here, cols], total.at[here, cols], last_sems, at, near))
    for at in range(len(sources)):
        last[at].wait()
    o_qkv[...] = total[:, : 3 * width]
    o_out[...] = total[:, 3 * width : 4 * width]


def finish_kernel(count, g_in, g_back, *rest):
    others, rest = rest[: 2 * count], rest[2 * count :]
    _, o_in, o_back, sum_in, sum_back, sems_s, sems_r, local = rest
    dp, group, core = lax.axis_index("dp"), lax.axis_index("expert"), lax.axis_index("context")
    near = (dp, group, 1 - core)
    greet([near])
    copies = []
    for at, (own, total, out) in enumerate(((g_in, sum_in, o_in), (g_back, sum_back, o_back))):
        value = own[...]
        for other in others[at * count : (at + 1) * count]:
            value = value + other[...].astype(F32)
        total[...] = value
        copies.append(send(total, out.at[core], (sems_s, sems_r), at, near))
        here = pltpu.make_async_copy(total, out.at[core], local.at[at])
        here.start()
        copies.append(here)
    for copy in copies:
        copy.wait()


def shards(
    inputs, key_mask, routes, priority, vectors, w_qkv, w_out, w_router, w_in, b_in, w_back, b_back, cotangent
):
    images, half, width = inputs.shape
    tokens = images * half
    groups = lax.axis_size("expert")
    dps = lax.axis_size("dp")
    per_device = w_in.shape[0]
    experts = groups * per_device
    ff = w_in.shape[2]
    cap = max(2, 3 * tokens // experts)
    cap_pad = up(cap, 16)
    half_pad = up(half, 16)
    hosted = groups // 2
    context = lax.axis_index("context")
    swap = [(0, 1), (1, 0)]
    V, A = pltpu.VMEM, pl.ANY
    dma = pltpu.SemaphoreType.DMA
    rows = w_qkv.shape[0]
    rows_back = ff // dps

    x = inputs.reshape(tokens, width)
    grad = cotangent.reshape(tokens, width)
    route_rows = routes.reshape(tokens, 2).T
    keys = priority.reshape(tokens) * tokens + jnp.arange(tokens, dtype=I32)

    mask = jnp.where(key_mask > 0, 0.0, -1e30).astype(F32)
    first, second = mask[:, :half], mask[:, half:]
    own = jnp.where(context == 0, first, second)
    other = jnp.where(context == 0, second, first)
    off = jnp.full((images, half_pad - half), -1e30, F32)
    bias = jnp.concatenate([own, off, other, off], axis=1)[:, None, :]
    keys_pad = 2 * half_pad

    made = comm_call(
        partial(start_kernel, dps, groups, images, cap, cap_pad),
        "front",
        0,
        [V] * 11 + [A] * 2,
        [
            ((dps, rows, 3 * width), BF, V),
            ((dps, rows, width), BF, V),
            ((experts, width), BF, V),
            ((hosted, dps, per_device, rows_back), BF, V),
            ((hosted, dps, per_device, rows), BF, V),
            ((8, width), F32, V),
            ((8, tokens), I32, V),
            ((tokens, width), BF, V),
            ((images, keys_pad, width), BF, V),
            ((images, keys_pad, width), BF, V),
            ((images, HEADS, half, keys_pad), BF, A),
            ((tokens, width), BF, V),
            ((tokens, width), F32, V),
            ((tokens, width), BF, V),
            ((width, ff), BF, A),
            ((hosted - 1, rows, ff), BF, A),
            ((ff, width), BF, A),
            ((hosted - 1, rows_back, width), BF, A),
        ],
        [
            pltpu.VMEM((tokens, width), BF),
            pltpu.VMEM((dps, rows, LANES), BF),
            pltpu.VMEM((dps, 8, rows), BF),
            pltpu.VMEM((images, HEADS, half, keys_pad), BF),
            pltpu.VMEM((rows, ff), F32),
            pltpu.VMEM((rows_back, width), F32),
            pltpu.VMEM((rows, ff), BF),
            pltpu.VMEM((rows_back, width), BF),
        ]
        + [dma((6 * (dps - 1),))] * 2
        + [dma((1 + 2 * (dps - 1),))] * 2
        + [dma((2 * hosted,))] * 2
        + [dma((2 * (dps + hosted),))] * 2
        + [dma((5,))],
        flops=2 * tokens * width * (8 * width + 4 * keys_pad),
        moved=40 * tokens * width,
    )(x, w_qkv, w_out, w_router, vectors, b_in, b_back, route_rows, keys[:, None], keys[None, :], bias, w_in, w_back)
    qkv_all, out_all, router_rows, b_ins, b_backs, vec, slots, q, k, v, p, o, after, acts, *expert_w = made
    qkv_all = qkv_all.reshape(width, 3 * width)
    out_all = out_all.reshape(width, width)
    row = ((half, width), lambda i: (i, 0))
    cube = ((1, keys_pad, width), lambda i: (i, 0, 0))
    prob = ((1, HEADS, half, keys_pad), lambda i: (i, 0, 0, 0))

    rows_all = 4 * cap_pad
    deep = hosted * cap_pad
    made = comm_call(
        partial(experts_kernel, groups, dps, images, cap_pad),
        "experts",
        2,
        [A, A, V, V, V, V, V, V] + [A] * 4,
        [
            ((tokens, width), F32, V),
            ((tokens, width), BF, V),
            ((experts, width), F32, V),
            ((rows, ff), F32, V),
            ((rows_back, width), F32, V),
            ((hosted - 1, width, ff), BF, A),
            ((hosted - 1, ff, width), BF, A),
            ((hosted, 2, 1, ff), F32, V),
            ((hosted, 2, 1, width), F32, V),
            ((hosted - 1, width, ff), BF, A),
            ((hosted - 1, ff, width), BF, A),
        ],
        [
            pltpu.VMEM((2, 4, tokens, width), BF),
            pltpu.VMEM((4, 8, tokens), F32),
            pltpu.VMEM((4, deep, 2 * width), BF),
            pltpu.VMEM((width, ff), BF),
            pltpu.VMEM((ff, width), BF),
            pltpu.VMEM((dps, rows_all, rows), BF),
            pltpu.VMEM((rows_all, ff), BF),
            pltpu.VMEM((rows_all, ff), BF),
            pltpu.VMEM((rows_all, width), BF),
            pltpu.VMEM((cap_pad, ff), BF),
            pltpu.VMEM((dps, rows, ff), BF),
            pltpu.VMEM((dps - 1, rows, ff), BF),
            pltpu.VMEM((dps, rows_back, width), BF),
            pltpu.VMEM((dps - 1, rows_back, width), BF),
            pltpu.VMEM((4, hosted, 1, tokens), F32),
            pltpu.VMEM((3, hosted, 1, tokens), F32),
            pltpu.VMEM((4, tokens, width), BF),
            pltpu.VMEM((4, tokens, width), BF),
            pltpu.VMEM((2, tokens, width), BF),
            pltpu.VMEM((2, tokens, width), BF),
            pltpu.VMEM((tokens, LANES), F32),
            dma((9,)),
            dma((9,)),
            dma((2,)),
            dma((2 * dps,)),
            dma((2 * dps,)),
            dma((9,)),
            dma((9,)),
            dma((2 * dps,)),
            dma((2,)),
            dma((2 * hosted * dps,)),
            dma((2 * hosted * dps,)),
            dma((2 * hosted,)),
        ],
        flops=14 * hosted * rows_all * width * ff,
        moved=20 * tokens * width + 8 * hosted * width * ff,
        vmem=63,
    )(acts, grad, after, router_rows, route_rows, slots, b_ins, b_backs, *expert_w)
    back_rows, output, g_router, g_in, g_back, g_in_other, g_back_other, g_b_in, g_b_back, *_ = made

    others = []
    for part in (g_in_other, g_back_other):
        part = lax.psum_scatter(part, "dp", scatter_dimension=1, tiled=True)
        for step in range(1, hosted):
            perm = [(at, (at + 2 * step) % groups) for at in range(groups)]
            others.append(lax.ppermute(part[step - 1], "expert", perm))

    halves = ((2, half, width), lambda i: (0, i, 0))
    fixed = lambda i: (0, 0)
    dh, dq, dk, dv, g_out, g_vec_two = call(
        backward_kernel,
        "backward",
        (images,),
        [row, row, row, row, None, None, row, cube, cube, prob],
        [
            (row, ((tokens, width), F32)),
            (row, ((tokens, width), BF)),
            (halves, ((2, tokens, width), BF)),
            (halves, ((2, tokens, width), BF)),
            (((width, width), fixed), ((width, width), F32)),
            (((8, width), fixed), ((8, width), F32)),
        ],
        flops=2 * tokens * width * (2 * width + 8 * keys_pad),
        moved=30 * tokens * width,
    )(grad, back_rows, after, o, vec, out_all, q, k, v, p)

    dk_got = lax.ppermute(dk[1], "context", swap)
    dv_got = lax.ppermute(dv[1], "context", swap)
    own_half = ((1, half, width), lambda i: (0, i, 0))
    dx, g_qkv, g_vec_one = call(
        input_kernel,
        "input",
        (images,),
        [row, row, row, own_half, row, own_half, row, None, None],
        [
            (row, ((tokens, width), BF)),
            (((width, 3 * width), fixed), ((width, 3 * width), F32)),
            (((8, width), fixed), ((8, width), F32)),
        ],
        flops=12 * tokens * width * width,
        moved=20 * tokens * width,
    )(x, dh, dq, dk, dk_got, dv, dv_got, vec, qkv_all)

    wide = 4 * width
    halves_of = rows // 2
    small = up(8 + 2 * hosted + experts, 8)
    grad_qkv, grad_out, grad_router, grad_vec, grad_b_in, grad_b_back = comm_call(
        partial(reduce_kernel, dps, groups),
        "reduce",
        1,
        [V] * 7,
        [
            ((rows, 3 * width), F32, V),
            ((rows, width), F32, V),
            ((experts, rows), F32, V),
            ((7, rows), F32, V),
            ((per_device, rows_back), F32, V),
            ((per_device, rows), F32, V),
        ],
        [
            pltpu.VMEM((dps, halves_of, wide), BF),
            pltpu.VMEM((dps, halves_of, wide), BF),
            pltpu.VMEM((dps - 1, halves_of, wide), BF),
            pltpu.VMEM((dps - 1, halves_of, wide), BF),
            pltpu.VMEM((8, LANES), BF),
            pltpu.VMEM((groups, halves_of, wide), BF),
            pltpu.VMEM((rows, wide), F32),
            pltpu.VMEM((2, dps, small, rows), F32),
            pltpu.VMEM((dps, small, rows), F32),
            pltpu.VMEM((dps - 1, small, rows), F32),
            pltpu.VMEM((groups, small, rows), F32),
            pltpu.VMEM((2, dps, 2 * hosted, rows_back), F32),
            pltpu.VMEM((dps, 2 * hosted, rows_back), F32),
            pltpu.VMEM((dps - 1, 2 * hosted, rows_back), F32),
            pltpu.VMEM((groups, 2 * hosted, rows_back), F32),
            dma((6,)), dma((6,)), dma((6 * dps,)), dma((6 * dps,)),
            dma((6 * groups,)), dma((6 * groups,)), dma((4,)), dma((4,)),
        ],
        moved=20 * width * wide,
    )(g_qkv, g_out, g_router, g_vec_one, g_vec_two, g_b_in, g_b_back)

    grad_w_in, grad_w_back = comm_call(
        partial(finish_kernel, hosted - 1),
        "finish",
        3,
        [V] * (2 * hosted + 1),
        [(w_in.shape, F32, A), (w_back.shape, F32, A)],
        [pltpu.VMEM((rows, ff), F32), pltpu.VMEM((rows_back, width), F32), dma((2,)), dma((2,)), dma((2,))],
        moved=16 * rows * ff,
    )(g_in, g_back, *others, grad_vec)
    return (
        output.reshape(images, half, width),
        dx.reshape(images, half, width),
        grad_vec,
        grad_qkv,
        grad_out,
        grad_router.T,
        grad_w_in,
        grad_b_in,
        grad_w_back,
        grad_b_back,
    )


def solution(mesh):
    tokens = P(("dp", "expert"), "context", None)
    by_rows = P("dp", None)
    experts = P("expert", "dp", None)
    expert_bias = P("expert", "dp")
    return jax.shard_map(
        shards,
        mesh=mesh,
        in_specs=(
            tokens,
            P(("dp", "expert"), None),
            P(("dp", "expert"), "context", None, None),
            tokens,
            P(None, "dp"),
            by_rows,
            by_rows,
            by_rows,
            experts,
            expert_bias,
            experts,
            expert_bias,
            tokens,
        ),
        out_specs=(
            tokens,
            tokens,
            P(None, "dp"),
            by_rows,
            by_rows,
            by_rows,
            experts,
            expert_bias,
            experts,
            expert_bias,
        ),
        check_vma=False,
    )
```

```python
from functools import partial

import jax
import jax.numpy as jnp
from jax import lax
from jax.experimental import pallas as pl
from jax.experimental.pallas import tpu as pltpu
from jax.sharding import PartitionSpec as P

HEADS = 8
EPSILON = 1e-06
LANES = 128
BF = jnp.bfloat16
F32 = jnp.float32
I32 = jnp.int32
MIB = 1 << 20


def up(size, unit):
    return -(-size // unit) * unit


def nn(a, b):
    return jnp.dot(a, b, preferred_element_type=F32)


def nt(a, b):
    return lax.dot_general(a, b, (((1,), (1,)), ((), ())), preferred_element_type=F32)


def tn(a, b):
    return lax.dot_general(a, b, (((0,), (0,)), ((), ())), preferred_element_type=F32)


def iota(shape, dim):
    return lax.broadcasted_iota(I32, shape, dim)


def normed(values):
    average = jnp.mean(values, axis=-1, keepdims=True)
    centred = values - average
    inv_scale = lax.rsqrt(jnp.mean(centred * centred, axis=-1, keepdims=True) + EPSILON)
    return centred * inv_scale, inv_scale


def norm_backward(grad, unit, inv_scale, gain):
    scaled = grad * gain
    centre = jnp.mean(scaled, axis=-1, keepdims=True)
    along = jnp.mean(scaled * unit, axis=-1, keepdims=True)
    return inv_scale * (scaled - centre - unit * along)


def gelu_parts(z):
    share = 0.5 * (1.0 + lax.erf(z * 0.7071067811865476))
    slope = share + z * (0.3989422804014327 * jnp.exp(-0.5 * z * z))
    return z * share, slope


def experts_kernel(
    groups, dps, images, cap_pad, acts, grad, after, router, routes, slots, b_in, b_back, *rest
):
    hosted = groups // 2
    w_in, kin_in, w_back, kin_back, rest = *rest[:4], rest[4:]
    back_rows, output, g_router, g_in, g_back, g_in_other, g_back_other, g_b_in, g_b_back = rest[:9]
    w_in_far, w_back_far, rest = rest[9], rest[10], rest[11:]
    tok, info, made_rows, w_in_v, w_back_v, rows_v, hidden, grad_pre, delta, slope = rest[:10]
    in_send, in_recv, back_send, back_recv, dots, dots_got, to_near, from_near, to_far, from_far = rest[10:20]
    places, x_s, x_r, w_sem, r_s, r_r, p_s, p_r, store_sem, load_sem, w_s, w_r, w_own = rest[20:]
    dp, group, core = lax.axis_index("dp"), lax.axis_index("expert"), lax.axis_index("context")
    tokens, width = output.shape
    ff = w_in_v.shape[1]
    rows_in, rows_back = width // dps, ff // dps
    mate = group + 1 - 2 * lax.rem(group, 2)
    near, across, diagonal = (dp, group, 1 - core), (dp, mate, core), (dp, mate, 1 - core)

    def remote(src, dst, sems, slot, target):
        return pltpu.make_async_remote_copy(
            src_ref=src, dst_ref=dst, send_sem=sems[0].at[slot], recv_sem=sems[1].at[slot],
            device_id=target, device_id_type=MESH,
        )

    pools = (info, tok.at[0], tok.at[1])
    moves = {}
    for at, pool in enumerate(pools):
        moves[at, 1] = remote(pool.at[0], pool.at[1], (x_s, x_r), 3 * at, near)
        moves[at, 2] = remote(pool.at[0], pool.at[2], (x_s, x_r), 3 * at + 1, across)
        moves[at, 3] = remote(pool.at[2], pool.at[3], (x_s, x_r), 3 * at + 2, near)

    def along(step):
        return (lax.rem(dp + step, dps), group, core)

    def sum_out(which, step):
        src, dst = ((in_send, in_recv), (back_send, back_recv))[which]
        return remote(src.at[step], dst.at[step - 1], (r_s, r_r), which * dps + step, along(step))

    def gather(at, which, step):
        kin, far = ((kin_in, w_in_far), (kin_back, w_back_far))[which]
        size = kin.shape[1]
        part = far.at[at, pl.ds(pl.multiple_of(dp * size, size), size)]
        if step == 0:
            return pltpu.make_async_copy(kin.at[at], part, w_own.at[2 * at + which])
        return remote(kin.at[at], part, (w_s, w_r), (2 * at + which) * dps + step, along(step))

    def load(which, wait):
        for at in range(hosted):
            copies = (
                pltpu.make_async_copy(w_in_far.at[at - 1] if at else w_in, w_in_v, w_sem.at[0]),
                pltpu.make_async_copy(w_back_far.at[at - 1] if at else w_back, w_back_v, w_sem.at[1]),
            )

            @pl.when(which == at)
            def _():
                if at and not wait:
                    for part in range(2):
                        for step in range(dps):
                            gather(at - 1, part, step).wait()
                for copy in copies:
                    copy.wait() if wait else copy.start()

    def store(which, to, step):
        return (
            pltpu.make_async_copy(
                in_send.at[step],
                g_in_other.at[which - 1, pl.ds(pl.multiple_of(to * rows_in, rows_in), rows_in)],
                store_sem.at[step],
            ),
            pltpu.make_async_copy(
                back_send.at[step],
                g_back_other.at[which - 1, pl.ds(pl.multiple_of(to * rows_back, rows_back), rows_back)],
                store_sem.at[dps + step],
            ),
        )

    mine = (
        pltpu.make_async_copy(acts, tok.at[0, 0], load_sem.at[0]),
        pltpu.make_async_copy(grad, tok.at[1, 0], load_sem.at[1]),
    )
    for copy in mine:
        copy.start()
    load(0, False)
    greet([near, across, diagonal] + [along(step) for step in range(1, dps)])
    mine[0].wait()
    for hop in (2, 1):
        moves[1, hop].start()
    for at in range(hosted - 1):
        for part in range(2):
            for step in range(dps):
                gather(at, part, step).start()
    logits = nt(router[...], tok[0, 0])
    logits = jnp.exp(logits - jnp.max(logits, axis=0, keepdims=True))
    probs = logits / jnp.sum(logits, axis=0, keepdims=True)
    ids = iota(probs.shape, 0)
    info[0, 2:4, :] = slots[0:2, :].astype(F32)
    for choice in range(2):
        info[0, choice : choice + 1, :] = jnp.sum(
            jnp.where(routes[choice : choice + 1, :] == ids, probs, 0.0), axis=0, keepdims=True
        )
    info[0, 4:8, :] = jnp.zeros((4, tokens), F32)
    mine[1].wait()
    for hop in (2, 1):
        moves[0, hop].start()
        moves[2, hop].start()
    g_b_in[...] = jnp.zeros_like(g_b_in)
    g_b_back[...] = jnp.zeros_like(g_b_back)

    def near_out(at):
        return remote(to_near.at[at], from_near.at[at], (p_s, p_r), at, near)

    def far_out(at):
        return remote(to_far.at[at], from_far.at[at], (p_s, p_r), 4 + at, across)

    def dots_out(source, target):
        return remote(dots.at[source], dots_got.at[source - 1], (p_s, p_r), 5 + source, target)

    def own_row(pair):
        pair = pair.astype(F32)
        return jnp.where(core == 0, pair[0:1], pair[1:2])

    half = tokens // images
    deep = hosted * cap_pad
    slot_ids = jnp.zeros((1, deep), F32)
    lane = iota((1, deep), 1)
    for which in range(hosted):
        first = (lax.rem(group + 2 * which, groups) * 2 + core - which) * cap_pad
        slot_ids = jnp.where(lane // cap_pad == which, (lane + first).astype(F32), slot_ids)

    def place(source):
        slot = info[source, 2:4, :]
        high = jnp.floor(slot * (1.0 / 64.0))
        parts = jnp.concatenate([high, slot - 64.0 * high, jnp.zeros((4, tokens), F32)], axis=0).astype(BF)
        row, col = iota((8, LANES), 0), iota((8, LANES), 1)
        weight = jnp.where(row == col, 64.0, jnp.where(row == col + 2, 1.0, 0.0))
        weight = jnp.where(col < 2, weight, 0.0).astype(BF)
        places[...] = tn(parts, weight)

    def summed(source, image):
        rows = pl.ds(pl.multiple_of(image * half, 8), half)
        hit = (places[rows, 0:1] == slot_ids) | (places[rows, 1:2] == slot_ids)
        return rows, nn(jnp.where(hit, 1.0, 0.0).astype(BF), made_rows[source])

    def to_core(source, at):
        place(source)

        def chunk(image, _):
            rows, part = summed(source, image)
            to_near[at, rows, :] = part[:, :width].astype(BF)
            to_near[at + 1, rows, :] = part[:, width:].astype(BF)
            return 0

        lax.fori_loop(0, images, chunk, 0)
        near_out(at).start()
        near_out(at + 1).start()

    def to_chip():
        place(2)
        near_out(0).wait_recv()
        near_out(1).wait_recv()

        def chunk(image, _):
            rows, part = summed(2, image)
            to_far[0, rows, :] = (part[:, :width] + from_near[0, rows, :].astype(F32)).astype(BF)
            to_far[1, rows, :] = (part[:, width:] + from_near[1, rows, :].astype(F32)).astype(BF)
            return 0

        lax.fori_loop(0, images, chunk, 0)
        far_out(0).start()
        far_out(1).start()

    def expert(which, _):
        load(which, True)
        own = lax.rem(group + 2 * which, groups) * 2 + core
        last = which // (hosted - 1)

        def block(turn, _):
            source = turn + (3 - 2 * turn) * last

            @pl.when(jnp.logical_and(which == 0, source == 1))
            def _():
                for at in range(3):
                    moves[at, 1].wait_recv()

            @pl.when(jnp.logical_and(which == 0, source == 2))
            def _():
                for at in range(3):
                    moves[at, 2].wait_recv()
                    moves[at, 3].start()

            @pl.when(jnp.logical_and(which == 0, source == 3))
            def _():
                for at in range(3):
                    moves[at, 3].wait_recv()

            rows = pl.ds(pl.multiple_of(source * cap_pad, 16), cap_pad)
            spot = pl.ds(pl.multiple_of(which * cap_pad, 16), cap_pad)
            ids = iota((cap_pad, tokens), 0) + own * cap_pad
            hit_first = ids == info[source, 2:3, :].astype(I32)
            hit_second = ids == info[source, 3:4, :].astype(I32)
            hit = jnp.logical_or(hit_first, hit_second)
            one_hot = jnp.where(hit, 1.0, 0.0).astype(BF)
            gate = jnp.where(hit_first, info[source, 0:1, :], 0.0) + jnp.where(hit_second, info[source, 1:2, :], 0.0)
            gate = jnp.sum(gate, axis=1, keepdims=True)
            acts_in = nn(one_hot, tok[0, source]).astype(BF)
            for part in range(dps):
                rows_v[part, rows, :] = acts_in[:, part * rows_in : (part + 1) * rows_in]
            for part in range(dps):
                cols = slice(part * rows_back, (part + 1) * rows_back)
                z = nn(acts_in, w_in_v[:, cols]) + own_row(b_in[which, part])
                value, rise = gelu_parts(z)
                hidden[rows, cols] = value.astype(BF)
                slope[:, cols] = rise.astype(BF)
            bias = jnp.concatenate([own_row(b_back[which, part]) for part in range(dps)], axis=1)
            made = (nn(hidden[rows, :], w_back_v[...]) + bias).astype(BF).astype(F32)
            made_rows[source, spot, width:] = (gate * made).astype(BF)
            got_grad = nn(one_hot, tok[1, source])
            low = (gate * got_grad).astype(BF)
            delta[rows, :] = low
            g_b_back[which, core] += jnp.sum(low.astype(F32), axis=0, keepdims=True)
            dot = jnp.sum(made * got_grad, axis=1, keepdims=True)
            dots[source, which] = jnp.sum(jnp.where(hit, dot, 0.0), axis=0, keepdims=True)
            for part in range(dps):
                cols = slice(part * rows_back, (part + 1) * rows_back)
                dz = nt(low, w_back_v[cols, :]) * slope[:, cols].astype(F32)
                g_b_in[which, core, :, cols] += jnp.sum(dz, axis=0, keepdims=True)
                grad_pre[rows, cols] = dz.astype(BF)
            made_rows[source, spot, :width] = nt(grad_pre[rows, :], w_in_v[...]).astype(BF)

            @pl.when(jnp.logical_and(last == 1, source == 3))
            def _():
                dots_out(3, diagonal).start()
                to_core(3, 0)

            @pl.when(jnp.logical_and(last == 1, source == 2))
            def _():
                dots_out(2, across).start()
                to_chip()

            @pl.when(jnp.logical_and(last == 1, source == 1))
            def _():
                dots_out(1, near).start()
                to_core(1, 2)

            return 0

        lax.fori_loop(0, 4, block, 0)
        @pl.when(which + 1 < hosted)
        def _():
            load(which + 1, False)

        def weights(step, _):
            step = lax.rem(step + 1, dps)
            to = lax.rem(dp + step, dps)
            part_back = tn(hidden[:, pl.ds(pl.multiple_of(to * rows_back, LANES), rows_back)], delta[...])
            part_in = tn(rows_v[to], grad_pre[...])

            @pl.when(jnp.logical_and(which == 1, step > 0))
            def _():
                sum_out(0, step).wait_send()
                sum_out(1, step).wait_send()

            @pl.when(which > 1)
            def _():
                for copy in store(which - 1, to, step):
                    copy.wait()

            back_send[step] = part_back.astype(BF)
            in_send[step] = part_in.astype(BF)

            @pl.when(jnp.logical_and(which == 0, step > 0))
            def _():
                sum_out(1, step).start()
                sum_out(0, step).start()

            @pl.when(jnp.logical_and(which == 0, step == 0))
            def _():
                g_back[...] = part_back
                g_in[...] = part_in

            @pl.when(which > 0)
            def _():
                for copy in store(which, to, step):
                    copy.start()

            return 0

        lax.fori_loop(0, dps, weights, 0)
        return 0

    lax.fori_loop(0, hosted, expert, 0)
    for source, target in ((1, near), (2, across), (3, diagonal)):
        dots_out(source, target).wait_recv()
    at_near, at_far = 1 - core, core
    whole = jnp.zeros(probs.shape, F32)
    for which in range(hosted):
        here, there = lax.rem(group + 2 * which, groups) * 2, lax.rem(mate + 2 * which, groups) * 2
        whole = jnp.where(ids == here + core, dots[0, which], whole)
        whole = jnp.where(ids == here + at_near, dots_got[0, which], whole)
        whole = jnp.where(ids == there + at_far, dots_got[1, which], whole)
        whole = jnp.where(ids == there + at_near, dots_got[2, which], whole)
    low = (probs * (whole - jnp.sum(probs * whole, axis=0, keepdims=True))).astype(BF)
    g_router[...] = nn(low, tok[0, 0])
    back_rows[...] = tn(low, router[...])
    place(0)
    near_out(2).wait_recv()
    near_out(3).wait_recv()
    far_out(0).wait_recv()
    far_out(1).wait_recv()

    def chunk(image, _):
        rows, part = summed(0, image)
        back_rows[rows, :] += part[:, :width] + from_near[2, rows, :].astype(F32) + from_far[0, rows, :].astype(F32)
        out = part[:, width:] + from_near[3, rows, :].astype(F32) + from_far[1, rows, :].astype(F32)
        output[rows, :] = (after[rows, :] + out).astype(BF)
        return 0

    lax.fori_loop(0, images, chunk, 0)
    for step in range(1, dps):
        for which in range(2):
            sum_out(which, step).wait_recv()
        g_back[...] += back_recv[step - 1].astype(F32)
        g_in[...] += in_recv[step - 1].astype(F32)

    for step in range(dps):
        for copy in store(hosted - 1, lax.rem(dp + step, dps), step):
            copy.wait()
    for copy in moves.values():
        copy.wait_send()
    for at in range(4):
        near_out(at).wait_send()
    for at in range(2):
        far_out(at).wait_send()
    for source, target in ((1, near), (2, across), (3, diagonal)):
        dots_out(source, target).wait_send()


def forward_image(
    half, image, dps, x, x_other, bias, vec, w_qkv, w_out, q_ref, k_ref, v_ref, p_ref, o_ref, h_ref, a_ref
):
    width = x.shape[1]
    rows = pl.ds(pl.multiple_of(image * half, 8), half)
    half_pad = up(half, 16)
    head_dim = width // HEADS
    scale = head_dim ** (-0.5)
    gain, offset, bias_q, bias_v = (vec[row : row + 1, :] for row in range(4))
    own = x[rows, :].astype(F32)
    unit, _ = normed(own)
    acts = (unit * gain + offset).astype(BF)
    unit, _ = normed(x_other[rows, :].astype(F32))
    other = (unit * gain + offset).astype(BF)

    def weight(at):
        return w_qkv[:, :, at * width : (at + 1) * width].reshape(width, width)

    q_ref[rows, :] = ((nn(acts, weight(0)) + bias_q).astype(BF).astype(F32) * scale).astype(BF)
    pad = jnp.zeros((half_pad - half, width), BF)
    for part, piece in enumerate((acts, other)):
        start = part * half_pad
        k_ref[image, pl.ds(start, half), :] = nn(piece, weight(1)).astype(BF)
        v_ref[image, pl.ds(start, half), :] = (nn(piece, weight(2)) + bias_v).astype(BF)
        if half_pad > half:
            k_ref[image, pl.ds(start + half, half_pad - half), :] = pad
            v_ref[image, pl.ds(start + half, half_pad - half), :] = pad
    low = iota((1, LANES), 1) < head_dim
    zero = jnp.zeros((), BF)
    for pair in range(width // LANES):
        cols = pl.ds(pair * LANES, LANES)
        q_pair, k_pair, v_pair = q_ref[rows, cols], k_ref[image, :, cols], v_ref[image, :, cols]
        mixed = []
        for sub in range(2):
            mask = low if sub == 0 else jnp.logical_not(low)
            scores = nt(jnp.where(mask, q_pair, zero), k_pair) + bias[image]
            raised = jnp.exp(scores - jnp.max(scores, axis=1, keepdims=True))
            probs = (raised * (1.0 / jnp.sum(raised, axis=1, keepdims=True))).astype(BF)
            p_ref[image, 2 * pair + sub] = probs
            mixed.append(nn(probs, v_pair))
        o_ref[rows, cols] = jnp.where(low, mixed[0], mixed[1]).astype(BF)
    after = own + nn(o_ref[rows, :], w_out[...].reshape(width, width)) + vec[4:5, :]
    h_ref[rows, :] = after
    unit, _ = normed(after)
    a_ref[rows, :] = (unit * vec[5:6, :] + vec[6:7, :]).astype(BF)


def backward_image(
    half, image, grad, back_ref, h_ref, o_ref, vec, w_out, q_ref, k_ref, v_ref, p_ref,
    dh_ref, dq_ref, dk_ref, dv_ref, g_out, g_vec,
):
    width = grad.shape[1]
    rows = pl.ds(pl.multiple_of(image * half, 8), half)
    head_dim = width // HEADS
    half_pad = up(half, 16)
    lane = iota((1, LANES), 1)
    back = back_ref[rows, :]
    unit, inv_scale = normed(h_ref[rows, :])
    dh = grad[rows, :].astype(F32) + norm_backward(back, unit, inv_scale, vec[5:6, :])
    dh_ref[rows, :] = dh
    dh_low = dh.astype(BF)
    g_out[...] += tn(o_ref[rows, :], dh_low)
    g_vec[4:5, :] += jnp.sum(dh, axis=0, keepdims=True)
    g_vec[5:6, :] += jnp.sum(back * unit, axis=0, keepdims=True)
    g_vec[6:7, :] += jnp.sum(back, axis=0, keepdims=True)
    do = nt(dh_low, w_out[...].reshape(width, width)).astype(BF)
    low = lane < head_dim
    zero = jnp.zeros((), BF)
    scale = head_dim ** (-0.5)
    for pair in range(width // LANES):
        cols = slice(pair * LANES, (pair + 1) * LANES)
        do_pair = do[:, cols]
        q_pair, k_pair, v_pair = q_ref[rows, cols], k_ref[image, :, cols], v_ref[image, :, cols]
        dq, dk, dv = [], [], []
        for sub in range(2):
            mask = low if sub == 0 else jnp.logical_not(low)
            p_low = p_ref[2 * pair + sub]
            p = p_low.astype(F32)
            dp = nt(jnp.where(mask, do_pair, zero), v_pair)
            inner = jnp.sum(p * dp, axis=1, keepdims=True)
            ds = (p * (dp - inner)).astype(BF)
            dv.append(tn(p_low, do_pair))
            dk.append(tn(ds, q_pair))
            dq.append(nn(ds, k_pair))
        dq_ref[rows, cols] = (jnp.where(low, dq[0], dq[1]) * scale).astype(BF)
        dk_pair = jnp.where(low, dk[0], dk[1]).astype(BF)
        dv_pair = jnp.where(low, dv[0], dv[1]).astype(BF)
        for part in range(2):
            dk_ref[part, rows, cols] = dk_pair[part * half_pad : part * half_pad + half]
            dv_ref[part, rows, cols] = dv_pair[part * half_pad : part * half_pad + half]


def input_image(half, image, x_ref, dh_ref, dq_ref, dk_ref, dk_got, dv_ref, dv_got, vec, w_qkv, dx_ref, g_qkv, g_vec):
    width = x_ref.shape[1]
    rows = pl.ds(pl.multiple_of(image * half, 8), half)
    unit, inv_scale = normed(x_ref[rows, :].astype(F32))
    acts = (unit * vec[0:1, :] + vec[1:2, :]).astype(BF)
    dq = dq_ref[rows, :]
    dk = (dk_ref[0, rows, :].astype(F32) + dk_got[rows, :].astype(F32)).astype(BF)
    dv = (dv_ref[0, rows, :].astype(F32) + dv_got[rows, :].astype(F32)).astype(BF)
    da = jnp.zeros(unit.shape, F32)
    for at, piece in enumerate((dq, dk, dv)):
        cols = slice(at * width, (at + 1) * width)
        g_qkv[:, cols] += tn(acts, piece)
        da = da + nt(piece, w_qkv[:, :, cols].reshape(width, width))
    dx_ref[rows, :] = (dh_ref[rows, :] + norm_backward(da, unit, inv_scale, vec[0:1, :])).astype(BF)
    g_vec[0:1, :] += jnp.sum(da * unit, axis=0, keepdims=True)
    g_vec[1:2, :] += jnp.sum(da, axis=0, keepdims=True)
    g_vec[2:3, :] += jnp.sum(dq.astype(F32), axis=0, keepdims=True)
    g_vec[3:4, :] += jnp.sum(dv.astype(F32), axis=0, keepdims=True)


MESH = pl.DeviceIdType.MESH


def send(src, dst, sems, slot, device):
    copy = pltpu.make_async_remote_copy(
        src_ref=src, dst_ref=dst, send_sem=sems[0].at[slot], recv_sem=sems[1].at[slot],
        device_id=device, device_id_type=MESH,
    )
    copy.start()
    return copy


def greet(devices):
    barrier = pltpu.get_barrier_semaphore()
    for device in devices:
        pl.semaphore_signal(barrier, inc=1, device_id=device, device_id_type=MESH)
    pl.semaphore_wait(barrier, len(devices))


def comm_call(body, name, number, ins, outs, scratch, flops=0, moved=0, vmem=56):
    return pl.pallas_call(
        body,
        name=name,
        in_specs=[pl.BlockSpec(memory_space=space) for space in ins],
        out_specs=[pl.BlockSpec(memory_space=space) for _, _, space in outs],
        out_shape=[jax.ShapeDtypeStruct(shape, dtype) for shape, dtype, _ in outs],
        scratch_shapes=list(scratch),
        cost_estimate=pl.CostEstimate(flops=int(flops), bytes_accessed=int(moved), transcendentals=0),
        compiler_params=pltpu.CompilerParams(
            vmem_limit_bytes=vmem * MIB, collective_id=number, has_side_effects=True
        ),
    )


def start_kernel(
    dps, groups, images, cap, cap_pad, x, w_qkv, w_out, w_router, vectors, b_in, b_back, routes, key_col, key_row, bias,
    w_in, w_back,
    qkv_all, out_all, router_rows, b_in_all, back_all, vec, slots,
    q_ref, k_ref, v_ref, p_ref, o_ref, h_ref, a_ref, in_all, in_kin, back_w_all, back_kin,
    x_other, router_all, vec_all, p_all, w_in_f, w_back_f, w_in_v, w_back_v,
    far_send, far_recv, near_send, near_recv, deep_send, deep_recv, w_s, w_r, local,
):
    dp, group, core = lax.axis_index("dp"), lax.axis_index("expert"), lax.axis_index("context")
    rows = w_qkv.shape[0]
    half = rows // 2
    hosted = groups // 2
    near = (dp, group, 1 - core)
    peers = [(lax.rem(dp + step, dps), group, core) for step in range(1, dps)]
    kin = [(dp, lax.rem(group + 2 * step, groups), core) for step in range(1, hosted)]
    loads = [
        pltpu.make_async_copy(w_in.at[core], w_in_f, local.at[0]),
        pltpu.make_async_copy(w_back.at[core], w_back_f, local.at[1]),
    ]
    for copy in loads:
        copy.start()
    greet(peers + kin + [near])
    far, close, deep = (far_send, far_recv), (near_send, near_recv), (deep_send, deep_recv)
    waits = [send(x, x_other, close, 0, near)]
    qkv_all[dp] = w_qkv[...].astype(BF)
    own = pl.ds(pl.multiple_of(core * half, half), half)
    copies = []
    for step, peer in enumerate(peers):
        copies.append(send(qkv_all.at[dp, own], qkv_all.at[dp, own], far, step * 6, peer))
    out_all[dp] = w_out[...].astype(BF)
    spare = router_all.shape[2] - w_router.shape[1]
    router_all[dp] = jnp.concatenate([w_router[...], jnp.zeros((rows, spare), F32)], axis=1).astype(BF)
    vec_all[dp] = jnp.concatenate([vectors[...], jnp.zeros((1, rows), F32)], axis=0).astype(BF)
    b_in_all[0, dp] = b_in[...].astype(BF)
    back_all[0, dp] = b_back[...].astype(BF)
    for step, peer in enumerate(peers):
        copies.append(send(out_all.at[dp, own], out_all.at[dp, own], far, step * 6 + 1, peer))
    smalls, biases = [], []
    for step, peer in enumerate(peers):
        for at, ref in enumerate((router_all, vec_all)):
            smalls.append(send(ref.at[dp], ref.at[dp], far, step * 6 + 2 + at, peer))
        for at, ref in enumerate((b_in_all, back_all)):
            biases.append(send(ref.at[0, dp], ref.at[0, dp], far, step * 6 + 4 + at, peer))
    own_copies = []
    for at, (wide, low, out, kin_out) in enumerate(
        ((w_in_f, w_in_v, in_all, in_kin), (w_back_f, w_back_v, back_w_all, back_kin))
    ):
        loads[at].wait()
        low[...] = wide[...].astype(BF)
        size = low.shape[0]
        part = pl.ds(pl.multiple_of(dp * size, size), size)
        for step, peer in enumerate(kin):
            own_copies.append(
                send(low, kin_out.at[hosted - 2 - step], (w_s, w_r), at * (dps + hosted) + dps + step, peer)
            )
        for step, peer in enumerate(peers):
            own_copies.append(send(low, out.at[part], (w_s, w_r), at * (dps + hosted) + step, peer))
        here = pltpu.make_async_copy(low, out.at[part], local.at[2 + at])
        here.start()
        own_copies.append(here)

    tokens = routes.shape[1]
    experts = w_router.shape[1]
    ids = iota((experts, tokens), 0)
    before = jnp.where(key_col[...] < key_row[...], 1.0, 0.0).astype(BF)
    first = jnp.where(routes[0:1, :] == ids, 1.0, 0.0)
    second = jnp.where(routes[1:2, :] == ids, 1.0, 0.0)
    count = jnp.sum(first, axis=1, keepdims=True)
    rank_first = jnp.sum(nn(first.astype(BF), before) * first, axis=0, keepdims=True)
    rank_second = jnp.sum((nn(second.astype(BF), before) + count) * second, axis=0, keepdims=True)
    ranks = jnp.concatenate([rank_first, rank_second], axis=0).astype(I32)
    owned = jnp.where(ranks < cap, routes[...] * cap_pad + ranks, -1)
    slots[...] = jnp.concatenate([owned, jnp.full((6, tokens), -1, I32)], axis=0)

    for copy in biases:
        copy.wait()
    for step, peer in enumerate(kin):
        for at, ref in enumerate((b_in_all, back_all)):
            waits.append(send(ref.at[0], ref.at[hosted - 1 - step], deep, 2 * step + at, peer))
    for at, copy in enumerate(copies):
        step, ref = at % len(peers), (qkv_all, out_all)[at // len(peers)]
        copy.wait()
        source = lax.rem(dp - step - 1 + dps, dps)
        waits.append(send(ref.at[source, own], ref.at[source, own], close, 1 + at, near))
    for copy in smalls:
        copy.wait()
    vec[...] = jnp.concatenate([vec_all[at].astype(F32) for at in range(dps)], axis=1)
    turned = [router_all[at].astype(F32).T[: w_router.shape[1]] for at in range(dps)]
    router_rows[...] = jnp.concatenate(turned, axis=1).astype(BF)
    for copy in waits:
        copy.wait()

    half = tokens // images

    def image_step(image, _):
        forward_image(
            half, image, dps, x, x_other, bias, vec, qkv_all, out_all, q_ref, k_ref, v_ref, p_all, o_ref, h_ref, a_ref
        )
        pltpu.make_async_copy(p_all.at[image], p_ref.at[image], local.at[4]).start()
        return 0

    lax.fori_loop(0, images, image_step, 0)
    pltpu.make_async_copy(p_all, p_ref, local.at[4]).wait()
    for copy in own_copies:
        copy.wait()


def back_kernel(
    dps, groups, images, grad, back_rows, h_ref, o_ref, vec, w_out, q_ref, k_ref, v_ref, x_ref, w_qkv,
    g_router, g_in, g_back, b_in, b_back, p_all, in_other, back_other,
    dx_ref, o_qkv, o_out, o_router, o_vec, o_in, o_back, w_in_sum, w_back_sum, in_recv, back_recv,
    sum_in, sum_back, p_two, dh_ref, dq_ref, dk_ref, dv_ref, dk_got, dv_got, g_out, g_qkv, g_vec,
    in_stage, back_stage, in_to, back_to, in_from, back_from,
    near_out, near_in, far_out, far_in, deep_in, total,
    small_near, small_far, small_got, small_deep, bin_near, bin_far, bin_got, bin_deep,
    near_s, near_r, far_s, far_r, deep_s, deep_r, last_s, last_r,
    p_sem, d_s, d_r, e_s, e_r, stage_sem, kin_s, kin_r, home_s, home_r, home_sem,
):
    dp, group, core = lax.axis_index("dp"), lax.axis_index("expert"), lax.axis_index("context")
    tokens, width = dx_ref.shape
    hosted = groups // 2
    token_half = tokens // images
    rows = width // dps
    half = rows // 2
    near = (dp, group, 1 - core)
    peers = [(lax.rem(dp + step, dps), group, core) for step in range(1, dps)]
    others = [(dp, lax.rem(group + step, groups), core) for step in range(1, groups)]

    def remote(src, dst, sems, slot, target):
        return pltpu.make_async_remote_copy(
            src_ref=src, dst_ref=dst, send_sem=sems[0].at[slot], recv_sem=sems[1].at[slot],
            device_id=target, device_id_type=MESH,
        )

    sets = (
        (back_other, back_recv, back_stage, back_to, back_from, g_back, w_back_sum),
        (in_other, in_recv, in_stage, in_to, in_from, g_in, w_in_sum),
    )

    def sum_out(which, part, at, step):
        other, recv = sets[which][:2]
        size = recv.shape[2]
        piece = size // 2
        target = lax.rem(dp + step, dps)
        src = other.at[at, pl.ds(pl.multiple_of(target * size, size) + part * piece, piece)]
        dst = recv.at[at, step - 1, pl.ds(part * piece, piece)]
        slot = ((which * 2 + part) * (hosted - 1) + at) * dps + step
        return remote(src, dst, (e_s, e_r), slot, peers[step - 1])

    def home_out(which, part, at):
        to, back = sets[which][3:5]
        piece = to.shape[1] // 2
        here = pl.ds(part * piece, piece)
        target = (dp, lax.rem(group + 2 * (at + 1), groups), core)
        slot = (which * 2 + part) * (hosted - 1) + at
        return pltpu.make_async_remote_copy(
            src_ref=to.at[at, here], dst_ref=back.at[hosted - 2 - at, here],
            send_sem=kin_s.at[slot], recv_sem=kin_r.at[(which * 2 + part) * (hosted - 1) + hosted - 2 - at],
            device_id=target, device_id_type=MESH,
        )

    def home_in(which, part, at):
        to, back = sets[which][3:5]
        piece = to.shape[1] // 2
        here = pl.ds(part * piece, piece)
        slot = (which * 2 + part) * (hosted - 1) + at
        return pltpu.make_async_remote_copy(
            src_ref=to.at[at, here], dst_ref=back.at[at, here], send_sem=kin_s.at[slot], recv_sem=kin_r.at[slot],
            device_id=near, device_id_type=MESH,
        )

    def send_home(which, part):
        other, recv, stage, to = sets[which][:4]
        size = recv.shape[2]
        piece = size // 2
        here = pl.ds(part * piece, piece)
        for at in range(hosted - 1):
            for step in range(1, dps):
                sum_out(which, part, at, step).wait_recv()
            own = other.at[at, pl.ds(pl.multiple_of(dp * size, size) + part * piece, piece)]
            copies = (
                pltpu.make_async_copy(recv.at[at, :, here], stage.at[pl.ds(0, dps - 1)], stage_sem.at[0]),
                pltpu.make_async_copy(own, stage.at[dps - 1], stage_sem.at[1]),
            )
            for copy in copies:
                copy.start()
            for copy in copies:
                copy.wait()
            value = stage[0].astype(F32)
            for step in range(1, dps):
                value = value + stage[step].astype(F32)
            to[at, here, :] = value.astype(BF)
            home_out(which, part, at).start()

    def load(image):
        slot = lax.rem(image, 2)
        return pltpu.make_async_copy(p_all.at[image], p_two.at[slot], p_sem.at[slot])

    def swap(image, which):
        here = pl.ds(pl.multiple_of(image * token_half, 8), token_half)
        src, dst = ((dk_ref, dk_got), (dv_ref, dv_got))[which]
        return remote(src.at[1, here], dst.at[here], (d_s, d_r), 2 * image + which, near)

    load(0).start()
    greet(peers + others + [near])
    for which in range(2):
        for part in range(2):
            for at in range(hosted - 1):
                for step in range(1, dps):
                    sum_out(which, part, at, step).start()
    g_out[...] = jnp.zeros_like(g_out)
    g_qkv[...] = jnp.zeros_like(g_qkv)
    g_vec[...] = jnp.zeros_like(g_vec)

    def back_step(image, _):
        load(image).wait()

        @pl.when(image + 1 < images)
        def _():
            load(image + 1).start()

        backward_image(
            token_half, image, grad, back_rows, h_ref, o_ref, vec, w_out, q_ref, k_ref, v_ref,
            p_two.at[lax.rem(image, 2)], dh_ref, dq_ref, dk_ref, dv_ref, g_out, g_vec,
        )
        swap(image, 0).start()
        swap(image, 1).start()

        @pl.when(image == images - 2)
        def _():
            send_home(0, 0)

        return 0

    lax.fori_loop(0, images, back_step, 0)
    send_home(0, 1)

    near_sems, far_sems, deep_sems, last_sems = (near_s, near_r), (far_s, far_r), (deep_s, deep_r), (last_s, last_r)
    sources = [(g_out, 0)] + [(g_qkv, at) for at in range(0, g_qkv.shape[1], width)]
    theirs = pl.multiple_of((1 - core) * half, half)
    ours = pl.multiple_of(core * half, half)

    def cols_of(at):
        return pl.ds(width * at, width)

    def to_core(at):
        ref, lane = sources[at]
        for block in range(dps):
            near_out[block, :, cols_of(at)] = ref[pl.ds(block * rows + theirs, half), lane : lane + width].astype(BF)
        return send(near_out.at[:, :, cols_of(at)], near_in.at[:, :, cols_of(at)], near_sems, 2 + at, near)

    first = [to_core(0)]

    def input_step(image, _):
        swap(image, 0).wait_recv()
        swap(image, 1).wait_recv()
        input_image(
            token_half, image, x_ref, dh_ref, dq_ref, dk_ref, dk_got, dv_ref, dv_got, vec, w_qkv, dx_ref, g_qkv, g_vec
        )
        return 0

    lax.fori_loop(0, images, input_step, 0)
    for at in range(1, len(sources)):
        first.append(to_core(at))

    deep = small_near.shape[2]
    tall = 2 * hosted
    router = 8 + tall
    bias_rows = [b_back[at // 2, at % 2] for at in range(tall)]
    bias_in = jnp.concatenate([b_in[at // 2, at % 2] for at in range(tall)], axis=0)
    small = [g_vec[...]] + bias_rows + [g_router[...]]
    spare = deep - router - g_router.shape[0]
    small = jnp.concatenate(small + ([jnp.zeros((spare, width), F32)] if spare else []), axis=0)
    for at in range(dps):
        small_near[0, at] = small[:, at * rows : (at + 1) * rows]
        bin_near[0, at] = bias_in[:, at * bin_near.shape[3] : (at + 1) * bin_near.shape[3]]
    firsts = [
        send(small_near.at[0], small_near.at[1], near_sems, 0, near),
        send(bin_near.at[0], bin_near.at[1], near_sems, 1, near),
    ]
    second = []
    for at, (ref, lane) in enumerate(sources):
        cols = cols_of(at)
        first[at].wait()
        for step, peer in enumerate(peers):
            target = lax.rem(dp + step + 1, dps)
            block = ref[pl.ds(pl.multiple_of(target * rows, rows) + ours, half), lane : lane + width]
            far_out[step, :, cols] = (block + near_in[target, :, cols].astype(F32)).astype(BF)
            second.append(
                send(far_out.at[step, :, cols], far_in.at[step, :, cols], far_sems, (2 + at) * dps + step, peer)
            )
    for copy in firsts:
        copy.wait()
    small_far[...] = small_near[0] + small_near[1]
    bin_far[...] = bin_near[0] + bin_near[1]
    smalls = []
    for step, peer in enumerate(peers):
        target = lax.rem(dp + step + 1, dps)
        smalls.append(send(small_far.at[target], small_got.at[step], far_sems, step, peer))
        smalls.append(send(bin_far.at[target], bin_got.at[step], far_sems, dps + step, peer))
    send_home(1, 0)
    third = []
    for at, (ref, lane) in enumerate(sources):
        cols = cols_of(at)
        mine = ref[pl.ds(pl.multiple_of(dp * rows, rows) + ours, half), lane : lane + width]
        mine = mine + near_in[dp, :, cols].astype(F32)
        for step in range(dps - 1):
            second[at * (dps - 1) + step].wait()
            mine = mine + far_in[step, :, cols].astype(F32)
        deep_in[group, :, cols] = mine.astype(BF)
        for step, peer in enumerate(others):
            third.append(
                send(deep_in.at[group, :, cols], deep_in.at[group, :, cols], deep_sems, at * groups + step, peer)
            )
    send_home(1, 1)
    for copy in smalls:
        copy.wait()
    lone = small_far[dp]
    lone_in = bin_far[dp]
    for step in range(dps - 1):
        lone = lone + small_got[step]
        lone_in = lone_in + bin_got[step]
    small_deep[group] = lone
    bin_deep[group] = lone_in
    deep_small = []
    for step, peer in enumerate(others):
        slot = len(sources) * groups + step
        deep_small.append(send(small_deep.at[group], small_deep.at[group], deep_sems, slot, peer))
        deep_small.append(send(bin_deep.at[group], bin_deep.at[group], deep_sems, groups + slot, peer))
    last = []
    here = pl.ds(ours, half)
    for at in range(len(sources)):
        cols = cols_of(at)
        for step in range(groups - 1):
            third[at * (groups - 1) + step].wait()
        done = deep_in[0, :, cols].astype(F32)
        for source in range(1, groups):
            done = done + deep_in[source, :, cols].astype(F32)
        total[here, cols] = done
        last.append(send(total.at[here, cols], total.at[here, cols], last_sems, at, near))
    for copy in deep_small:
        copy.wait()
    lone = small_deep[0]
    for at in range(1, groups):
        lone = lone + small_deep[at]
    o_vec[...] = lone[0:7]
    o_router[...] = lone[router : router + o_router.shape[0]]
    grad_in, grad_back = jnp.zeros(o_in.shape, F32), jnp.zeros(o_back.shape, F32)
    for at in range(groups):
        away = lax.rem(group - at + groups, groups)
        kin = lax.rem(away, 2) == 0
        pick_in, pick_back = jnp.zeros(o_in.shape, F32), jnp.zeros(o_back.shape, F32)
        for which in range(hosted):
            found = away // 2 == which
            pick_in = jnp.where(found, bin_deep[at, 2 * which : 2 * which + 2], pick_in)
            pick_back = jnp.where(found, small_deep[at, 8 + 2 * which : 10 + 2 * which], pick_back)
        grad_in = grad_in + jnp.where(kin, pick_in, 0.0)
        grad_back = grad_back + jnp.where(kin, pick_back, 0.0)
    o_in[...] = grad_in
    o_back[...] = grad_back
    for copy in last:
        copy.wait()
    o_qkv[...] = total[:, width : 4 * width]
    o_out[...] = total[:, :width]

    stores = []
    for which, (_, _, _, to, back, own, out) in enumerate(sets):
        for part in range(2):
            for at in range(hosted - 1):
                home_in(which, part, at).wait_recv()
        value = own[...]
        for at in range(hosted - 1):
            value = value + back[at].astype(F32)
        whole = (sum_back, sum_in)[which]
        whole[...] = value
        stores.append(send(whole, out.at[core], (home_s, home_r), which, near))
        copy = pltpu.make_async_copy(whole, out.at[core], home_sem.at[which])
        copy.start()
        stores.append(copy)
    for which in range(2):
        for part in range(2):
            for at in range(hosted - 1):
                home_out(which, part, at).wait_send()
                for step in range(1, dps):
                    sum_out(which, part, at, step).wait_send()
    for image in range(images):
        for which in range(2):
            swap(image, which).wait_send()
    for copy in stores:
        copy.wait()


def shards(
    inputs, key_mask, routes, priority, vectors, w_qkv, w_out, w_router, w_in, b_in, w_back, b_back, cotangent
):
    images, half, width = inputs.shape
    tokens = images * half
    groups = lax.axis_size("expert")
    dps = lax.axis_size("dp")
    per_device = w_in.shape[0]
    experts = groups * per_device
    ff = w_in.shape[2]
    cap = max(2, 3 * tokens // experts)
    cap_pad = up(cap, 16)
    half_pad = up(half, 16)
    hosted = groups // 2
    context = lax.axis_index("context")
    V, A = pltpu.VMEM, pl.ANY
    dma = pltpu.SemaphoreType.DMA
    rows = w_qkv.shape[0]
    rows_back = ff // dps

    x = inputs.reshape(tokens, width)
    grad = cotangent.reshape(tokens, width)
    route_rows = routes.reshape(tokens, 2).T
    keys = priority.reshape(tokens) * tokens + jnp.arange(tokens, dtype=I32)

    mask = jnp.where(key_mask > 0, 0.0, -1e30).astype(F32)
    first, second = mask[:, :half], mask[:, half:]
    own = jnp.where(context == 0, first, second)
    other = jnp.where(context == 0, second, first)
    off = jnp.full((images, half_pad - half), -1e30, F32)
    bias = jnp.concatenate([own, off, other, off], axis=1)[:, None, :]
    keys_pad = 2 * half_pad

    made = comm_call(
        partial(start_kernel, dps, groups, images, cap, cap_pad),
        "front",
        0,
        [V] * 11 + [A] * 2,
        [
            ((dps, rows, 3 * width), BF, V),
            ((dps, rows, width), BF, V),
            ((experts, width), BF, V),
            ((hosted, dps, per_device, rows_back), BF, V),
            ((hosted, dps, per_device, rows), BF, V),
            ((8, width), F32, V),
            ((8, tokens), I32, V),
            ((tokens, width), BF, V),
            ((images, keys_pad, width), BF, V),
            ((images, keys_pad, width), BF, V),
            ((images, HEADS, half, keys_pad), BF, A),
            ((tokens, width), BF, V),
            ((tokens, width), F32, V),
            ((tokens, width), BF, V),
            ((width, ff), BF, A),
            ((hosted - 1, rows, ff), BF, A),
            ((ff, width), BF, A),
            ((hosted - 1, rows_back, width), BF, A),
        ],
        [
            pltpu.VMEM((tokens, width), BF),
            pltpu.VMEM((dps, rows, LANES), BF),
            pltpu.VMEM((dps, 8, rows), BF),
            pltpu.VMEM((images, HEADS, half, keys_pad), BF),
            pltpu.VMEM((rows, ff), F32),
            pltpu.VMEM((rows_back, width), F32),
            pltpu.VMEM((rows, ff), BF),
            pltpu.VMEM((rows_back, width), BF),
        ]
        + [dma((6 * (dps - 1),))] * 2
        + [dma((1 + 2 * (dps - 1),))] * 2
        + [dma((2 * hosted,))] * 2
        + [dma((2 * (dps + hosted),))] * 2
        + [dma((5,))],
        flops=2 * tokens * width * (8 * width + 4 * keys_pad),
        moved=40 * tokens * width,
    )(x, w_qkv, w_out, w_router, vectors, b_in, b_back, route_rows, keys[:, None], keys[None, :], bias, w_in, w_back)
    qkv_all, out_all, router_rows, b_ins, b_backs, vec, slots, q, k, v, p, o, after, acts, *expert_w = made

    rows_all = 4 * cap_pad
    deep = hosted * cap_pad
    made = comm_call(
        partial(experts_kernel, groups, dps, images, cap_pad),
        "experts",
        2,
        [A, A, V, V, V, V, V, V] + [A] * 4,
        [
            ((tokens, width), F32, V),
            ((tokens, width), BF, V),
            ((experts, width), F32, V),
            ((rows, ff), F32, V),
            ((rows_back, width), F32, V),
            ((hosted - 1, width, ff), BF, A),
            ((hosted - 1, ff, width), BF, A),
            ((hosted, 2, 1, ff), F32, V),
            ((hosted, 2, 1, width), F32, V),
            ((hosted - 1, width, ff), BF, A),
            ((hosted - 1, ff, width), BF, A),
        ],
        [
            pltpu.VMEM((2, 4, tokens, width), BF),
            pltpu.VMEM((4, 8, tokens), F32),
            pltpu.VMEM((4, deep, 2 * width), BF),
            pltpu.VMEM((width, ff), BF),
            pltpu.VMEM((ff, width), BF),
            pltpu.VMEM((dps, rows_all, rows), BF),
            pltpu.VMEM((rows_all, ff), BF),
            pltpu.VMEM((rows_all, ff), BF),
            pltpu.VMEM((rows_all, width), BF),
            pltpu.VMEM((cap_pad, ff), BF),
            pltpu.VMEM((dps, rows, ff), BF),
            pltpu.VMEM((dps - 1, rows, ff), BF),
            pltpu.VMEM((dps, rows_back, width), BF),
            pltpu.VMEM((dps - 1, rows_back, width), BF),
            pltpu.VMEM((4, hosted, 1, tokens), F32),
            pltpu.VMEM((3, hosted, 1, tokens), F32),
            pltpu.VMEM((4, tokens, width), BF),
            pltpu.VMEM((4, tokens, width), BF),
            pltpu.VMEM((2, tokens, width), BF),
            pltpu.VMEM((2, tokens, width), BF),
            pltpu.VMEM((tokens, LANES), F32),
            dma((9,)),
            dma((9,)),
            dma((2,)),
            dma((2 * dps,)),
            dma((2 * dps,)),
            dma((9,)),
            dma((9,)),
            dma((2 * dps,)),
            dma((2,)),
            dma((2 * hosted * dps,)),
            dma((2 * hosted * dps,)),
            dma((2 * hosted,)),
        ],
        flops=14 * hosted * rows_all * width * ff,
        moved=20 * tokens * width + 8 * hosted * width * ff,
        vmem=63,
    )(acts, grad, after, router_rows, route_rows, slots, b_ins, b_backs, *expert_w)
    back_rows, output, g_router, g_in, g_back, g_in_other, g_back_other, g_b_in, g_b_back, *_ = made

    wide = 4 * width
    halves_of = rows // 2
    small = up(8 + 2 * hosted + experts, 8)
    kin_slots = 4 * (hosted - 1)
    made = comm_call(
        partial(back_kernel, dps, groups, images),
        "back",
        1,
        [V] * 16 + [A] * 3,
        [
            ((tokens, width), BF, V),
            ((rows, 3 * width), F32, V),
            ((rows, width), F32, V),
            ((experts, rows), F32, V),
            ((7, rows), F32, V),
            ((per_device, rows_back), F32, V),
            ((per_device, rows), F32, V),
            (w_in.shape, F32, A),
            (w_back.shape, F32, A),
            ((hosted - 1, dps - 1, rows, ff), BF, A),
            ((hosted - 1, dps - 1, rows_back, width), BF, A),
        ],
        [
            pltpu.VMEM((rows, ff), F32),
            pltpu.VMEM((rows_back, width), F32),
            pltpu.VMEM((2, HEADS, half, keys_pad), BF),
            pltpu.VMEM((tokens, width), F32),
            pltpu.VMEM((tokens, width), BF),
            pltpu.VMEM((2, tokens, width), BF),
            pltpu.VMEM((2, tokens, width), BF),
            pltpu.VMEM((tokens, width), BF),
            pltpu.VMEM((tokens, width), BF),
            pltpu.VMEM((width, width), F32),
            pltpu.VMEM((width, 3 * width), F32),
            pltpu.VMEM((8, width), F32),
            pltpu.VMEM((dps, rows // 2, ff), BF),
            pltpu.VMEM((dps, rows_back // 2, width), BF),
            pltpu.VMEM((hosted - 1, rows, ff), BF),
            pltpu.VMEM((hosted - 1, rows_back, width), BF),
            pltpu.VMEM((hosted - 1, rows, ff), BF),
            pltpu.VMEM((hosted - 1, rows_back, width), BF),
            pltpu.VMEM((dps, halves_of, wide), BF),
            pltpu.VMEM((dps, halves_of, wide), BF),
            pltpu.VMEM((dps - 1, halves_of, wide), BF),
            pltpu.VMEM((dps - 1, halves_of, wide), BF),
            pltpu.VMEM((groups, halves_of, wide), BF),
            pltpu.VMEM((rows, wide), F32),
            pltpu.VMEM((2, dps, small, rows), F32),
            pltpu.VMEM((dps, small, rows), F32),
            pltpu.VMEM((dps - 1, small, rows), F32),
            pltpu.VMEM((groups, small, rows), F32),
            pltpu.VMEM((2, dps, 2 * hosted, rows_back), F32),
            pltpu.VMEM((dps, 2 * hosted, rows_back), F32),
            pltpu.VMEM((dps - 1, 2 * hosted, rows_back), F32),
            pltpu.VMEM((groups, 2 * hosted, rows_back), F32),
            dma((6,)), dma((6,)), dma((6 * dps,)), dma((6 * dps,)),
            dma((6 * groups,)), dma((6 * groups,)), dma((4,)), dma((4,)),
            dma((2,)), dma((2 * images,)), dma((2 * images,)), dma((kin_slots * dps,)), dma((kin_slots * dps,)),
            dma((2,)), dma((kin_slots,)), dma((kin_slots,)), dma((2,)), dma((2,)), dma((2,)),
        ],
        flops=2 * tokens * width * (8 * width + 8 * keys_pad),
        moved=60 * tokens * width,
        vmem=62,
    )(
        grad, back_rows, after, o, vec, out_all, q, k, v, x, qkv_all, g_router, g_in, g_back, g_b_in, g_b_back,
        p, g_in_other, g_back_other,
    )
    dx, grad_qkv, grad_out, grad_router, grad_vec, grad_b_in, grad_b_back, grad_w_in, grad_w_back, *_ = made
    return (
        output.reshape(images, half, width),
        dx.reshape(images, half, width),
        grad_vec,
        grad_qkv,
        grad_out,
        grad_router.T,
        grad_w_in,
        grad_b_in,
        grad_w_back,
        grad_b_back,
    )


def solution(mesh):
    tokens = P(("dp", "expert"), "context", None)
    by_rows = P("dp", None)
    experts = P("expert", "dp", None)
    expert_bias = P("expert", "dp")
    return jax.shard_map(
        shards,
        mesh=mesh,
        in_specs=(
            tokens,
            P(("dp", "expert"), None),
            P(("dp", "expert"), "context", None, None),
            tokens,
            P(None, "dp"),
            by_rows,
            by_rows,
            by_rows,
            experts,
            expert_bias,
            experts,
            expert_bias,
            tokens,
        ),
        out_specs=(
            tokens,
            tokens,
            P(None, "dp"),
            by_rows,
            by_rows,
            by_rows,
            experts,
            expert_bias,
            experts,
            expert_bias,
        ),
        check_vma=False,
    )
```

```python
from functools import partial

import jax
import jax.numpy as jnp
from jax import lax
from jax.experimental import pallas as pl
from jax.experimental.pallas import tpu as pltpu
from jax.sharding import PartitionSpec as P

HEADS = 8
EPSILON = 1e-06
LANES = 128
BF = jnp.bfloat16
F32 = jnp.float32
I32 = jnp.int32
MIB = 1 << 20


def up(size, unit):
    return -(-size // unit) * unit


def nn(a, b):
    return jnp.dot(a, b, preferred_element_type=F32)


def nt(a, b):
    return lax.dot_general(a, b, (((1,), (1,)), ((), ())), preferred_element_type=F32)


def tn(a, b):
    return lax.dot_general(a, b, (((0,), (0,)), ((), ())), preferred_element_type=F32)


def iota(shape, dim):
    return lax.broadcasted_iota(I32, shape, dim)


def normed(values):
    average = jnp.mean(values, axis=-1, keepdims=True)
    centred = values - average
    inv_scale = lax.rsqrt(jnp.mean(centred * centred, axis=-1, keepdims=True) + EPSILON)
    return centred * inv_scale, inv_scale


def norm_backward(grad, unit, inv_scale, gain):
    scaled = grad * gain
    centre = jnp.mean(scaled, axis=-1, keepdims=True)
    along = jnp.mean(scaled * unit, axis=-1, keepdims=True)
    return inv_scale * (scaled - centre - unit * along)


def gelu_parts(z):
    share = 0.5 * (1.0 + lax.erf(z * 0.7071067811865476))
    slope = share + z * (0.3989422804014327 * jnp.exp(-0.5 * z * z))
    return z * share, slope


def experts_kernel(
    groups, dps, images, cap_pad, acts, grad, after, router, routes, slots, b_in, b_back, *rest
):
    hosted = groups // 2
    w_in, kin_in, w_back, kin_back, grads, rest = *rest[:5], rest[5:]
    back_rows, mixed, far_rows, g_router, g_in, g_back, g_in_other, g_back_other, g_b_in, g_b_back = rest[:10]
    w_in_far, w_back_far, rest = rest[10], rest[11], rest[12:]
    tok, info, made_rows, w_in_v, w_back_v, rows_v, hidden, grad_pre, delta, slope = rest[:10]
    in_send, in_recv, back_send, back_recv, dots, dots_got, to_near, from_near, to_far, from_far = rest[10:20]
    places, x_s, x_r, w_sem, r_s, r_r, p_s, p_r, store_sem, load_sem, w_s, w_r, w_own = rest[20:]
    dp, group, core = lax.axis_index("dp"), lax.axis_index("expert"), lax.axis_index("context")
    tokens, width = mixed.shape
    ff = w_in_v.shape[1]
    rows_in, rows_back = width // dps, ff // dps
    mate = group + 1 - 2 * lax.rem(group, 2)
    near, across, diagonal = (dp, group, 1 - core), (dp, mate, core), (dp, mate, 1 - core)

    def remote(src, dst, sems, slot, target):
        return pltpu.make_async_remote_copy(
            src_ref=src, dst_ref=dst, send_sem=sems[0].at[slot], recv_sem=sems[1].at[slot],
            device_id=target, device_id_type=MESH,
        )

    pools = (info, tok.at[0])
    moves = {}
    for at, pool in enumerate(pools):
        moves[at, 1] = remote(pool.at[0], pool.at[1], (x_s, x_r), 3 * at, near)
        moves[at, 2] = remote(pool.at[0], pool.at[2], (x_s, x_r), 3 * at + 1, across)
        moves[at, 3] = remote(pool.at[2], pool.at[3], (x_s, x_r), 3 * at + 2, near)

    def along(step):
        return (lax.rem(dp + step, dps), group, core)

    def sum_out(which, step):
        src, dst = ((in_send, in_recv), (back_send, back_recv))[which]
        return remote(src.at[step], dst.at[step - 1], (r_s, r_r), which * dps + step, along(step))

    def gather(at, which, step):
        kin, far = ((kin_in, w_in_far), (kin_back, w_back_far))[which]
        size = kin.shape[1]
        part = far.at[at, pl.ds(pl.multiple_of(dp * size, size), size)]
        if step == 0:
            return pltpu.make_async_copy(kin.at[at], part, w_own.at[2 * at + which])
        target = (square(dp)[step - 1], group, core) if dps == 4 else along(step)
        return remote(kin.at[at], part, (w_s, w_r), (2 * at + which) * dps + step - 1, target)

    def onward(at, which):
        kin, far = ((kin_in, w_in_far), (kin_back, w_back_far))[which]
        return [
            remote(ref, ref, (w_s, w_r), (2 * at + which) * dps + 2 + slot, (target, group, core))
            for slot, (ref, target) in enumerate(relay(far.at[at], kin.shape[1], dp))
        ]

    direct = 3 if dps == 4 else dps

    def load(which, wait):
        for at in range(hosted):
            copies = (
                pltpu.make_async_copy(w_in_far.at[at - 1] if at else w_in, w_in_v, w_sem.at[0]),
                pltpu.make_async_copy(w_back_far.at[at - 1] if at else w_back, w_back_v, w_sem.at[1]),
            )

            @pl.when(which == at)
            def _():
                if at and not wait:
                    for part in range(2):
                        gather(at - 1, part, 0).wait()
                        for step in range(1, direct):
                            if dps == 4:
                                gather(at - 1, part, step).wait_send()
                            else:
                                gather(at - 1, part, step).wait()
                        if dps == 4:
                            for copy in onward(at - 1, part):
                                copy.wait()
                for copy in copies:
                    copy.wait() if wait else copy.start()

    def store(which, to, step):
        return (
            pltpu.make_async_copy(
                in_send.at[step],
                g_in_other.at[which - 1, pl.ds(pl.multiple_of(to * rows_in, rows_in), rows_in)],
                store_sem.at[step],
            ),
            pltpu.make_async_copy(
                back_send.at[step],
                g_back_other.at[which - 1, pl.ds(pl.multiple_of(to * rows_back, rows_back), rows_back)],
                store_sem.at[dps + step],
            ),
        )

    mine = (
        pltpu.make_async_copy(acts, tok.at[0, 0], load_sem.at[0]),
        pltpu.make_async_copy(grad, tok.at[1, 0], load_sem.at[1]),
        pltpu.make_async_copy(grads, tok.at[1, pl.ds(1, 3)], load_sem.at[2]),
    )
    for copy in mine:
        copy.start()
    load(0, False)
    greet([near, across, diagonal] + [along(step) for step in range(1, dps)])
    mine[0].wait()
    for hop in (2, 1):
        moves[1, hop].start()
    for at in range(hosted - 1):
        for part in range(2):
            for step in range(direct):
                gather(at, part, step).start()
    logits = nt(router[...], tok[0, 0])
    logits = jnp.exp(logits - jnp.max(logits, axis=0, keepdims=True))
    probs = logits / jnp.sum(logits, axis=0, keepdims=True)
    ids = iota(probs.shape, 0)
    info[0, 2:4, :] = slots[0:2, :].astype(F32)
    for choice in range(2):
        info[0, choice : choice + 1, :] = jnp.sum(
            jnp.where(routes[choice : choice + 1, :] == ids, probs, 0.0), axis=0, keepdims=True
        )
    info[0, 4:8, :] = jnp.zeros((4, tokens), F32)
    for hop in (2, 1):
        moves[0, hop].start()
    mine[1].wait()
    mine[2].wait()
    g_b_in[...] = jnp.zeros_like(g_b_in)
    g_b_back[...] = jnp.zeros_like(g_b_back)

    def near_out(at):
        return remote(to_near.at[at], from_near.at[at], (p_s, p_r), at, near)

    def far_out():
        return remote(to_far, from_far, (p_s, p_r), 4, across)

    def dots_out(source, target):
        return remote(dots.at[source], dots_got.at[source - 1], (p_s, p_r), 5 + source, target)

    def own_row(pair):
        pair = pair.astype(F32)
        return jnp.where(core == 0, pair[0:1], pair[1:2])

    half = tokens // images
    deep = hosted * cap_pad
    slot_ids = jnp.zeros((1, deep), F32)
    lane = iota((1, deep), 1)
    for which in range(hosted):
        first = (lax.rem(group + 2 * which, groups) * 2 + core - which) * cap_pad
        slot_ids = jnp.where(lane // cap_pad == which, (lane + first).astype(F32), slot_ids)

    def place(source):
        slot = info[source, 2:4, :]
        high = jnp.floor(slot * (1.0 / 64.0))
        parts = jnp.concatenate([high, slot - 64.0 * high, jnp.zeros((4, tokens), F32)], axis=0).astype(BF)
        row, col = iota((8, LANES), 0), iota((8, LANES), 1)
        weight = jnp.where(row == col, 64.0, jnp.where(row == col + 2, 1.0, 0.0))
        weight = jnp.where(col < 2, weight, 0.0).astype(BF)
        places[...] = tn(parts, weight)

    def summed(source, image):
        rows = pl.ds(pl.multiple_of(image * half, 8), half)
        hit = (places[rows, 0:1] == slot_ids) | (places[rows, 1:2] == slot_ids)
        return rows, nn(jnp.where(hit, 1.0, 0.0).astype(BF), made_rows[source])

    def to_core(source, at):
        place(source)

        def chunk(image, _):
            rows, part = summed(source, image)
            to_near[at, rows, :] = part[:, :width].astype(BF)
            to_near[at + 1, rows, :] = part[:, width:].astype(BF)
            return 0

        lax.fori_loop(0, images, chunk, 0)
        near_out(at).start()
        near_out(at + 1).start()

    def to_chip():
        place(2)
        near_out(0).wait_recv()
        near_out(1).wait_recv()

        def chunk(image, _):
            rows, part = summed(2, image)
            to_far[rows, :] = (part[:, :width] + from_near[0, rows, :].astype(F32)).astype(BF)
            far_rows[rows, :] = (part[:, width:] + from_near[1, rows, :].astype(F32)).astype(BF)
            return 0

        lax.fori_loop(0, images, chunk, 0)
        far_out().start()

    def expert(which, _):
        load(which, True)
        own = lax.rem(group + 2 * which, groups) * 2 + core
        last = which // (hosted - 1)

        def block(turn, _):
            source = turn + (3 - 2 * turn) * last

            @pl.when(jnp.logical_and(which == 0, source == 1))
            def _():
                for at in range(2):
                    moves[at, 1].wait_recv()

            @pl.when(jnp.logical_and(which == 0, source == 2))
            def _():
                for at in range(2):
                    moves[at, 2].wait_recv()
                    moves[at, 3].start()

            @pl.when(jnp.logical_and(which == 0, source == 3))
            def _():
                for at in range(2):
                    moves[at, 3].wait_recv()

            rows = pl.ds(pl.multiple_of(source * cap_pad, 16), cap_pad)
            spot = pl.ds(pl.multiple_of(which * cap_pad, 16), cap_pad)
            ids = iota((cap_pad, tokens), 0) + own * cap_pad
            hit_first = ids == info[source, 2:3, :].astype(I32)
            hit_second = ids == info[source, 3:4, :].astype(I32)
            hit = jnp.logical_or(hit_first, hit_second)
            one_hot = jnp.where(hit, 1.0, 0.0).astype(BF)
            gate = jnp.where(hit_first, info[source, 0:1, :], 0.0) + jnp.where(hit_second, info[source, 1:2, :], 0.0)
            gate = jnp.sum(gate, axis=1, keepdims=True)
            acts_in = nn(one_hot, tok[0, source]).astype(BF)
            for part in range(dps):
                rows_v[part, rows, :] = acts_in[:, part * rows_in : (part + 1) * rows_in]
            for part in range(dps):
                cols = slice(part * rows_back, (part + 1) * rows_back)
                z = nn(acts_in, w_in_v[:, cols]) + own_row(b_in[which, part])
                value, rise = gelu_parts(z)
                hidden[rows, cols] = value.astype(BF)
                slope[:, cols] = rise.astype(BF)
            bias = jnp.concatenate([own_row(b_back[which, part]) for part in range(dps)], axis=1)
            made = (nn(hidden[rows, :], w_back_v[...]) + bias).astype(BF).astype(F32)
            made_rows[source, spot, width:] = (gate * made).astype(BF)
            got_grad = nn(one_hot, tok[1, source])
            low = (gate * got_grad).astype(BF)
            delta[rows, :] = low
            g_b_back[which, core] += jnp.sum(low.astype(F32), axis=0, keepdims=True)
            dot = jnp.sum(made * got_grad, axis=1, keepdims=True)
            dots[source, which] = jnp.sum(jnp.where(hit, dot, 0.0), axis=0, keepdims=True)
            for part in range(dps):
                cols = slice(part * rows_back, (part + 1) * rows_back)
                dz = nt(low, w_back_v[cols, :]) * slope[:, cols].astype(F32)
                g_b_in[which, core, :, cols] += jnp.sum(dz, axis=0, keepdims=True)
                grad_pre[rows, cols] = dz.astype(BF)
            made_rows[source, spot, :width] = nt(grad_pre[rows, :], w_in_v[...]).astype(BF)

            if dps == 4:
                for part in range(2):

                    @pl.when(jnp.logical_and(which == 0, turn == 1 + part))
                    def _():
                        for at in range(hosted - 1):
                            for step in range(1, direct):
                                gather(at, part, step).wait_recv()
                            for copy in onward(at, part):
                                copy.start()

            @pl.when(jnp.logical_and(last == 1, source == 3))
            def _():
                dots_out(3, diagonal).start()
                to_core(3, 0)

            @pl.when(jnp.logical_and(last == 1, source == 2))
            def _():
                dots_out(2, across).start()
                to_chip()

            @pl.when(jnp.logical_and(last == 1, source == 1))
            def _():
                dots_out(1, near).start()
                to_core(1, 2)

            return 0

        lax.fori_loop(0, 4, block, 0)
        @pl.when(which + 1 < hosted)
        def _():
            load(which + 1, False)

        def weights(step, _):
            step = lax.rem(step + 1, dps)
            to = lax.rem(dp + step, dps)
            part_back = tn(hidden[:, pl.ds(pl.multiple_of(to * rows_back, LANES), rows_back)], delta[...])
            part_in = tn(rows_v[to], grad_pre[...])

            @pl.when(jnp.logical_and(which == 1, step > 0))
            def _():
                sum_out(0, step).wait_send()
                sum_out(1, step).wait_send()

            @pl.when(which > 1)
            def _():
                for copy in store(which - 1, to, step):
                    copy.wait()

            back_send[step] = part_back.astype(BF)
            in_send[step] = part_in.astype(BF)

            @pl.when(jnp.logical_and(which == 0, step > 0))
            def _():
                sum_out(1, step).start()
                sum_out(0, step).start()

            @pl.when(jnp.logical_and(which == 0, step == 0))
            def _():
                g_back[...] = part_back
                g_in[...] = part_in

            @pl.when(which > 0)
            def _():
                for copy in store(which, to, step):
                    copy.start()

            return 0

        lax.fori_loop(0, dps, weights, 0)
        return 0

    lax.fori_loop(0, hosted, expert, 0)
    for source, target in ((1, near), (2, across), (3, diagonal)):
        dots_out(source, target).wait_recv()
    at_near, at_far = 1 - core, core
    whole = jnp.zeros(probs.shape, F32)
    for which in range(hosted):
        here, there = lax.rem(group + 2 * which, groups) * 2, lax.rem(mate + 2 * which, groups) * 2
        whole = jnp.where(ids == here + core, dots[0, which], whole)
        whole = jnp.where(ids == here + at_near, dots_got[0, which], whole)
        whole = jnp.where(ids == there + at_far, dots_got[1, which], whole)
        whole = jnp.where(ids == there + at_near, dots_got[2, which], whole)
    low = (probs * (whole - jnp.sum(probs * whole, axis=0, keepdims=True))).astype(BF)
    g_router[...] = nn(low, tok[0, 0])
    back_rows[...] = tn(low, router[...])
    place(0)
    near_out(2).wait_recv()
    near_out(3).wait_recv()
    far_out().wait_recv()

    def chunk(image, _):
        rows, part = summed(0, image)
        back_rows[rows, :] += part[:, :width] + from_near[2, rows, :].astype(F32) + from_far[rows, :].astype(F32)
        mixed[rows, :] = after[rows, :] + part[:, width:] + from_near[3, rows, :].astype(F32)
        return 0

    lax.fori_loop(0, images, chunk, 0)
    for step in range(1, dps):
        for which in range(2):
            sum_out(which, step).wait_recv()
        g_back[...] += back_recv[step - 1].astype(F32)
        g_in[...] += in_recv[step - 1].astype(F32)

    for step in range(dps):
        for copy in store(hosted - 1, lax.rem(dp + step, dps), step):
            copy.wait()
    for copy in moves.values():
        copy.wait_send()
    for at in range(4):
        near_out(at).wait_send()
    far_out().wait_send()
    for source, target in ((1, near), (2, across), (3, diagonal)):
        dots_out(source, target).wait_send()


def forward_image(
    half, image, dps, x, x_other, bias, vec, w_qkv, w_out, q_ref, k_ref, v_ref, p_ref, o_ref, h_ref, a_ref
):
    width = x.shape[1]
    rows = pl.ds(pl.multiple_of(image * half, 8), half)
    half_pad = up(half, 16)
    head_dim = width // HEADS
    scale = head_dim ** (-0.5)
    gain, offset, bias_q, bias_v = (vec[row : row + 1, :] for row in range(4))
    own = x[rows, :].astype(F32)
    unit, _ = normed(own)
    acts = (unit * gain + offset).astype(BF)
    unit, _ = normed(x_other[rows, :].astype(F32))
    other = (unit * gain + offset).astype(BF)

    def weight(at):
        return w_qkv[:, :, at * width : (at + 1) * width].reshape(width, width)

    q_ref[rows, :] = ((nn(acts, weight(0)) + bias_q).astype(BF).astype(F32) * scale).astype(BF)
    pad = jnp.zeros((half_pad - half, width), BF)
    for part, piece in enumerate((acts, other)):
        start = part * half_pad
        k_ref[image, pl.ds(start, half), :] = nn(piece, weight(1)).astype(BF)
        v_ref[image, pl.ds(start, half), :] = (nn(piece, weight(2)) + bias_v).astype(BF)
        if half_pad > half:
            k_ref[image, pl.ds(start + half, half_pad - half), :] = pad
            v_ref[image, pl.ds(start + half, half_pad - half), :] = pad
    low = iota((1, LANES), 1) < head_dim
    zero = jnp.zeros((), BF)
    for pair in range(width // LANES):
        cols = pl.ds(pair * LANES, LANES)
        q_pair, k_pair, v_pair = q_ref[rows, cols], k_ref[image, :, cols], v_ref[image, :, cols]
        mixed = []
        for sub in range(2):
            mask = low if sub == 0 else jnp.logical_not(low)
            scores = nt(jnp.where(mask, q_pair, zero), k_pair) + bias[image]
            raised = jnp.exp(scores - jnp.max(scores, axis=1, keepdims=True))
            probs = (raised * (1.0 / jnp.sum(raised, axis=1, keepdims=True))).astype(BF)
            p_ref[image, 2 * pair + sub] = probs
            mixed.append(nn(probs, v_pair))
        o_ref[rows, cols] = jnp.where(low, mixed[0], mixed[1]).astype(BF)
    after = own + nn(o_ref[rows, :], w_out[...].reshape(width, width)) + vec[4:5, :]
    h_ref[rows, :] = after
    unit, _ = normed(after)
    a_ref[rows, :] = (unit * vec[5:6, :] + vec[6:7, :]).astype(BF)


def backward_image(
    half, image, grad, back_ref, h_ref, o_ref, vec, w_out, q_ref, k_ref, v_ref, p_ref,
    dh_ref, dq_ref, dk_ref, dv_ref, g_out, g_vec,
):
    width = grad.shape[1]
    rows = pl.ds(pl.multiple_of(image * half, 8), half)
    head_dim = width // HEADS
    half_pad = up(half, 16)
    lane = iota((1, LANES), 1)
    back = back_ref[rows, :]
    unit, inv_scale = normed(h_ref[rows, :])
    dh = grad[rows, :].astype(F32) + norm_backward(back, unit, inv_scale, vec[5:6, :])
    dh_ref[rows, :] = dh
    dh_low = dh.astype(BF)
    g_out[...] += tn(o_ref[rows, :], dh_low)
    g_vec[4:5, :] += jnp.sum(dh, axis=0, keepdims=True)
    g_vec[5:6, :] += jnp.sum(back * unit, axis=0, keepdims=True)
    g_vec[6:7, :] += jnp.sum(back, axis=0, keepdims=True)
    do = nt(dh_low, w_out[...].reshape(width, width)).astype(BF)
    low = lane < head_dim
    zero = jnp.zeros((), BF)
    scale = head_dim ** (-0.5)
    for pair in range(width // LANES):
        cols = slice(pair * LANES, (pair + 1) * LANES)
        do_pair = do[:, cols]
        q_pair, k_pair, v_pair = q_ref[rows, cols], k_ref[image, :, cols], v_ref[image, :, cols]
        dq, dk, dv = [], [], []
        for sub in range(2):
            mask = low if sub == 0 else jnp.logical_not(low)
            p_low = p_ref[2 * pair + sub]
            p = p_low.astype(F32)
            dp = nt(jnp.where(mask, do_pair, zero), v_pair)
            inner = jnp.sum(p * dp, axis=1, keepdims=True)
            ds = (p * (dp - inner)).astype(BF)
            dv.append(tn(p_low, do_pair))
            dk.append(tn(ds, q_pair))
            dq.append(nn(ds, k_pair))
        dq_ref[rows, cols] = (jnp.where(low, dq[0], dq[1]) * scale).astype(BF)
        dk_pair = jnp.where(low, dk[0], dk[1]).astype(BF)
        dv_pair = jnp.where(low, dv[0], dv[1]).astype(BF)
        for part in range(2):
            dk_ref[part, rows, cols] = dk_pair[part * half_pad : part * half_pad + half]
            dv_ref[part, rows, cols] = dv_pair[part * half_pad : part * half_pad + half]


def input_image(half, image, x_ref, dh_ref, dq_ref, dk_ref, dk_got, dv_ref, dv_got, vec, w_qkv, dx_ref, g_qkv, g_vec):
    width = x_ref.shape[1]
    rows = pl.ds(pl.multiple_of(image * half, 8), half)
    unit, inv_scale = normed(x_ref[rows, :].astype(F32))
    acts = (unit * vec[0:1, :] + vec[1:2, :]).astype(BF)
    dq = dq_ref[rows, :]
    dk = (dk_ref[0, rows, :].astype(F32) + dk_got[rows, :].astype(F32)).astype(BF)
    dv = (dv_ref[0, rows, :].astype(F32) + dv_got[rows, :].astype(F32)).astype(BF)
    da = jnp.zeros(unit.shape, F32)
    for at, piece in enumerate((dq, dk, dv)):
        cols = slice(at * width, (at + 1) * width)
        g_qkv[:, cols] += tn(acts, piece)
        da = da + nt(piece, w_qkv[:, :, cols].reshape(width, width))
    dx_ref[rows, :] = (dh_ref[rows, :] + norm_backward(da, unit, inv_scale, vec[0:1, :])).astype(BF)
    g_vec[0:1, :] += jnp.sum(da * unit, axis=0, keepdims=True)
    g_vec[1:2, :] += jnp.sum(da, axis=0, keepdims=True)
    g_vec[2:3, :] += jnp.sum(dq.astype(F32), axis=0, keepdims=True)
    g_vec[3:4, :] += jnp.sum(dv.astype(F32), axis=0, keepdims=True)


MESH = pl.DeviceIdType.MESH


def send(src, dst, sems, slot, device):
    copy = pltpu.make_async_remote_copy(
        src_ref=src, dst_ref=dst, send_sem=sems[0].at[slot], recv_sem=sems[1].at[slot],
        device_id=device, device_id_type=MESH,
    )
    copy.start()
    return copy


def remote_copy(src, dst, sems, slot, device):
    return pltpu.make_async_remote_copy(
        src_ref=src, dst_ref=dst, send_sem=sems[0].at[slot], recv_sem=sems[1].at[slot],
        device_id=device, device_id_type=MESH,
    )


def square(dp):
    return dp + 1 - 2 * lax.rem(dp, 2), lax.rem(dp + 2, 4)


def relay(ref, size, dp):
    side, across = square(dp)
    half = size // 2
    return (
        (ref.at[pl.ds(pl.multiple_of(across * size, size) + half, half)], side),
        (ref.at[pl.ds(pl.multiple_of(side * size, size), half)], across),
    )


def greet(devices):
    barrier = pltpu.get_barrier_semaphore()
    for device in devices:
        pl.semaphore_signal(barrier, inc=1, device_id=device, device_id_type=MESH)
    pl.semaphore_wait(barrier, len(devices))


def comm_call(body, name, number, ins, outs, scratch, flops=0, moved=0, vmem=56):
    return pl.pallas_call(
        body,
        name=name,
        in_specs=[pl.BlockSpec(memory_space=space) for space in ins],
        out_specs=[pl.BlockSpec(memory_space=space) for _, _, space in outs],
        out_shape=[jax.ShapeDtypeStruct(shape, dtype) for shape, dtype, _ in outs],
        scratch_shapes=list(scratch),
        cost_estimate=pl.CostEstimate(flops=int(flops), bytes_accessed=int(moved), transcendentals=0),
        compiler_params=pltpu.CompilerParams(
            vmem_limit_bytes=vmem * MIB, collective_id=number, has_side_effects=True
        ),
    )


def start_kernel(
    dps, groups, images, cap, cap_pad, x, w_qkv, w_out, w_router, vectors, b_in, b_back, routes, key_col, key_row, bias,
    w_in, w_back, grad,
    qkv_all, out_all, router_rows, b_in_all, back_all, vec, slots,
    q_ref, k_ref, v_ref, p_ref, o_ref, h_ref, a_ref, in_all, in_kin, back_w_all, back_kin, grads,
    x_other, router_all, vec_all, p_all, w_in_f, w_back_f, w_in_v, w_back_v,
    far_send, far_recv, near_send, near_recv, deep_send, deep_recv, w_s, w_r, local, rows_s, rows_r,
):
    dp, group, core = lax.axis_index("dp"), lax.axis_index("expert"), lax.axis_index("context")
    rows = w_qkv.shape[0]
    half = rows // 2
    hosted = groups // 2
    near = (dp, group, 1 - core)
    peers = [(lax.rem(dp + step, dps), group, core) for step in range(1, dps)]
    kin = [(dp, lax.rem(group + 2 * step, groups), core) for step in range(1, hosted)]
    loads = [
        pltpu.make_async_copy(w_in.at[core], w_in_f, local.at[0]),
        pltpu.make_async_copy(w_back.at[core], w_back_f, local.at[1]),
    ]
    for copy in loads:
        copy.start()
    mate = group + 1 - 2 * lax.rem(group, 2)
    across = (dp, mate, core)
    greet(peers + kin + [near, across])
    rows_out = [
        send(grad, grads.at[1], (rows_s, rows_r), 1, across),
        send(grad, grads.at[0], (rows_s, rows_r), 0, near),
    ]
    far, close, deep = (far_send, far_recv), (near_send, near_recv), (deep_send, deep_recv)
    waits = [send(x, x_other, close, 0, near)]
    qkv_all[dp] = w_qkv[...].astype(BF)
    own = pl.ds(pl.multiple_of(core * half, half), half)
    copies = []
    for step, peer in enumerate(peers):
        copies.append(send(qkv_all.at[dp, own], qkv_all.at[dp, own], far, step * 6, peer))
    out_all[dp] = w_out[...].astype(BF)
    spare = router_all.shape[2] - w_router.shape[1]
    router_all[dp] = jnp.concatenate([w_router[...], jnp.zeros((rows, spare), F32)], axis=1).astype(BF)
    vec_all[dp] = jnp.concatenate([vectors[...], jnp.zeros((1, rows), F32)], axis=0).astype(BF)
    b_in_all[0, dp] = b_in[...].astype(BF)
    back_all[0, dp] = b_back[...].astype(BF)
    for step, peer in enumerate(peers):
        copies.append(send(out_all.at[dp, own], out_all.at[dp, own], far, step * 6 + 1, peer))
    smalls, biases = [], []
    for step, peer in enumerate(peers):
        for at, ref in enumerate((router_all, vec_all)):
            smalls.append(send(ref.at[dp], ref.at[dp], far, step * 6 + 2 + at, peer))
        for at, ref in enumerate((b_in_all, back_all)):
            biases.append(send(ref.at[0, dp], ref.at[0, dp], far, step * 6 + 4 + at, peer))
    own_copies, direct = [], ([], [])
    for at, (wide, low, out, kin_out) in enumerate(
        ((w_in_f, w_in_v, in_all, in_kin), (w_back_f, w_back_v, back_w_all, back_kin))
    ):
        loads[at].wait()
        low[...] = wide[...].astype(BF)
        size = low.shape[0]
        part = pl.ds(pl.multiple_of(dp * size, size), size)
        for step, peer in enumerate(kin):
            own_copies.append(
                send(low, kin_out.at[hosted - 2 - step], (w_s, w_r), at * (dps + hosted) + dps + step, peer)
            )
        if dps == 4:
            for slot, target in enumerate(square(dp)):
                direct[at].append(
                    send(low, out.at[part], (w_s, w_r), at * (dps + hosted) + slot, (target, group, core))
                )
        else:
            for step, peer in enumerate(peers):
                own_copies.append(send(low, out.at[part], (w_s, w_r), at * (dps + hosted) + step, peer))
        here = pltpu.make_async_copy(low, out.at[part], local.at[2 + at])
        here.start()
        own_copies.append(here)

    def onward(at):
        out, size = ((in_all, w_in_v.shape[0]), (back_w_all, w_back_v.shape[0]))[at]
        return [
            remote_copy(ref, ref, (w_s, w_r), at * (dps + hosted) + 2 + slot, (target, group, core))
            for slot, (ref, target) in enumerate(relay(out, size, dp))
        ]

    def pass_on(at):
        for copy in direct[at]:
            copy.wait_recv()
        for copy in onward(at):
            copy.start()

    tokens = routes.shape[1]
    experts = w_router.shape[1]
    ids = iota((experts, tokens), 0)
    before = jnp.where(key_col[...] < key_row[...], 1.0, 0.0).astype(BF)
    first = jnp.where(routes[0:1, :] == ids, 1.0, 0.0)
    second = jnp.where(routes[1:2, :] == ids, 1.0, 0.0)
    count = jnp.sum(first, axis=1, keepdims=True)
    rank_first = jnp.sum(nn(first.astype(BF), before) * first, axis=0, keepdims=True)
    rank_second = jnp.sum((nn(second.astype(BF), before) + count) * second, axis=0, keepdims=True)
    ranks = jnp.concatenate([rank_first, rank_second], axis=0).astype(I32)
    owned = jnp.where(ranks < cap, routes[...] * cap_pad + ranks, -1)
    slots[...] = jnp.concatenate([owned, jnp.full((6, tokens), -1, I32)], axis=0)

    for copy in biases:
        copy.wait()
    for step, peer in enumerate(kin):
        for at, ref in enumerate((b_in_all, back_all)):
            waits.append(send(ref.at[0], ref.at[hosted - 1 - step], deep, 2 * step + at, peer))
    for at, copy in enumerate(copies):
        step, ref = at % len(peers), (qkv_all, out_all)[at // len(peers)]
        copy.wait()
        source = lax.rem(dp - step - 1 + dps, dps)
        waits.append(send(ref.at[source, own], ref.at[source, own], close, 1 + at, near))
    for copy in smalls:
        copy.wait()
    vec[...] = jnp.concatenate([vec_all[at].astype(F32) for at in range(dps)], axis=1)
    turned = [router_all[at].astype(F32).T[: w_router.shape[1]] for at in range(dps)]
    router_rows[...] = jnp.concatenate(turned, axis=1).astype(BF)
    for copy in waits:
        copy.wait()

    half = tokens // images

    def image_step(image, _):
        forward_image(
            half, image, dps, x, x_other, bias, vec, qkv_all, out_all, q_ref, k_ref, v_ref, p_all, o_ref, h_ref, a_ref
        )
        pltpu.make_async_copy(p_all.at[image], p_ref.at[image], local.at[4]).start()
        if dps == 4:

            @pl.when(image == images - 2)
            def _():
                pass_on(0)

        return 0

    lax.fori_loop(0, images, image_step, 0)
    if dps == 4:
        pass_on(1)
    rows_out[0].wait()
    rows_out[0] = send(grads.at[1], grads.at[2], (rows_s, rows_r), 2, near)
    pltpu.make_async_copy(p_all, p_ref, local.at[4]).wait()
    for copy in rows_out:
        copy.wait()
    for copy in own_copies:
        copy.wait()
    if dps == 4:
        for at in range(2):
            for copy in direct[at]:
                copy.wait_send()
            for copy in onward(at):
                copy.wait()


def back_kernel(
    dps, groups, images, grad, back_rows, h_ref, o_ref, vec, w_out, q_ref, k_ref, v_ref, x_ref, w_qkv,
    g_router, g_in, g_back, b_in, b_back, mixed, p_all, in_other, back_other, far_rows,
    dx_ref, output, o_qkv, o_out, o_router, o_vec, o_in, o_back, w_in_sum, w_back_sum, in_recv, back_recv,
    sum_in, sum_back, p_two, dh_ref, dq_ref, dk_ref, dv_ref, dk_got, dv_got, g_out, g_qkv, g_vec,
    in_stage, back_stage, in_to, back_to, in_from, back_from,
    near_out, near_in, far_out, far_in, deep_in, total,
    small_near, small_far, small_got, small_deep, bin_near, bin_far, bin_got, bin_deep,
    got_rows, near_s, near_r, far_s, far_r, deep_s, deep_r, last_s, last_r,
    rows_s, rows_r, p_sem, d_s, d_r, e_s, e_r, stage_sem, kin_s, kin_r, home_s, home_r, home_sem,
):
    dp, group, core = lax.axis_index("dp"), lax.axis_index("expert"), lax.axis_index("context")
    tokens, width = dx_ref.shape
    hosted = groups // 2
    token_half = tokens // images
    rows = width // dps
    half = rows // 2
    near = (dp, group, 1 - core)
    peers = [(lax.rem(dp + step, dps), group, core) for step in range(1, dps)]
    others = [(dp, lax.rem(group + step, groups), core) for step in range(1, groups)]

    def remote(src, dst, sems, slot, target):
        return pltpu.make_async_remote_copy(
            src_ref=src, dst_ref=dst, send_sem=sems[0].at[slot], recv_sem=sems[1].at[slot],
            device_id=target, device_id_type=MESH,
        )

    sets = (
        (back_other, back_recv, back_stage, back_to, back_from, g_back, w_back_sum),
        (in_other, in_recv, in_stage, in_to, in_from, g_in, w_in_sum),
    )

    def sum_out(which, part, at, step):
        other, recv = sets[which][:2]
        size = recv.shape[2]
        piece = size // 2
        target = lax.rem(dp + step, dps)
        src = other.at[at, pl.ds(pl.multiple_of(target * size, size) + part * piece, piece)]
        dst = recv.at[at, step - 1, pl.ds(part * piece, piece)]
        slot = ((which * 2 + part) * (hosted - 1) + at) * dps + step
        return remote(src, dst, (e_s, e_r), slot, peers[step - 1])

    def home_out(which, part, at):
        to, back = sets[which][3:5]
        piece = to.shape[1] // 2
        here = pl.ds(part * piece, piece)
        target = (dp, lax.rem(group + 2 * (at + 1), groups), core)
        slot = (which * 2 + part) * (hosted - 1) + at
        return pltpu.make_async_remote_copy(
            src_ref=to.at[at, here], dst_ref=back.at[hosted - 2 - at, here],
            send_sem=kin_s.at[slot], recv_sem=kin_r.at[(which * 2 + part) * (hosted - 1) + hosted - 2 - at],
            device_id=target, device_id_type=MESH,
        )

    def home_in(which, part, at):
        to, back = sets[which][3:5]
        piece = to.shape[1] // 2
        here = pl.ds(part * piece, piece)
        slot = (which * 2 + part) * (hosted - 1) + at
        return pltpu.make_async_remote_copy(
            src_ref=to.at[at, here], dst_ref=back.at[at, here], send_sem=kin_s.at[slot], recv_sem=kin_r.at[slot],
            device_id=near, device_id_type=MESH,
        )

    def send_home(which, part):
        other, recv, stage, to = sets[which][:4]
        size = recv.shape[2]
        piece = size // 2
        here = pl.ds(part * piece, piece)
        for at in range(hosted - 1):
            for step in range(1, dps):
                sum_out(which, part, at, step).wait_recv()
            own = other.at[at, pl.ds(pl.multiple_of(dp * size, size) + part * piece, piece)]
            copies = (
                pltpu.make_async_copy(recv.at[at, :, here], stage.at[pl.ds(0, dps - 1)], stage_sem.at[0]),
                pltpu.make_async_copy(own, stage.at[dps - 1], stage_sem.at[1]),
            )
            for copy in copies:
                copy.start()
            for copy in copies:
                copy.wait()
            value = stage[0].astype(F32)
            for step in range(1, dps):
                value = value + stage[step].astype(F32)
            to[at, here, :] = value.astype(BF)
            home_out(which, part, at).start()

    def load(image):
        slot = lax.rem(image, 2)
        return pltpu.make_async_copy(p_all.at[image], p_two.at[slot], p_sem.at[slot])

    def swap(image, which):
        here = pl.ds(pl.multiple_of(image * token_half, 8), token_half)
        src, dst = ((dk_ref, dk_got), (dv_ref, dv_got))[which]
        return remote(src.at[1, here], dst.at[here], (d_s, d_r), 2 * image + which, near)

    load(0).start()
    greet(peers + others + [near])
    for which in range(2):
        for part in range(2):
            for at in range(hosted - 1):
                for step in range(1, dps):
                    sum_out(which, part, at, step).start()
    mate = group + 1 - 2 * lax.rem(group, 2)
    rows_out = send(far_rows, got_rows, (rows_s, rows_r), 0, (dp, mate, core))
    g_out[...] = jnp.zeros_like(g_out)
    g_qkv[...] = jnp.zeros_like(g_qkv)
    g_vec[...] = jnp.zeros_like(g_vec)

    def back_step(image, _):
        load(image).wait()

        @pl.when(image + 1 < images)
        def _():
            load(image + 1).start()

        backward_image(
            token_half, image, grad, back_rows, h_ref, o_ref, vec, w_out, q_ref, k_ref, v_ref,
            p_two.at[lax.rem(image, 2)], dh_ref, dq_ref, dk_ref, dv_ref, g_out, g_vec,
        )
        swap(image, 0).start()
        swap(image, 1).start()

        @pl.when(image == images - 2)
        def _():
            send_home(0, 0)

        return 0

    lax.fori_loop(0, images, back_step, 0)
    send_home(0, 1)

    near_sems, far_sems, deep_sems, last_sems = (near_s, near_r), (far_s, far_r), (deep_s, deep_r), (last_s, last_r)
    sources = [(g_out, 0)] + [(g_qkv, at) for at in range(0, g_qkv.shape[1], width)]
    theirs = pl.multiple_of((1 - core) * half, half)
    ours = pl.multiple_of(core * half, half)

    def cols_of(at):
        return pl.ds(width * at, width)

    def to_core(at):
        ref, lane = sources[at]
        for block in range(dps):
            near_out[block, :, cols_of(at)] = ref[pl.ds(block * rows + theirs, half), lane : lane + width].astype(BF)
        return send(near_out.at[:, :, cols_of(at)], near_in.at[:, :, cols_of(at)], near_sems, 2 + at, near)

    first = [to_core(0)]

    def input_step(image, _):
        swap(image, 0).wait_recv()
        swap(image, 1).wait_recv()
        input_image(
            token_half, image, x_ref, dh_ref, dq_ref, dk_ref, dk_got, dv_ref, dv_got, vec, w_qkv, dx_ref, g_qkv, g_vec
        )
        return 0

    lax.fori_loop(0, images, input_step, 0)
    for at in range(1, len(sources)):
        first.append(to_core(at))

    deep = small_near.shape[2]
    tall = 2 * hosted
    router = 8 + tall
    bias_rows = [b_back[at // 2, at % 2] for at in range(tall)]
    bias_in = jnp.concatenate([b_in[at // 2, at % 2] for at in range(tall)], axis=0)
    small = [g_vec[...]] + bias_rows + [g_router[...]]
    spare = deep - router - g_router.shape[0]
    small = jnp.concatenate(small + ([jnp.zeros((spare, width), F32)] if spare else []), axis=0)
    for at in range(dps):
        small_near[0, at] = small[:, at * rows : (at + 1) * rows]
        bin_near[0, at] = bias_in[:, at * bin_near.shape[3] : (at + 1) * bin_near.shape[3]]
    firsts = [
        send(small_near.at[0], small_near.at[1], near_sems, 0, near),
        send(bin_near.at[0], bin_near.at[1], near_sems, 1, near),
    ]
    second = []
    for at, (ref, lane) in enumerate(sources):
        cols = cols_of(at)
        first[at].wait()
        for step, peer in enumerate(peers):
            target = lax.rem(dp + step + 1, dps)
            block = ref[pl.ds(pl.multiple_of(target * rows, rows) + ours, half), lane : lane + width]
            far_out[step, :, cols] = (block + near_in[target, :, cols].astype(F32)).astype(BF)
            second.append(
                send(far_out.at[step, :, cols], far_in.at[step, :, cols], far_sems, (2 + at) * dps + step, peer)
            )
    for copy in firsts:
        copy.wait()
    small_far[...] = small_near[0] + small_near[1]
    bin_far[...] = bin_near[0] + bin_near[1]
    smalls = []
    for step, peer in enumerate(peers):
        target = lax.rem(dp + step + 1, dps)
        smalls.append(send(small_far.at[target], small_got.at[step], far_sems, step, peer))
        smalls.append(send(bin_far.at[target], bin_got.at[step], far_sems, dps + step, peer))
    send_home(1, 0)
    third = []
    for at, (ref, lane) in enumerate(sources):
        cols = cols_of(at)
        mine = ref[pl.ds(pl.multiple_of(dp * rows, rows) + ours, half), lane : lane + width]
        mine = mine + near_in[dp, :, cols].astype(F32)
        for step in range(dps - 1):
            second[at * (dps - 1) + step].wait()
            mine = mine + far_in[step, :, cols].astype(F32)
        deep_in[group, :, cols] = mine.astype(BF)
        for step, peer in enumerate(others):
            third.append(
                send(deep_in.at[group, :, cols], deep_in.at[group, :, cols], deep_sems, at * groups + step, peer)
            )
    send_home(1, 1)
    for copy in smalls:
        copy.wait()
    lone = small_far[dp]
    lone_in = bin_far[dp]
    for step in range(dps - 1):
        lone = lone + small_got[step]
        lone_in = lone_in + bin_got[step]
    small_deep[group] = lone
    bin_deep[group] = lone_in
    deep_small = []
    for step, peer in enumerate(others):
        slot = len(sources) * groups + step
        deep_small.append(send(small_deep.at[group], small_deep.at[group], deep_sems, slot, peer))
        deep_small.append(send(bin_deep.at[group], bin_deep.at[group], deep_sems, groups + slot, peer))
    rows_out.wait()
    output[...] = (mixed[...] + got_rows[...].astype(F32)).astype(BF)
    last = []
    here = pl.ds(ours, half)
    for at in range(len(sources)):
        cols = cols_of(at)
        for step in range(groups - 1):
            third[at * (groups - 1) + step].wait()
        done = deep_in[0, :, cols].astype(F32)
        for source in range(1, groups):
            done = done + deep_in[source, :, cols].astype(F32)
        total[here, cols] = done
        last.append(send(total.at[here, cols], total.at[here, cols], last_sems, at, near))
    for copy in deep_small:
        copy.wait()
    lone = small_deep[0]
    for at in range(1, groups):
        lone = lone + small_deep[at]
    o_vec[...] = lone[0:7]
    o_router[...] = lone[router : router + o_router.shape[0]]
    grad_in, grad_back = jnp.zeros(o_in.shape, F32), jnp.zeros(o_back.shape, F32)
    for at in range(groups):
        away = lax.rem(group - at + groups, groups)
        kin = lax.rem(away, 2) == 0
        pick_in, pick_back = jnp.zeros(o_in.shape, F32), jnp.zeros(o_back.shape, F32)
        for which in range(hosted):
            found = away // 2 == which
            pick_in = jnp.where(found, bin_deep[at, 2 * which : 2 * which + 2], pick_in)
            pick_back = jnp.where(found, small_deep[at, 8 + 2 * which : 10 + 2 * which], pick_back)
        grad_in = grad_in + jnp.where(kin, pick_in, 0.0)
        grad_back = grad_back + jnp.where(kin, pick_back, 0.0)
    o_in[...] = grad_in
    o_back[...] = grad_back
    for copy in last:
        copy.wait()
    o_qkv[...] = total[:, width : 4 * width]
    o_out[...] = total[:, :width]

    stores = []
    for which, (_, _, _, to, back, own, out) in enumerate(sets):
        for part in range(2):
            for at in range(hosted - 1):
                home_in(which, part, at).wait_recv()
        value = own[...]
        for at in range(hosted - 1):
            value = value + back[at].astype(F32)
        whole = (sum_back, sum_in)[which]
        whole[...] = value
        stores.append(send(whole, out.at[core], (home_s, home_r), which, near))
        copy = pltpu.make_async_copy(whole, out.at[core], home_sem.at[which])
        copy.start()
        stores.append(copy)
    for which in range(2):
        for part in range(2):
            for at in range(hosted - 1):
                home_out(which, part, at).wait_send()
                for step in range(1, dps):
                    sum_out(which, part, at, step).wait_send()
    for image in range(images):
        for which in range(2):
            swap(image, which).wait_send()
    for copy in stores:
        copy.wait()


def shards(
    inputs, key_mask, routes, priority, vectors, w_qkv, w_out, w_router, w_in, b_in, w_back, b_back, cotangent
):
    images, half, width = inputs.shape
    tokens = images * half
    groups = lax.axis_size("expert")
    dps = lax.axis_size("dp")
    per_device = w_in.shape[0]
    experts = groups * per_device
    ff = w_in.shape[2]
    cap = max(2, 3 * tokens // experts)
    cap_pad = up(cap, 16)
    half_pad = up(half, 16)
    hosted = groups // 2
    context = lax.axis_index("context")
    V, A = pltpu.VMEM, pl.ANY
    dma = pltpu.SemaphoreType.DMA
    rows = w_qkv.shape[0]
    rows_back = ff // dps

    x = inputs.reshape(tokens, width)
    grad = cotangent.reshape(tokens, width)
    route_rows = routes.reshape(tokens, 2).T
    keys = priority.reshape(tokens) * tokens + jnp.arange(tokens, dtype=I32)

    mask = jnp.where(key_mask > 0, 0.0, -1e30).astype(F32)
    first, second = mask[:, :half], mask[:, half:]
    own = jnp.where(context == 0, first, second)
    other = jnp.where(context == 0, second, first)
    off = jnp.full((images, half_pad - half), -1e30, F32)
    bias = jnp.concatenate([own, off, other, off], axis=1)[:, None, :]
    keys_pad = 2 * half_pad

    made = comm_call(
        partial(start_kernel, dps, groups, images, cap, cap_pad),
        "front",
        0,
        [V] * 11 + [A] * 3,
        [
            ((dps, rows, 3 * width), BF, V),
            ((dps, rows, width), BF, V),
            ((experts, width), BF, V),
            ((hosted, dps, per_device, rows_back), BF, V),
            ((hosted, dps, per_device, rows), BF, V),
            ((8, width), F32, V),
            ((8, tokens), I32, V),
            ((tokens, width), BF, V),
            ((images, keys_pad, width), BF, V),
            ((images, keys_pad, width), BF, V),
            ((images, HEADS, half, keys_pad), BF, A),
            ((tokens, width), BF, V),
            ((tokens, width), F32, V),
            ((tokens, width), BF, V),
            ((width, ff), BF, A),
            ((hosted - 1, rows, ff), BF, A),
            ((ff, width), BF, A),
            ((hosted - 1, rows_back, width), BF, A),
            ((3, tokens, width), BF, A),
        ],
        [
            pltpu.VMEM((tokens, width), BF),
            pltpu.VMEM((dps, rows, LANES), BF),
            pltpu.VMEM((dps, 8, rows), BF),
            pltpu.VMEM((images, HEADS, half, keys_pad), BF),
            pltpu.VMEM((rows, ff), F32),
            pltpu.VMEM((rows_back, width), F32),
            pltpu.VMEM((rows, ff), BF),
            pltpu.VMEM((rows_back, width), BF),
        ]
        + [dma((6 * (dps - 1),))] * 2
        + [dma((1 + 2 * (dps - 1),))] * 2
        + [dma((2 * hosted,))] * 2
        + [dma((2 * (dps + hosted),))] * 2
        + [dma((5,))]
        + [dma((3,))] * 2,
        flops=2 * tokens * width * (8 * width + 4 * keys_pad),
        moved=40 * tokens * width,
    )(x, w_qkv, w_out, w_router, vectors, b_in, b_back, route_rows, keys[:, None], keys[None, :], bias, w_in, w_back, grad)
    qkv_all, out_all, router_rows, b_ins, b_backs, vec, slots, q, k, v, p, o, after, acts, *expert_w, grads = made

    rows_all = 4 * cap_pad
    deep = hosted * cap_pad
    made = comm_call(
        partial(experts_kernel, groups, dps, images, cap_pad),
        "experts",
        2,
        [A, A, V, V, V, V, V, V] + [A] * 5,
        [
            ((tokens, width), F32, V),
            ((tokens, width), F32, V),
            ((tokens, width), BF, V),
            ((experts, width), F32, V),
            ((rows, ff), F32, V),
            ((rows_back, width), F32, V),
            ((hosted - 1, width, ff), BF, A),
            ((hosted - 1, ff, width), BF, A),
            ((hosted, 2, 1, ff), F32, V),
            ((hosted, 2, 1, width), F32, V),
            ((hosted - 1, width, ff), BF, A),
            ((hosted - 1, ff, width), BF, A),
        ],
        [
            pltpu.VMEM((2, 4, tokens, width), BF),
            pltpu.VMEM((4, 8, tokens), F32),
            pltpu.VMEM((4, deep, 2 * width), BF),
            pltpu.VMEM((width, ff), BF),
            pltpu.VMEM((ff, width), BF),
            pltpu.VMEM((dps, rows_all, rows), BF),
            pltpu.VMEM((rows_all, ff), BF),
            pltpu.VMEM((rows_all, ff), BF),
            pltpu.VMEM((rows_all, width), BF),
            pltpu.VMEM((cap_pad, ff), BF),
            pltpu.VMEM((dps, rows, ff), BF),
            pltpu.VMEM((dps - 1, rows, ff), BF),
            pltpu.VMEM((dps, rows_back, width), BF),
            pltpu.VMEM((dps - 1, rows_back, width), BF),
            pltpu.VMEM((4, hosted, 1, tokens), F32),
            pltpu.VMEM((3, hosted, 1, tokens), F32),
            pltpu.VMEM((4, tokens, width), BF),
            pltpu.VMEM((4, tokens, width), BF),
            pltpu.VMEM((tokens, width), BF),
            pltpu.VMEM((tokens, width), BF),
            pltpu.VMEM((tokens, LANES), F32),
            dma((6,)),
            dma((6,)),
            dma((2,)),
            dma((2 * dps,)),
            dma((2 * dps,)),
            dma((9,)),
            dma((9,)),
            dma((2 * dps,)),
            dma((3,)),
            dma((2 * hosted * dps,)),
            dma((2 * hosted * dps,)),
            dma((2 * hosted,)),
        ],
        flops=14 * hosted * rows_all * width * ff,
        moved=20 * tokens * width + 8 * hosted * width * ff,
        vmem=63,
    )(acts, grad, after, router_rows, route_rows, slots, b_ins, b_backs, *expert_w, grads)
    back_rows, mixed, far_rows, g_router, g_in, g_back, g_in_other, g_back_other, g_b_in, g_b_back, *_ = made

    wide = 4 * width
    halves_of = rows // 2
    small = up(8 + 2 * hosted + experts, 8)
    kin_slots = 4 * (hosted - 1)
    made = comm_call(
        partial(back_kernel, dps, groups, images),
        "back",
        1,
        [V] * 17 + [A] * 4,
        [
            ((tokens, width), BF, V),
            ((tokens, width), BF, V),
            ((rows, 3 * width), F32, V),
            ((rows, width), F32, V),
            ((experts, rows), F32, V),
            ((7, rows), F32, V),
            ((per_device, rows_back), F32, V),
            ((per_device, rows), F32, V),
            (w_in.shape, F32, A),
            (w_back.shape, F32, A),
            ((hosted - 1, dps - 1, rows, ff), BF, A),
            ((hosted - 1, dps - 1, rows_back, width), BF, A),
        ],
        [
            pltpu.VMEM((rows, ff), F32),
            pltpu.VMEM((rows_back, width), F32),
            pltpu.VMEM((2, HEADS, half, keys_pad), BF),
            pltpu.VMEM((tokens, width), F32),
            pltpu.VMEM((tokens, width), BF),
            pltpu.VMEM((2, tokens, width), BF),
            pltpu.VMEM((2, tokens, width), BF),
            pltpu.VMEM((tokens, width), BF),
            pltpu.VMEM((tokens, width), BF),
            pltpu.VMEM((width, width), F32),
            pltpu.VMEM((width, 3 * width), F32),
            pltpu.VMEM((8, width), F32),
            pltpu.VMEM((dps, rows // 2, ff), BF),
            pltpu.VMEM((dps, rows_back // 2, width), BF),
            pltpu.VMEM((hosted - 1, rows, ff), BF),
            pltpu.VMEM((hosted - 1, rows_back, width), BF),
            pltpu.VMEM((hosted - 1, rows, ff), BF),
            pltpu.VMEM((hosted - 1, rows_back, width), BF),
            pltpu.VMEM((dps, halves_of, wide), BF),
            pltpu.VMEM((dps, halves_of, wide), BF),
            pltpu.VMEM((dps - 1, halves_of, wide), BF),
            pltpu.VMEM((dps - 1, halves_of, wide), BF),
            pltpu.VMEM((groups, halves_of, wide), BF),
            pltpu.VMEM((rows, wide), F32),
            pltpu.VMEM((2, dps, small, rows), F32),
            pltpu.VMEM((dps, small, rows), F32),
            pltpu.VMEM((dps - 1, small, rows), F32),
            pltpu.VMEM((groups, small, rows), F32),
            pltpu.VMEM((2, dps, 2 * hosted, rows_back), F32),
            pltpu.VMEM((dps, 2 * hosted, rows_back), F32),
            pltpu.VMEM((dps - 1, 2 * hosted, rows_back), F32),
            pltpu.VMEM((groups, 2 * hosted, rows_back), F32),
            pltpu.VMEM((tokens, width), BF),
            dma((6,)), dma((6,)), dma((6 * dps,)), dma((6 * dps,)),
            dma((6 * groups,)), dma((6 * groups,)), dma((4,)), dma((4,)), dma((1,)), dma((1,)),
            dma((2,)), dma((2 * images,)), dma((2 * images,)), dma((kin_slots * dps,)), dma((kin_slots * dps,)),
            dma((2,)), dma((kin_slots,)), dma((kin_slots,)), dma((2,)), dma((2,)), dma((2,)),
        ],
        flops=2 * tokens * width * (8 * width + 8 * keys_pad),
        moved=60 * tokens * width,
        vmem=62,
    )(
        grad, back_rows, after, o, vec, out_all, q, k, v, x, qkv_all, g_router, g_in, g_back, g_b_in, g_b_back, mixed,
        p, g_in_other, g_back_other, far_rows,
    )
    dx, output, grad_qkv, grad_out, grad_router, grad_vec, grad_b_in, grad_b_back, grad_w_in, grad_w_back, *_ = made
    return (
        output.reshape(images, half, width),
        dx.reshape(images, half, width),
        grad_vec,
        grad_qkv,
        grad_out,
        grad_router.T,
        grad_w_in,
        grad_b_in,
        grad_w_back,
        grad_b_back,
    )


def solution(mesh):
    tokens = P(("dp", "expert"), "context", None)
    by_rows = P("dp", None)
    experts = P("expert", "dp", None)
    expert_bias = P("expert", "dp")
    return jax.shard_map(
        shards,
        mesh=mesh,
        in_specs=(
            tokens,
            P(("dp", "expert"), None),
            P(("dp", "expert"), "context", None, None),
            tokens,
            P(None, "dp"),
            by_rows,
            by_rows,
            by_rows,
            experts,
            expert_bias,
            experts,
            expert_bias,
            tokens,
        ),
        out_specs=(
            tokens,
            tokens,
            P(None, "dp"),
            by_rows,
            by_rows,
            by_rows,
            experts,
            expert_bias,
            experts,
            expert_bias,
        ),
        check_vma=False,
    )
```

```python
from functools import partial

import jax
import jax.numpy as jnp
from jax import lax
from jax.experimental import pallas as pl
from jax.experimental.pallas import tpu as pltpu
from jax.sharding import PartitionSpec as P

HEADS = 8
EPSILON = 1e-06
LANES = 128
BF = jnp.bfloat16
F32 = jnp.float32
I32 = jnp.int32
MIB = 1 << 20


def up(size, unit):
    return -(-size // unit) * unit


def nn(a, b):
    return jnp.dot(a, b, preferred_element_type=F32)


def nt(a, b):
    return lax.dot_general(a, b, (((1,), (1,)), ((), ())), preferred_element_type=F32)


def tn(a, b):
    return lax.dot_general(a, b, (((0,), (0,)), ((), ())), preferred_element_type=F32)


def iota(shape, dim):
    return lax.broadcasted_iota(I32, shape, dim)


def normed(values):
    average = jnp.mean(values, axis=-1, keepdims=True)
    centred = values - average
    inv_scale = lax.rsqrt(jnp.mean(centred * centred, axis=-1, keepdims=True) + EPSILON)
    return centred * inv_scale, inv_scale


def norm_backward(grad, unit, inv_scale, gain):
    scaled = grad * gain
    centre = jnp.mean(scaled, axis=-1, keepdims=True)
    along = jnp.mean(scaled * unit, axis=-1, keepdims=True)
    return inv_scale * (scaled - centre - unit * along)


def gelu_parts(z):
    share = 0.5 * (1.0 + lax.erf(z * 0.7071067811865476))
    slope = share + z * (0.3989422804014327 * jnp.exp(-0.5 * z * z))
    return z * share, slope


def experts_kernel(
    groups, dps, images, cap_pad, acts, grad, after, router, routes, slots, b_in, b_back, *rest
):
    hosted = groups // 2
    w_in, kin_in, w_back, kin_back, grads, rest = *rest[:5], rest[5:]
    back_rows, mixed, far_rows, g_router, g_in, g_back, g_in_other, g_back_other, g_b_in, g_b_back = rest[:10]
    w_in_far, w_back_far, rest = rest[10], rest[11], rest[12:]
    tok, info, made_rows, w_in_v, w_back_v, rows_v, hidden, grad_pre, delta, slope = rest[:10]
    in_send, in_recv, back_send, back_recv, dots, dots_got, to_near, from_near, to_far, from_far = rest[10:20]
    places, x_s, x_r, w_sem, r_s, r_r, p_s, p_r, store_sem, load_sem, w_s, w_r = rest[20:]
    dp, group, core = lax.axis_index("dp"), lax.axis_index("expert"), lax.axis_index("context")
    tokens, width = mixed.shape
    ff = w_in_v.shape[1]
    rows_in, rows_back = width // dps, ff // dps
    mate = group + 1 - 2 * lax.rem(group, 2)
    near, across, diagonal = (dp, group, 1 - core), (dp, mate, core), (dp, mate, 1 - core)

    def remote(src, dst, sems, slot, target):
        return pltpu.make_async_remote_copy(
            src_ref=src, dst_ref=dst, send_sem=sems[0].at[slot], recv_sem=sems[1].at[slot],
            device_id=target, device_id_type=MESH,
        )

    pools = (info, tok.at[0])
    moves = {}
    for at, pool in enumerate(pools):
        moves[at, 1] = remote(pool.at[0], pool.at[1], (x_s, x_r), 3 * at, near)
        moves[at, 2] = remote(pool.at[0], pool.at[2], (x_s, x_r), 3 * at + 1, across)
        moves[at, 3] = remote(pool.at[2], pool.at[3], (x_s, x_r), 3 * at + 2, near)

    def along(step):
        return (lax.rem(dp + step, dps), group, core)

    def sum_out(which, step):
        src, dst = ((in_send, in_recv), (back_send, back_recv))[which]
        return remote(src.at[step], dst.at[step - 1], (r_s, r_r), which * dps + step, along(step))

    def gather(at, which, step):
        kin, far = ((kin_in, w_in_far), (kin_back, w_back_far))[which]
        size = kin.shape[1]
        part = far.at[at, pl.ds(pl.multiple_of(dp * size, size), size)]
        target = (square(dp)[step - 1], group, core) if dps == 4 else along(step)
        return remote(kin.at[at], part, (w_s, w_r), (2 * at + which) * dps + step - 1, target)

    def onward(at, which):
        kin, far = ((kin_in, w_in_far), (kin_back, w_back_far))[which]
        return [
            remote(ref, ref, (w_s, w_r), (2 * at + which) * dps + 2 + slot, (target, group, core))
            for slot, (ref, target) in enumerate(relay(far.at[at], kin.shape[1], dp))
        ]

    direct = 3 if dps == 4 else dps

    def load(which, wait):
        for at in range(hosted):
            copies = []
            for part, (whole, kin, far, held) in enumerate(
                ((w_in, kin_in, w_in_far, w_in_v), (w_back, kin_back, w_back_far, w_back_v))
            ):
                if at == 0:
                    copies.append(pltpu.make_async_copy(whole, held, w_sem.at[part * dps]))
                    continue
                size = kin.shape[1]
                for step in range(dps):
                    here = pl.ds(pl.multiple_of(lax.rem(dp + step, dps) * size, size), size)
                    src = far.at[at - 1, here] if step else kin.at[at - 1]
                    copies.append(pltpu.make_async_copy(src, held.at[here], w_sem.at[part * dps + step]))

            @pl.when(which == at)
            def _():
                if at and not wait:
                    for part in range(2):
                        for step in range(1, direct):
                            if dps == 4:
                                gather(at - 1, part, step).wait_send()
                            else:
                                gather(at - 1, part, step).wait()
                        if dps == 4:
                            for copy in onward(at - 1, part):
                                copy.wait()
                for copy in copies:
                    copy.wait() if wait else copy.start()

    def store(which, to, step):
        return (
            pltpu.make_async_copy(
                in_send.at[step],
                g_in_other.at[which - 1, pl.ds(pl.multiple_of(to * rows_in, rows_in), rows_in)],
                store_sem.at[step],
            ),
            pltpu.make_async_copy(
                back_send.at[step],
                g_back_other.at[which - 1, pl.ds(pl.multiple_of(to * rows_back, rows_back), rows_back)],
                store_sem.at[dps + step],
            ),
        )

    mine = (
        pltpu.make_async_copy(acts, tok.at[0, 0], load_sem.at[0]),
        pltpu.make_async_copy(grad, tok.at[1, 0], load_sem.at[1]),
        pltpu.make_async_copy(grads, tok.at[1, pl.ds(1, 3)], load_sem.at[2]),
    )
    for copy in mine:
        copy.start()
    load(0, False)
    greet([near, across, diagonal] + [along(step) for step in range(1, dps)])
    mine[0].wait()
    for hop in (2, 1):
        moves[1, hop].start()
    for at in range(hosted - 1):
        for part in range(2):
            for step in range(1, direct):
                gather(at, part, step).start()
    logits = nt(router[...], tok[0, 0])
    logits = jnp.exp(logits - jnp.max(logits, axis=0, keepdims=True))
    probs = logits / jnp.sum(logits, axis=0, keepdims=True)
    ids = iota(probs.shape, 0)
    info[0, 2:4, :] = slots[0:2, :].astype(F32)
    for choice in range(2):
        info[0, choice : choice + 1, :] = jnp.sum(
            jnp.where(routes[choice : choice + 1, :] == ids, probs, 0.0), axis=0, keepdims=True
        )
    info[0, 4:8, :] = jnp.zeros((4, tokens), F32)
    for hop in (2, 1):
        moves[0, hop].start()
    mine[1].wait()
    mine[2].wait()
    g_b_in[...] = jnp.zeros_like(g_b_in)
    g_b_back[...] = jnp.zeros_like(g_b_back)

    def near_out(at):
        return remote(to_near.at[at], from_near.at[at], (p_s, p_r), at, near)

    def far_out():
        return remote(to_far, from_far, (p_s, p_r), 4, across)

    def dots_out(source, target):
        return remote(dots.at[source], dots_got.at[source - 1], (p_s, p_r), 5 + source, target)

    def own_row(pair):
        pair = pair.astype(F32)
        return jnp.where(core == 0, pair[0:1], pair[1:2])

    half = tokens // images
    deep = hosted * cap_pad
    slot_ids = jnp.zeros((1, deep), F32)
    lane = iota((1, deep), 1)
    for which in range(hosted):
        first = (lax.rem(group + 2 * which, groups) * 2 + core - which) * cap_pad
        slot_ids = jnp.where(lane // cap_pad == which, (lane + first).astype(F32), slot_ids)

    def place(source):
        slot = info[source, 2:4, :]
        high = jnp.floor(slot * (1.0 / 64.0))
        parts = jnp.concatenate([high, slot - 64.0 * high, jnp.zeros((4, tokens), F32)], axis=0).astype(BF)
        row, col = iota((8, LANES), 0), iota((8, LANES), 1)
        weight = jnp.where(row == col, 64.0, jnp.where(row == col + 2, 1.0, 0.0))
        weight = jnp.where(col < 2, weight, 0.0).astype(BF)
        places[...] = tn(parts, weight)

    def summed(source, image):
        rows = pl.ds(pl.multiple_of(image * half, 8), half)
        hit = (places[rows, 0:1] == slot_ids) | (places[rows, 1:2] == slot_ids)
        return rows, nn(jnp.where(hit, 1.0, 0.0).astype(BF), made_rows[source])

    def to_core(source, at):
        place(source)

        def chunk(image, _):
            rows, part = summed(source, image)
            to_near[at, rows, :] = part[:, :width].astype(BF)
            to_near[at + 1, rows, :] = part[:, width:].astype(BF)
            return 0

        lax.fori_loop(0, images, chunk, 0)
        near_out(at).start()
        near_out(at + 1).start()

    def to_chip():
        place(2)
        near_out(0).wait_recv()
        near_out(1).wait_recv()

        def chunk(image, _):
            rows, part = summed(2, image)
            to_far[rows, :] = (part[:, :width] + from_near[0, rows, :].astype(F32)).astype(BF)
            far_rows[rows, :] = (part[:, width:] + from_near[1, rows, :].astype(F32)).astype(BF)
            return 0

        lax.fori_loop(0, images, chunk, 0)
        far_out().start()

    def expert(which, _):
        load(which, True)
        own = lax.rem(group + 2 * which, groups) * 2 + core
        last = which // (hosted - 1)

        def block(turn, _):
            source = turn + (3 - 2 * turn) * last

            @pl.when(jnp.logical_and(which == 0, source == 1))
            def _():
                for at in range(2):
                    moves[at, 1].wait_recv()

            @pl.when(jnp.logical_and(which == 0, source == 2))
            def _():
                for at in range(2):
                    moves[at, 2].wait_recv()
                    moves[at, 3].start()

            @pl.when(jnp.logical_and(which == 0, source == 3))
            def _():
                for at in range(2):
                    moves[at, 3].wait_recv()

            rows = pl.ds(pl.multiple_of(source * cap_pad, 16), cap_pad)
            spot = pl.ds(pl.multiple_of(which * cap_pad, 16), cap_pad)
            ids = iota((cap_pad, tokens), 0) + own * cap_pad
            hit_first = ids == info[source, 2:3, :].astype(I32)
            hit_second = ids == info[source, 3:4, :].astype(I32)
            hit = jnp.logical_or(hit_first, hit_second)
            one_hot = jnp.where(hit, 1.0, 0.0).astype(BF)
            gate = jnp.where(hit_first, info[source, 0:1, :], 0.0) + jnp.where(hit_second, info[source, 1:2, :], 0.0)
            gate = jnp.sum(gate, axis=1, keepdims=True)
            acts_in = nn(one_hot, tok[0, source]).astype(BF)
            for part in range(dps):
                rows_v[part, rows, :] = acts_in[:, part * rows_in : (part + 1) * rows_in]
            for part in range(dps):
                cols = slice(part * rows_back, (part + 1) * rows_back)
                z = nn(acts_in, w_in_v[:, cols]) + own_row(b_in[which, part])
                value, rise = gelu_parts(z)
                hidden[rows, cols] = value.astype(BF)
                slope[:, cols] = rise.astype(BF)
            bias = jnp.concatenate([own_row(b_back[which, part]) for part in range(dps)], axis=1)
            made = (nn(hidden[rows, :], w_back_v[...]) + bias).astype(BF).astype(F32)
            made_rows[source, spot, width:] = (gate * made).astype(BF)
            got_grad = nn(one_hot, tok[1, source])
            low = (gate * got_grad).astype(BF)
            delta[rows, :] = low
            g_b_back[which, core] += jnp.sum(low.astype(F32), axis=0, keepdims=True)
            dot = jnp.sum(made * got_grad, axis=1, keepdims=True)
            dots[source, which] = jnp.sum(jnp.where(hit, dot, 0.0), axis=0, keepdims=True)
            for part in range(dps):
                cols = slice(part * rows_back, (part + 1) * rows_back)
                dz = nt(low, w_back_v[cols, :]) * slope[:, cols].astype(F32)
                g_b_in[which, core, :, cols] += jnp.sum(dz, axis=0, keepdims=True)
                grad_pre[rows, cols] = dz.astype(BF)
            made_rows[source, spot, :width] = nt(grad_pre[rows, :], w_in_v[...]).astype(BF)

            if dps == 4:
                for part in range(2):

                    @pl.when(jnp.logical_and(which == 0, turn == 1 + part))
                    def _():
                        for at in range(hosted - 1):
                            for step in range(1, direct):
                                gather(at, part, step).wait_recv()
                            for copy in onward(at, part):
                                copy.start()

            @pl.when(jnp.logical_and(last == 1, source == 3))
            def _():
                dots_out(3, diagonal).start()
                to_core(3, 0)

            @pl.when(jnp.logical_and(last == 1, source == 2))
            def _():
                dots_out(2, across).start()
                to_chip()

            @pl.when(jnp.logical_and(last == 1, source == 1))
            def _():
                dots_out(1, near).start()
                to_core(1, 2)

            return 0

        lax.fori_loop(0, 4, block, 0)
        @pl.when(which + 1 < hosted)
        def _():
            load(which + 1, False)

        def weights(step, _):
            step = lax.rem(step + 1, dps)
            to = lax.rem(dp + step, dps)
            part_back = tn(hidden[:, pl.ds(pl.multiple_of(to * rows_back, LANES), rows_back)], delta[...])
            part_in = tn(rows_v[to], grad_pre[...])

            @pl.when(jnp.logical_and(which == 1, step > 0))
            def _():
                sum_out(0, step).wait_send()
                sum_out(1, step).wait_send()

            @pl.when(which > 1)
            def _():
                for copy in store(which - 1, to, step):
                    copy.wait()

            back_send[step] = part_back.astype(BF)
            in_send[step] = part_in.astype(BF)

            @pl.when(jnp.logical_and(which == 0, step > 0))
            def _():
                sum_out(1, step).start()
                sum_out(0, step).start()

            @pl.when(jnp.logical_and(which == 0, step == 0))
            def _():
                g_back[...] = part_back
                g_in[...] = part_in

            @pl.when(which > 0)
            def _():
                for copy in store(which, to, step):
                    copy.start()

            return 0

        lax.fori_loop(0, dps, weights, 0)
        return 0

    lax.fori_loop(0, hosted, expert, 0)
    for source, target in ((1, near), (2, across), (3, diagonal)):
        dots_out(source, target).wait_recv()
    at_near, at_far = 1 - core, core
    whole = jnp.zeros(probs.shape, F32)
    for which in range(hosted):
        here, there = lax.rem(group + 2 * which, groups) * 2, lax.rem(mate + 2 * which, groups) * 2
        whole = jnp.where(ids == here + core, dots[0, which], whole)
        whole = jnp.where(ids == here + at_near, dots_got[0, which], whole)
        whole = jnp.where(ids == there + at_far, dots_got[1, which], whole)
        whole = jnp.where(ids == there + at_near, dots_got[2, which], whole)
    low = (probs * (whole - jnp.sum(probs * whole, axis=0, keepdims=True))).astype(BF)
    g_router[...] = nn(low, tok[0, 0])
    back_rows[...] = tn(low, router[...])
    place(0)
    near_out(2).wait_recv()
    near_out(3).wait_recv()
    far_out().wait_recv()

    def chunk(image, _):
        rows, part = summed(0, image)
        back_rows[rows, :] += part[:, :width] + from_near[2, rows, :].astype(F32) + from_far[rows, :].astype(F32)
        mixed[rows, :] = after[rows, :] + part[:, width:] + from_near[3, rows, :].astype(F32)
        return 0

    lax.fori_loop(0, images, chunk, 0)
    for step in range(1, dps):
        for which in range(2):
            sum_out(which, step).wait_recv()
        g_back[...] += back_recv[step - 1].astype(F32)
        g_in[...] += in_recv[step - 1].astype(F32)

    for step in range(dps):
        for copy in store(hosted - 1, lax.rem(dp + step, dps), step):
            copy.wait()
    for copy in moves.values():
        copy.wait_send()
    for at in range(4):
        near_out(at).wait_send()
    far_out().wait_send()
    for source, target in ((1, near), (2, across), (3, diagonal)):
        dots_out(source, target).wait_send()


def forward_image(
    half, image, dps, x, x_other, bias, vec, w_qkv, w_out, q_ref, k_ref, v_ref, p_ref, o_ref, h_ref, a_ref
):
    width = x.shape[1]
    rows = pl.ds(pl.multiple_of(image * half, 8), half)
    half_pad = up(half, 16)
    head_dim = width // HEADS
    scale = head_dim ** (-0.5)
    gain, offset, bias_q, bias_v = (vec[row : row + 1, :] for row in range(4))
    own = x[rows, :].astype(F32)
    unit, _ = normed(own)
    acts = (unit * gain + offset).astype(BF)
    unit, _ = normed(x_other[rows, :].astype(F32))
    other = (unit * gain + offset).astype(BF)

    def weight(at):
        return w_qkv[:, :, at * width : (at + 1) * width].reshape(width, width)

    q_ref[rows, :] = ((nn(acts, weight(0)) + bias_q).astype(BF).astype(F32) * scale).astype(BF)
    pad = jnp.zeros((half_pad - half, width), BF)
    for part, piece in enumerate((acts, other)):
        start = part * half_pad
        k_ref[image, pl.ds(start, half), :] = nn(piece, weight(1)).astype(BF)
        v_ref[image, pl.ds(start, half), :] = (nn(piece, weight(2)) + bias_v).astype(BF)
        if half_pad > half:
            k_ref[image, pl.ds(start + half, half_pad - half), :] = pad
            v_ref[image, pl.ds(start + half, half_pad - half), :] = pad
    low = iota((1, LANES), 1) < head_dim
    zero = jnp.zeros((), BF)
    for pair in range(width // LANES):
        cols = pl.ds(pair * LANES, LANES)
        q_pair, k_pair, v_pair = q_ref[rows, cols], k_ref[image, :, cols], v_ref[image, :, cols]
        mixed = []
        for sub in range(2):
            mask = low if sub == 0 else jnp.logical_not(low)
            scores = nt(jnp.where(mask, q_pair, zero), k_pair) + bias[image]
            raised = jnp.exp(scores - jnp.max(scores, axis=1, keepdims=True))
            probs = (raised * (1.0 / jnp.sum(raised, axis=1, keepdims=True))).astype(BF)
            p_ref[image, 2 * pair + sub] = probs
            mixed.append(nn(probs, v_pair))
        o_ref[rows, cols] = jnp.where(low, mixed[0], mixed[1]).astype(BF)
    after = own + nn(o_ref[rows, :], w_out[...].reshape(width, width)) + vec[4:5, :]
    h_ref[rows, :] = after
    unit, _ = normed(after)
    a_ref[rows, :] = (unit * vec[5:6, :] + vec[6:7, :]).astype(BF)


def backward_image(
    half, image, grad, back_ref, h_ref, o_ref, vec, w_out, q_ref, k_ref, v_ref, p_ref,
    dh_ref, dq_ref, dk_ref, dv_ref, g_out, g_vec,
):
    width = grad.shape[1]
    rows = pl.ds(pl.multiple_of(image * half, 8), half)
    head_dim = width // HEADS
    half_pad = up(half, 16)
    lane = iota((1, LANES), 1)
    back = back_ref[rows, :]
    unit, inv_scale = normed(h_ref[rows, :])
    dh = grad[rows, :].astype(F32) + norm_backward(back, unit, inv_scale, vec[5:6, :])
    dh_ref[rows, :] = dh
    dh_low = dh.astype(BF)
    g_out[...] += tn(o_ref[rows, :], dh_low)
    g_vec[4:5, :] += jnp.sum(dh, axis=0, keepdims=True)
    g_vec[5:6, :] += jnp.sum(back * unit, axis=0, keepdims=True)
    g_vec[6:7, :] += jnp.sum(back, axis=0, keepdims=True)
    do = nt(dh_low, w_out[...].reshape(width, width)).astype(BF)
    low = lane < head_dim
    zero = jnp.zeros((), BF)
    scale = head_dim ** (-0.5)
    for pair in range(width // LANES):
        cols = slice(pair * LANES, (pair + 1) * LANES)
        do_pair = do[:, cols]
        q_pair, k_pair, v_pair = q_ref[rows, cols], k_ref[image, :, cols], v_ref[image, :, cols]
        dq, dk, dv = [], [], []
        for sub in range(2):
            mask = low if sub == 0 else jnp.logical_not(low)
            p_low = p_ref[2 * pair + sub]
            p = p_low.astype(F32)
            dp = nt(jnp.where(mask, do_pair, zero), v_pair)
            inner = jnp.sum(p * dp, axis=1, keepdims=True)
            ds = (p * (dp - inner)).astype(BF)
            dv.append(tn(p_low, do_pair))
            dk.append(tn(ds, q_pair))
            dq.append(nn(ds, k_pair))
        dq_ref[rows, cols] = (jnp.where(low, dq[0], dq[1]) * scale).astype(BF)
        dk_pair = jnp.where(low, dk[0], dk[1]).astype(BF)
        dv_pair = jnp.where(low, dv[0], dv[1]).astype(BF)
        for part in range(2):
            dk_ref[part, rows, cols] = dk_pair[part * half_pad : part * half_pad + half]
            dv_ref[part, rows, cols] = dv_pair[part * half_pad : part * half_pad + half]


def input_image(half, image, x_ref, dh_ref, dq_ref, dk_ref, dk_got, dv_ref, dv_got, vec, w_qkv, dx_ref, g_qkv, g_vec):
    width = x_ref.shape[1]
    rows = pl.ds(pl.multiple_of(image * half, 8), half)
    unit, inv_scale = normed(x_ref[rows, :].astype(F32))
    acts = (unit * vec[0:1, :] + vec[1:2, :]).astype(BF)
    dq = dq_ref[rows, :]
    dk = (dk_ref[0, rows, :].astype(F32) + dk_got[rows, :].astype(F32)).astype(BF)
    dv = (dv_ref[0, rows, :].astype(F32) + dv_got[rows, :].astype(F32)).astype(BF)
    da = jnp.zeros(unit.shape, F32)
    for at, piece in enumerate((dq, dk, dv)):
        cols = slice(at * width, (at + 1) * width)
        g_qkv[:, cols] += tn(acts, piece)
        da = da + nt(piece, w_qkv[:, :, cols].reshape(width, width))
    dx_ref[rows, :] = (dh_ref[rows, :] + norm_backward(da, unit, inv_scale, vec[0:1, :])).astype(BF)
    g_vec[0:1, :] += jnp.sum(da * unit, axis=0, keepdims=True)
    g_vec[1:2, :] += jnp.sum(da, axis=0, keepdims=True)
    g_vec[2:3, :] += jnp.sum(dq.astype(F32), axis=0, keepdims=True)
    g_vec[3:4, :] += jnp.sum(dv.astype(F32), axis=0, keepdims=True)


MESH = pl.DeviceIdType.MESH


def send(src, dst, sems, slot, device):
    copy = pltpu.make_async_remote_copy(
        src_ref=src, dst_ref=dst, send_sem=sems[0].at[slot], recv_sem=sems[1].at[slot],
        device_id=device, device_id_type=MESH,
    )
    copy.start()
    return copy


def remote_copy(src, dst, sems, slot, device):
    return pltpu.make_async_remote_copy(
        src_ref=src, dst_ref=dst, send_sem=sems[0].at[slot], recv_sem=sems[1].at[slot],
        device_id=device, device_id_type=MESH,
    )


def square(dp):
    return dp + 1 - 2 * lax.rem(dp, 2), lax.rem(dp + 2, 4)


def relay(ref, size, dp):
    side, across = square(dp)
    half = size // 2
    return (
        (ref.at[pl.ds(pl.multiple_of(across * size, size) + half, half)], side),
        (ref.at[pl.ds(pl.multiple_of(side * size, size), half)], across),
    )


def greet(devices):
    barrier = pltpu.get_barrier_semaphore()
    for device in devices:
        pl.semaphore_signal(barrier, inc=1, device_id=device, device_id_type=MESH)
    pl.semaphore_wait(barrier, len(devices))


def comm_call(body, name, number, ins, outs, scratch, flops=0, moved=0, vmem=56):
    return pl.pallas_call(
        body,
        name=name,
        in_specs=[pl.BlockSpec(memory_space=space) for space in ins],
        out_specs=[pl.BlockSpec(memory_space=space) for _, _, space in outs],
        out_shape=[jax.ShapeDtypeStruct(shape, dtype) for shape, dtype, _ in outs],
        scratch_shapes=list(scratch),
        cost_estimate=pl.CostEstimate(flops=int(flops), bytes_accessed=int(moved), transcendentals=0),
        compiler_params=pltpu.CompilerParams(
            vmem_limit_bytes=vmem * MIB, collective_id=number, has_side_effects=True
        ),
    )


def start_kernel(
    dps, groups, images, cap, cap_pad, x, w_qkv, w_out, w_router, vectors, b_in, b_back, routes, key_col, key_row, bias,
    w_in, w_back, grad,
    qkv_all, out_all, router_rows, b_in_all, back_all, vec, slots,
    q_ref, k_ref, v_ref, p_ref, o_ref, h_ref, a_ref, in_all, in_kin, back_w_all, back_kin, grads,
    x_other, router_all, vec_all, p_all, w_in_f, w_back_f, w_in_v, w_back_v,
    far_send, far_recv, near_send, near_recv, deep_send, deep_recv, w_s, w_r, local, rows_s, rows_r,
):
    dp, group, core = lax.axis_index("dp"), lax.axis_index("expert"), lax.axis_index("context")
    rows = w_qkv.shape[0]
    half = rows // 2
    hosted = groups // 2
    near = (dp, group, 1 - core)
    peers = [(lax.rem(dp + step, dps), group, core) for step in range(1, dps)]
    kin = [(dp, lax.rem(group + 2 * step, groups), core) for step in range(1, hosted)]
    loads = [
        pltpu.make_async_copy(w_in.at[core], w_in_f, local.at[0]),
        pltpu.make_async_copy(w_back.at[core], w_back_f, local.at[1]),
    ]
    for copy in loads:
        copy.start()
    mate = group + 1 - 2 * lax.rem(group, 2)
    across = (dp, mate, core)
    greet(peers + kin + [near, across])
    rows_out = [
        send(grad, grads.at[1], (rows_s, rows_r), 1, across),
        send(grad, grads.at[0], (rows_s, rows_r), 0, near),
    ]
    far, close, deep = (far_send, far_recv), (near_send, near_recv), (deep_send, deep_recv)
    waits = [send(x, x_other, close, 0, near)]
    qkv_all[dp] = w_qkv[...].astype(BF)
    own = pl.ds(pl.multiple_of(core * half, half), half)
    copies = []
    for step, peer in enumerate(peers):
        copies.append(send(qkv_all.at[dp, own], qkv_all.at[dp, own], far, step * 6, peer))
    out_all[dp] = w_out[...].astype(BF)
    spare = router_all.shape[2] - w_router.shape[1]
    router_all[dp] = jnp.concatenate([w_router[...], jnp.zeros((rows, spare), F32)], axis=1).astype(BF)
    vec_all[dp] = jnp.concatenate([vectors[...], jnp.zeros((1, rows), F32)], axis=0).astype(BF)
    b_in_all[0, dp] = b_in[...].astype(BF)
    back_all[0, dp] = b_back[...].astype(BF)
    for step, peer in enumerate(peers):
        copies.append(send(out_all.at[dp, own], out_all.at[dp, own], far, step * 6 + 1, peer))
    smalls, biases = [], []
    for step, peer in enumerate(peers):
        for at, ref in enumerate((router_all, vec_all)):
            smalls.append(send(ref.at[dp], ref.at[dp], far, step * 6 + 2 + at, peer))
        for at, ref in enumerate((b_in_all, back_all)):
            biases.append(send(ref.at[0, dp], ref.at[0, dp], far, step * 6 + 4 + at, peer))
    own_copies, direct = [], ([], [])
    for at, (wide, low, out, kin_out) in enumerate(
        ((w_in_f, w_in_v, in_all, in_kin), (w_back_f, w_back_v, back_w_all, back_kin))
    ):
        loads[at].wait()
        low[...] = wide[...].astype(BF)
        size = low.shape[0]
        part = pl.ds(pl.multiple_of(dp * size, size), size)
        for step, peer in enumerate(kin):
            own_copies.append(
                send(low, kin_out.at[hosted - 2 - step], (w_s, w_r), at * (dps + hosted) + dps + step, peer)
            )
        if dps == 4:
            for slot, target in enumerate(square(dp)):
                direct[at].append(
                    send(low, out.at[part], (w_s, w_r), at * (dps + hosted) + slot, (target, group, core))
                )
        else:
            for step, peer in enumerate(peers):
                own_copies.append(send(low, out.at[part], (w_s, w_r), at * (dps + hosted) + step, peer))
        here = pltpu.make_async_copy(low, out.at[part], local.at[2 + at])
        here.start()
        own_copies.append(here)

    def onward(at):
        out, size = ((in_all, w_in_v.shape[0]), (back_w_all, w_back_v.shape[0]))[at]
        return [
            remote_copy(ref, ref, (w_s, w_r), at * (dps + hosted) + 2 + slot, (target, group, core))
            for slot, (ref, target) in enumerate(relay(out, size, dp))
        ]

    def pass_on(at):
        for copy in direct[at]:
            copy.wait_recv()
        for copy in onward(at):
            copy.start()

    tokens = routes.shape[1]
    experts = w_router.shape[1]
    ids = iota((experts, tokens), 0)
    before = jnp.where(key_col[...] < key_row[...], 1.0, 0.0).astype(BF)
    first = jnp.where(routes[0:1, :] == ids, 1.0, 0.0)
    second = jnp.where(routes[1:2, :] == ids, 1.0, 0.0)
    count = jnp.sum(first, axis=1, keepdims=True)
    rank_first = jnp.sum(nn(first.astype(BF), before) * first, axis=0, keepdims=True)
    rank_second = jnp.sum((nn(second.astype(BF), before) + count) * second, axis=0, keepdims=True)
    ranks = jnp.concatenate([rank_first, rank_second], axis=0).astype(I32)
    owned = jnp.where(ranks < cap, routes[...] * cap_pad + ranks, -1)
    slots[...] = jnp.concatenate([owned, jnp.full((6, tokens), -1, I32)], axis=0)

    for copy in biases:
        copy.wait()
    for step, peer in enumerate(kin):
        for at, ref in enumerate((b_in_all, back_all)):
            waits.append(send(ref.at[0], ref.at[hosted - 1 - step], deep, 2 * step + at, peer))
    for at, copy in enumerate(copies):
        step, ref = at % len(peers), (qkv_all, out_all)[at // len(peers)]
        copy.wait()
        source = lax.rem(dp - step - 1 + dps, dps)
        waits.append(send(ref.at[source, own], ref.at[source, own], close, 1 + at, near))
    for copy in smalls:
        copy.wait()
    vec[...] = jnp.concatenate([vec_all[at].astype(F32) for at in range(dps)], axis=1)
    turned = [router_all[at].astype(F32).T[: w_router.shape[1]] for at in range(dps)]
    router_rows[...] = jnp.concatenate(turned, axis=1).astype(BF)
    for copy in waits:
        copy.wait()

    half = tokens // images

    def image_step(image, _):
        forward_image(
            half, image, dps, x, x_other, bias, vec, qkv_all, out_all, q_ref, k_ref, v_ref, p_all, o_ref, h_ref, a_ref
        )
        pltpu.make_async_copy(p_all.at[image], p_ref.at[image], local.at[4]).start()
        if dps == 4:

            @pl.when(image == images - 2)
            def _():
                pass_on(0)

        return 0

    lax.fori_loop(0, images, image_step, 0)
    if dps == 4:
        pass_on(1)
    rows_out[0].wait()
    rows_out[0] = send(grads.at[1], grads.at[2], (rows_s, rows_r), 2, near)
    pltpu.make_async_copy(p_all, p_ref, local.at[4]).wait()
    for copy in rows_out:
        copy.wait()
    for copy in own_copies:
        copy.wait()
    if dps == 4:
        for at in range(2):
            for copy in direct[at]:
                copy.wait_send()
            for copy in onward(at):
                copy.wait()


def back_kernel(
    dps, groups, images, grad, back_rows, h_ref, o_ref, vec, w_out, q_ref, k_ref, v_ref, x_ref, w_qkv,
    g_router, g_in, g_back, b_in, b_back, mixed, p_all, in_other, back_other, far_rows,
    dx_ref, output, o_qkv, o_out, o_router, o_vec, o_in, o_back, w_in_sum, w_back_sum, in_recv, back_recv,
    sum_in, sum_back, p_two, dh_ref, dq_ref, dk_ref, dv_ref, dk_got, dv_got, g_out, g_qkv, g_vec,
    in_stage, back_stage, in_to, back_to, in_from, back_from,
    near_out, near_in, far_out, far_in, deep_in, deep_out, deep_all, total,
    small_near, small_far, small_got, small_deep, bin_near, bin_far, bin_got, bin_deep,
    got_rows, near_s, near_r, far_s, far_r, deep_s, deep_r, last_s, last_r,
    rows_s, rows_r, p_sem, d_s, d_r, e_s, e_r, stage_sem, kin_s, kin_r, home_s, home_r, home_sem,
):
    dp, group, core = lax.axis_index("dp"), lax.axis_index("expert"), lax.axis_index("context")
    tokens, width = dx_ref.shape
    hosted = groups // 2
    token_half = tokens // images
    rows = width // dps
    half = rows // 2
    near = (dp, group, 1 - core)
    peers = [(lax.rem(dp + step, dps), group, core) for step in range(1, dps)]
    others = [(dp, lax.rem(group + step, groups), core) for step in range(1, groups)]

    def remote(src, dst, sems, slot, target):
        return pltpu.make_async_remote_copy(
            src_ref=src, dst_ref=dst, send_sem=sems[0].at[slot], recv_sem=sems[1].at[slot],
            device_id=target, device_id_type=MESH,
        )

    sets = (
        (back_other, back_recv, back_stage, back_to, back_from, g_back, w_back_sum),
        (in_other, in_recv, in_stage, in_to, in_from, g_in, w_in_sum),
    )

    def sum_out(which, part, at, step):
        other, recv = sets[which][:2]
        size = recv.shape[2]
        piece = size // 2
        target = lax.rem(dp + step, dps)
        src = other.at[at, pl.ds(pl.multiple_of(target * size, size) + part * piece, piece)]
        dst = recv.at[at, step - 1, pl.ds(part * piece, piece)]
        slot = ((which * 2 + part) * (hosted - 1) + at) * dps + step
        return remote(src, dst, (e_s, e_r), slot, peers[step - 1])

    def piece_out(which, part, at, kind):
        other, recv, stage = sets[which][:3]
        size = recv.shape[2]
        piece = size // 2
        side, over = square(dp)
        corner = lax.rem(side + 2, 4)
        share = (corner, side, over)[kind]
        via = (over if part == 0 else side, side, over)[kind]
        place = (2, 0, 1)[kind]
        if kind == part + 1:
            src = stage.at[2 + part]
        else:
            src = other.at[at, pl.ds(pl.multiple_of(share * size, size) + part * piece, piece)]
        dst = recv.at[at, place, pl.ds(part * piece, piece)]
        slot = ((which * 2 + part) * (hosted - 1) + at) * dps + kind
        return remote(src, dst, (e_s, e_r), slot, (via, group, core))

    def at_once(which):
        for at in range(hosted - 1):
            for part, kind in ((0, 0), (1, 0), (1, 1), (0, 2)):
                piece_out(which, part, at, kind).start()

    def relayed(which):
        other, recv, stage = sets[which][:3]
        size = recv.shape[2]
        piece = size // 2
        for at in range(hosted - 1):
            for part in range(2):
                here = pl.ds(part * piece, piece)
                share = square(dp)[part]
                piece_out(which, part, at, 0).wait_recv()
                own = other.at[at, pl.ds(pl.multiple_of(share * size, size) + part * piece, piece)]
                copies = (
                    pltpu.make_async_copy(recv.at[at, 2, here], stage.at[0], stage_sem.at[0]),
                    pltpu.make_async_copy(own, stage.at[1], stage_sem.at[1]),
                )
                for copy in copies:
                    copy.start()
                for copy in copies:
                    copy.wait()
                if at:
                    piece_out(which, part, at - 1, part + 1).wait_send()
                stage[2 + part] = (stage[0].astype(F32) + stage[1].astype(F32)).astype(BF)
                piece_out(which, part, at, part + 1).start()

    def home_out(which, part, at):
        to, back = sets[which][3:5]
        piece = to.shape[1] // 2
        here = pl.ds(part * piece, piece)
        target = (dp, lax.rem(group + 2 * (at + 1), groups), core)
        slot = (which * 2 + part) * (hosted - 1) + at
        return pltpu.make_async_remote_copy(
            src_ref=to.at[at, here], dst_ref=back.at[hosted - 2 - at, here],
            send_sem=kin_s.at[slot], recv_sem=kin_r.at[(which * 2 + part) * (hosted - 1) + hosted - 2 - at],
            device_id=target, device_id_type=MESH,
        )

    def home_in(which, part, at):
        to, back = sets[which][3:5]
        piece = to.shape[1] // 2
        here = pl.ds(part * piece, piece)
        slot = (which * 2 + part) * (hosted - 1) + at
        return pltpu.make_async_remote_copy(
            src_ref=to.at[at, here], dst_ref=back.at[at, here], send_sem=kin_s.at[slot], recv_sem=kin_r.at[slot],
            device_id=near, device_id_type=MESH,
        )

    def send_home(which, part):
        other, recv, stage, to = sets[which][:4]
        size = recv.shape[2]
        piece = size // 2
        here = pl.ds(part * piece, piece)
        count = 2 if dps == 4 else dps - 1
        if dps == 4 and part == 0:
            for side in range(2):
                piece_out(which, side, hosted - 2, side + 1).wait_send()
        for at in range(hosted - 1):
            if dps == 4:
                for kind in (1, 2):
                    piece_out(which, part, at, kind).wait_recv()
            else:
                for step in range(1, dps):
                    sum_out(which, part, at, step).wait_recv()
            own = other.at[at, pl.ds(pl.multiple_of(dp * size, size) + part * piece, piece)]
            copies = (
                pltpu.make_async_copy(recv.at[at, pl.ds(0, count), here], stage.at[pl.ds(0, count)], stage_sem.at[0]),
                pltpu.make_async_copy(own, stage.at[count], stage_sem.at[1]),
            )
            for copy in copies:
                copy.start()
            for copy in copies:
                copy.wait()
            value = stage[0].astype(F32)
            for step in range(count):
                value = value + stage[step + 1].astype(F32)
            to[at, here, :] = value.astype(BF)
            home_out(which, part, at).start()

    def load(image):
        slot = lax.rem(image, 2)
        return pltpu.make_async_copy(p_all.at[image], p_two.at[slot], p_sem.at[slot])

    def swap(image, which):
        here = pl.ds(pl.multiple_of(image * token_half, 8), token_half)
        src, dst = ((dk_ref, dk_got), (dv_ref, dv_got))[which]
        return remote(src.at[1, here], dst.at[here], (d_s, d_r), 2 * image + which, near)

    load(0).start()
    greet(peers + others + [near])
    if dps == 4:
        at_once(0)
    else:
        for which in range(2):
            for part in range(2):
                for at in range(hosted - 1):
                    for step in range(1, dps):
                        sum_out(which, part, at, step).start()
    mate = group + 1 - 2 * lax.rem(group, 2)
    rows_out = send(far_rows, got_rows, (rows_s, rows_r), 0, (dp, mate, core))
    g_out[...] = jnp.zeros_like(g_out)
    g_qkv[...] = jnp.zeros_like(g_qkv)
    g_vec[...] = jnp.zeros_like(g_vec)

    def back_step(image, _):
        load(image).wait()

        @pl.when(image + 1 < images)
        def _():
            load(image + 1).start()

        backward_image(
            token_half, image, grad, back_rows, h_ref, o_ref, vec, w_out, q_ref, k_ref, v_ref,
            p_two.at[lax.rem(image, 2)], dh_ref, dq_ref, dk_ref, dv_ref, g_out, g_vec,
        )
        swap(image, 0).start()
        swap(image, 1).start()

        if dps == 4:

            @pl.when(image == 0)
            def _():
                relayed(0)
                at_once(1)

        @pl.when(image == images - 2)
        def _():
            send_home(0, 0)
            send_home(0, 1)

        return 0

    lax.fori_loop(0, images, back_step, 0)
    if dps == 4:
        relayed(1)

    near_sems, far_sems, deep_sems, last_sems = (near_s, near_r), (far_s, far_r), (deep_s, deep_r), (last_s, last_r)
    sources = [(g_out, 0)] + [(g_qkv, at) for at in range(0, g_qkv.shape[1], width)]
    theirs = pl.multiple_of((1 - core) * half, half)
    ours = pl.multiple_of(core * half, half)

    def cols_of(at):
        return pl.ds(width * at, width)

    def to_core(at):
        ref, lane = sources[at]
        for block in range(dps):
            near_out[block, :, cols_of(at)] = ref[pl.ds(block * rows + theirs, half), lane : lane + width].astype(BF)
        return send(near_out.at[:, :, cols_of(at)], near_in.at[:, :, cols_of(at)], near_sems, 2 + at, near)

    first = [to_core(0)]

    def input_step(image, _):
        swap(image, 0).wait_recv()
        swap(image, 1).wait_recv()
        input_image(
            token_half, image, x_ref, dh_ref, dq_ref, dk_ref, dk_got, dv_ref, dv_got, vec, w_qkv, dx_ref, g_qkv, g_vec
        )
        return 0

    lax.fori_loop(0, images, input_step, 0)
    for at in range(1, len(sources)):
        first.append(to_core(at))

    deep = small_near.shape[2]
    tall = 2 * hosted
    router = 8 + tall
    bias_rows = [b_back[at // 2, at % 2] for at in range(tall)]
    bias_in = jnp.concatenate([b_in[at // 2, at % 2] for at in range(tall)], axis=0)
    small = [g_vec[...]] + bias_rows + [g_router[...]]
    spare = deep - router - g_router.shape[0]
    small = jnp.concatenate(small + ([jnp.zeros((spare, width), F32)] if spare else []), axis=0)
    for at in range(dps):
        small_near[0, at] = small[:, at * rows : (at + 1) * rows]
        bin_near[0, at] = bias_in[:, at * bin_near.shape[3] : (at + 1) * bin_near.shape[3]]
    firsts = [
        send(small_near.at[0], small_near.at[1], near_sems, 0, near),
        send(bin_near.at[0], bin_near.at[1], near_sems, 1, near),
    ]
    send_home(1, 0)
    send_home(1, 1)
    second = []
    for at, (ref, lane) in enumerate(sources):
        cols = cols_of(at)
        first[at].wait()
        for step, peer in enumerate(peers):
            target = lax.rem(dp + step + 1, dps)
            block = ref[pl.ds(pl.multiple_of(target * rows, rows) + ours, half), lane : lane + width]
            far_out[step, :, cols] = (block + near_in[target, :, cols].astype(F32)).astype(BF)
            second.append(
                send(far_out.at[step, :, cols], far_in.at[step, :, cols], far_sems, (2 + at) * dps + step, peer)
            )
    for copy in firsts:
        copy.wait()
    small_far[...] = small_near[0] + small_near[1]
    bin_far[...] = bin_near[0] + bin_near[1]
    smalls = []
    for step, peer in enumerate(peers):
        target = lax.rem(dp + step + 1, dps)
        smalls.append(send(small_far.at[target], small_got.at[step], far_sems, step, peer))
        smalls.append(send(bin_far.at[target], bin_got.at[step], far_sems, dps + step, peer))
    third = []
    few = half // groups
    split = few % 16 == 0
    for at, (ref, lane) in enumerate(sources):
        cols = cols_of(at)
        mine = ref[pl.ds(pl.multiple_of(dp * rows, rows) + ours, half), lane : lane + width]
        mine = mine + near_in[dp, :, cols].astype(F32)
        for step in range(dps - 1):
            second[at * (dps - 1) + step].wait()
            mine = mine + far_in[step, :, cols].astype(F32)
        if split:
            deep_out[:, cols] = mine.astype(BF)
            deep_in[group, :few, cols] = deep_out[pl.ds(pl.multiple_of(group * few, few), few), cols]
            for step, peer in enumerate(others):
                to = pl.multiple_of(lax.rem(group + step + 1, groups) * few, few)
                src = deep_out.at[pl.ds(to, few), cols]
                third.append(send(src, deep_in.at[group, pl.ds(0, few), cols], deep_sems, at * groups + step, peer))
        else:
            deep_in[group, :, cols] = mine.astype(BF)
            for step, peer in enumerate(others):
                part = deep_in.at[group, :, cols]
                third.append(send(part, part, deep_sems, at * groups + step, peer))
    for copy in smalls:
        copy.wait()
    lone = small_far[dp]
    lone_in = bin_far[dp]
    for step in range(dps - 1):
        lone = lone + small_got[step]
        lone_in = lone_in + bin_got[step]
    small_deep[group] = lone
    bin_deep[group] = lone_in
    deep_small = []
    for step, peer in enumerate(others):
        slot = len(sources) * groups + step
        deep_small.append(send(small_deep.at[group], small_deep.at[group], deep_sems, slot, peer))
        deep_small.append(send(bin_deep.at[group], bin_deep.at[group], deep_sems, groups + slot, peer))
    last, fourth = [], []
    here = pl.ds(ours, half)
    for at in range(len(sources) if split else 0):
        cols = cols_of(at)
        for step in range(groups - 1):
            third[at * (groups - 1) + step].wait()
        done = deep_in[0, :few, cols].astype(F32)
        for source in range(1, groups):
            done = done + deep_in[source, :few, cols].astype(F32)
        part = deep_all.at[pl.ds(pl.multiple_of(group * few, few), few), cols]
        part[...] = done.astype(BF)
        for step, peer in enumerate(others):
            fourth.append(send(part, part, deep_sems, (6 + at) * groups + step, peer))
    rows_out.wait()
    output[...] = (mixed[...] + got_rows[...].astype(F32)).astype(BF)
    for at in range(len(sources)):
        cols = cols_of(at)
        if split:
            for step in range(groups - 1):
                fourth[at * (groups - 1) + step].wait()
            done = deep_all[:, cols].astype(F32)
        else:
            for step in range(groups - 1):
                third[at * (groups - 1) + step].wait()
            done = deep_in[0, :, cols].astype(F32)
            for source in range(1, groups):
                done = done + deep_in[source, :, cols].astype(F32)
        total[here, cols] = done
        last.append(send(total.at[here, cols], total.at[here, cols], last_sems, at, near))
    for copy in deep_small:
        copy.wait()
    lone = small_deep[0]
    for at in range(1, groups):
        lone = lone + small_deep[at]
    o_vec[...] = lone[0:7]
    o_router[...] = lone[router : router + o_router.shape[0]]
    grad_in, grad_back = jnp.zeros(o_in.shape, F32), jnp.zeros(o_back.shape, F32)
    for at in range(groups):
        away = lax.rem(group - at + groups, groups)
        kin = lax.rem(away, 2) == 0
        pick_in, pick_back = jnp.zeros(o_in.shape, F32), jnp.zeros(o_back.shape, F32)
        for which in range(hosted):
            found = away // 2 == which
            pick_in = jnp.where(found, bin_deep[at, 2 * which : 2 * which + 2], pick_in)
            pick_back = jnp.where(found, small_deep[at, 8 + 2 * which : 10 + 2 * which], pick_back)
        grad_in = grad_in + jnp.where(kin, pick_in, 0.0)
        grad_back = grad_back + jnp.where(kin, pick_back, 0.0)
    o_in[...] = grad_in
    o_back[...] = grad_back
    for copy in last:
        copy.wait()
    o_qkv[...] = total[:, width : 4 * width]
    o_out[...] = total[:, :width]

    stores = []
    for which, (_, _, _, to, back, own, out) in enumerate(sets):
        for part in range(2):
            for at in range(hosted - 1):
                home_in(which, part, at).wait_recv()
        value = own[...]
        for at in range(hosted - 1):
            value = value + back[at].astype(F32)
        whole = (sum_back, sum_in)[which]
        whole[...] = value
        stores.append(send(whole, out.at[core], (home_s, home_r), which, near))
        copy = pltpu.make_async_copy(whole, out.at[core], home_sem.at[which])
        copy.start()
        stores.append(copy)
    for which in range(2):
        for part in range(2):
            for at in range(hosted - 1):
                home_out(which, part, at).wait_send()
                if dps == 4:
                    for kind in (0, 2 - part):
                        piece_out(which, part, at, kind).wait_send()
                else:
                    for step in range(1, dps):
                        sum_out(which, part, at, step).wait_send()
    for image in range(images):
        for which in range(2):
            swap(image, which).wait_send()
    for copy in stores:
        copy.wait()


def hand_over_kernel(count, *refs):
    given, kept, held, (loads, stores) = refs[:count], refs[count : 2 * count], refs[2 * count : 3 * count], refs[3 * count :]
    ins = [pltpu.make_async_copy(given[at], held[at], loads.at[at]) for at in range(count)]
    outs = [pltpu.make_async_copy(held[at], kept[at], stores.at[at]) for at in range(count)]
    for copy in ins:
        copy.start()
    for at in range(count):
        ins[at].wait()
        outs[at].start()
    for copy in outs:
        copy.wait()


def hand_over(arrays):
    return pl.pallas_call(
        partial(hand_over_kernel, len(arrays)),
        name="hand_over",
        in_specs=[pl.BlockSpec(memory_space=pl.ANY)] * len(arrays),
        out_specs=[pl.BlockSpec(memory_space=pl.ANY)] * len(arrays),
        out_shape=[jax.ShapeDtypeStruct(array.shape, array.dtype) for array in arrays],
        scratch_shapes=[pltpu.VMEM(array.shape, array.dtype) for array in arrays]
        + [pltpu.SemaphoreType.DMA((len(arrays),))] * 2,
        compiler_params=pltpu.CompilerParams(vmem_limit_bytes=63 * MIB),
    )(*arrays)


def shards(
    inputs, key_mask, routes, priority, vectors, w_qkv, w_out, w_router, w_in, b_in, w_back, b_back, cotangent
):
    images, half, width = inputs.shape
    tokens = images * half
    groups = lax.axis_size("expert")
    dps = lax.axis_size("dp")
    per_device = w_in.shape[0]
    experts = groups * per_device
    ff = w_in.shape[2]
    cap = max(2, 3 * tokens // experts)
    cap_pad = up(cap, 16)
    half_pad = up(half, 16)
    hosted = groups // 2
    context = lax.axis_index("context")
    V, A = pltpu.VMEM, pl.ANY
    dma = pltpu.SemaphoreType.DMA
    rows = w_qkv.shape[0]
    rows_back = ff // dps

    x = inputs.reshape(tokens, width)
    grad = cotangent.reshape(tokens, width)
    route_rows = routes.reshape(tokens, 2).T
    keys = priority.reshape(tokens) * tokens + jnp.arange(tokens, dtype=I32)

    mask = jnp.where(key_mask > 0, 0.0, -1e30).astype(F32)
    first, second = mask[:, :half], mask[:, half:]
    own = jnp.where(context == 0, first, second)
    other = jnp.where(context == 0, second, first)
    off = jnp.full((images, half_pad - half), -1e30, F32)
    bias = jnp.concatenate([own, off, other, off], axis=1)[:, None, :]
    keys_pad = 2 * half_pad

    made = comm_call(
        partial(start_kernel, dps, groups, images, cap, cap_pad),
        "front",
        0,
        [V] * 11 + [A] * 3,
        [
            ((dps, rows, 3 * width), BF, V),
            ((dps, rows, width), BF, V),
            ((experts, width), BF, V),
            ((hosted, dps, per_device, rows_back), BF, V),
            ((hosted, dps, per_device, rows), BF, V),
            ((8, width), F32, V),
            ((8, tokens), I32, V),
            ((tokens, width), BF, V),
            ((images, keys_pad, width), BF, V),
            ((images, keys_pad, width), BF, V),
            ((images, HEADS, half, keys_pad), BF, A),
            ((tokens, width), BF, V),
            ((tokens, width), F32, V),
            ((tokens, width), BF, V),
            ((width, ff), BF, A),
            ((hosted - 1, rows, ff), BF, A),
            ((ff, width), BF, A),
            ((hosted - 1, rows_back, width), BF, A),
            ((3, tokens, width), BF, A),
        ],
        [
            pltpu.VMEM((tokens, width), BF),
            pltpu.VMEM((dps, rows, LANES), BF),
            pltpu.VMEM((dps, 8, rows), BF),
            pltpu.VMEM((images, HEADS, half, keys_pad), BF),
            pltpu.VMEM((rows, ff), F32),
            pltpu.VMEM((rows_back, width), F32),
            pltpu.VMEM((rows, ff), BF),
            pltpu.VMEM((rows_back, width), BF),
        ]
        + [dma((6 * (dps - 1),))] * 2
        + [dma((1 + 2 * (dps - 1),))] * 2
        + [dma((2 * hosted,))] * 2
        + [dma((2 * (dps + hosted),))] * 2
        + [dma((5,))]
        + [dma((3,))] * 2,
        flops=2 * tokens * width * (8 * width + 4 * keys_pad),
        moved=40 * tokens * width,
    )(x, w_qkv, w_out, w_router, vectors, b_in, b_back, route_rows, keys[:, None], keys[None, :], bias, w_in, w_back, grad)
    qkv_all, out_all, router_rows, b_ins, b_backs, vec, slots, q, k, v, p, o, after, acts, *expert_w, grads = made

    rows_all = 4 * cap_pad
    deep = hosted * cap_pad
    made = comm_call(
        partial(experts_kernel, groups, dps, images, cap_pad),
        "experts",
        2,
        [A, A, V, V, V, V, V, V] + [A] * 5,
        [
            ((tokens, width), F32, V),
            ((tokens, width), F32, V),
            ((tokens, width), BF, V),
            ((experts, width), F32, V),
            ((rows, ff), F32, V),
            ((rows_back, width), F32, V),
            ((hosted - 1, width, ff), BF, A),
            ((hosted - 1, ff, width), BF, A),
            ((hosted, 2, 1, ff), F32, V),
            ((hosted, 2, 1, width), F32, V),
            ((hosted - 1, width, ff), BF, A),
            ((hosted - 1, ff, width), BF, A),
        ],
        [
            pltpu.VMEM((2, 4, tokens, width), BF),
            pltpu.VMEM((4, 8, tokens), F32),
            pltpu.VMEM((4, deep, 2 * width), BF),
            pltpu.VMEM((width, ff), BF),
            pltpu.VMEM((ff, width), BF),
            pltpu.VMEM((dps, rows_all, rows), BF),
            pltpu.VMEM((rows_all, ff), BF),
            pltpu.VMEM((rows_all, ff), BF),
            pltpu.VMEM((rows_all, width), BF),
            pltpu.VMEM((cap_pad, ff), BF),
            pltpu.VMEM((dps, rows, ff), BF),
            pltpu.VMEM((dps - 1, rows, ff), BF),
            pltpu.VMEM((dps, rows_back, width), BF),
            pltpu.VMEM((dps - 1, rows_back, width), BF),
            pltpu.VMEM((4, hosted, 1, tokens), F32),
            pltpu.VMEM((3, hosted, 1, tokens), F32),
            pltpu.VMEM((4, tokens, width), BF),
            pltpu.VMEM((4, tokens, width), BF),
            pltpu.VMEM((tokens, width), BF),
            pltpu.VMEM((tokens, width), BF),
            pltpu.VMEM((tokens, LANES), F32),
            dma((6,)),
            dma((6,)),
            dma((2 * dps,)),
            dma((2 * dps,)),
            dma((2 * dps,)),
            dma((9,)),
            dma((9,)),
            dma((2 * dps,)),
            dma((3,)),
            dma((2 * hosted * dps,)),
            dma((2 * hosted * dps,)),
        ],
        flops=14 * hosted * rows_all * width * ff,
        moved=20 * tokens * width + 8 * hosted * width * ff,
        vmem=63,
    )(acts, grad, after, router_rows, route_rows, slots, b_ins, b_backs, *expert_w, grads)
    back_rows, mixed, far_rows, g_router, g_in, g_back, g_in_other, g_back_other, g_b_in, g_b_back, *_ = made

    wide = 4 * width
    halves_of = rows // 2
    small = up(8 + 2 * hosted + experts, 8)
    kin_slots = 4 * (hosted - 1)
    made = comm_call(
        partial(back_kernel, dps, groups, images),
        "back",
        1,
        [V] * 17 + [A] * 4,
        [
            ((tokens, width), BF, V),
            ((tokens, width), BF, V),
            ((rows, 3 * width), F32, V),
            ((rows, width), F32, V),
            ((experts, rows), F32, V),
            ((7, rows), F32, V),
            ((per_device, rows_back), F32, V),
            ((per_device, rows), F32, V),
            (w_in.shape, F32, A),
            (w_back.shape, F32, A),
            ((hosted - 1, dps - 1, rows, ff), BF, A),
            ((hosted - 1, dps - 1, rows_back, width), BF, A),
        ],
        [
            pltpu.VMEM((rows, ff), F32),
            pltpu.VMEM((rows_back, width), F32),
            pltpu.VMEM((2, HEADS, half, keys_pad), BF),
            pltpu.VMEM((tokens, width), F32),
            pltpu.VMEM((tokens, width), BF),
            pltpu.VMEM((2, tokens, width), BF),
            pltpu.VMEM((2, tokens, width), BF),
            pltpu.VMEM((tokens, width), BF),
            pltpu.VMEM((tokens, width), BF),
            pltpu.VMEM((width, width), F32),
            pltpu.VMEM((width, 3 * width), F32),
            pltpu.VMEM((8, width), F32),
            pltpu.VMEM((dps, rows // 2, ff), BF),
            pltpu.VMEM((dps, rows_back // 2, width), BF),
            pltpu.VMEM((hosted - 1, rows, ff), BF),
            pltpu.VMEM((hosted - 1, rows_back, width), BF),
            pltpu.VMEM((hosted - 1, rows, ff), BF),
            pltpu.VMEM((hosted - 1, rows_back, width), BF),
            pltpu.VMEM((dps, halves_of, wide), BF),
            pltpu.VMEM((dps, halves_of, wide), BF),
            pltpu.VMEM((dps - 1, halves_of, wide), BF),
            pltpu.VMEM((dps - 1, halves_of, wide), BF),
            pltpu.VMEM((groups, halves_of, wide), BF),
            pltpu.VMEM((halves_of, wide), BF),
            pltpu.VMEM((halves_of, wide), BF),
            pltpu.VMEM((rows, wide), F32),
            pltpu.VMEM((2, dps, small, rows), F32),
            pltpu.VMEM((dps, small, rows), F32),
            pltpu.VMEM((dps - 1, small, rows), F32),
            pltpu.VMEM((groups, small, rows), F32),
            pltpu.VMEM((2, dps, 2 * hosted, rows_back), F32),
            pltpu.VMEM((dps, 2 * hosted, rows_back), F32),
            pltpu.VMEM((dps - 1, 2 * hosted, rows_back), F32),
            pltpu.VMEM((groups, 2 * hosted, rows_back), F32),
            pltpu.VMEM((tokens, width), BF),
            dma((6,)), dma((6,)), dma((6 * dps,)), dma((6 * dps,)),
            dma((10 * groups,)), dma((10 * groups,)), dma((4,)), dma((4,)), dma((1,)), dma((1,)),
            dma((2,)), dma((2 * images,)), dma((2 * images,)), dma((kin_slots * dps,)), dma((kin_slots * dps,)),
            dma((2,)), dma((kin_slots,)), dma((kin_slots,)), dma((2,)), dma((2,)), dma((2,)),
        ],
        flops=2 * tokens * width * (8 * width + 8 * keys_pad),
        moved=60 * tokens * width,
        vmem=62,
    )(
        grad, back_rows, after, o, vec, out_all, q, k, v, x, qkv_all, g_router, g_in, g_back, g_b_in, g_b_back, mixed,
        p, g_in_other, g_back_other, far_rows,
    )
    dx, output, grad_qkv, grad_out, grad_router, grad_vec, grad_b_in, grad_b_back, grad_w_in, grad_w_back, *_ = made
    passed = hand_over([output, dx, grad_vec, grad_qkv, grad_out, grad_w_in, grad_b_in, grad_w_back, grad_b_back])
    output, dx, grad_vec, grad_qkv, grad_out, grad_w_in, grad_b_in, grad_w_back, grad_b_back = passed
    return (
        output.reshape(images, half, width),
        dx.reshape(images, half, width),
        grad_vec,
        grad_qkv,
        grad_out,
        grad_router.T,
        grad_w_in,
        grad_b_in,
        grad_w_back,
        grad_b_back,
    )


def solution(mesh):
    tokens = P(("dp", "expert"), "context", None)
    by_rows = P("dp", None)
    experts = P("expert", "dp", None)
    expert_bias = P("expert", "dp")
    return jax.shard_map(
        shards,
        mesh=mesh,
        in_specs=(
            tokens,
            P(("dp", "expert"), None),
            P(("dp", "expert"), "context", None, None),
            tokens,
            P(None, "dp"),
            by_rows,
            by_rows,
            by_rows,
            experts,
            expert_bias,
            experts,
            expert_bias,
            tokens,
        ),
        out_specs=(
            tokens,
            tokens,
            P(None, "dp"),
            by_rows,
            by_rows,
            by_rows,
            experts,
            expert_bias,
            experts,
            expert_bias,
        ),
        check_vma=False,
    )
```

```python
from functools import partial

import jax
import jax.numpy as jnp
from jax import lax
from jax.experimental import pallas as pl
from jax.experimental.pallas import tpu as pltpu
from jax.sharding import PartitionSpec as P

HEADS = 8
EPSILON = 1e-06
LANES = 128
BF = jnp.bfloat16
F32 = jnp.float32
I32 = jnp.int32
MIB = 1 << 20


def up(size, unit):
    return -(-size // unit) * unit


def nn(a, b):
    return jnp.dot(a, b, preferred_element_type=F32)


def nt(a, b):
    return lax.dot_general(a, b, (((1,), (1,)), ((), ())), preferred_element_type=F32)


def tn(a, b):
    return lax.dot_general(a, b, (((0,), (0,)), ((), ())), preferred_element_type=F32)


def iota(shape, dim):
    return lax.broadcasted_iota(I32, shape, dim)


def normed(values):
    average = jnp.mean(values, axis=-1, keepdims=True)
    centred = values - average
    inv_scale = lax.rsqrt(jnp.mean(centred * centred, axis=-1, keepdims=True) + EPSILON)
    return centred * inv_scale, inv_scale


def norm_backward(grad, unit, inv_scale, gain):
    scaled = grad * gain
    centre = jnp.mean(scaled, axis=-1, keepdims=True)
    along = jnp.mean(scaled * unit, axis=-1, keepdims=True)
    return inv_scale * (scaled - centre - unit * along)


def gelu_parts(z):
    share = 0.5 * (1.0 + lax.erf(z * 0.7071067811865476))
    slope = share + z * (0.3989422804014327 * jnp.exp(-0.5 * z * z))
    return z * share, slope


def experts_kernel(
    groups, dps, images, cap_pad, acts, grad, after, router, routes, slots, b_in, b_back, *rest
):
    hosted = groups // 2
    w_in, kin_in, w_back, kin_back, grads, rest = *rest[:5], rest[5:]
    back_rows, mixed, far_rows, g_router, g_in, g_back, g_in_other, g_back_other, g_b_in, g_b_back = rest[:10]
    w_in_far, w_back_far, rest = rest[10], rest[11], rest[12:]
    tok, info, made_rows, w_in_v, w_back_v, rows_v, hidden, grad_pre, delta, slope = rest[:10]
    in_send, in_recv, back_send, back_recv, dots, dots_got, to_near, from_near, to_far, from_far = rest[10:20]
    places, x_s, x_r, w_sem, r_s, r_r, p_s, p_r, store_sem, load_sem, w_s, w_r = rest[20:]
    dp, group, core = lax.axis_index("dp"), lax.axis_index("expert"), lax.axis_index("context")
    tokens, width = mixed.shape
    ff = w_in_v.shape[1]
    rows_in, rows_back = width // dps, ff // dps
    mate = group + 1 - 2 * lax.rem(group, 2)
    near, across, diagonal = (dp, group, 1 - core), (dp, mate, core), (dp, mate, 1 - core)

    def remote(src, dst, sems, slot, target):
        return pltpu.make_async_remote_copy(
            src_ref=src, dst_ref=dst, send_sem=sems[0].at[slot], recv_sem=sems[1].at[slot],
            device_id=target, device_id_type=MESH,
        )

    pools = (info, tok.at[0])
    moves = {}
    for at, pool in enumerate(pools):
        moves[at, 1] = remote(pool.at[0], pool.at[1], (x_s, x_r), 3 * at, near)
        moves[at, 2] = remote(pool.at[0], pool.at[2], (x_s, x_r), 3 * at + 1, across)
        moves[at, 3] = remote(pool.at[2], pool.at[3], (x_s, x_r), 3 * at + 2, near)

    def along(step):
        return (lax.rem(dp + step, dps), group, core)

    def sum_out(which, step):
        src, dst = ((in_send, in_recv), (back_send, back_recv))[which]
        return remote(src.at[step], dst.at[step - 1], (r_s, r_r), which * dps + step, along(step))

    def gather(at, which, step):
        kin, far = ((kin_in, w_in_far), (kin_back, w_back_far))[which]
        size = kin.shape[1]
        part = far.at[at, pl.ds(pl.multiple_of(dp * size, size), size)]
        target = (square(dp)[step - 1], group, core) if dps == 4 else along(step)
        return remote(kin.at[at], part, (w_s, w_r), (2 * at + which) * dps + step - 1, target)

    def onward(at, which):
        kin, far = ((kin_in, w_in_far), (kin_back, w_back_far))[which]
        return [
            remote(ref, ref, (w_s, w_r), (2 * at + which) * dps + 2 + slot, (target, group, core))
            for slot, (ref, target) in enumerate(relay(far.at[at], kin.shape[1], dp))
        ]

    direct = 3 if dps == 4 else dps

    def load(which, wait):
        for at in range(hosted):
            copies = []
            for part, (whole, kin, far, held) in enumerate(
                ((w_in, kin_in, w_in_far, w_in_v), (w_back, kin_back, w_back_far, w_back_v))
            ):
                if at == 0:
                    copies.append(pltpu.make_async_copy(whole, held, w_sem.at[part * dps]))
                    continue
                size = kin.shape[1]
                for step in range(dps):
                    here = pl.ds(pl.multiple_of(lax.rem(dp + step, dps) * size, size), size)
                    src = far.at[at - 1, here] if step else kin.at[at - 1]
                    copies.append(pltpu.make_async_copy(src, held.at[here], w_sem.at[part * dps + step]))

            @pl.when(which == at)
            def _():
                if at and not wait:
                    for part in range(2):
                        for step in range(1, direct):
                            if dps == 4:
                                gather(at - 1, part, step).wait_send()
                            else:
                                gather(at - 1, part, step).wait()
                        if dps == 4:
                            for copy in onward(at - 1, part):
                                copy.wait()
                for copy in copies:
                    copy.wait() if wait else copy.start()

    def store(which, to, step):
        return (
            pltpu.make_async_copy(
                in_send.at[step],
                g_in_other.at[which - 1, pl.ds(pl.multiple_of(to * rows_in, rows_in), rows_in)],
                store_sem.at[step],
            ),
            pltpu.make_async_copy(
                back_send.at[step],
                g_back_other.at[which - 1, pl.ds(pl.multiple_of(to * rows_back, rows_back), rows_back)],
                store_sem.at[dps + step],
            ),
        )

    mine = (
        pltpu.make_async_copy(acts, tok.at[0, 0], load_sem.at[0]),
        pltpu.make_async_copy(grad, tok.at[1, 0], load_sem.at[1]),
        pltpu.make_async_copy(grads, tok.at[1, pl.ds(1, 3)], load_sem.at[2]),
    )
    for copy in mine:
        copy.start()
    load(0, False)
    greet([near, across, diagonal] + [along(step) for step in range(1, dps)])
    mine[0].wait()
    for hop in (2, 1):
        moves[1, hop].start()
    for at in range(hosted - 1):
        for part in range(2):
            for step in range(1, direct):
                gather(at, part, step).start()
    logits = nt(router[...], tok[0, 0])
    logits = jnp.exp(logits - jnp.max(logits, axis=0, keepdims=True))
    probs = logits / jnp.sum(logits, axis=0, keepdims=True)
    ids = iota(probs.shape, 0)
    info[0, 2:4, :] = slots[0:2, :].astype(F32)
    for choice in range(2):
        info[0, choice : choice + 1, :] = jnp.sum(
            jnp.where(routes[choice : choice + 1, :] == ids, probs, 0.0), axis=0, keepdims=True
        )
    info[0, 4:8, :] = jnp.zeros((4, tokens), F32)
    for hop in (2, 1):
        moves[0, hop].start()
    mine[1].wait()
    mine[2].wait()
    g_b_in[...] = jnp.zeros_like(g_b_in)
    g_b_back[...] = jnp.zeros_like(g_b_back)

    def near_out(at):
        return remote(to_near.at[at], from_near.at[at], (p_s, p_r), at, near)

    def far_out():
        return remote(to_far, from_far, (p_s, p_r), 4, across)

    def dots_out(source, target):
        return remote(dots.at[source], dots_got.at[source - 1], (p_s, p_r), 5 + source, target)

    def own_row(pair):
        pair = pair.astype(F32)
        return jnp.where(core == 0, pair[0:1], pair[1:2])

    half = tokens // images
    deep = hosted * cap_pad
    slot_ids = jnp.zeros((1, deep), F32)
    lane = iota((1, deep), 1)
    for which in range(hosted):
        first = (lax.rem(group + 2 * which, groups) * 2 + core - which) * cap_pad
        slot_ids = jnp.where(lane // cap_pad == which, (lane + first).astype(F32), slot_ids)

    def place(source):
        slot = info[source, 2:4, :]
        high = jnp.floor(slot * (1.0 / 64.0))
        parts = jnp.concatenate([high, slot - 64.0 * high, jnp.zeros((4, tokens), F32)], axis=0).astype(BF)
        row, col = iota((8, LANES), 0), iota((8, LANES), 1)
        weight = jnp.where(row == col, 64.0, jnp.where(row == col + 2, 1.0, 0.0))
        weight = jnp.where(col < 2, weight, 0.0).astype(BF)
        places[...] = tn(parts, weight)

    def summed(source, image):
        rows = pl.ds(pl.multiple_of(image * half, 8), half)
        hit = (places[rows, 0:1] == slot_ids) | (places[rows, 1:2] == slot_ids)
        return rows, nn(jnp.where(hit, 1.0, 0.0).astype(BF), made_rows[source])

    def to_core(source, at):
        place(source)

        def chunk(image, _):
            rows, part = summed(source, image)
            to_near[at, rows, :] = part[:, :width].astype(BF)
            to_near[at + 1, rows, :] = part[:, width:].astype(BF)
            return 0

        lax.fori_loop(0, images, chunk, 0)
        near_out(at).start()
        near_out(at + 1).start()

    def to_chip():
        place(2)
        near_out(0).wait_recv()
        near_out(1).wait_recv()

        def chunk(image, _):
            rows, part = summed(2, image)
            to_far[rows, :] = (part[:, :width] + from_near[0, rows, :].astype(F32)).astype(BF)
            far_rows[rows, :] = (part[:, width:] + from_near[1, rows, :].astype(F32)).astype(BF)
            return 0

        lax.fori_loop(0, images, chunk, 0)
        far_out().start()

    def expert(which, _):
        load(which, True)
        own = lax.rem(group + 2 * which, groups) * 2 + core
        last = which // (hosted - 1)

        def block(turn, _):
            source = turn + (3 - 2 * turn) * last

            @pl.when(jnp.logical_and(which == 0, source == 1))
            def _():
                for at in range(2):
                    moves[at, 1].wait_recv()

            @pl.when(jnp.logical_and(which == 0, source == 2))
            def _():
                for at in range(2):
                    moves[at, 2].wait_recv()
                    moves[at, 3].start()

            @pl.when(jnp.logical_and(which == 0, source == 3))
            def _():
                for at in range(2):
                    moves[at, 3].wait_recv()

            rows = pl.ds(pl.multiple_of(source * cap_pad, 16), cap_pad)
            spot = pl.ds(pl.multiple_of(which * cap_pad, 16), cap_pad)
            ids = iota((cap_pad, tokens), 0) + own * cap_pad
            hit_first = ids == info[source, 2:3, :].astype(I32)
            hit_second = ids == info[source, 3:4, :].astype(I32)
            hit = jnp.logical_or(hit_first, hit_second)
            one_hot = jnp.where(hit, 1.0, 0.0).astype(BF)
            gate = jnp.where(hit_first, info[source, 0:1, :], 0.0) + jnp.where(hit_second, info[source, 1:2, :], 0.0)
            gate = jnp.sum(gate, axis=1, keepdims=True)
            acts_in = nn(one_hot, tok[0, source]).astype(BF)
            for part in range(dps):
                rows_v[part, rows, :] = acts_in[:, part * rows_in : (part + 1) * rows_in]
            for part in range(dps):
                cols = slice(part * rows_back, (part + 1) * rows_back)
                z = nn(acts_in, w_in_v[:, cols]) + own_row(b_in[which, part])
                value, rise = gelu_parts(z)
                hidden[rows, cols] = value.astype(BF)
                slope[:, cols] = rise.astype(BF)
            bias = jnp.concatenate([own_row(b_back[which, part]) for part in range(dps)], axis=1)
            made = (nn(hidden[rows, :], w_back_v[...]) + bias).astype(BF).astype(F32)
            made_rows[source, spot, width:] = (gate * made).astype(BF)
            got_grad = nn(one_hot, tok[1, source])
            low = (gate * got_grad).astype(BF)
            delta[rows, :] = low
            g_b_back[which, core] += jnp.sum(low.astype(F32), axis=0, keepdims=True)
            dot = jnp.sum(made * got_grad, axis=1, keepdims=True)
            dots[source, which] = jnp.sum(jnp.where(hit, dot, 0.0), axis=0, keepdims=True)
            for part in range(dps):
                cols = slice(part * rows_back, (part + 1) * rows_back)
                dz = nt(low, w_back_v[cols, :]) * slope[:, cols].astype(F32)
                g_b_in[which, core, :, cols] += jnp.sum(dz, axis=0, keepdims=True)
                grad_pre[rows, cols] = dz.astype(BF)
            made_rows[source, spot, :width] = nt(grad_pre[rows, :], w_in_v[...]).astype(BF)

            if dps == 4:
                for part in range(2):

                    @pl.when(jnp.logical_and(which == 0, turn == 1 + part))
                    def _():
                        for at in range(hosted - 1):
                            for step in range(1, direct):
                                gather(at, part, step).wait_recv()
                            for copy in onward(at, part):
                                copy.start()

            @pl.when(jnp.logical_and(last == 1, source == 3))
            def _():
                dots_out(3, diagonal).start()
                to_core(3, 0)

            @pl.when(jnp.logical_and(last == 1, source == 2))
            def _():
                dots_out(2, across).start()
                to_chip()

            @pl.when(jnp.logical_and(last == 1, source == 1))
            def _():
                dots_out(1, near).start()
                to_core(1, 2)

            return 0

        lax.fori_loop(0, 4, block, 0)
        @pl.when(which + 1 < hosted)
        def _():
            load(which + 1, False)

        def weights(step, _):
            step = lax.rem(step + 1, dps)
            to = lax.rem(dp + step, dps)
            part_back = tn(hidden[:, pl.ds(pl.multiple_of(to * rows_back, LANES), rows_back)], delta[...])
            part_in = tn(rows_v[to], grad_pre[...])

            @pl.when(jnp.logical_and(which == 1, step > 0))
            def _():
                sum_out(0, step).wait_send()
                sum_out(1, step).wait_send()

            @pl.when(which > 1)
            def _():
                for copy in store(which - 1, to, step):
                    copy.wait()

            back_send[step] = part_back.astype(BF)
            in_send[step] = part_in.astype(BF)

            @pl.when(jnp.logical_and(which == 0, step > 0))
            def _():
                sum_out(1, step).start()
                sum_out(0, step).start()

            @pl.when(jnp.logical_and(which == 0, step == 0))
            def _():
                g_back[...] = part_back
                g_in[...] = part_in

            @pl.when(which > 0)
            def _():
                for copy in store(which, to, step):
                    copy.start()

            return 0

        lax.fori_loop(0, dps, weights, 0)
        return 0

    lax.fori_loop(0, hosted, expert, 0)
    for source, target in ((1, near), (2, across), (3, diagonal)):
        dots_out(source, target).wait_recv()
    at_near, at_far = 1 - core, core
    whole = jnp.zeros(probs.shape, F32)
    for which in range(hosted):
        here, there = lax.rem(group + 2 * which, groups) * 2, lax.rem(mate + 2 * which, groups) * 2
        whole = jnp.where(ids == here + core, dots[0, which], whole)
        whole = jnp.where(ids == here + at_near, dots_got[0, which], whole)
        whole = jnp.where(ids == there + at_far, dots_got[1, which], whole)
        whole = jnp.where(ids == there + at_near, dots_got[2, which], whole)
    low = (probs * (whole - jnp.sum(probs * whole, axis=0, keepdims=True))).astype(BF)
    g_router[...] = nn(low, tok[0, 0])
    back_rows[...] = tn(low, router[...])
    place(0)
    near_out(2).wait_recv()
    near_out(3).wait_recv()
    far_out().wait_recv()

    def chunk(image, _):
        rows, part = summed(0, image)
        back_rows[rows, :] += part[:, :width] + from_near[2, rows, :].astype(F32) + from_far[rows, :].astype(F32)
        mixed[rows, :] = after[rows, :] + part[:, width:] + from_near[3, rows, :].astype(F32)
        return 0

    lax.fori_loop(0, images, chunk, 0)
    for step in range(1, dps):
        for which in range(2):
            sum_out(which, step).wait_recv()
        g_back[...] += back_recv[step - 1].astype(F32)
        g_in[...] += in_recv[step - 1].astype(F32)

    for step in range(dps):
        for copy in store(hosted - 1, lax.rem(dp + step, dps), step):
            copy.wait()
    for copy in moves.values():
        copy.wait_send()
    for at in range(4):
        near_out(at).wait_send()
    far_out().wait_send()
    for source, target in ((1, near), (2, across), (3, diagonal)):
        dots_out(source, target).wait_send()


def forward_image(
    half, image, dps, x, x_other, bias, vec, w_qkv, w_out, q_ref, k_ref, v_ref, p_ref, o_ref, h_ref, a_ref
):
    width = x.shape[1]
    rows = pl.ds(pl.multiple_of(image * half, 8), half)
    half_pad = up(half, 16)
    head_dim = width // HEADS
    scale = head_dim ** (-0.5)
    gain, offset, bias_q, bias_v = (vec[row : row + 1, :] for row in range(4))
    own = x[rows, :].astype(F32)
    unit, _ = normed(own)
    acts = (unit * gain + offset).astype(BF)
    unit, _ = normed(x_other[rows, :].astype(F32))
    other = (unit * gain + offset).astype(BF)

    def weight(at):
        return w_qkv[:, :, at * width : (at + 1) * width].reshape(width, width)

    q_ref[rows, :] = ((nn(acts, weight(0)) + bias_q).astype(BF).astype(F32) * scale).astype(BF)
    pad = jnp.zeros((half_pad - half, width), BF)
    for part, piece in enumerate((acts, other)):
        start = part * half_pad
        k_ref[image, pl.ds(start, half), :] = nn(piece, weight(1)).astype(BF)
        v_ref[image, pl.ds(start, half), :] = (nn(piece, weight(2)) + bias_v).astype(BF)
        if half_pad > half:
            k_ref[image, pl.ds(start + half, half_pad - half), :] = pad
            v_ref[image, pl.ds(start + half, half_pad - half), :] = pad
    low = iota((1, LANES), 1) < head_dim
    zero = jnp.zeros((), BF)
    for pair in range(width // LANES):
        cols = pl.ds(pair * LANES, LANES)
        q_pair, k_pair, v_pair = q_ref[rows, cols], k_ref[image, :, cols], v_ref[image, :, cols]
        mixed = []
        for sub in range(2):
            mask = low if sub == 0 else jnp.logical_not(low)
            scores = nt(jnp.where(mask, q_pair, zero), k_pair) + bias[image]
            raised = jnp.exp(scores - jnp.max(scores, axis=1, keepdims=True))
            probs = (raised * (1.0 / jnp.sum(raised, axis=1, keepdims=True))).astype(BF)
            p_ref[image, 2 * pair + sub] = probs
            mixed.append(nn(probs, v_pair))
        o_ref[rows, cols] = jnp.where(low, mixed[0], mixed[1]).astype(BF)
    after = own + nn(o_ref[rows, :], w_out[...].reshape(width, width)) + vec[4:5, :]
    h_ref[rows, :] = after
    unit, _ = normed(after)
    a_ref[rows, :] = (unit * vec[5:6, :] + vec[6:7, :]).astype(BF)


def backward_image(
    half, image, grad, back_ref, h_ref, o_ref, vec, w_out, q_ref, k_ref, v_ref, p_ref,
    dh_ref, dq_ref, dk_ref, dv_ref, g_out, g_vec,
):
    width = grad.shape[1]
    rows = pl.ds(pl.multiple_of(image * half, 8), half)
    head_dim = width // HEADS
    half_pad = up(half, 16)
    lane = iota((1, LANES), 1)
    back = back_ref[rows, :]
    unit, inv_scale = normed(h_ref[rows, :])
    dh = grad[rows, :].astype(F32) + norm_backward(back, unit, inv_scale, vec[5:6, :])
    dh_ref[rows, :] = dh
    dh_low = dh.astype(BF)
    g_out[...] += tn(o_ref[rows, :], dh_low)
    g_vec[4:5, :] += jnp.sum(dh, axis=0, keepdims=True)
    g_vec[5:6, :] += jnp.sum(back * unit, axis=0, keepdims=True)
    g_vec[6:7, :] += jnp.sum(back, axis=0, keepdims=True)
    do = nt(dh_low, w_out[...].reshape(width, width)).astype(BF)
    low = lane < head_dim
    zero = jnp.zeros((), BF)
    scale = head_dim ** (-0.5)
    for pair in range(width // LANES):
        cols = slice(pair * LANES, (pair + 1) * LANES)
        do_pair = do[:, cols]
        q_pair, k_pair, v_pair = q_ref[rows, cols], k_ref[image, :, cols], v_ref[image, :, cols]
        dq, dk, dv = [], [], []
        for sub in range(2):
            mask = low if sub == 0 else jnp.logical_not(low)
            p_low = p_ref[2 * pair + sub]
            p = p_low.astype(F32)
            dp = nt(jnp.where(mask, do_pair, zero), v_pair)
            inner = jnp.sum(p * dp, axis=1, keepdims=True)
            ds = (p * (dp - inner)).astype(BF)
            dv.append(tn(p_low, do_pair))
            dk.append(tn(ds, q_pair))
            dq.append(nn(ds, k_pair))
        dq_ref[rows, cols] = (jnp.where(low, dq[0], dq[1]) * scale).astype(BF)
        dk_pair = jnp.where(low, dk[0], dk[1]).astype(BF)
        dv_pair = jnp.where(low, dv[0], dv[1]).astype(BF)
        for part in range(2):
            dk_ref[part, rows, cols] = dk_pair[part * half_pad : part * half_pad + half]
            dv_ref[part, rows, cols] = dv_pair[part * half_pad : part * half_pad + half]


def input_image(half, image, x_ref, dh_ref, dq_ref, dk_ref, dk_got, dv_ref, dv_got, vec, w_qkv, dx_ref, g_qkv, g_vec):
    width = x_ref.shape[1]
    rows = pl.ds(pl.multiple_of(image * half, 8), half)
    unit, inv_scale = normed(x_ref[rows, :].astype(F32))
    acts = (unit * vec[0:1, :] + vec[1:2, :]).astype(BF)
    dq = dq_ref[rows, :]
    dk = (dk_ref[0, rows, :].astype(F32) + dk_got[rows, :].astype(F32)).astype(BF)
    dv = (dv_ref[0, rows, :].astype(F32) + dv_got[rows, :].astype(F32)).astype(BF)
    da = jnp.zeros(unit.shape, F32)
    for at, piece in enumerate((dq, dk, dv)):
        cols = slice(at * width, (at + 1) * width)
        g_qkv[:, cols] += tn(acts, piece)
        da = da + nt(piece, w_qkv[:, :, cols].reshape(width, width))
    dx_ref[rows, :] = (dh_ref[rows, :] + norm_backward(da, unit, inv_scale, vec[0:1, :])).astype(BF)
    g_vec[0:1, :] += jnp.sum(da * unit, axis=0, keepdims=True)
    g_vec[1:2, :] += jnp.sum(da, axis=0, keepdims=True)
    g_vec[2:3, :] += jnp.sum(dq.astype(F32), axis=0, keepdims=True)
    g_vec[3:4, :] += jnp.sum(dv.astype(F32), axis=0, keepdims=True)


MESH = pl.DeviceIdType.MESH


def send(src, dst, sems, slot, device):
    copy = pltpu.make_async_remote_copy(
        src_ref=src, dst_ref=dst, send_sem=sems[0].at[slot], recv_sem=sems[1].at[slot],
        device_id=device, device_id_type=MESH,
    )
    copy.start()
    return copy


def remote_copy(src, dst, sems, slot, device):
    return pltpu.make_async_remote_copy(
        src_ref=src, dst_ref=dst, send_sem=sems[0].at[slot], recv_sem=sems[1].at[slot],
        device_id=device, device_id_type=MESH,
    )


def square(dp):
    return dp + 1 - 2 * lax.rem(dp, 2), lax.rem(dp + 2, 4)


def relay(ref, size, dp):
    side, across = square(dp)
    half = size // 2
    return (
        (ref.at[pl.ds(pl.multiple_of(across * size, size) + half, half)], side),
        (ref.at[pl.ds(pl.multiple_of(side * size, size), half)], across),
    )


def greet(devices):
    barrier = pltpu.get_barrier_semaphore()
    for device in devices:
        pl.semaphore_signal(barrier, inc=1, device_id=device, device_id_type=MESH)
    pl.semaphore_wait(barrier, len(devices))


def comm_call(body, name, number, ins, outs, scratch, flops=0, moved=0, vmem=56):
    return pl.pallas_call(
        body,
        name=name,
        in_specs=[pl.BlockSpec(memory_space=space) for space in ins],
        out_specs=[pl.BlockSpec(memory_space=space) for _, _, space in outs],
        out_shape=[jax.ShapeDtypeStruct(shape, dtype) for shape, dtype, _ in outs],
        scratch_shapes=list(scratch),
        cost_estimate=pl.CostEstimate(flops=int(flops), bytes_accessed=int(moved), transcendentals=0),
        compiler_params=pltpu.CompilerParams(
            vmem_limit_bytes=vmem * MIB, collective_id=number, has_side_effects=True
        ),
    )


def start_kernel(
    dps, groups, images, cap, cap_pad, x, w_qkv, w_out, w_router, vectors, b_in, b_back, routes, priority, bias,
    w_in, w_back, grad,
    qkv_all, out_all, router_rows, b_in_all, back_all, vec, slots,
    q_ref, k_ref, v_ref, p_ref, o_ref, h_ref, a_ref, in_all, in_kin, back_w_all, back_kin, grads,
    x_other, router_all, vec_all, p_all, w_in_f, w_back_f, w_in_v, w_back_v,
    far_send, far_recv, near_send, near_recv, deep_send, deep_recv, w_s, w_r, local, rows_s, rows_r,
):
    dp, group, core = lax.axis_index("dp"), lax.axis_index("expert"), lax.axis_index("context")
    rows = w_qkv.shape[0]
    half = rows // 2
    hosted = groups // 2
    near = (dp, group, 1 - core)
    peers = [(lax.rem(dp + step, dps), group, core) for step in range(1, dps)]
    kin = [(dp, lax.rem(group + 2 * step, groups), core) for step in range(1, hosted)]
    loads = [
        pltpu.make_async_copy(w_in.at[core], w_in_f, local.at[0]),
        pltpu.make_async_copy(w_back.at[core], w_back_f, local.at[1]),
    ]
    for copy in loads:
        copy.start()
    mate = group + 1 - 2 * lax.rem(group, 2)
    across = (dp, mate, core)
    greet(peers + kin + [near, across])
    rows_out = [
        send(grad, grads.at[1], (rows_s, rows_r), 1, across),
        send(grad, grads.at[0], (rows_s, rows_r), 0, near),
    ]
    far, close, deep = (far_send, far_recv), (near_send, near_recv), (deep_send, deep_recv)
    waits = [send(x, x_other, close, 0, near)]
    qkv_all[dp] = w_qkv[...].astype(BF)
    own = pl.ds(pl.multiple_of(core * half, half), half)
    copies = []
    for step, peer in enumerate(peers):
        copies.append(send(qkv_all.at[dp, own], qkv_all.at[dp, own], far, step * 6, peer))
    out_all[dp] = w_out[...].astype(BF)
    router_all[dp] = w_router[...].astype(BF)
    vec_all[dp] = jnp.concatenate([vectors[...], jnp.zeros((1, rows), F32)], axis=0).astype(BF)
    b_in_all[0, dp] = b_in[...].astype(BF)
    back_all[0, dp] = b_back[...].astype(BF)
    for step, peer in enumerate(peers):
        copies.append(send(out_all.at[dp, own], out_all.at[dp, own], far, step * 6 + 1, peer))
    smalls, biases = [], []
    for step, peer in enumerate(peers):
        for at, ref in enumerate((router_all, vec_all)):
            smalls.append(send(ref.at[dp], ref.at[dp], far, step * 6 + 2 + at, peer))
        for at, ref in enumerate((b_in_all, back_all)):
            biases.append(send(ref.at[0, dp], ref.at[0, dp], far, step * 6 + 4 + at, peer))
    own_copies, direct = [], ([], [])
    for at, (wide, low, out, kin_out) in enumerate(
        ((w_in_f, w_in_v, in_all, in_kin), (w_back_f, w_back_v, back_w_all, back_kin))
    ):
        loads[at].wait()
        low[...] = wide[...].astype(BF)
        size = low.shape[0]
        part = pl.ds(pl.multiple_of(dp * size, size), size)
        for step, peer in enumerate(kin):
            own_copies.append(
                send(low, kin_out.at[hosted - 2 - step], (w_s, w_r), at * (dps + hosted) + dps + step, peer)
            )
        if dps == 4:
            for slot, target in enumerate(square(dp)):
                direct[at].append(
                    send(low, out.at[part], (w_s, w_r), at * (dps + hosted) + slot, (target, group, core))
                )
        else:
            for step, peer in enumerate(peers):
                own_copies.append(send(low, out.at[part], (w_s, w_r), at * (dps + hosted) + step, peer))
        here = pltpu.make_async_copy(low, out.at[part], local.at[2 + at])
        here.start()
        own_copies.append(here)

    def onward(at):
        out, size = ((in_all, w_in_v.shape[0]), (back_w_all, w_back_v.shape[0]))[at]
        return [
            remote_copy(ref, ref, (w_s, w_r), at * (dps + hosted) + 2 + slot, (target, group, core))
            for slot, (ref, target) in enumerate(relay(out, size, dp))
        ]

    def pass_on(at):
        for copy in direct[at]:
            copy.wait_recv()
        for copy in onward(at):
            copy.start()

    tokens = routes.shape[1]
    experts = w_router.shape[0]
    ids = iota((experts, tokens), 0)
    order = priority[...].astype(F32)
    high = jnp.floor(order * (1.0 / 256.0))
    parts = jnp.concatenate([high, order - 256.0 * high, jnp.zeros((6, tokens), F32)], axis=0).astype(BF)
    place = iota((8, LANES), 0)
    weight = jnp.where(place == 0, 256.0, jnp.where(place == 1, 1.0, 0.0)).astype(BF)
    column = tn(parts, weight)[:, 0:1]
    tied = jnp.logical_and(column == order, iota((tokens, 1), 0) < iota((1, tokens), 1))
    before = jnp.where(jnp.logical_or(column < order, tied), 1.0, 0.0).astype(BF)
    first = jnp.where(routes[0:1, :] == ids, 1.0, 0.0)
    second = jnp.where(routes[1:2, :] == ids, 1.0, 0.0)
    count = jnp.sum(first, axis=1, keepdims=True)
    rank_first = jnp.sum(nn(first.astype(BF), before) * first, axis=0, keepdims=True)
    rank_second = jnp.sum((nn(second.astype(BF), before) + count) * second, axis=0, keepdims=True)
    ranks = jnp.concatenate([rank_first, rank_second], axis=0).astype(I32)
    owned = jnp.where(ranks < cap, routes[...] * cap_pad + ranks, -1)
    slots[...] = jnp.concatenate([owned, jnp.full((6, tokens), -1, I32)], axis=0)

    for copy in biases:
        copy.wait()
    for step, peer in enumerate(kin):
        for at, ref in enumerate((b_in_all, back_all)):
            waits.append(send(ref.at[0], ref.at[hosted - 1 - step], deep, 2 * step + at, peer))
    for at, copy in enumerate(copies):
        step, ref = at % len(peers), (qkv_all, out_all)[at // len(peers)]
        copy.wait()
        source = lax.rem(dp - step - 1 + dps, dps)
        waits.append(send(ref.at[source, own], ref.at[source, own], close, 1 + at, near))
    for copy in smalls:
        copy.wait()
    vec[...] = jnp.concatenate([vec_all[at].astype(F32) for at in range(dps)], axis=1)
    router_rows[...] = jnp.concatenate([router_all[at].astype(F32) for at in range(dps)], axis=1).astype(BF)
    for copy in waits:
        copy.wait()

    half = tokens // images

    def image_step(image, _):
        forward_image(
            half, image, dps, x, x_other, bias, vec, qkv_all, out_all, q_ref, k_ref, v_ref, p_all, o_ref, h_ref, a_ref
        )
        pltpu.make_async_copy(p_all.at[image], p_ref.at[image], local.at[4]).start()
        if dps == 4:

            @pl.when(image == images - 2)
            def _():
                pass_on(0)

        return 0

    lax.fori_loop(0, images, image_step, 0)
    if dps == 4:
        pass_on(1)
    rows_out[0].wait()
    rows_out[0] = send(grads.at[1], grads.at[2], (rows_s, rows_r), 2, near)
    pltpu.make_async_copy(p_all, p_ref, local.at[4]).wait()
    for copy in rows_out:
        copy.wait()
    for copy in own_copies:
        copy.wait()
    if dps == 4:
        for at in range(2):
            for copy in direct[at]:
                copy.wait_send()
            for copy in onward(at):
                copy.wait()


def back_kernel(
    dps, groups, images, grad, back_rows, h_ref, o_ref, vec, w_out, q_ref, k_ref, v_ref, x_ref, w_qkv,
    g_router, g_in, g_back, b_in, b_back, mixed, p_all, in_other, back_other, far_rows,
    dx_ref, output, o_qkv, o_out, o_router, o_vec, o_in, o_back, w_in_sum, w_back_sum, in_recv, back_recv,
    sum_in, sum_back, p_two, dh_ref, dq_ref, dk_ref, dv_ref, dk_got, dv_got, g_out, g_qkv, g_vec,
    in_stage, back_stage, in_to, back_to, in_from, back_from,
    near_out, near_in, far_out, far_in, deep_in, deep_out, deep_all, total,
    small_near, small_far, small_got, small_deep, bin_near, bin_far, bin_got, bin_deep,
    got_rows, near_s, near_r, far_s, far_r, deep_s, deep_r, last_s, last_r,
    rows_s, rows_r, p_sem, d_s, d_r, e_s, e_r, stage_sem, kin_s, kin_r, home_s, home_r, home_sem,
):
    dp, group, core = lax.axis_index("dp"), lax.axis_index("expert"), lax.axis_index("context")
    tokens, width = dx_ref.shape
    hosted = groups // 2
    token_half = tokens // images
    rows = width // dps
    half = rows // 2
    near = (dp, group, 1 - core)
    peers = [(lax.rem(dp + step, dps), group, core) for step in range(1, dps)]
    others = [(dp, lax.rem(group + step, groups), core) for step in range(1, groups)]

    def remote(src, dst, sems, slot, target):
        return pltpu.make_async_remote_copy(
            src_ref=src, dst_ref=dst, send_sem=sems[0].at[slot], recv_sem=sems[1].at[slot],
            device_id=target, device_id_type=MESH,
        )

    sets = (
        (back_other, back_recv, back_stage, back_to, back_from, g_back, w_back_sum),
        (in_other, in_recv, in_stage, in_to, in_from, g_in, w_in_sum),
    )

    def sum_out(which, part, at, step):
        other, recv = sets[which][:2]
        size = recv.shape[2]
        piece = size // 2
        target = lax.rem(dp + step, dps)
        src = other.at[at, pl.ds(pl.multiple_of(target * size, size) + part * piece, piece)]
        dst = recv.at[at, step - 1, pl.ds(part * piece, piece)]
        slot = ((which * 2 + part) * (hosted - 1) + at) * dps + step
        return remote(src, dst, (e_s, e_r), slot, peers[step - 1])

    def piece_out(which, part, at, kind):
        other, recv, stage = sets[which][:3]
        size = recv.shape[2]
        piece = size // 2
        side, over = square(dp)
        corner = lax.rem(side + 2, 4)
        share = (corner, side, over)[kind]
        via = (over if part == 0 else side, side, over)[kind]
        place = (2, 0, 1)[kind]
        if kind == part + 1:
            src = stage.at[2 + part]
        else:
            src = other.at[at, pl.ds(pl.multiple_of(share * size, size) + part * piece, piece)]
        dst = recv.at[at, place, pl.ds(part * piece, piece)]
        slot = ((which * 2 + part) * (hosted - 1) + at) * dps + kind
        return remote(src, dst, (e_s, e_r), slot, (via, group, core))

    def at_once(which):
        for at in range(hosted - 1):
            for part, kind in ((0, 0), (1, 0), (1, 1), (0, 2)):
                piece_out(which, part, at, kind).start()

    def relayed(which):
        other, recv, stage = sets[which][:3]
        size = recv.shape[2]
        piece = size // 2
        for at in range(hosted - 1):
            for part in range(2):
                here = pl.ds(part * piece, piece)
                share = square(dp)[part]
                piece_out(which, part, at, 0).wait_recv()
                own = other.at[at, pl.ds(pl.multiple_of(share * size, size) + part * piece, piece)]
                copies = (
                    pltpu.make_async_copy(recv.at[at, 2, here], stage.at[0], stage_sem.at[0]),
                    pltpu.make_async_copy(own, stage.at[1], stage_sem.at[1]),
                )
                for copy in copies:
                    copy.start()
                for copy in copies:
                    copy.wait()
                if at:
                    piece_out(which, part, at - 1, part + 1).wait_send()
                stage[2 + part] = (stage[0].astype(F32) + stage[1].astype(F32)).astype(BF)
                piece_out(which, part, at, part + 1).start()

    def home_out(which, part, at):
        to, back = sets[which][3:5]
        piece = to.shape[1] // 2
        here = pl.ds(part * piece, piece)
        target = (dp, lax.rem(group + 2 * (at + 1), groups), core)
        slot = (which * 2 + part) * (hosted - 1) + at
        return pltpu.make_async_remote_copy(
            src_ref=to.at[at, here], dst_ref=back.at[hosted - 2 - at, here],
            send_sem=kin_s.at[slot], recv_sem=kin_r.at[(which * 2 + part) * (hosted - 1) + hosted - 2 - at],
            device_id=target, device_id_type=MESH,
        )

    def home_in(which, part, at):
        to, back = sets[which][3:5]
        piece = to.shape[1] // 2
        here = pl.ds(part * piece, piece)
        slot = (which * 2 + part) * (hosted - 1) + at
        return pltpu.make_async_remote_copy(
            src_ref=to.at[at, here], dst_ref=back.at[at, here], send_sem=kin_s.at[slot], recv_sem=kin_r.at[slot],
            device_id=near, device_id_type=MESH,
        )

    def send_home(which, part):
        other, recv, stage, to = sets[which][:4]
        size = recv.shape[2]
        piece = size // 2
        here = pl.ds(part * piece, piece)
        count = 2 if dps == 4 else dps - 1
        if dps == 4 and part == 0:
            for side in range(2):
                piece_out(which, side, hosted - 2, side + 1).wait_send()
        for at in range(hosted - 1):
            if dps == 4:
                for kind in (1, 2):
                    piece_out(which, part, at, kind).wait_recv()
            else:
                for step in range(1, dps):
                    sum_out(which, part, at, step).wait_recv()
            own = other.at[at, pl.ds(pl.multiple_of(dp * size, size) + part * piece, piece)]
            copies = (
                pltpu.make_async_copy(recv.at[at, pl.ds(0, count), here], stage.at[pl.ds(0, count)], stage_sem.at[0]),
                pltpu.make_async_copy(own, stage.at[count], stage_sem.at[1]),
            )
            for copy in copies:
                copy.start()
            for copy in copies:
                copy.wait()
            value = stage[0].astype(F32)
            for step in range(count):
                value = value + stage[step + 1].astype(F32)
            to[at, here, :] = value.astype(BF)
            home_out(which, part, at).start()

    def load(image):
        slot = lax.rem(image, 2)
        return pltpu.make_async_copy(p_all.at[image], p_two.at[slot], p_sem.at[slot])

    def swap(image, which):
        here = pl.ds(pl.multiple_of(image * token_half, 8), token_half)
        src, dst = ((dk_ref, dk_got), (dv_ref, dv_got))[which]
        return remote(src.at[1, here], dst.at[here], (d_s, d_r), 2 * image + which, near)

    load(0).start()
    greet(peers + others + [near])
    if dps == 4:
        at_once(0)
    else:
        for which in range(2):
            for part in range(2):
                for at in range(hosted - 1):
                    for step in range(1, dps):
                        sum_out(which, part, at, step).start()
    mate = group + 1 - 2 * lax.rem(group, 2)
    rows_out = send(far_rows, got_rows, (rows_s, rows_r), 0, (dp, mate, core))
    g_out[...] = jnp.zeros_like(g_out)
    g_qkv[...] = jnp.zeros_like(g_qkv)
    g_vec[...] = jnp.zeros_like(g_vec)

    def back_step(image, _):
        load(image).wait()

        @pl.when(image + 1 < images)
        def _():
            load(image + 1).start()

        backward_image(
            token_half, image, grad, back_rows, h_ref, o_ref, vec, w_out, q_ref, k_ref, v_ref,
            p_two.at[lax.rem(image, 2)], dh_ref, dq_ref, dk_ref, dv_ref, g_out, g_vec,
        )
        swap(image, 0).start()
        swap(image, 1).start()

        if dps == 4:

            @pl.when(image == 0)
            def _():
                relayed(0)
                at_once(1)

        @pl.when(image == images - 2)
        def _():
            send_home(0, 0)
            send_home(0, 1)

        return 0

    lax.fori_loop(0, images, back_step, 0)
    if dps == 4:
        relayed(1)

    near_sems, far_sems, deep_sems, last_sems = (near_s, near_r), (far_s, far_r), (deep_s, deep_r), (last_s, last_r)
    sources = [(g_out, 0)] + [(g_qkv, at) for at in range(0, g_qkv.shape[1], width)]
    theirs = pl.multiple_of((1 - core) * half, half)
    ours = pl.multiple_of(core * half, half)

    def cols_of(at):
        return pl.ds(width * at, width)

    def to_core(at):
        ref, lane = sources[at]
        for block in range(dps):
            near_out[block, :, cols_of(at)] = ref[pl.ds(block * rows + theirs, half), lane : lane + width].astype(BF)
        return send(near_out.at[:, :, cols_of(at)], near_in.at[:, :, cols_of(at)], near_sems, 2 + at, near)

    first = [to_core(0)]

    def input_step(image, _):
        swap(image, 0).wait_recv()
        swap(image, 1).wait_recv()
        input_image(
            token_half, image, x_ref, dh_ref, dq_ref, dk_ref, dk_got, dv_ref, dv_got, vec, w_qkv, dx_ref, g_qkv, g_vec
        )
        return 0

    lax.fori_loop(0, images, input_step, 0)
    for at in range(1, len(sources)):
        first.append(to_core(at))

    deep = small_near.shape[2]
    tall = 2 * hosted
    router = 8 + tall
    bias_rows = [b_back[at // 2, at % 2] for at in range(tall)]
    bias_in = jnp.concatenate([b_in[at // 2, at % 2] for at in range(tall)], axis=0)
    small = [g_vec[...]] + bias_rows + [g_router[...]]
    spare = deep - router - g_router.shape[0]
    small = jnp.concatenate(small + ([jnp.zeros((spare, width), F32)] if spare else []), axis=0)
    for at in range(dps):
        small_near[0, at] = small[:, at * rows : (at + 1) * rows]
        bin_near[0, at] = bias_in[:, at * bin_near.shape[3] : (at + 1) * bin_near.shape[3]]
    firsts = [
        send(small_near.at[0], small_near.at[1], near_sems, 0, near),
        send(bin_near.at[0], bin_near.at[1], near_sems, 1, near),
    ]
    send_home(1, 0)
    send_home(1, 1)
    second = []
    for at, (ref, lane) in enumerate(sources):
        cols = cols_of(at)
        first[at].wait()
        for step, peer in enumerate(peers):
            target = lax.rem(dp + step + 1, dps)
            block = ref[pl.ds(pl.multiple_of(target * rows, rows) + ours, half), lane : lane + width]
            far_out[step, :, cols] = (block + near_in[target, :, cols].astype(F32)).astype(BF)
            second.append(
                send(far_out.at[step, :, cols], far_in.at[step, :, cols], far_sems, (2 + at) * dps + step, peer)
            )
    for copy in firsts:
        copy.wait()
    small_far[...] = small_near[0] + small_near[1]
    bin_far[...] = bin_near[0] + bin_near[1]
    smalls = []
    for step, peer in enumerate(peers):
        target = lax.rem(dp + step + 1, dps)
        smalls.append(send(small_far.at[target], small_got.at[step], far_sems, step, peer))
        smalls.append(send(bin_far.at[target], bin_got.at[step], far_sems, dps + step, peer))
    third = []
    few = half // groups
    split = few % 16 == 0
    for at, (ref, lane) in enumerate(sources):
        cols = cols_of(at)
        mine = ref[pl.ds(pl.multiple_of(dp * rows, rows) + ours, half), lane : lane + width]
        mine = mine + near_in[dp, :, cols].astype(F32)
        for step in range(dps - 1):
            second[at * (dps - 1) + step].wait()
            mine = mine + far_in[step, :, cols].astype(F32)
        if split:
            deep_out[:, cols] = mine.astype(BF)
            deep_in[group, :few, cols] = deep_out[pl.ds(pl.multiple_of(group * few, few), few), cols]
            for step, peer in enumerate(others):
                to = pl.multiple_of(lax.rem(group + step + 1, groups) * few, few)
                src = deep_out.at[pl.ds(to, few), cols]
                third.append(send(src, deep_in.at[group, pl.ds(0, few), cols], deep_sems, at * groups + step, peer))
        else:
            deep_in[group, :, cols] = mine.astype(BF)
            for step, peer in enumerate(others):
                part = deep_in.at[group, :, cols]
                third.append(send(part, part, deep_sems, at * groups + step, peer))
    for copy in smalls:
        copy.wait()
    lone = small_far[dp]
    lone_in = bin_far[dp]
    for step in range(dps - 1):
        lone = lone + small_got[step]
        lone_in = lone_in + bin_got[step]
    small_deep[group] = lone
    bin_deep[group] = lone_in
    deep_small = []
    for step, peer in enumerate(others):
        slot = len(sources) * groups + step
        deep_small.append(send(small_deep.at[group], small_deep.at[group], deep_sems, slot, peer))
        deep_small.append(send(bin_deep.at[group], bin_deep.at[group], deep_sems, groups + slot, peer))
    last, fourth = [], []
    here = pl.ds(ours, half)
    for at in range(len(sources) if split else 0):
        cols = cols_of(at)
        for step in range(groups - 1):
            third[at * (groups - 1) + step].wait()
        done = deep_in[0, :few, cols].astype(F32)
        for source in range(1, groups):
            done = done + deep_in[source, :few, cols].astype(F32)
        part = deep_all.at[pl.ds(pl.multiple_of(group * few, few), few), cols]
        part[...] = done.astype(BF)
        for step, peer in enumerate(others):
            fourth.append(send(part, part, deep_sems, (6 + at) * groups + step, peer))
    rows_out.wait()
    output[...] = (mixed[...] + got_rows[...].astype(F32)).astype(BF)
    for at in range(len(sources)):
        cols = cols_of(at)
        if split:
            for step in range(groups - 1):
                fourth[at * (groups - 1) + step].wait()
            done = deep_all[:, cols].astype(F32)
        else:
            for step in range(groups - 1):
                third[at * (groups - 1) + step].wait()
            done = deep_in[0, :, cols].astype(F32)
            for source in range(1, groups):
                done = done + deep_in[source, :, cols].astype(F32)
        total[here, cols] = done
        last.append(send(total.at[here, cols], total.at[here, cols], last_sems, at, near))
    for copy in deep_small:
        copy.wait()
    lone = small_deep[0]
    for at in range(1, groups):
        lone = lone + small_deep[at]
    o_vec[...] = lone[0:7]
    o_router[...] = lone[router : router + o_router.shape[0]]
    grad_in, grad_back = jnp.zeros(o_in.shape, F32), jnp.zeros(o_back.shape, F32)
    for at in range(groups):
        away = lax.rem(group - at + groups, groups)
        kin = lax.rem(away, 2) == 0
        pick_in, pick_back = jnp.zeros(o_in.shape, F32), jnp.zeros(o_back.shape, F32)
        for which in range(hosted):
            found = away // 2 == which
            pick_in = jnp.where(found, bin_deep[at, 2 * which : 2 * which + 2], pick_in)
            pick_back = jnp.where(found, small_deep[at, 8 + 2 * which : 10 + 2 * which], pick_back)
        grad_in = grad_in + jnp.where(kin, pick_in, 0.0)
        grad_back = grad_back + jnp.where(kin, pick_back, 0.0)
    o_in[...] = grad_in
    o_back[...] = grad_back
    for copy in last:
        copy.wait()
    o_qkv[...] = total[:, width : 4 * width]
    o_out[...] = total[:, :width]

    stores = []
    for which, (_, _, _, to, back, own, out) in enumerate(sets):
        for part in range(2):
            for at in range(hosted - 1):
                home_in(which, part, at).wait_recv()
        value = own[...]
        for at in range(hosted - 1):
            value = value + back[at].astype(F32)
        whole = (sum_back, sum_in)[which]
        whole[...] = value
        stores.append(send(whole, out.at[core], (home_s, home_r), which, near))
        copy = pltpu.make_async_copy(whole, out.at[core], home_sem.at[which])
        copy.start()
        stores.append(copy)
    for which in range(2):
        for part in range(2):
            for at in range(hosted - 1):
                home_out(which, part, at).wait_send()
                if dps == 4:
                    for kind in (0, 2 - part):
                        piece_out(which, part, at, kind).wait_send()
                else:
                    for step in range(1, dps):
                        sum_out(which, part, at, step).wait_send()
    for image in range(images):
        for which in range(2):
            swap(image, which).wait_send()
    for copy in stores:
        copy.wait()


def hand_over_kernel(count, *refs):
    given, kept, held, (loads, stores) = refs[:count], refs[count : 2 * count], refs[2 * count : 3 * count], refs[3 * count :]
    ins = [pltpu.make_async_copy(given[at], held[at], loads.at[at]) for at in range(count)]
    outs = [pltpu.make_async_copy(held[at], kept[at], stores.at[at]) for at in range(count)]
    for copy in ins:
        copy.start()
    for at in range(count):
        ins[at].wait()
        outs[at].start()
    for copy in outs:
        copy.wait()


def hand_over(arrays):
    return pl.pallas_call(
        partial(hand_over_kernel, len(arrays)),
        name="hand_over",
        in_specs=[pl.BlockSpec(memory_space=pl.ANY)] * len(arrays),
        out_specs=[pl.BlockSpec(memory_space=pl.ANY)] * len(arrays),
        out_shape=[jax.ShapeDtypeStruct(array.shape, array.dtype) for array in arrays],
        scratch_shapes=[pltpu.VMEM(array.shape, array.dtype) for array in arrays]
        + [pltpu.SemaphoreType.DMA((len(arrays),))] * 2,
        compiler_params=pltpu.CompilerParams(vmem_limit_bytes=63 * MIB),
    )(*arrays)


def shards(
    inputs, key_mask, routes, priority, vectors, w_qkv, w_out, w_router, w_in, b_in, w_back, b_back, cotangent
):
    images, half, width = inputs.shape
    tokens = images * half
    groups = lax.axis_size("expert")
    dps = lax.axis_size("dp")
    per_device = w_in.shape[0]
    experts = groups * per_device
    ff = w_in.shape[2]
    cap = max(2, 3 * tokens // experts)
    cap_pad = up(cap, 16)
    half_pad = up(half, 16)
    hosted = groups // 2
    context = lax.axis_index("context")
    V, A = pltpu.VMEM, pl.ANY
    dma = pltpu.SemaphoreType.DMA
    rows = w_qkv.shape[0]
    rows_back = ff // dps

    x = inputs.reshape(tokens, width)
    grad = cotangent.reshape(tokens, width)
    route_rows = routes.reshape(tokens, 2).T

    mask = jnp.where(key_mask > 0, 0.0, -1e30).astype(F32)
    first, second = mask[:, :half], mask[:, half:]
    own = jnp.where(context == 0, first, second)
    other = jnp.where(context == 0, second, first)
    off = jnp.full((images, half_pad - half), -1e30, F32)
    bias = jnp.concatenate([own, off, other, off], axis=1)[:, None, :]
    keys_pad = 2 * half_pad

    made = comm_call(
        partial(start_kernel, dps, groups, images, cap, cap_pad),
        "front",
        0,
        [V] * 10 + [A] * 3,
        [
            ((dps, rows, 3 * width), BF, V),
            ((dps, rows, width), BF, V),
            ((experts, width), BF, V),
            ((hosted, dps, per_device, rows_back), BF, V),
            ((hosted, dps, per_device, rows), BF, V),
            ((8, width), F32, V),
            ((8, tokens), I32, V),
            ((tokens, width), BF, V),
            ((images, keys_pad, width), BF, V),
            ((images, keys_pad, width), BF, V),
            ((images, HEADS, half, keys_pad), BF, A),
            ((tokens, width), BF, V),
            ((tokens, width), F32, V),
            ((tokens, width), BF, V),
            ((width, ff), BF, A),
            ((hosted - 1, rows, ff), BF, A),
            ((ff, width), BF, A),
            ((hosted - 1, rows_back, width), BF, A),
            ((3, tokens, width), BF, A),
        ],
        [
            pltpu.VMEM((tokens, width), BF),
            pltpu.VMEM((dps, experts, rows), BF),
            pltpu.VMEM((dps, 8, rows), BF),
            pltpu.VMEM((images, HEADS, half, keys_pad), BF),
            pltpu.VMEM((rows, ff), F32),
            pltpu.VMEM((rows_back, width), F32),
            pltpu.VMEM((rows, ff), BF),
            pltpu.VMEM((rows_back, width), BF),
        ]
        + [dma((6 * (dps - 1),))] * 2
        + [dma((1 + 2 * (dps - 1),))] * 2
        + [dma((2 * hosted,))] * 2
        + [dma((2 * (dps + hosted),))] * 2
        + [dma((5,))]
        + [dma((3,))] * 2,
        flops=2 * tokens * width * (8 * width + 4 * keys_pad),
        moved=40 * tokens * width,
    )(x, w_qkv, w_out, w_router.T, vectors, b_in, b_back, route_rows, priority.reshape(1, tokens), bias, w_in, w_back, grad)
    qkv_all, out_all, router_rows, b_ins, b_backs, vec, slots, q, k, v, p, o, after, acts, *expert_w, grads = made

    rows_all = 4 * cap_pad
    deep = hosted * cap_pad
    made = comm_call(
        partial(experts_kernel, groups, dps, images, cap_pad),
        "experts",
        2,
        [A, A, V, V, V, V, V, V] + [A] * 5,
        [
            ((tokens, width), F32, V),
            ((tokens, width), F32, V),
            ((tokens, width), BF, V),
            ((experts, width), F32, V),
            ((rows, ff), F32, V),
            ((rows_back, width), F32, V),
            ((hosted - 1, width, ff), BF, A),
            ((hosted - 1, ff, width), BF, A),
            ((hosted, 2, 1, ff), F32, V),
            ((hosted, 2, 1, width), F32, V),
            ((hosted - 1, width, ff), BF, A),
            ((hosted - 1, ff, width), BF, A),
        ],
        [
            pltpu.VMEM((2, 4, tokens, width), BF),
            pltpu.VMEM((4, 8, tokens), F32),
            pltpu.VMEM((4, deep, 2 * width), BF),
            pltpu.VMEM((width, ff), BF),
            pltpu.VMEM((ff, width), BF),
            pltpu.VMEM((dps, rows_all, rows), BF),
            pltpu.VMEM((rows_all, ff), BF),
            pltpu.VMEM((rows_all, ff), BF),
            pltpu.VMEM((rows_all, width), BF),
            pltpu.VMEM((cap_pad, ff), BF),
            pltpu.VMEM((dps, rows, ff), BF),
            pltpu.VMEM((dps - 1, rows, ff), BF),
            pltpu.VMEM((dps, rows_back, width), BF),
            pltpu.VMEM((dps - 1, rows_back, width), BF),
            pltpu.VMEM((4, hosted, 1, tokens), F32),
            pltpu.VMEM((3, hosted, 1, tokens), F32),
            pltpu.VMEM((4, tokens, width), BF),
            pltpu.VMEM((4, tokens, width), BF),
            pltpu.VMEM((tokens, width), BF),
            pltpu.VMEM((tokens, width), BF),
            pltpu.VMEM((tokens, LANES), F32),
            dma((6,)),
            dma((6,)),
            dma((2 * dps,)),
            dma((2 * dps,)),
            dma((2 * dps,)),
            dma((9,)),
            dma((9,)),
            dma((2 * dps,)),
            dma((3,)),
            dma((2 * hosted * dps,)),
            dma((2 * hosted * dps,)),
        ],
        flops=14 * hosted * rows_all * width * ff,
        moved=20 * tokens * width + 8 * hosted * width * ff,
        vmem=63,
    )(acts, grad, after, router_rows, route_rows, slots, b_ins, b_backs, *expert_w, grads)
    back_rows, mixed, far_rows, g_router, g_in, g_back, g_in_other, g_back_other, g_b_in, g_b_back, *_ = made

    wide = 4 * width
    halves_of = rows // 2
    small = up(8 + 2 * hosted + experts, 8)
    kin_slots = 4 * (hosted - 1)
    made = comm_call(
        partial(back_kernel, dps, groups, images),
        "back",
        1,
        [V] * 17 + [A] * 4,
        [
            ((tokens, width), BF, V),
            ((tokens, width), BF, V),
            ((rows, 3 * width), F32, V),
            ((rows, width), F32, V),
            ((experts, rows), F32, V),
            ((7, rows), F32, V),
            ((per_device, rows_back), F32, V),
            ((per_device, rows), F32, V),
            (w_in.shape, F32, A),
            (w_back.shape, F32, A),
            ((hosted - 1, dps - 1, rows, ff), BF, A),
            ((hosted - 1, dps - 1, rows_back, width), BF, A),
        ],
        [
            pltpu.VMEM((rows, ff), F32),
            pltpu.VMEM((rows_back, width), F32),
            pltpu.VMEM((2, HEADS, half, keys_pad), BF),
            pltpu.VMEM((tokens, width), F32),
            pltpu.VMEM((tokens, width), BF),
            pltpu.VMEM((2, tokens, width), BF),
            pltpu.VMEM((2, tokens, width), BF),
            pltpu.VMEM((tokens, width), BF),
            pltpu.VMEM((tokens, width), BF),
            pltpu.VMEM((width, width), F32),
            pltpu.VMEM((width, 3 * width), F32),
            pltpu.VMEM((8, width), F32),
            pltpu.VMEM((dps, rows // 2, ff), BF),
            pltpu.VMEM((dps, rows_back // 2, width), BF),
            pltpu.VMEM((hosted - 1, rows, ff), BF),
            pltpu.VMEM((hosted - 1, rows_back, width), BF),
            pltpu.VMEM((hosted - 1, rows, ff), BF),
            pltpu.VMEM((hosted - 1, rows_back, width), BF),
            pltpu.VMEM((dps, halves_of, wide), BF),
            pltpu.VMEM((dps, halves_of, wide), BF),
            pltpu.VMEM((dps - 1, halves_of, wide), BF),
            pltpu.VMEM((dps - 1, halves_of, wide), BF),
            pltpu.VMEM((groups, halves_of, wide), BF),
            pltpu.VMEM((halves_of, wide), BF),
            pltpu.VMEM((halves_of, wide), BF),
            pltpu.VMEM((rows, wide), F32),
            pltpu.VMEM((2, dps, small, rows), F32),
            pltpu.VMEM((dps, small, rows), F32),
            pltpu.VMEM((dps - 1, small, rows), F32),
            pltpu.VMEM((groups, small, rows), F32),
            pltpu.VMEM((2, dps, 2 * hosted, rows_back), F32),
            pltpu.VMEM((dps, 2 * hosted, rows_back), F32),
            pltpu.VMEM((dps - 1, 2 * hosted, rows_back), F32),
            pltpu.VMEM((groups, 2 * hosted, rows_back), F32),
            pltpu.VMEM((tokens, width), BF),
            dma((6,)), dma((6,)), dma((6 * dps,)), dma((6 * dps,)),
            dma((10 * groups,)), dma((10 * groups,)), dma((4,)), dma((4,)), dma((1,)), dma((1,)),
            dma((2,)), dma((2 * images,)), dma((2 * images,)), dma((kin_slots * dps,)), dma((kin_slots * dps,)),
            dma((2,)), dma((kin_slots,)), dma((kin_slots,)), dma((2,)), dma((2,)), dma((2,)),
        ],
        flops=2 * tokens * width * (8 * width + 8 * keys_pad),
        moved=60 * tokens * width,
        vmem=62,
    )(
        grad, back_rows, after, o, vec, out_all, q, k, v, x, qkv_all, g_router, g_in, g_back, g_b_in, g_b_back, mixed,
        p, g_in_other, g_back_other, far_rows,
    )
    dx, output, grad_qkv, grad_out, grad_router, grad_vec, grad_b_in, grad_b_back, grad_w_in, grad_w_back, *_ = made
    passed = hand_over([output, dx, grad_router, grad_vec, grad_qkv, grad_out, grad_w_in, grad_b_in, grad_w_back, grad_b_back])
    output, dx, grad_router, grad_vec, grad_qkv, grad_out, grad_w_in, grad_b_in, grad_w_back, grad_b_back = passed
    return (
        output.reshape(images, half, width),
        dx.reshape(images, half, width),
        grad_vec,
        grad_qkv,
        grad_out,
        grad_router.T,
        grad_w_in,
        grad_b_in,
        grad_w_back,
        grad_b_back,
    )


def solution(mesh):
    tokens = P(("dp", "expert"), "context", None)
    by_rows = P("dp", None)
    experts = P("expert", "dp", None)
    expert_bias = P("expert", "dp")
    return jax.shard_map(
        shards,
        mesh=mesh,
        in_specs=(
            tokens,
            P(("dp", "expert"), None),
            P(("dp", "expert"), "context", None, None),
            tokens,
            P(None, "dp"),
            by_rows,
            by_rows,
            by_rows,
            experts,
            expert_bias,
            experts,
            expert_bias,
            tokens,
        ),
        out_specs=(
            tokens,
            tokens,
            P(None, "dp"),
            by_rows,
            by_rows,
            by_rows,
            experts,
            expert_bias,
            experts,
            expert_bias,
        ),
        check_vma=False,
    )
```

```python
from functools import partial

import jax
import jax.numpy as jnp
from jax import lax
from jax.experimental import pallas as pl
from jax.experimental.pallas import tpu as pltpu
from jax.sharding import PartitionSpec as P

HEADS = 8
EPSILON = 1e-06
LANES = 128
BF = jnp.bfloat16
F32 = jnp.float32
I32 = jnp.int32
MIB = 1 << 20


def up(size, unit):
    return -(-size // unit) * unit


def nn(a, b):
    return jnp.dot(a, b, preferred_element_type=F32)


def nt(a, b):
    return lax.dot_general(a, b, (((1,), (1,)), ((), ())), preferred_element_type=F32)


def tn(a, b):
    return lax.dot_general(a, b, (((0,), (0,)), ((), ())), preferred_element_type=F32)


def iota(shape, dim):
    return lax.broadcasted_iota(I32, shape, dim)


def normed(values):
    average = jnp.mean(values, axis=-1, keepdims=True)
    centred = values - average
    inv_scale = lax.rsqrt(jnp.mean(centred * centred, axis=-1, keepdims=True) + EPSILON)
    return centred * inv_scale, inv_scale


def norm_backward(grad, unit, inv_scale, gain):
    scaled = grad * gain
    centre = jnp.mean(scaled, axis=-1, keepdims=True)
    along = jnp.mean(scaled * unit, axis=-1, keepdims=True)
    return inv_scale * (scaled - centre - unit * along)


def gelu_parts(z):
    share = 0.5 * (1.0 + lax.erf(z * 0.7071067811865476))
    slope = share + z * (0.3989422804014327 * jnp.exp(-0.5 * z * z))
    return z * share, slope


def experts_kernel(
    groups, dps, images, cap_pad, acts, grad, after, router, routes, slots, b_in, b_back, *rest
):
    hosted = groups // 2
    w_in, kin_in, w_back, kin_back, grads, rest = *rest[:5], rest[5:]
    back_rows, mixed, far_rows, g_router, g_in, g_back, g_in_other, g_back_other, g_b_in, g_b_back = rest[:10]
    w_in_far, w_back_far, rest = rest[10], rest[11], rest[12:]
    tok, info, made_rows, w_in_v, w_back_v, rows_v, hidden, grad_pre, delta, slope = rest[:10]
    in_send, in_recv, back_send, back_recv, dots, dots_got, to_near, from_near, to_far, from_far = rest[10:20]
    places, x_s, x_r, w_sem, r_s, r_r, p_s, p_r, store_sem, load_sem, w_s, w_r = rest[20:]
    dp, group, core = lax.axis_index("dp"), lax.axis_index("expert"), lax.axis_index("context")
    tokens, width = mixed.shape
    ff = w_in_v.shape[1]
    rows_in, rows_back = width // dps, ff // dps
    mate = group + 1 - 2 * lax.rem(group, 2)
    near, across, diagonal = (dp, group, 1 - core), (dp, mate, core), (dp, mate, 1 - core)

    def remote(src, dst, sems, slot, target):
        return pltpu.make_async_remote_copy(
            src_ref=src, dst_ref=dst, send_sem=sems[0].at[slot], recv_sem=sems[1].at[slot],
            device_id=target, device_id_type=MESH,
        )

    pools = (info, tok.at[0])
    moves = {}
    for at, pool in enumerate(pools):
        moves[at, 1] = remote(pool.at[0], pool.at[1], (x_s, x_r), 3 * at, near)
        moves[at, 2] = remote(pool.at[0], pool.at[2], (x_s, x_r), 3 * at + 1, across)
        moves[at, 3] = remote(pool.at[2], pool.at[3], (x_s, x_r), 3 * at + 2, near)

    def along(step):
        return (lax.rem(dp + step, dps), group, core)

    def sum_out(which, step):
        src, dst = ((in_send, in_recv), (back_send, back_recv))[which]
        return remote(src.at[step], dst.at[step - 1], (r_s, r_r), which * dps + step, along(step))

    def gather(at, which, step):
        kin, far = ((kin_in, w_in_far), (kin_back, w_back_far))[which]
        size = kin.shape[1]
        part = far.at[at, pl.ds(pl.multiple_of(dp * size, size), size)]
        target = (square(dp)[step - 1], group, core) if dps == 4 else along(step)
        return remote(kin.at[at], part, (w_s, w_r), (2 * at + which) * dps + step - 1, target)

    def onward(at, which):
        kin, far = ((kin_in, w_in_far), (kin_back, w_back_far))[which]
        return [
            remote(ref, ref, (w_s, w_r), (2 * at + which) * dps + 2 + slot, (target, group, core))
            for slot, (ref, target) in enumerate(relay(far.at[at], kin.shape[1], dp))
        ]

    direct = 3 if dps == 4 else dps

    def load(which, wait):
        for at in range(hosted):
            copies = []
            for part, (whole, kin, far, held) in enumerate(
                ((w_in, kin_in, w_in_far, w_in_v), (w_back, kin_back, w_back_far, w_back_v))
            ):
                if at == 0:
                    copies.append(pltpu.make_async_copy(whole, held, w_sem.at[part * dps]))
                    continue
                size = kin.shape[1]
                for step in range(dps):
                    here = pl.ds(pl.multiple_of(lax.rem(dp + step, dps) * size, size), size)
                    src = far.at[at - 1, here] if step else kin.at[at - 1]
                    copies.append(pltpu.make_async_copy(src, held.at[here], w_sem.at[part * dps + step]))

            @pl.when(which == at)
            def _():
                if at and not wait:
                    for part in range(2):
                        for step in range(1, direct):
                            if dps == 4:
                                gather(at - 1, part, step).wait_send()
                            else:
                                gather(at - 1, part, step).wait()
                        if dps == 4:
                            for copy in onward(at - 1, part):
                                copy.wait()
                for copy in copies:
                    copy.wait() if wait else copy.start()

    def store(which, to, step):
        return (
            pltpu.make_async_copy(
                in_send.at[step],
                g_in_other.at[which - 1, pl.ds(pl.multiple_of(to * rows_in, rows_in), rows_in)],
                store_sem.at[step],
            ),
            pltpu.make_async_copy(
                back_send.at[step],
                g_back_other.at[which - 1, pl.ds(pl.multiple_of(to * rows_back, rows_back), rows_back)],
                store_sem.at[dps + step],
            ),
        )

    mine = (
        pltpu.make_async_copy(acts, tok.at[0, 0], load_sem.at[0]),
        pltpu.make_async_copy(grad, tok.at[1, 0], load_sem.at[1]),
        pltpu.make_async_copy(grads, tok.at[1, pl.ds(1, 3)], load_sem.at[2]),
    )
    for copy in mine:
        copy.start()
    load(0, False)
    greet([near, across, diagonal] + [along(step) for step in range(1, dps)])
    mine[0].wait()
    for hop in (2, 1):
        moves[1, hop].start()
    for at in range(hosted - 1):
        for part in range(2):
            for step in range(1, direct):
                gather(at, part, step).start()
    logits = nt(router[...], tok[0, 0])
    logits = jnp.exp(logits - jnp.max(logits, axis=0, keepdims=True))
    probs = logits / jnp.sum(logits, axis=0, keepdims=True)
    ids = iota(probs.shape, 0)
    info[0, 2:4, :] = slots[0:2, :].astype(F32)
    for choice in range(2):
        info[0, choice : choice + 1, :] = jnp.sum(
            jnp.where(routes[choice : choice + 1, :] == ids, probs, 0.0), axis=0, keepdims=True
        )
    info[0, 4:8, :] = jnp.zeros((4, tokens), F32)
    for hop in (2, 1):
        moves[0, hop].start()
    mine[1].wait()
    mine[2].wait()
    g_b_in[...] = jnp.zeros_like(g_b_in)
    g_b_back[...] = jnp.zeros_like(g_b_back)

    def near_out(at):
        return remote(to_near.at[at], from_near.at[at], (p_s, p_r), at, near)

    def far_out():
        return remote(to_far, from_far, (p_s, p_r), 4, across)

    def dots_out(source, target):
        return remote(dots.at[source], dots_got.at[source - 1], (p_s, p_r), 5 + source, target)

    def own_row(pair):
        pair = pair.astype(F32)
        return jnp.where(core == 0, pair[0:1], pair[1:2])

    half = tokens // images
    deep = hosted * cap_pad
    slot_ids = jnp.zeros((1, deep), F32)
    lane = iota((1, deep), 1)
    for which in range(hosted):
        first = (lax.rem(group + 2 * which, groups) * 2 + core - which) * cap_pad
        slot_ids = jnp.where(lane // cap_pad == which, (lane + first).astype(F32), slot_ids)

    def place(source):
        slot = info[source, 2:4, :]
        high = jnp.floor(slot * (1.0 / 64.0))
        parts = jnp.concatenate([high, slot - 64.0 * high, jnp.zeros((4, tokens), F32)], axis=0).astype(BF)
        row, col = iota((8, LANES), 0), iota((8, LANES), 1)
        weight = jnp.where(row == col, 64.0, jnp.where(row == col + 2, 1.0, 0.0))
        weight = jnp.where(col < 2, weight, 0.0).astype(BF)
        places[...] = tn(parts, weight)

    def summed(source, image):
        rows = pl.ds(pl.multiple_of(image * half, 8), half)
        hit = (places[rows, 0:1] == slot_ids) | (places[rows, 1:2] == slot_ids)
        return rows, nn(jnp.where(hit, 1.0, 0.0).astype(BF), made_rows[source])

    def to_core(source, at):
        place(source)

        def chunk(image, _):
            rows, part = summed(source, image)
            to_near[at, rows, :] = part[:, :width].astype(BF)
            to_near[at + 1, rows, :] = part[:, width:].astype(BF)
            return 0

        lax.fori_loop(0, images, chunk, 0)
        near_out(at).start()
        near_out(at + 1).start()

    def to_chip():
        place(2)
        near_out(0).wait_recv()
        near_out(1).wait_recv()

        def chunk(image, _):
            rows, part = summed(2, image)
            to_far[rows, :] = (part[:, :width] + from_near[0, rows, :].astype(F32)).astype(BF)
            far_rows[rows, :] = (part[:, width:] + from_near[1, rows, :].astype(F32)).astype(BF)
            return 0

        lax.fori_loop(0, images, chunk, 0)
        far_out().start()

    def expert(which, _):
        load(which, True)
        own = lax.rem(group + 2 * which, groups) * 2 + core
        last = which // (hosted - 1)

        def block(turn, _):
            source = turn + (3 - 2 * turn) * last

            @pl.when(jnp.logical_and(which == 0, source == 1))
            def _():
                for at in range(2):
                    moves[at, 1].wait_recv()

            @pl.when(jnp.logical_and(which == 0, source == 2))
            def _():
                for at in range(2):
                    moves[at, 2].wait_recv()
                    moves[at, 3].start()

            @pl.when(jnp.logical_and(which == 0, source == 3))
            def _():
                for at in range(2):
                    moves[at, 3].wait_recv()

            rows = pl.ds(pl.multiple_of(source * cap_pad, 16), cap_pad)
            spot = pl.ds(pl.multiple_of(which * cap_pad, 16), cap_pad)
            ids = iota((cap_pad, tokens), 0) + own * cap_pad
            hit_first = ids == info[source, 2:3, :].astype(I32)
            hit_second = ids == info[source, 3:4, :].astype(I32)
            hit = jnp.logical_or(hit_first, hit_second)
            one_hot = jnp.where(hit, 1.0, 0.0).astype(BF)
            gate = jnp.where(hit_first, info[source, 0:1, :], 0.0) + jnp.where(hit_second, info[source, 1:2, :], 0.0)
            gate = jnp.sum(gate, axis=1, keepdims=True)
            acts_in = nn(one_hot, tok[0, source]).astype(BF)
            for part in range(dps):
                rows_v[part, rows, :] = acts_in[:, part * rows_in : (part + 1) * rows_in]
            for part in range(dps):
                cols = slice(part * rows_back, (part + 1) * rows_back)
                z = nn(acts_in, w_in_v[:, cols]) + own_row(b_in[which, part])
                value, rise = gelu_parts(z)
                hidden[rows, cols] = value.astype(BF)
                slope[:, cols] = rise.astype(BF)
            bias = jnp.concatenate([own_row(b_back[which, part]) for part in range(dps)], axis=1)
            made = (nn(hidden[rows, :], w_back_v[...]) + bias).astype(BF).astype(F32)
            made_rows[source, spot, width:] = (gate * made).astype(BF)
            got_grad = nn(one_hot, tok[1, source])
            low = (gate * got_grad).astype(BF)
            delta[rows, :] = low
            g_b_back[which, core] += jnp.sum(low.astype(F32), axis=0, keepdims=True)
            dot = jnp.sum(made * got_grad, axis=1, keepdims=True)
            dots[source, which] = jnp.sum(jnp.where(hit, dot, 0.0), axis=0, keepdims=True)
            for part in range(dps):
                cols = slice(part * rows_back, (part + 1) * rows_back)
                dz = nt(low, w_back_v[cols, :]) * slope[:, cols].astype(F32)
                g_b_in[which, core, :, cols] += jnp.sum(dz, axis=0, keepdims=True)
                grad_pre[rows, cols] = dz.astype(BF)
            made_rows[source, spot, :width] = nt(grad_pre[rows, :], w_in_v[...]).astype(BF)

            if dps == 4:
                for part in range(2):

                    @pl.when(jnp.logical_and(which == 0, turn == 1 + part))
                    def _():
                        for at in range(hosted - 1):
                            for step in range(1, direct):
                                gather(at, part, step).wait_recv()
                            for copy in onward(at, part):
                                copy.start()

            @pl.when(jnp.logical_and(last == 1, source == 3))
            def _():
                dots_out(3, diagonal).start()
                to_core(3, 0)

            @pl.when(jnp.logical_and(last == 1, source == 2))
            def _():
                dots_out(2, across).start()
                to_chip()

            @pl.when(jnp.logical_and(last == 1, source == 1))
            def _():
                dots_out(1, near).start()
                to_core(1, 2)

            return 0

        lax.fori_loop(0, 4, block, 0)
        @pl.when(which + 1 < hosted)
        def _():
            load(which + 1, False)

        def weights(step, _):
            step = lax.rem(step + 1, dps)
            to = lax.rem(dp + step, dps)
            part_back = tn(hidden[:, pl.ds(pl.multiple_of(to * rows_back, LANES), rows_back)], delta[...])
            part_in = tn(rows_v[to], grad_pre[...])

            @pl.when(jnp.logical_and(which == 1, step > 0))
            def _():
                sum_out(0, step).wait_send()
                sum_out(1, step).wait_send()

            @pl.when(which > 1)
            def _():
                for copy in store(which - 1, to, step):
                    copy.wait()

            back_send[step] = part_back.astype(BF)
            in_send[step] = part_in.astype(BF)

            @pl.when(jnp.logical_and(which == 0, step > 0))
            def _():
                sum_out(1, step).start()
                sum_out(0, step).start()

            @pl.when(jnp.logical_and(which == 0, step == 0))
            def _():
                g_back[...] = part_back
                g_in[...] = part_in

            @pl.when(which > 0)
            def _():
                for copy in store(which, to, step):
                    copy.start()

            return 0

        lax.fori_loop(0, dps, weights, 0)
        return 0

    lax.fori_loop(0, hosted, expert, 0)
    for source, target in ((1, near), (2, across), (3, diagonal)):
        dots_out(source, target).wait_recv()
    at_near, at_far = 1 - core, core
    whole = jnp.zeros(probs.shape, F32)
    for which in range(hosted):
        here, there = lax.rem(group + 2 * which, groups) * 2, lax.rem(mate + 2 * which, groups) * 2
        whole = jnp.where(ids == here + core, dots[0, which], whole)
        whole = jnp.where(ids == here + at_near, dots_got[0, which], whole)
        whole = jnp.where(ids == there + at_far, dots_got[1, which], whole)
        whole = jnp.where(ids == there + at_near, dots_got[2, which], whole)
    low = (probs * (whole - jnp.sum(probs * whole, axis=0, keepdims=True))).astype(BF)
    g_router[...] = nn(low, tok[0, 0])
    back_rows[...] = tn(low, router[...])
    place(0)
    near_out(2).wait_recv()
    near_out(3).wait_recv()
    far_out().wait_recv()

    def chunk(image, _):
        rows, part = summed(0, image)
        back_rows[rows, :] += part[:, :width] + from_near[2, rows, :].astype(F32) + from_far[rows, :].astype(F32)
        mixed[rows, :] = after[rows, :] + part[:, width:] + from_near[3, rows, :].astype(F32)
        return 0

    lax.fori_loop(0, images, chunk, 0)
    for step in range(1, dps):
        for which in range(2):
            sum_out(which, step).wait_recv()
        g_back[...] += back_recv[step - 1].astype(F32)
        g_in[...] += in_recv[step - 1].astype(F32)

    for step in range(dps):
        for copy in store(hosted - 1, lax.rem(dp + step, dps), step):
            copy.wait()
    for copy in moves.values():
        copy.wait_send()
    for at in range(4):
        near_out(at).wait_send()
    far_out().wait_send()
    for source, target in ((1, near), (2, across), (3, diagonal)):
        dots_out(source, target).wait_send()


def forward_image(
    half, image, dps, x, x_other, bias, vec, w_qkv, w_out, q_ref, k_ref, v_ref, p_ref, o_ref, h_ref, a_ref
):
    width = x.shape[1]
    rows = pl.ds(pl.multiple_of(image * half, 8), half)
    half_pad = up(half, 16)
    head_dim = width // HEADS
    scale = head_dim ** (-0.5)
    gain, offset, bias_q, bias_v = (vec[row : row + 1, :] for row in range(4))
    own = x[rows, :].astype(F32)
    unit, _ = normed(own)
    acts = (unit * gain + offset).astype(BF)
    unit, _ = normed(x_other[rows, :].astype(F32))
    other = (unit * gain + offset).astype(BF)

    def weight(at):
        return w_qkv[:, :, at * width : (at + 1) * width].reshape(width, width)

    q_ref[rows, :] = ((nn(acts, weight(0)) + bias_q).astype(BF).astype(F32) * scale).astype(BF)
    pad = jnp.zeros((half_pad - half, width), BF)
    for part, piece in enumerate((acts, other)):
        start = part * half_pad
        k_ref[image, pl.ds(start, half), :] = nn(piece, weight(1)).astype(BF)
        v_ref[image, pl.ds(start, half), :] = (nn(piece, weight(2)) + bias_v).astype(BF)
        if half_pad > half:
            k_ref[image, pl.ds(start + half, half_pad - half), :] = pad
            v_ref[image, pl.ds(start + half, half_pad - half), :] = pad
    low = iota((1, LANES), 1) < head_dim
    zero = jnp.zeros((), BF)
    for pair in range(width // LANES):
        cols = pl.ds(pair * LANES, LANES)
        q_pair, k_pair, v_pair = q_ref[rows, cols], k_ref[image, :, cols], v_ref[image, :, cols]
        mixed = []
        for sub in range(2):
            mask = low if sub == 0 else jnp.logical_not(low)
            scores = nt(jnp.where(mask, q_pair, zero), k_pair) + bias[image]
            raised = jnp.exp(scores - jnp.max(scores, axis=1, keepdims=True))
            probs = (raised * (1.0 / jnp.sum(raised, axis=1, keepdims=True))).astype(BF)
            p_ref[image, 2 * pair + sub] = probs
            mixed.append(nn(probs, v_pair))
        o_ref[rows, cols] = jnp.where(low, mixed[0], mixed[1]).astype(BF)
    after = own + nn(o_ref[rows, :], w_out[...].reshape(width, width)) + vec[4:5, :]
    h_ref[rows, :] = after
    unit, _ = normed(after)
    a_ref[rows, :] = (unit * vec[5:6, :] + vec[6:7, :]).astype(BF)


def backward_image(
    half, image, grad, back_ref, h_ref, o_ref, vec, w_out, q_ref, k_ref, v_ref, p_ref,
    dh_ref, dq_ref, dk_ref, dv_ref, g_out, g_vec,
):
    width = grad.shape[1]
    rows = pl.ds(pl.multiple_of(image * half, 8), half)
    head_dim = width // HEADS
    half_pad = up(half, 16)
    lane = iota((1, LANES), 1)
    back = back_ref[rows, :]
    unit, inv_scale = normed(h_ref[rows, :])
    dh = grad[rows, :].astype(F32) + norm_backward(back, unit, inv_scale, vec[5:6, :])
    dh_ref[rows, :] = dh
    dh_low = dh.astype(BF)
    g_out[...] += tn(o_ref[rows, :], dh_low)
    g_vec[4:5, :] += jnp.sum(dh, axis=0, keepdims=True)
    g_vec[5:6, :] += jnp.sum(back * unit, axis=0, keepdims=True)
    g_vec[6:7, :] += jnp.sum(back, axis=0, keepdims=True)
    do = nt(dh_low, w_out[...].reshape(width, width)).astype(BF)
    low = lane < head_dim
    zero = jnp.zeros((), BF)
    scale = head_dim ** (-0.5)
    for pair in range(width // LANES):
        cols = slice(pair * LANES, (pair + 1) * LANES)
        do_pair = do[:, cols]
        q_pair, k_pair, v_pair = q_ref[rows, cols], k_ref[image, :, cols], v_ref[image, :, cols]
        dq, dk, dv = [], [], []
        for sub in range(2):
            mask = low if sub == 0 else jnp.logical_not(low)
            p_low = p_ref[2 * pair + sub]
            p = p_low.astype(F32)
            dp = nt(jnp.where(mask, do_pair, zero), v_pair)
            inner = jnp.sum(p * dp, axis=1, keepdims=True)
            ds = (p * (dp - inner)).astype(BF)
            dv.append(tn(p_low, do_pair))
            dk.append(tn(ds, q_pair))
            dq.append(nn(ds, k_pair))
        dq_ref[rows, cols] = (jnp.where(low, dq[0], dq[1]) * scale).astype(BF)
        dk_pair = jnp.where(low, dk[0], dk[1]).astype(BF)
        dv_pair = jnp.where(low, dv[0], dv[1]).astype(BF)
        for part in range(2):
            dk_ref[part, rows, cols] = dk_pair[part * half_pad : part * half_pad + half]
            dv_ref[part, rows, cols] = dv_pair[part * half_pad : part * half_pad + half]


def input_image(half, image, x_ref, dh_ref, dq_ref, dk_ref, dk_got, dv_ref, dv_got, vec, w_qkv, dx_ref, g_qkv, g_vec):
    width = x_ref.shape[1]
    rows = pl.ds(pl.multiple_of(image * half, 8), half)
    unit, inv_scale = normed(x_ref[rows, :].astype(F32))
    acts = (unit * vec[0:1, :] + vec[1:2, :]).astype(BF)
    dq = dq_ref[rows, :]
    dk = (dk_ref[0, rows, :].astype(F32) + dk_got[rows, :].astype(F32)).astype(BF)
    dv = (dv_ref[0, rows, :].astype(F32) + dv_got[rows, :].astype(F32)).astype(BF)
    da = jnp.zeros(unit.shape, F32)
    for at, piece in enumerate((dq, dk, dv)):
        cols = slice(at * width, (at + 1) * width)
        g_qkv[:, cols] += tn(acts, piece)
        da = da + nt(piece, w_qkv[:, :, cols].reshape(width, width))
    dx_ref[rows, :] = (dh_ref[rows, :] + norm_backward(da, unit, inv_scale, vec[0:1, :])).astype(BF)
    g_vec[0:1, :] += jnp.sum(da * unit, axis=0, keepdims=True)
    g_vec[1:2, :] += jnp.sum(da, axis=0, keepdims=True)
    g_vec[2:3, :] += jnp.sum(dq.astype(F32), axis=0, keepdims=True)
    g_vec[3:4, :] += jnp.sum(dv.astype(F32), axis=0, keepdims=True)


MESH = pl.DeviceIdType.MESH


def send(src, dst, sems, slot, device):
    copy = pltpu.make_async_remote_copy(
        src_ref=src, dst_ref=dst, send_sem=sems[0].at[slot], recv_sem=sems[1].at[slot],
        device_id=device, device_id_type=MESH,
    )
    copy.start()
    return copy


def remote_copy(src, dst, sems, slot, device):
    return pltpu.make_async_remote_copy(
        src_ref=src, dst_ref=dst, send_sem=sems[0].at[slot], recv_sem=sems[1].at[slot],
        device_id=device, device_id_type=MESH,
    )


def square(dp):
    return dp + 1 - 2 * lax.rem(dp, 2), lax.rem(dp + 2, 4)


def relay(ref, size, dp):
    side, across = square(dp)
    half = size // 2
    return (
        (ref.at[pl.ds(pl.multiple_of(across * size, size) + half, half)], side),
        (ref.at[pl.ds(pl.multiple_of(side * size, size), half)], across),
    )


def greet(devices):
    barrier = pltpu.get_barrier_semaphore()
    for device in devices:
        pl.semaphore_signal(barrier, inc=1, device_id=device, device_id_type=MESH)
    pl.semaphore_wait(barrier, len(devices))


def comm_call(body, name, number, ins, outs, scratch, flops=0, moved=0, vmem=56):
    return pl.pallas_call(
        body,
        name=name,
        in_specs=[pl.BlockSpec(memory_space=space) for space in ins],
        out_specs=[pl.BlockSpec(memory_space=space) for _, _, space in outs],
        out_shape=[jax.ShapeDtypeStruct(shape, dtype) for shape, dtype, _ in outs],
        scratch_shapes=list(scratch),
        cost_estimate=pl.CostEstimate(flops=int(flops), bytes_accessed=int(moved), transcendentals=0),
        compiler_params=pltpu.CompilerParams(
            vmem_limit_bytes=vmem * MIB, collective_id=number, has_side_effects=True
        ),
    )


def start_kernel(
    dps, groups, images, cap, cap_pad, x, w_qkv, w_out, w_router, vectors, b_in, b_back, routes, priority, key_mask,
    w_in, w_back, grad,
    qkv_all, out_all, router_rows, b_in_all, back_all, vec, slots,
    q_ref, k_ref, v_ref, p_ref, o_ref, h_ref, a_ref, in_all, in_kin, back_w_all, back_kin, grads,
    x_other, bias, router_all, vec_all, p_all, w_in_f, w_back_f, w_in_v, w_back_v,
    far_send, far_recv, near_send, near_recv, deep_send, deep_recv, w_s, w_r, local, rows_s, rows_r,
):
    dp, group, core = lax.axis_index("dp"), lax.axis_index("expert"), lax.axis_index("context")
    rows = w_qkv.shape[0]
    half = rows // 2
    hosted = groups // 2
    near = (dp, group, 1 - core)
    peers = [(lax.rem(dp + step, dps), group, core) for step in range(1, dps)]
    kin = [(dp, lax.rem(group + 2 * step, groups), core) for step in range(1, hosted)]
    loads = [
        pltpu.make_async_copy(w_in.at[core], w_in_f, local.at[0]),
        pltpu.make_async_copy(w_back.at[core], w_back_f, local.at[1]),
    ]
    for copy in loads:
        copy.start()
    mate = group + 1 - 2 * lax.rem(group, 2)
    across = (dp, mate, core)
    greet(peers + kin + [near, across])
    rows_out = [
        send(grad, grads.at[1], (rows_s, rows_r), 1, across),
        send(grad, grads.at[0], (rows_s, rows_r), 0, near),
    ]
    far, close, deep = (far_send, far_recv), (near_send, near_recv), (deep_send, deep_recv)
    waits = [send(x, x_other, close, 0, near)]
    qkv_all[dp] = w_qkv[...].astype(BF)
    own = pl.ds(pl.multiple_of(core * half, half), half)
    copies = []
    for step, peer in enumerate(peers):
        copies.append(send(qkv_all.at[dp, own], qkv_all.at[dp, own], far, step * 6, peer))
    out_all[dp] = w_out[...].astype(BF)
    router_all[dp] = w_router[...].astype(BF)
    vec_all[dp] = jnp.concatenate([vectors[...], jnp.zeros((1, rows), F32)], axis=0).astype(BF)
    b_in_all[0, dp] = b_in[...].astype(BF)
    back_all[0, dp] = b_back[...].astype(BF)
    for step, peer in enumerate(peers):
        copies.append(send(out_all.at[dp, own], out_all.at[dp, own], far, step * 6 + 1, peer))
    smalls, biases = [], []
    for step, peer in enumerate(peers):
        for at, ref in enumerate((router_all, vec_all)):
            smalls.append(send(ref.at[dp], ref.at[dp], far, step * 6 + 2 + at, peer))
        for at, ref in enumerate((b_in_all, back_all)):
            biases.append(send(ref.at[0, dp], ref.at[0, dp], far, step * 6 + 4 + at, peer))
    own_copies, direct = [], ([], [])
    for at, (wide, low, out, kin_out) in enumerate(
        ((w_in_f, w_in_v, in_all, in_kin), (w_back_f, w_back_v, back_w_all, back_kin))
    ):
        loads[at].wait()
        low[...] = wide[...].astype(BF)
        size = low.shape[0]
        part = pl.ds(pl.multiple_of(dp * size, size), size)
        for step, peer in enumerate(kin):
            own_copies.append(
                send(low, kin_out.at[hosted - 2 - step], (w_s, w_r), at * (dps + hosted) + dps + step, peer)
            )
        if dps == 4:
            for slot, target in enumerate(square(dp)):
                direct[at].append(
                    send(low, out.at[part], (w_s, w_r), at * (dps + hosted) + slot, (target, group, core))
                )
        else:
            for step, peer in enumerate(peers):
                own_copies.append(send(low, out.at[part], (w_s, w_r), at * (dps + hosted) + step, peer))
        here = pltpu.make_async_copy(low, out.at[part], local.at[2 + at])
        here.start()
        own_copies.append(here)

    def onward(at):
        out, size = ((in_all, w_in_v.shape[0]), (back_w_all, w_back_v.shape[0]))[at]
        return [
            remote_copy(ref, ref, (w_s, w_r), at * (dps + hosted) + 2 + slot, (target, group, core))
            for slot, (ref, target) in enumerate(relay(out, size, dp))
        ]

    def pass_on(at):
        for copy in direct[at]:
            copy.wait_recv()
        for copy in onward(at):
            copy.start()

    tokens = routes.shape[1]
    experts = w_router.shape[0]
    ids = iota((experts, tokens), 0)
    order = priority[...].astype(F32)
    high = jnp.floor(order * (1.0 / 256.0))
    parts = jnp.concatenate([high, order - 256.0 * high, jnp.zeros((6, tokens), F32)], axis=0).astype(BF)
    place = iota((8, LANES), 0)
    weight = jnp.where(place == 0, 256.0, jnp.where(place == 1, 1.0, 0.0)).astype(BF)
    column = tn(parts, weight)[:, 0:1]
    tied = jnp.logical_and(column == order, iota((tokens, 1), 0) < iota((1, tokens), 1))
    before = jnp.where(jnp.logical_or(column < order, tied), 1.0, 0.0).astype(BF)
    first = jnp.where(routes[0:1, :] == ids, 1.0, 0.0)
    second = jnp.where(routes[1:2, :] == ids, 1.0, 0.0)
    count = jnp.sum(first, axis=1, keepdims=True)
    rank_first = jnp.sum(nn(first.astype(BF), before) * first, axis=0, keepdims=True)
    rank_second = jnp.sum((nn(second.astype(BF), before) + count) * second, axis=0, keepdims=True)
    ranks = jnp.concatenate([rank_first, rank_second], axis=0).astype(I32)
    owned = jnp.where(ranks < cap, routes[...] * cap_pad + ranks, -1)
    slots[...] = jnp.concatenate([owned, jnp.full((6, tokens), -1, I32)], axis=0)

    for copy in biases:
        copy.wait()
    for step, peer in enumerate(kin):
        for at, ref in enumerate((b_in_all, back_all)):
            waits.append(send(ref.at[0], ref.at[hosted - 1 - step], deep, 2 * step + at, peer))
    for at, copy in enumerate(copies):
        step, ref = at % len(peers), (qkv_all, out_all)[at // len(peers)]
        copy.wait()
        source = lax.rem(dp - step - 1 + dps, dps)
        waits.append(send(ref.at[source, own], ref.at[source, own], close, 1 + at, near))
    for copy in smalls:
        copy.wait()
    vec[...] = jnp.concatenate([vec_all[at].astype(F32) for at in range(dps)], axis=1)
    router_rows[...] = jnp.concatenate([router_all[at].astype(F32) for at in range(dps)], axis=1).astype(BF)
    for copy in waits:
        copy.wait()

    half = tokens // images
    mask = jnp.where(key_mask[...] > 0, 0.0, -1e30)
    first, second = mask[:, :half], mask[:, half:]
    gap = bias.shape[2] // 2 - half
    for part in range(2):
        bias_part = jnp.where(core == part, first, second)
        for image in range(images):
            bias[image, :, part * (half + gap) : part * (half + gap) + half] = bias_part[image : image + 1]
            if gap:
                bias[image, :, part * (half + gap) + half : (part + 1) * (half + gap)] = jnp.full((1, gap), -1e30, F32)

    def image_step(image, _):
        forward_image(
            half, image, dps, x, x_other, bias, vec, qkv_all, out_all, q_ref, k_ref, v_ref, p_all, o_ref, h_ref, a_ref
        )
        pltpu.make_async_copy(p_all.at[image], p_ref.at[image], local.at[4]).start()
        if dps == 4:

            @pl.when(image == images - 2)
            def _():
                pass_on(0)

        return 0

    lax.fori_loop(0, images, image_step, 0)
    if dps == 4:
        pass_on(1)
    rows_out[0].wait()
    rows_out[0] = send(grads.at[1], grads.at[2], (rows_s, rows_r), 2, near)
    pltpu.make_async_copy(p_all, p_ref, local.at[4]).wait()
    for copy in rows_out:
        copy.wait()
    for copy in own_copies:
        copy.wait()
    if dps == 4:
        for at in range(2):
            for copy in direct[at]:
                copy.wait_send()
            for copy in onward(at):
                copy.wait()


def back_kernel(
    dps, groups, images, grad, back_rows, h_ref, o_ref, vec, w_out, q_ref, k_ref, v_ref, x_ref, w_qkv,
    g_router, g_in, g_back, b_in, b_back, mixed, p_all, in_other, back_other, far_rows,
    dx_ref, output, o_qkv, o_out, o_router, o_vec, o_in, o_back, w_in_sum, w_back_sum, in_recv, back_recv,
    sum_in, sum_back, p_two, dh_ref, dq_ref, dk_ref, dv_ref, dk_got, dv_got, g_out, g_qkv, g_vec,
    in_stage, back_stage, in_to, back_to, in_from, back_from,
    near_out, near_in, far_out, far_in, deep_in, deep_out, deep_all, total,
    small_near, small_far, small_got, small_deep, bin_near, bin_far, bin_got, bin_deep,
    got_rows, near_s, near_r, far_s, far_r, deep_s, deep_r, last_s, last_r,
    rows_s, rows_r, p_sem, d_s, d_r, e_s, e_r, stage_sem, kin_s, kin_r, home_s, home_r, home_sem,
):
    dp, group, core = lax.axis_index("dp"), lax.axis_index("expert"), lax.axis_index("context")
    tokens, width = dx_ref.shape
    hosted = groups // 2
    token_half = tokens // images
    rows = width // dps
    half = rows // 2
    near = (dp, group, 1 - core)
    peers = [(lax.rem(dp + step, dps), group, core) for step in range(1, dps)]
    others = [(dp, lax.rem(group + step, groups), core) for step in range(1, groups)]

    def remote(src, dst, sems, slot, target):
        return pltpu.make_async_remote_copy(
            src_ref=src, dst_ref=dst, send_sem=sems[0].at[slot], recv_sem=sems[1].at[slot],
            device_id=target, device_id_type=MESH,
        )

    sets = (
        (back_other, back_recv, back_stage, back_to, back_from, g_back, w_back_sum),
        (in_other, in_recv, in_stage, in_to, in_from, g_in, w_in_sum),
    )

    def sum_out(which, part, at, step):
        other, recv = sets[which][:2]
        size = recv.shape[2]
        piece = size // 2
        target = lax.rem(dp + step, dps)
        src = other.at[at, pl.ds(pl.multiple_of(target * size, size) + part * piece, piece)]
        dst = recv.at[at, step - 1, pl.ds(part * piece, piece)]
        slot = ((which * 2 + part) * (hosted - 1) + at) * dps + step
        return remote(src, dst, (e_s, e_r), slot, peers[step - 1])

    def piece_out(which, part, at, kind):
        other, recv, stage = sets[which][:3]
        size = recv.shape[2]
        piece = size // 2
        side, over = square(dp)
        corner = lax.rem(side + 2, 4)
        share = (corner, side, over)[kind]
        via = (over if part == 0 else side, side, over)[kind]
        place = (2, 0, 1)[kind]
        if kind == part + 1:
            src = stage.at[2 + part]
        else:
            src = other.at[at, pl.ds(pl.multiple_of(share * size, size) + part * piece, piece)]
        dst = recv.at[at, place, pl.ds(part * piece, piece)]
        slot = ((which * 2 + part) * (hosted - 1) + at) * dps + kind
        return remote(src, dst, (e_s, e_r), slot, (via, group, core))

    def at_once(which):
        for at in range(hosted - 1):
            for part, kind in ((0, 0), (1, 0), (1, 1), (0, 2)):
                piece_out(which, part, at, kind).start()

    def relayed(which):
        other, recv, stage = sets[which][:3]
        size = recv.shape[2]
        piece = size // 2
        for at in range(hosted - 1):
            for part in range(2):
                here = pl.ds(part * piece, piece)
                share = square(dp)[part]
                piece_out(which, part, at, 0).wait_recv()
                own = other.at[at, pl.ds(pl.multiple_of(share * size, size) + part * piece, piece)]
                copies = (
                    pltpu.make_async_copy(recv.at[at, 2, here], stage.at[0], stage_sem.at[0]),
                    pltpu.make_async_copy(own, stage.at[1], stage_sem.at[1]),
                )
                for copy in copies:
                    copy.start()
                for copy in copies:
                    copy.wait()
                if at:
                    piece_out(which, part, at - 1, part + 1).wait_send()
                stage[2 + part] = (stage[0].astype(F32) + stage[1].astype(F32)).astype(BF)
                piece_out(which, part, at, part + 1).start()

    def home_out(which, part, at):
        to, back = sets[which][3:5]
        piece = to.shape[1] // 2
        here = pl.ds(part * piece, piece)
        target = (dp, lax.rem(group + 2 * (at + 1), groups), core)
        slot = (which * 2 + part) * (hosted - 1) + at
        return pltpu.make_async_remote_copy(
            src_ref=to.at[at, here], dst_ref=back.at[hosted - 2 - at, here],
            send_sem=kin_s.at[slot], recv_sem=kin_r.at[(which * 2 + part) * (hosted - 1) + hosted - 2 - at],
            device_id=target, device_id_type=MESH,
        )

    def home_in(which, part, at):
        to, back = sets[which][3:5]
        piece = to.shape[1] // 2
        here = pl.ds(part * piece, piece)
        slot = (which * 2 + part) * (hosted - 1) + at
        return pltpu.make_async_remote_copy(
            src_ref=to.at[at, here], dst_ref=back.at[at, here], send_sem=kin_s.at[slot], recv_sem=kin_r.at[slot],
            device_id=near, device_id_type=MESH,
        )

    def send_home(which, part):
        other, recv, stage, to = sets[which][:4]
        size = recv.shape[2]
        piece = size // 2
        here = pl.ds(part * piece, piece)
        count = 2 if dps == 4 else dps - 1
        if dps == 4 and part == 0:
            for side in range(2):
                piece_out(which, side, hosted - 2, side + 1).wait_send()
        for at in range(hosted - 1):
            if dps == 4:
                for kind in (1, 2):
                    piece_out(which, part, at, kind).wait_recv()
            else:
                for step in range(1, dps):
                    sum_out(which, part, at, step).wait_recv()
            own = other.at[at, pl.ds(pl.multiple_of(dp * size, size) + part * piece, piece)]
            copies = (
                pltpu.make_async_copy(recv.at[at, pl.ds(0, count), here], stage.at[pl.ds(0, count)], stage_sem.at[0]),
                pltpu.make_async_copy(own, stage.at[count], stage_sem.at[1]),
            )
            for copy in copies:
                copy.start()
            for copy in copies:
                copy.wait()
            value = stage[0].astype(F32)
            for step in range(count):
                value = value + stage[step + 1].astype(F32)
            to[at, here, :] = value.astype(BF)
            home_out(which, part, at).start()

    def load(image):
        slot = lax.rem(image, 2)
        return pltpu.make_async_copy(p_all.at[image], p_two.at[slot], p_sem.at[slot])

    def swap(image, which):
        here = pl.ds(pl.multiple_of(image * token_half, 8), token_half)
        src, dst = ((dk_ref, dk_got), (dv_ref, dv_got))[which]
        return remote(src.at[1, here], dst.at[here], (d_s, d_r), 2 * image + which, near)

    load(0).start()
    greet(peers + others + [near])
    if dps == 4:
        at_once(0)
    else:
        for which in range(2):
            for part in range(2):
                for at in range(hosted - 1):
                    for step in range(1, dps):
                        sum_out(which, part, at, step).start()
    mate = group + 1 - 2 * lax.rem(group, 2)
    rows_out = send(far_rows, got_rows, (rows_s, rows_r), 0, (dp, mate, core))
    g_out[...] = jnp.zeros_like(g_out)
    g_qkv[...] = jnp.zeros_like(g_qkv)
    g_vec[...] = jnp.zeros_like(g_vec)

    def back_step(image, _):
        load(image).wait()

        @pl.when(image + 1 < images)
        def _():
            load(image + 1).start()

        backward_image(
            token_half, image, grad, back_rows, h_ref, o_ref, vec, w_out, q_ref, k_ref, v_ref,
            p_two.at[lax.rem(image, 2)], dh_ref, dq_ref, dk_ref, dv_ref, g_out, g_vec,
        )
        swap(image, 0).start()
        swap(image, 1).start()

        if dps == 4:

            @pl.when(image == 0)
            def _():
                relayed(0)
                at_once(1)

        @pl.when(image == images - 2)
        def _():
            send_home(0, 0)
            send_home(0, 1)

        return 0

    lax.fori_loop(0, images, back_step, 0)
    if dps == 4:
        relayed(1)

    near_sems, far_sems, deep_sems, last_sems = (near_s, near_r), (far_s, far_r), (deep_s, deep_r), (last_s, last_r)
    sources = [(g_out, 0)] + [(g_qkv, at) for at in range(0, g_qkv.shape[1], width)]
    theirs = pl.multiple_of((1 - core) * half, half)
    ours = pl.multiple_of(core * half, half)

    def cols_of(at):
        return pl.ds(width * at, width)

    def to_core(at):
        ref, lane = sources[at]
        for block in range(dps):
            near_out[block, :, cols_of(at)] = ref[pl.ds(block * rows + theirs, half), lane : lane + width].astype(BF)
        return send(near_out.at[:, :, cols_of(at)], near_in.at[:, :, cols_of(at)], near_sems, 2 + at, near)

    first = [to_core(0)]

    def input_step(image, _):
        swap(image, 0).wait_recv()
        swap(image, 1).wait_recv()
        input_image(
            token_half, image, x_ref, dh_ref, dq_ref, dk_ref, dk_got, dv_ref, dv_got, vec, w_qkv, dx_ref, g_qkv, g_vec
        )
        return 0

    lax.fori_loop(0, images, input_step, 0)
    for at in range(1, len(sources)):
        first.append(to_core(at))

    deep = small_near.shape[2]
    tall = 2 * hosted
    router = 8 + tall
    bias_rows = [b_back[at // 2, at % 2] for at in range(tall)]
    bias_in = jnp.concatenate([b_in[at // 2, at % 2] for at in range(tall)], axis=0)
    small = [g_vec[...]] + bias_rows + [g_router[...]]
    spare = deep - router - g_router.shape[0]
    small = jnp.concatenate(small + ([jnp.zeros((spare, width), F32)] if spare else []), axis=0)
    for at in range(dps):
        small_near[0, at] = small[:, at * rows : (at + 1) * rows]
        bin_near[0, at] = bias_in[:, at * bin_near.shape[3] : (at + 1) * bin_near.shape[3]]
    firsts = [
        send(small_near.at[0], small_near.at[1], near_sems, 0, near),
        send(bin_near.at[0], bin_near.at[1], near_sems, 1, near),
    ]
    send_home(1, 0)
    send_home(1, 1)
    second = []
    for at, (ref, lane) in enumerate(sources):
        cols = cols_of(at)
        first[at].wait()
        for step, peer in enumerate(peers):
            target = lax.rem(dp + step + 1, dps)
            block = ref[pl.ds(pl.multiple_of(target * rows, rows) + ours, half), lane : lane + width]
            far_out[step, :, cols] = (block + near_in[target, :, cols].astype(F32)).astype(BF)
            second.append(
                send(far_out.at[step, :, cols], far_in.at[step, :, cols], far_sems, (2 + at) * dps + step, peer)
            )
    for copy in firsts:
        copy.wait()
    small_far[...] = small_near[0] + small_near[1]
    bin_far[...] = bin_near[0] + bin_near[1]
    smalls = []
    for step, peer in enumerate(peers):
        target = lax.rem(dp + step + 1, dps)
        smalls.append(send(small_far.at[target], small_got.at[step], far_sems, step, peer))
        smalls.append(send(bin_far.at[target], bin_got.at[step], far_sems, dps + step, peer))
    third = []
    few = half // groups
    split = few % 16 == 0
    for at, (ref, lane) in enumerate(sources):
        cols = cols_of(at)
        mine = ref[pl.ds(pl.multiple_of(dp * rows, rows) + ours, half), lane : lane + width]
        mine = mine + near_in[dp, :, cols].astype(F32)
        for step in range(dps - 1):
            second[at * (dps - 1) + step].wait()
            mine = mine + far_in[step, :, cols].astype(F32)
        if split:
            deep_out[:, cols] = mine.astype(BF)
            deep_in[group, :few, cols] = deep_out[pl.ds(pl.multiple_of(group * few, few), few), cols]
            for step, peer in enumerate(others):
                to = pl.multiple_of(lax.rem(group + step + 1, groups) * few, few)
                src = deep_out.at[pl.ds(to, few), cols]
                third.append(send(src, deep_in.at[group, pl.ds(0, few), cols], deep_sems, at * groups + step, peer))
        else:
            deep_in[group, :, cols] = mine.astype(BF)
            for step, peer in enumerate(others):
                part = deep_in.at[group, :, cols]
                third.append(send(part, part, deep_sems, at * groups + step, peer))
    for copy in smalls:
        copy.wait()
    lone = small_far[dp]
    lone_in = bin_far[dp]
    for step in range(dps - 1):
        lone = lone + small_got[step]
        lone_in = lone_in + bin_got[step]
    small_deep[group] = lone
    bin_deep[group] = lone_in
    deep_small = []
    for step, peer in enumerate(others):
        slot = len(sources) * groups + step
        deep_small.append(send(small_deep.at[group], small_deep.at[group], deep_sems, slot, peer))
        deep_small.append(send(bin_deep.at[group], bin_deep.at[group], deep_sems, groups + slot, peer))
    last, fourth = [], []
    here = pl.ds(ours, half)
    for at in range(len(sources) if split else 0):
        cols = cols_of(at)
        for step in range(groups - 1):
            third[at * (groups - 1) + step].wait()
        done = deep_in[0, :few, cols].astype(F32)
        for source in range(1, groups):
            done = done + deep_in[source, :few, cols].astype(F32)
        part = deep_all.at[pl.ds(pl.multiple_of(group * few, few), few), cols]
        part[...] = done.astype(BF)
        for step, peer in enumerate(others):
            fourth.append(send(part, part, deep_sems, (6 + at) * groups + step, peer))
    rows_out.wait()
    output[...] = (mixed[...] + got_rows[...].astype(F32)).astype(BF)
    for at in range(len(sources)):
        cols = cols_of(at)
        if split:
            for step in range(groups - 1):
                fourth[at * (groups - 1) + step].wait()
            done = deep_all[:, cols].astype(F32)
        else:
            for step in range(groups - 1):
                third[at * (groups - 1) + step].wait()
            done = deep_in[0, :, cols].astype(F32)
            for source in range(1, groups):
                done = done + deep_in[source, :, cols].astype(F32)
        total[here, cols] = done
        last.append(send(total.at[here, cols], total.at[here, cols], last_sems, at, near))
    for copy in deep_small:
        copy.wait()
    lone = small_deep[0]
    for at in range(1, groups):
        lone = lone + small_deep[at]
    o_vec[...] = lone[0:7]
    o_router[...] = lone[router : router + o_router.shape[0]]
    grad_in, grad_back = jnp.zeros(o_in.shape, F32), jnp.zeros(o_back.shape, F32)
    for at in range(groups):
        away = lax.rem(group - at + groups, groups)
        kin = lax.rem(away, 2) == 0
        pick_in, pick_back = jnp.zeros(o_in.shape, F32), jnp.zeros(o_back.shape, F32)
        for which in range(hosted):
            found = away // 2 == which
            pick_in = jnp.where(found, bin_deep[at, 2 * which : 2 * which + 2], pick_in)
            pick_back = jnp.where(found, small_deep[at, 8 + 2 * which : 10 + 2 * which], pick_back)
        grad_in = grad_in + jnp.where(kin, pick_in, 0.0)
        grad_back = grad_back + jnp.where(kin, pick_back, 0.0)
    o_in[...] = grad_in
    o_back[...] = grad_back
    for copy in last:
        copy.wait()
    o_qkv[...] = total[:, width : 4 * width]
    o_out[...] = total[:, :width]

    stores = []
    for which, (_, _, _, to, back, own, out) in enumerate(sets):
        for part in range(2):
            for at in range(hosted - 1):
                home_in(which, part, at).wait_recv()
        value = own[...]
        for at in range(hosted - 1):
            value = value + back[at].astype(F32)
        whole = (sum_back, sum_in)[which]
        whole[...] = value
        stores.append(send(whole, out.at[core], (home_s, home_r), which, near))
        copy = pltpu.make_async_copy(whole, out.at[core], home_sem.at[which])
        copy.start()
        stores.append(copy)
    for which in range(2):
        for part in range(2):
            for at in range(hosted - 1):
                home_out(which, part, at).wait_send()
                if dps == 4:
                    for kind in (0, 2 - part):
                        piece_out(which, part, at, kind).wait_send()
                else:
                    for step in range(1, dps):
                        sum_out(which, part, at, step).wait_send()
    for image in range(images):
        for which in range(2):
            swap(image, which).wait_send()
    for copy in stores:
        copy.wait()


def hand_over_kernel(count, *refs):
    given, kept, held, (loads, stores) = refs[:count], refs[count : 2 * count], refs[2 * count : 3 * count], refs[3 * count :]
    ins = [pltpu.make_async_copy(given[at], held[at], loads.at[at]) for at in range(count)]
    outs = [pltpu.make_async_copy(held[at], kept[at], stores.at[at]) for at in range(count)]
    for copy in ins:
        copy.start()
    for at in range(count):
        ins[at].wait()
        outs[at].start()
    for copy in outs:
        copy.wait()


def hand_over(arrays):
    return pl.pallas_call(
        partial(hand_over_kernel, len(arrays)),
        name="hand_over",
        in_specs=[pl.BlockSpec(memory_space=pl.ANY)] * len(arrays),
        out_specs=[pl.BlockSpec(memory_space=pl.ANY)] * len(arrays),
        out_shape=[jax.ShapeDtypeStruct(array.shape, array.dtype) for array in arrays],
        scratch_shapes=[pltpu.VMEM(array.shape, array.dtype) for array in arrays]
        + [pltpu.SemaphoreType.DMA((len(arrays),))] * 2,
        compiler_params=pltpu.CompilerParams(vmem_limit_bytes=63 * MIB),
    )(*arrays)


def shards(
    inputs, key_mask, routes, priority, vectors, w_qkv, w_out, w_router, w_in, b_in, w_back, b_back, cotangent
):
    images, half, width = inputs.shape
    tokens = images * half
    groups = lax.axis_size("expert")
    dps = lax.axis_size("dp")
    per_device = w_in.shape[0]
    experts = groups * per_device
    ff = w_in.shape[2]
    cap = max(2, 3 * tokens // experts)
    cap_pad = up(cap, 16)
    half_pad = up(half, 16)
    hosted = groups // 2
    V, A = pltpu.VMEM, pl.ANY
    dma = pltpu.SemaphoreType.DMA
    rows = w_qkv.shape[0]
    rows_back = ff // dps

    x = inputs.reshape(tokens, width)
    grad = cotangent.reshape(tokens, width)
    route_rows = routes.reshape(tokens, 2).T

    keys_pad = 2 * half_pad

    made = comm_call(
        partial(start_kernel, dps, groups, images, cap, cap_pad),
        "front",
        0,
        [V] * 10 + [A] * 3,
        [
            ((dps, rows, 3 * width), BF, V),
            ((dps, rows, width), BF, V),
            ((experts, width), BF, V),
            ((hosted, dps, per_device, rows_back), BF, V),
            ((hosted, dps, per_device, rows), BF, V),
            ((8, width), F32, V),
            ((8, tokens), I32, V),
            ((tokens, width), BF, V),
            ((images, keys_pad, width), BF, V),
            ((images, keys_pad, width), BF, V),
            ((images, HEADS, half, keys_pad), BF, A),
            ((tokens, width), BF, V),
            ((tokens, width), F32, V),
            ((tokens, width), BF, V),
            ((width, ff), BF, A),
            ((hosted - 1, rows, ff), BF, A),
            ((ff, width), BF, A),
            ((hosted - 1, rows_back, width), BF, A),
            ((3, tokens, width), BF, A),
        ],
        [
            pltpu.VMEM((tokens, width), BF),
            pltpu.VMEM((images, 1, keys_pad), F32),
            pltpu.VMEM((dps, experts, rows), BF),
            pltpu.VMEM((dps, 8, rows), BF),
            pltpu.VMEM((images, HEADS, half, keys_pad), BF),
            pltpu.VMEM((rows, ff), F32),
            pltpu.VMEM((rows_back, width), F32),
            pltpu.VMEM((rows, ff), BF),
            pltpu.VMEM((rows_back, width), BF),
        ]
        + [dma((6 * (dps - 1),))] * 2
        + [dma((1 + 2 * (dps - 1),))] * 2
        + [dma((2 * hosted,))] * 2
        + [dma((2 * (dps + hosted),))] * 2
        + [dma((5,))]
        + [dma((3,))] * 2,
        flops=2 * tokens * width * (8 * width + 4 * keys_pad),
        moved=40 * tokens * width,
    )(x, w_qkv, w_out, w_router.T, vectors, b_in, b_back, route_rows, priority.reshape(1, tokens), key_mask, w_in, w_back, grad)
    qkv_all, out_all, router_rows, b_ins, b_backs, vec, slots, q, k, v, p, o, after, acts, *expert_w, grads = made

    rows_all = 4 * cap_pad
    deep = hosted * cap_pad
    made = comm_call(
        partial(experts_kernel, groups, dps, images, cap_pad),
        "experts",
        2,
        [A, A, V, V, V, V, V, V] + [A] * 5,
        [
            ((tokens, width), F32, V),
            ((tokens, width), F32, V),
            ((tokens, width), BF, V),
            ((experts, width), F32, V),
            ((rows, ff), F32, V),
            ((rows_back, width), F32, V),
            ((hosted - 1, width, ff), BF, A),
            ((hosted - 1, ff, width), BF, A),
            ((hosted, 2, 1, ff), F32, V),
            ((hosted, 2, 1, width), F32, V),
            ((hosted - 1, width, ff), BF, A),
            ((hosted - 1, ff, width), BF, A),
        ],
        [
            pltpu.VMEM((2, 4, tokens, width), BF),
            pltpu.VMEM((4, 8, tokens), F32),
            pltpu.VMEM((4, deep, 2 * width), BF),
            pltpu.VMEM((width, ff), BF),
            pltpu.VMEM((ff, width), BF),
            pltpu.VMEM((dps, rows_all, rows), BF),
            pltpu.VMEM((rows_all, ff), BF),
            pltpu.VMEM((rows_all, ff), BF),
            pltpu.VMEM((rows_all, width), BF),
            pltpu.VMEM((cap_pad, ff), BF),
            pltpu.VMEM((dps, rows, ff), BF),
            pltpu.VMEM((dps - 1, rows, ff), BF),
            pltpu.VMEM((dps, rows_back, width), BF),
            pltpu.VMEM((dps - 1, rows_back, width), BF),
            pltpu.VMEM((4, hosted, 1, tokens), F32),
            pltpu.VMEM((3, hosted, 1, tokens), F32),
            pltpu.VMEM((4, tokens, width), BF),
            pltpu.VMEM((4, tokens, width), BF),
            pltpu.VMEM((tokens, width), BF),
            pltpu.VMEM((tokens, width), BF),
            pltpu.VMEM((tokens, LANES), F32),
            dma((6,)),
            dma((6,)),
            dma((2 * dps,)),
            dma((2 * dps,)),
            dma((2 * dps,)),
            dma((9,)),
            dma((9,)),
            dma((2 * dps,)),
            dma((3,)),
            dma((2 * hosted * dps,)),
            dma((2 * hosted * dps,)),
        ],
        flops=14 * hosted * rows_all * width * ff,
        moved=20 * tokens * width + 8 * hosted * width * ff,
        vmem=63,
    )(acts, grad, after, router_rows, route_rows, slots, b_ins, b_backs, *expert_w, grads)
    back_rows, mixed, far_rows, g_router, g_in, g_back, g_in_other, g_back_other, g_b_in, g_b_back, *_ = made

    wide = 4 * width
    halves_of = rows // 2
    small = up(8 + 2 * hosted + experts, 8)
    kin_slots = 4 * (hosted - 1)
    made = comm_call(
        partial(back_kernel, dps, groups, images),
        "back",
        1,
        [V] * 17 + [A] * 4,
        [
            ((tokens, width), BF, V),
            ((tokens, width), BF, V),
            ((rows, 3 * width), F32, V),
            ((rows, width), F32, V),
            ((experts, rows), F32, V),
            ((7, rows), F32, V),
            ((per_device, rows_back), F32, V),
            ((per_device, rows), F32, V),
            (w_in.shape, F32, A),
            (w_back.shape, F32, A),
            ((hosted - 1, dps - 1, rows, ff), BF, A),
            ((hosted - 1, dps - 1, rows_back, width), BF, A),
        ],
        [
            pltpu.VMEM((rows, ff), F32),
            pltpu.VMEM((rows_back, width), F32),
            pltpu.VMEM((2, HEADS, half, keys_pad), BF),
            pltpu.VMEM((tokens, width), F32),
            pltpu.VMEM((tokens, width), BF),
            pltpu.VMEM((2, tokens, width), BF),
            pltpu.VMEM((2, tokens, width), BF),
            pltpu.VMEM((tokens, width), BF),
            pltpu.VMEM((tokens, width), BF),
            pltpu.VMEM((width, width), F32),
            pltpu.VMEM((width, 3 * width), F32),
            pltpu.VMEM((8, width), F32),
            pltpu.VMEM((dps, rows // 2, ff), BF),
            pltpu.VMEM((dps, rows_back // 2, width), BF),
            pltpu.VMEM((hosted - 1, rows, ff), BF),
            pltpu.VMEM((hosted - 1, rows_back, width), BF),
            pltpu.VMEM((hosted - 1, rows, ff), BF),
            pltpu.VMEM((hosted - 1, rows_back, width), BF),
            pltpu.VMEM((dps, halves_of, wide), BF),
            pltpu.VMEM((dps, halves_of, wide), BF),
            pltpu.VMEM((dps - 1, halves_of, wide), BF),
            pltpu.VMEM((dps - 1, halves_of, wide), BF),
            pltpu.VMEM((groups, halves_of, wide), BF),
            pltpu.VMEM((halves_of, wide), BF),
            pltpu.VMEM((halves_of, wide), BF),
            pltpu.VMEM((rows, wide), F32),
            pltpu.VMEM((2, dps, small, rows), F32),
            pltpu.VMEM((dps, small, rows), F32),
            pltpu.VMEM((dps - 1, small, rows), F32),
            pltpu.VMEM((groups, small, rows), F32),
            pltpu.VMEM((2, dps, 2 * hosted, rows_back), F32),
            pltpu.VMEM((dps, 2 * hosted, rows_back), F32),
            pltpu.VMEM((dps - 1, 2 * hosted, rows_back), F32),
            pltpu.VMEM((groups, 2 * hosted, rows_back), F32),
            pltpu.VMEM((tokens, width), BF),
            dma((6,)), dma((6,)), dma((6 * dps,)), dma((6 * dps,)),
            dma((10 * groups,)), dma((10 * groups,)), dma((4,)), dma((4,)), dma((1,)), dma((1,)),
            dma((2,)), dma((2 * images,)), dma((2 * images,)), dma((kin_slots * dps,)), dma((kin_slots * dps,)),
            dma((2,)), dma((kin_slots,)), dma((kin_slots,)), dma((2,)), dma((2,)), dma((2,)),
        ],
        flops=2 * tokens * width * (8 * width + 8 * keys_pad),
        moved=60 * tokens * width,
        vmem=62,
    )(
        grad, back_rows, after, o, vec, out_all, q, k, v, x, qkv_all, g_router, g_in, g_back, g_b_in, g_b_back, mixed,
        p, g_in_other, g_back_other, far_rows,
    )
    dx, output, grad_qkv, grad_out, grad_router, grad_vec, grad_b_in, grad_b_back, grad_w_in, grad_w_back, *_ = made
    passed = hand_over([output, dx, grad_router, grad_vec, grad_qkv, grad_out, grad_w_in, grad_b_in, grad_w_back, grad_b_back])
    output, dx, grad_router, grad_vec, grad_qkv, grad_out, grad_w_in, grad_b_in, grad_w_back, grad_b_back = passed
    return (
        output.reshape(images, half, width),
        dx.reshape(images, half, width),
        grad_vec,
        grad_qkv,
        grad_out,
        grad_router.T,
        grad_w_in,
        grad_b_in,
        grad_w_back,
        grad_b_back,
    )


def solution(mesh):
    tokens = P(("dp", "expert"), "context", None)
    by_rows = P("dp", None)
    experts = P("expert", "dp", None)
    expert_bias = P("expert", "dp")
    return jax.shard_map(
        shards,
        mesh=mesh,
        in_specs=(
            tokens,
            P(("dp", "expert"), None),
            P(("dp", "expert"), "context", None, None),
            tokens,
            P(None, "dp"),
            by_rows,
            by_rows,
            by_rows,
            experts,
            expert_bias,
            experts,
            expert_bias,
            tokens,
        ),
        out_specs=(
            tokens,
            tokens,
            P(None, "dp"),
            by_rows,
            by_rows,
            by_rows,
            experts,
            expert_bias,
            experts,
            expert_bias,
        ),
        check_vma=False,
    )
```
